32 devices in a mesh: fsdp: 8 (over y, x, core), seq: 4 (over z).
Axes of the slice: x: 2, y: 2, z: 4, core: 2. Of those that a mesh axis runs over, the one named last changes fastest.
Arguments:
- inputs: float32 [8, 3072, 768], P('fsdp', 'seq'), may hold values from -6 to 6
- conditioning: float32 [8, 128], P('fsdp'), may hold values from -6 to 6
- cotangent: float32 [8, 3072, 768], P('fsdp', 'seq'), may hold values from -6 to 6
- attn_gain: float32 [768], P('fsdp'), may hold values from 0.25 to 1.75
- mlp_gain: float32 [768], P('fsdp'), may hold values from 0.25 to 1.75
- qkv_weight: float32 [768, 2304], P('fsdp'), may hold values from -0.21875 to 0.21875
- out_weight: float32 [768, 768], P('fsdp'), may hold values from -3 to 3
- up_weight: float32 [768, 3072], P('fsdp'), may hold values from -0.21875 to 0.21875
- up_bias: float32 [3072], P('fsdp'), may hold values from -3 to 3
- down_weight: float32 [3072, 768], P('fsdp'), may hold values from -0.109375 to 0.109375
- down_bias: float32 [768], P('fsdp'), may hold values from -3 to 3
- mod_weight: float32 [128, 4608], P(None, 'fsdp'), may hold values from -0.375 to 0.375
- mod_bias: float32 [4608], P('fsdp'), may hold values from -2 to 2
Outputs:
- output: float32 [8, 3072, 768], P('fsdp', 'seq')
- inputs_grad: float32 [8, 3072, 768], P('fsdp', 'seq')
- conditioning_grad: float32 [8, 128], P('fsdp')
- attn_gain_grad: float32 [768], P('fsdp')
- mlp_gain_grad: float32 [768], P('fsdp')
- qkv_weight_grad: float32 [768, 2304], P('fsdp')
- out_weight_grad: float32 [768, 768], P('fsdp')
- up_weight_grad: float32 [768, 3072], P('fsdp')
- up_bias_grad: float32 [3072], P('fsdp')
- down_weight_grad: float32 [3072, 768], P('fsdp')
- down_bias_grad: float32 [768], P('fsdp')
- mod_weight_grad: float32 [128, 4608], P(None, 'fsdp')
- mod_bias_grad: float32 [4608], P('fsdp')
The draws below stay inside these ranges and needn't reach their ends.
All inputs are finite; a program needn't handle non-finite values.
Results may differ from the reference program's by a relative error of at most 0.015.
The reference program's roundings to bfloat16 on the way count: a program that leaves them out, or rounds other values in their place, can miss the bound.
Values may be sent and summed in bfloat16 or wider, within the bound.
A program may use at most 192 MiB of HBM per device.

```python
import math
import jax
import jax.numpy as jnp
from jax import lax

H = 12
HD = 64
FF = 3072
CD = 128
D = 768
LENGTH = 3072
BATCH = 8


def block_scale(key, shape, cuts, low, high):
    gain = 1.0
    for dim, shards_of in cuts:
        steps = jax.random.uniform(jax.random.fold_in(jax.random.fold_in(key, 6), dim), (shards_of,), jnp.float32, low / len(cuts), high / len(cuts))
        gain = gain * jnp.repeat(jnp.exp(steps), shape[dim] // shards_of).reshape((-1,) + (1,) * (len(shape) - 1 - dim))
    return gain


def centred(own_key, dims, width, most, cuts=(), kind=jnp.bfloat16):
    result = jax.random.normal(own_key, dims, jnp.float32) * width
    if len(cuts) > 0:
        result = block_scale(own_key, dims, cuts, -0.22, 0.18) * result
    return jnp.clip(result, min=-most, max=most).astype(kind)


def setup_inputs(seed: int = 0) -> dict:
    splits = jax.random.split(jax.random.key(seed), 14)
    return {
        "inputs": centred(splits[0], (BATCH, LENGTH, D), 1.0, 6.0, ((0, 8), (1, 4)), jnp.float32),
        "conditioning": centred(splits[1], (BATCH, CD), 1.0, 6.0, ((0, 8),), jnp.float32),
        "cotangent": centred(splits[2], (BATCH, LENGTH, D), 1.0, 6.0, ((0, 8), (1, 4)), jnp.float32),
        "attn_gain": jnp.clip(1.0 + 0.15 * jax.random.normal(splits[3], (D,), jnp.float32), 0.25, 1.75),
        "mlp_gain": jnp.clip(1.0 + 0.15 * jax.random.normal(splits[4], (D,), jnp.float32), 0.25, 1.75),
        "qkv_weight": centred(splits[5], (D, 3 * D), D ** -0.5, 0.21875, ((0, 8),), jnp.float32),
        "out_weight": centred(splits[6], (D, D), (max(1, D * 16 // LENGTH)) ** -0.5, 3.0, ((0, 8),), jnp.float32),
        "up_weight": centred(splits[7], (D, FF), D ** -0.5, 0.21875, ((0, 8),), jnp.float32),
        "up_bias": centred(splits[8], (FF,), 0.5, 3.0, ((0, 8),), jnp.float32),
        "down_weight": centred(splits[9], (FF, D), FF ** -0.5, 0.109375, ((0, 8),), jnp.float32),
        "down_bias": centred(splits[10], (D,), 0.5, 3.0, ((0, 8),), jnp.float32),
        "mod_weight": centred(splits[11], (CD, 6 * D), (2 * CD) ** -0.5, 0.375, ((1, 8),), jnp.float32),
        "mod_bias": centred(splits[12], (6 * D,), 0.3, 2.0, ((0, 8),), jnp.float32),
    }


@jax.custom_vjp
def low(v):
    return lax.optimization_barrier(v.astype(jnp.bfloat16)).astype(jnp.float32)

@jax.custom_vjp
def low_back(v):
    return v

def low_keep(v):
    return (low(v), None)

def low_pass(kept, grad):
    return (grad,)

def back_keep(v):
    return (v, None)

def back_low(kept, grad):
    return (low(grad),)
low.defvjp(low_keep, low_pass)
low_back.defvjp(back_keep, back_low)
HIGHEST = lax.Precision.HIGHEST
EPSILON = 1e-05

def normalize(values):
    centre = lax.optimization_barrier(jnp.mean(values, axis=-1, keepdims=True))
    shifted = values - centre
    variance = lax.optimization_barrier(jnp.mean(shifted * shifted, axis=-1, keepdims=True))
    return shifted * lax.rsqrt(variance + EPSILON)

def rotary_tables(length, head_dim):
    half_dim = head_dim // 2
    inv_freq = jnp.exp(-math.log(10000.0) * jnp.arange(half_dim, dtype=jnp.float32) * (2.0 / head_dim))
    angles = jnp.arange(length, dtype=jnp.float32)[:, None] * inv_freq[None, :]
    return (jnp.cos(angles), jnp.sin(angles))

def rotate(values, cosine_table, sine_table):
    half_dim = values.shape[-1] // 2
    first_half = values[..., :half_dim]
    second_half = values[..., half_dim:]
    cos_part = cosine_table[:, None, :]
    sin_part = sine_table[:, None, :]
    return jnp.concatenate([first_half * cos_part - second_half * sin_part, second_half * cos_part + first_half * sin_part], axis=-1)

def attend_block(query_block, key_rows, values):
    scaling = 1.0 / math.sqrt(HD)
    scores = low_back(jnp.einsum('qhd,khd->hqk', query_block, key_rows, precision=HIGHEST) * scaling)
    softmax_val = jax.nn.softmax(scores, axis=-1)
    return jnp.einsum('hqk,khd->qhd', low(softmax_val), values, precision=HIGHEST)

def forward(tokens, cond_row, attn_gain, mlp_gain, qkv_weight, out_weight, up_weight, up_bias, down_weight, down_bias, mod_weight, mod_bias):
    length = tokens.shape[0]
    model_width = tokens.shape[1]
    cond_act = jax.nn.silu(cond_row)
    modulation = jnp.dot(low(cond_act)[None, :], low(mod_weight), precision=HIGHEST)[0] + mod_bias
    shift_attn, scale_attn, gate_attn, shift_mlp, scale_mlp, gate_mlp = jnp.split(modulation, 6)
    normed_attn = normalize(tokens) * attn_gain
    attn_in = low(normed_attn * (1.0 + scale_attn) + shift_attn)
    qkv = low(low_back(jnp.dot(attn_in, low(qkv_weight), precision=HIGHEST)))
    head_split = qkv.reshape(length, 3, H, HD)
    cosine_table, sine_table = rotary_tables(length, HD)
    queries = low(rotate(head_split[:, 0], cosine_table, sine_table))
    key_rot = low(rotate(head_split[:, 1], cosine_table, sine_table))
    values = head_split[:, 2]
    block_rows = min(512, length)
    blocks = queries.reshape(length // block_rows, block_rows, H, HD)

    def attend_one(query_block):
        return attend_block(query_block, key_rot, values)
    mixed_rows = lax.map(jax.checkpoint(attend_one), blocks)
    mixed_rows = low(low_back(mixed_rows.reshape(length, model_width)))
    attn_out = low_back(jnp.dot(mixed_rows, low(out_weight), precision=HIGHEST))
    hidden = tokens + gate_attn * attn_out
    normed_mlp = normalize(hidden) * mlp_gain
    mlp_in = low(normed_mlp * (1.0 + scale_mlp) + shift_mlp)
    pre_act = low_back(jnp.dot(mlp_in, low(up_weight), precision=HIGHEST)) + up_bias
    up_act = low(jax.nn.gelu(pre_act, approximate=True))
    branch = low_back(jnp.dot(up_act, low(down_weight), precision=HIGHEST)) + down_bias
    return hidden + gate_mlp * branch

def reference(inputs, conditioning, cotangent, attn_gain, mlp_gain, qkv_weight, out_weight, up_weight, up_bias, down_weight, down_bias, mod_weight, mod_bias):
    params = (attn_gain, mlp_gain, qkv_weight, out_weight, up_weight, up_bias, down_weight, down_bias, mod_weight, mod_bias)

    def per_sequence(totals, block_items):
        row_tokens, cond_row, row_cot = block_items
        row_out, pullback = jax.vjp(forward, row_tokens, cond_row, *params)
        row_grads = pullback(row_cot)
        updated = tuple((total_val + grad_val for total_val, grad_val in zip(totals, row_grads[2:])))
        return (updated, (row_out, row_grads[0], row_grads[1]))
    zero_grads = tuple((jnp.zeros_like(param_val) for param_val in params))
    totals, (outputs, inputs_grad, conditioning_grad) = lax.scan(per_sequence, zero_grads, (inputs, conditioning, cotangent))
    return (outputs, inputs_grad, conditioning_grad, totals[0], totals[1], totals[2], totals[3], totals[4], totals[5], totals[6], totals[7], totals[8], totals[9])
```

```python
from functools import partial
import math

import jax
import jax.numpy as jnp
from jax import lax
from jax.experimental import pallas as pl
from jax.experimental.pallas import tpu as pltpu
from jax.sharding import PartitionSpec as P

H = 12
HD = 64
EPSILON = 1e-05
BF16 = jnp.bfloat16
F32 = jnp.float32
LOG2E = math.log2(math.e)
VMEM_LIMIT = 60 * 1024 * 1024


def mm(a, b, ca, cb):
    return lax.dot_general(a, b, (((ca,), (cb,)), ((), ())), preferred_element_type=F32)


def normalize(values):
    centre = jnp.mean(values, axis=-1, keepdims=True)
    shifted = values - centre
    variance = jnp.mean(shifted * shifted, axis=-1, keepdims=True)
    inv_std = lax.rsqrt(variance + EPSILON)
    return (shifted * inv_std, inv_std)


def norm_back(grad_hat, normed_hat, inv_std):
    mean_grad = jnp.mean(grad_hat, axis=-1, keepdims=True)
    mean_mixed = jnp.mean(grad_hat * normed_hat, axis=-1, keepdims=True)
    return inv_std * (grad_hat - mean_grad - normed_hat * mean_mixed)


def project_kernel(seq_count, w_ref, x_ref, cos_ref, sin_ref, out_ref):
    rows = mm(w_ref[...], x_ref[...], 0, 1).astype(BF16)
    cosine, sine = cos_ref[...], sin_ref[...]
    half = HD // 2
    for z in range(seq_count):
        for part in range(3):
            base = (z * 3 + part) * HD
            if part == 2:
                out_ref[z, part * HD : (part + 1) * HD, :] = rows[base : base + HD]
            else:
                a = rows[base : base + half].astype(F32)
                b = rows[base + half : base + HD].astype(F32)
                out_ref[z, part * HD : part * HD + half, :] = (a * cosine - b * sine).astype(BF16)
                out_ref[z, part * HD + half : (part + 1) * HD, :] = (b * cosine + a * sine).astype(BF16)


def project(weight, attn_in, cosine, sine, seq_count):
    tok = attn_in.shape[0]
    return pl.pallas_call(
        partial(project_kernel, seq_count),
        out_shape=jax.ShapeDtypeStruct((seq_count, 3 * HD, tok), BF16),
        compiler_params=pltpu.CompilerParams(vmem_limit_bytes=VMEM_LIMIT),
        cost_estimate=pl.CostEstimate(
            flops=2 * tok * weight.size, bytes_accessed=2 * weight.size * 3, transcendentals=0
        ),
        name="project",
    )(weight, attn_in, cosine, sine)


def attend_kernel(n, tok, sub, x_ref, o_ref, lse_ref, k_ref):
    step = pl.program_id(0)

    @pl.when(step == 0)
    def _():
        for c in range(n):
            k_ref[c * tok : (c + 1) * tok, :] = x_ref[c, HD : 2 * HD, :].T

    scale = LOG2E / math.sqrt(HD)
    width = tok // sub

    def score(i):
        q = x_ref[step, 0:HD, i * width : (i + 1) * width]
        return mm(k_ref[...], q, 1, 0)

    def soft(s):
        top = jnp.max(s, axis=0, keepdims=True) * scale
        p = jnp.exp2(s * scale - top)
        total = jnp.sum(p, axis=0, keepdims=True)
        return top, total, p.astype(BF16)

    def mix(i, top, total, p):
        o = None
        for c in range(n):
            part = mm(x_ref[c, 2 * HD : 3 * HD, :], p[c * tok : (c + 1) * tok], 1, 0)
            o = part if o is None else o + part
        o_ref[0, :, i * width : (i + 1) * width] = (o / total).astype(BF16)
        lse_ref[0, :, i * width : (i + 1) * width] = top + jnp.log2(total)

    scores = [score(0)]
    pending = None
    for i in range(sub):
        if i + 1 < sub:
            scores.append(score(i + 1))
        done = soft(scores[i])
        if pending is not None:
            mix(i - 1, *pending)
        pending = done
    mix(sub - 1, *pending)


def attend(x):
    n, _, tok = x.shape
    length = n * tok
    return pl.pallas_call(
        partial(attend_kernel, n, tok, 2),
        grid=(n,),
        in_specs=[pl.BlockSpec(x.shape, lambda i: (0, 0, 0))],
        out_specs=[
            pl.BlockSpec((1, HD, tok), lambda i: (i, 0, 0)),
            pl.BlockSpec((1, 1, tok), lambda i: (i, 0, 0)),
        ],
        out_shape=[
            jax.ShapeDtypeStruct((n, HD, tok), BF16),
            jax.ShapeDtypeStruct((n, 1, tok), F32),
        ],
        scratch_shapes=[pltpu.VMEM((length, HD), BF16)],
        compiler_params=pltpu.CompilerParams(vmem_limit_bytes=VMEM_LIMIT),
        cost_estimate=pl.CostEstimate(
            flops=16 * length * length * HD, bytes_accessed=8 * length * HD, transcendentals=length * length
        ),
        name="attend",
    )(x)


def attend_back_kernel(
    n, tok, sub, x_ref, g_ref, o_ref, lse_ref, cos_ref, sin_ref, out_ref, k_ref, v_ref, dk_ref, dv_ref
):
    step = pl.program_id(0)
    half = HD // 2

    @pl.when(step == 0)
    def _():
        for c in range(n):
            k_ref[c * tok : (c + 1) * tok, :] = x_ref[c, HD : 2 * HD, :].T
            v_ref[c * tok : (c + 1) * tok, :] = x_ref[c, 2 * HD : 3 * HD, :].T
        dk_ref[...] = jnp.zeros_like(dk_ref)
        dv_ref[...] = jnp.zeros_like(dv_ref)

    scale = LOG2E / math.sqrt(HD)
    width = tok // sub

    def turn_back(grad, cosine, sine):
        a, b = grad[:half], grad[half:]
        return (a * cosine + b * sine).astype(BF16), (b * cosine - a * sine).astype(BF16)

    for i in range(sub):
        cols = slice(i * width, (i + 1) * width)
        q = x_ref[step, 0:HD, cols]
        g = g_ref[step, :, cols]
        o = o_ref[step, :, cols]
        centre = jnp.sum(g.astype(F32) * o.astype(F32), axis=0, keepdims=True)
        s = mm(k_ref[...], q, 1, 0)
        dp = mm(v_ref[...], g, 1, 0)
        p = jnp.exp2(s * scale - lse_ref[step, :, cols])
        p_low = p.astype(BF16)
        ds = (p * (dp - centre)).astype(BF16)
        dv_ref[...] += mm(g, p_low, 1, 1)
        dk_ref[...] += mm(q, ds, 1, 1)
        dq = None
        for c in range(n):
            part = mm(x_ref[c, HD : 2 * HD, :], ds[c * tok : (c + 1) * tok], 1, 0)
            dq = part if dq is None else dq + part
        dq = dq * (1.0 / math.sqrt(HD))
        a, b = turn_back(dq, cos_ref[step, :, cols], sin_ref[step, :, cols])
        out_ref[step, 0:half, cols] = a
        out_ref[step, half:HD, cols] = b

    @pl.when(step == n - 1)
    def _():
        for c in range(n):
            dk = dk_ref[:, c * tok : (c + 1) * tok] * (1.0 / math.sqrt(HD))
            a, b = turn_back(dk, cos_ref[c], sin_ref[c])
            out_ref[c, HD : HD + half, :] = a
            out_ref[c, HD + half : 2 * HD, :] = b
            out_ref[c, 2 * HD : 3 * HD, :] = dv_ref[:, c * tok : (c + 1) * tok].astype(BF16)


def attend_back(x, g, o, lse, cosine, sine):
    n, _, tok = x.shape
    length = n * tok
    whole = lambda a: pl.BlockSpec(a.shape, lambda i: (0,) * a.ndim)
    return pl.pallas_call(
        partial(attend_back_kernel, n, tok, 2),
        grid=(n,),
        in_specs=[whole(a) for a in (x, g, o, lse, cosine, sine)],
        out_specs=whole(x),
        out_shape=jax.ShapeDtypeStruct(x.shape, BF16),
        scratch_shapes=[
            pltpu.VMEM((length, HD), BF16),
            pltpu.VMEM((length, HD), BF16),
            pltpu.VMEM((HD, length), F32),
            pltpu.VMEM((HD, length), F32),
        ],
        compiler_params=pltpu.CompilerParams(vmem_limit_bytes=VMEM_LIMIT),
        cost_estimate=pl.CostEstimate(
            flops=40 * length * length * HD, bytes_accessed=16 * length * HD, transcendentals=length * length
        ),
        name="attend_back",
    )(x, g, o, lse, cosine, sine)


def per_device(
    inputs,
    conditioning,
    cotangent,
    attn_gain,
    mlp_gain,
    qkv_weight,
    out_weight,
    up_weight,
    up_bias,
    down_weight,
    down_bias,
    mod_weight,
    mod_bias,
):
    n = lax.axis_size("seq")
    fs = lax.axis_size("fsdp")
    z = lax.axis_index("seq")
    me = lax.axis_index("fsdp")
    tokens = inputs[0]
    tok, width = tokens.shape
    slots = H // n
    gather = lambda a: lax.all_gather(a, "fsdp", axis=0, tiled=True)

    smalls = [attn_gain, mlp_gain, up_bias, down_bias, conditioning[0]]
    sizes = [a.shape[0] for a in smalls]
    packed = lax.all_gather(jnp.concatenate(smalls), "fsdp", axis=0)
    offsets = [sum(sizes[:i]) for i in range(len(sizes))]
    attn_gain_full, mlp_gain_full, up_bias_full, down_bias_full = (
        packed[:, o : o + s].reshape(-1) for o, s in zip(offsets[:4], sizes[:4])
    )
    cond_all = packed[:, offsets[4] :]
    cond_act_all = jax.nn.silu(cond_all)
    cond_low_all = cond_act_all.astype(BF16)
    mod_low = mod_weight.astype(BF16)
    mod_own = mm(cond_low_all, mod_low, 1, 0) + mod_bias[None, :]
    modulation = lax.all_to_all(mod_own, "fsdp", split_axis=0, concat_axis=0, tiled=True).reshape(-1)
    shift_attn, scale_attn, gate_attn, shift_mlp, scale_mlp, gate_mlp = jnp.split(modulation, 6)

    shard = qkv_weight.shape[0]
    qkv_low = qkv_weight.astype(BF16).reshape(shard, 3, n, slots, HD)
    qkv_slots = [
        gather(qkv_low[:, :, :, s].transpose(0, 2, 1, 3).reshape(shard, n * 3 * HD)) for s in range(slots)
    ]
    out_full = gather(out_weight.astype(BF16))
    up_full = gather(up_weight.astype(BF16))
    down_full = gather(down_weight.astype(BF16))

    inv_freq = jnp.exp(-math.log(10000.0) * jnp.arange(HD // 2, dtype=F32) * (2.0 / HD))
    angles = inv_freq[:, None] * jnp.arange(tok * n, dtype=F32)[None, :]
    cos_all = jnp.cos(angles).reshape(HD // 2, n, tok).transpose(1, 0, 2)
    sin_all = jnp.sin(angles).reshape(HD // 2, n, tok).transpose(1, 0, 2)
    cos_own = lax.dynamic_index_in_dim(cos_all, z, 0, keepdims=False)
    sin_own = lax.dynamic_index_in_dim(sin_all, z, 0, keepdims=False)

    hat_attn, inv_attn = normalize(tokens)
    normed_attn = hat_attn * attn_gain_full
    attn_in = (normed_attn * (1.0 + scale_attn) + shift_attn).astype(BF16)
    swap = lambda a: lax.all_to_all(a, "seq", split_axis=0, concat_axis=0, tiled=True)
    heads = [swap(project(w, attn_in, cos_own, sin_own, n)) for w in qkv_slots]
    mixed_heads, log_totals, mixed_back = [], [], []
    for x in heads:
        o, lse = attend(x)
        mixed_heads.append(o)
        log_totals.append(lse)
        mixed_back.append(swap(o))
    mixed = jnp.stack(mixed_back, axis=1).reshape(width, tok)

    attn_out = mm(mixed, out_full, 0, 0)
    hidden = tokens + gate_attn * attn_out
    hat_mlp, inv_mlp = normalize(hidden)
    normed_mlp = hat_mlp * mlp_gain_full
    mlp_in = (normed_mlp * (1.0 + scale_mlp) + shift_mlp).astype(BF16)
    pre_act = jnp.dot(mlp_in, up_full, preferred_element_type=F32) + up_bias_full
    gelu_act, gelu_pull = jax.vjp(partial(jax.nn.gelu, approximate=True), pre_act)
    up_act = gelu_act.astype(BF16)
    branch = jnp.dot(up_act, down_full, preferred_element_type=F32) + down_bias_full
    output = hidden + gate_mlp * branch
    grad_out = cotangent[0]
    grad_branch = gate_mlp * grad_out
    branch_low = grad_branch.astype(BF16)
    down_weight_grad = mm(up_act, branch_low, 0, 0)
    grad_act = mm(branch_low, down_full, 1, 1)
    grad_pre = gelu_pull(grad_act)[0]
    pre_low = grad_pre.astype(BF16)
    up_weight_grad = mm(mlp_in, pre_low, 0, 0)
    grad_mlp_in = mm(pre_low, up_full, 1, 1)
    grad_normed_mlp = grad_mlp_in * (1.0 + scale_mlp)
    grad_hidden = grad_out + norm_back(grad_normed_mlp * mlp_gain_full, hat_mlp, inv_mlp)
    attn_low = (gate_attn * grad_hidden).astype(BF16)
    out_weight_grad = mm(mixed, attn_low, 1, 0)
    grad_mixed = mm(out_full, attn_low, 1, 1).astype(BF16)
    grad_split = grad_mixed.reshape(n, slots, HD, tok)

    grad_slots = []
    for s in range(slots):
        g = swap(grad_split[:, s])
        grad_slots.append(swap(attend_back(heads[s], g, mixed_heads[s], log_totals[s], cos_all, sin_all)))

    scatter = lambda a: lax.psum_scatter(a.astype(BF16), "fsdp", scatter_dimension=0, tiled=True)
    qkv_parts = []
    grad_attn_in = None
    for s in range(slots):
        rows = grad_slots[s].reshape(n * 3 * HD, tok)
        qkv_parts.append(scatter(mm(attn_in, rows, 0, 1)))
        part = mm(rows, qkv_slots[s], 0, 1)
        grad_attn_in = part if grad_attn_in is None else grad_attn_in + part
    grad_normed_attn = grad_attn_in * (1.0 + scale_attn)
    inputs_grad = grad_hidden + norm_back(grad_normed_attn * attn_gain_full, hat_attn, inv_attn)

    part_down = scatter(down_weight_grad)
    part_up = scatter(up_weight_grad)
    part_out = scatter(out_weight_grad)
    vectors = jnp.concatenate(
        [
            jnp.sum(grad_attn_in, axis=0),
            jnp.sum(grad_attn_in * normed_attn, axis=0),
            jnp.sum(grad_hidden * attn_out, axis=0),
            jnp.sum(grad_mlp_in, axis=0),
            jnp.sum(grad_mlp_in * normed_mlp, axis=0),
            jnp.sum(grad_out * branch, axis=0),
            jnp.sum(grad_normed_attn * hat_attn, axis=0),
            jnp.sum(grad_normed_mlp * hat_mlp, axis=0),
            jnp.sum(grad_pre, axis=0),
            jnp.sum(grad_branch, axis=0),
        ]
    )
    summed = lax.all_gather(lax.psum(vectors, "seq"), "fsdp", axis=0)
    ff = up_bias.shape[0] * fs
    total = jnp.sum(summed, axis=0)
    own = lambda v: lax.dynamic_index_in_dim(v.reshape(fs, -1), me, 0, keepdims=False)
    mods = 6 * width
    attn_gain_grad = own(total[mods : mods + width])
    mlp_gain_grad = own(total[mods + width : mods + 2 * width])
    up_bias_grad = own(total[mods + 2 * width : mods + 2 * width + ff])
    down_bias_grad = own(total[mods + 2 * width + ff :])
    mod_bias_grad = own(total[:mods])
    own_mod = lax.dynamic_slice_in_dim(summed[:, :mods], me * (mods // fs), mods // fs, axis=1)
    mod_weight_grad = lax.dot_general(
        cond_low_all.astype(F32), own_mod, (((0,), (0,)), ((), ())), precision=lax.Precision.HIGHEST
    )
    cond_part = lax.dot_general(
        own_mod, mod_low.astype(F32), (((1,), (1,)), ((), ())), precision=lax.Precision.HIGHEST
    )
    grad_cond_act = lax.psum_scatter(cond_part, "fsdp", scatter_dimension=0, tiled=True)
    _, silu_pull = jax.vjp(jax.nn.silu, conditioning)
    conditioning_grad = silu_pull(grad_cond_act)[0]

    qkv_sum = lax.psum(jnp.stack(qkv_parts, axis=0), "seq").astype(F32)
    qkv_weight_grad = (
        qkv_sum.reshape(slots, shard, n, 3, HD).transpose(1, 3, 2, 0, 4).reshape(shard, 3 * width)
    )
    out_sum = lax.psum(part_out, "seq").astype(F32)
    up_sum = lax.psum(part_up, "seq").astype(F32)
    down_sum = lax.psum(part_down, "seq").astype(F32)
    return (
        output[None],
        inputs_grad[None],
        conditioning_grad,
        attn_gain_grad,
        mlp_gain_grad,
        qkv_weight_grad,
        out_sum,
        up_sum,
        up_bias_grad,
        down_sum,
        down_bias_grad,
        mod_weight_grad,
        mod_bias_grad,
    )


def solution(mesh):
    specs = (
        P("fsdp", "seq", None),
        P("fsdp", None),
        P("fsdp", "seq", None),
        P("fsdp"),
        P("fsdp"),
        P("fsdp", None),
        P("fsdp", None),
        P("fsdp", None),
        P("fsdp"),
        P("fsdp", None),
        P("fsdp"),
        P(None, "fsdp"),
        P("fsdp"),
    )
    out_specs = (specs[0], specs[0], specs[1]) + specs[3:]
    return jax.shard_map(per_device, mesh=mesh, in_specs=specs, out_specs=out_specs, check_vma=False)
```

```python
from functools import partial
import math

import jax
import jax.numpy as jnp
from jax import lax
from jax.experimental import pallas as pl
from jax.experimental.pallas import tpu as pltpu
from jax.sharding import PartitionSpec as P

H = 12
HD = 64
EPSILON = 1e-05
BF16 = jnp.bfloat16
F32 = jnp.float32
LOG2E = math.log2(math.e)
VMEM_LIMIT = 60 * 1024 * 1024


def mm(a, b, ca, cb):
    return lax.dot_general(a, b, (((ca,), (cb,)), ((), ())), preferred_element_type=F32)


def normalize(values):
    centre = jnp.mean(values, axis=-1, keepdims=True)
    shifted = values - centre
    variance = jnp.mean(shifted * shifted, axis=-1, keepdims=True)
    inv_std = lax.rsqrt(variance + EPSILON)
    return (shifted * inv_std, inv_std)


def norm_back(grad_hat, normed_hat, inv_std):
    mean_grad = jnp.mean(grad_hat, axis=-1, keepdims=True)
    mean_mixed = jnp.mean(grad_hat * normed_hat, axis=-1, keepdims=True)
    return inv_std * (grad_hat - mean_grad - normed_hat * mean_mixed)


def project_kernel(seq_count, w_ref, x_ref, cos_ref, sin_ref, out_ref):
    rows = mm(w_ref[...], x_ref[...], 0, 1).astype(BF16)
    cosine, sine = cos_ref[...], sin_ref[...]
    half = HD // 2
    for z in range(seq_count):
        for part in range(3):
            base = (z * 3 + part) * HD
            if part == 2:
                out_ref[z, part * HD : (part + 1) * HD, :] = rows[base : base + HD]
            else:
                a = rows[base : base + half].astype(F32)
                b = rows[base + half : base + HD].astype(F32)
                out_ref[z, part * HD : part * HD + half, :] = (a * cosine - b * sine).astype(BF16)
                out_ref[z, part * HD + half : (part + 1) * HD, :] = (b * cosine + a * sine).astype(BF16)


def project(weight, attn_in, cosine, sine, seq_count):
    tok = attn_in.shape[0]
    return pl.pallas_call(
        partial(project_kernel, seq_count),
        out_shape=jax.ShapeDtypeStruct((seq_count, 3 * HD, tok), BF16),
        compiler_params=pltpu.CompilerParams(vmem_limit_bytes=VMEM_LIMIT),
        cost_estimate=pl.CostEstimate(
            flops=2 * tok * weight.size, bytes_accessed=2 * weight.size * 3, transcendentals=0
        ),
        name="project",
    )(weight, attn_in, cosine, sine)


def attend_kernel(n, tok, sub, x_ref, o_ref, lse_ref, k_ref):
    step = pl.program_id(0)

    @pl.when(step == 0)
    def _():
        for c in range(n):
            k_ref[c * tok : (c + 1) * tok, :] = x_ref[c, HD : 2 * HD, :].T

    scale = LOG2E / math.sqrt(HD)
    width = tok // sub

    def score(i):
        q = x_ref[step, 0:HD, i * width : (i + 1) * width]
        return mm(k_ref[...], q, 1, 0)

    def soft(s):
        top = jnp.max(s, axis=0, keepdims=True) * scale
        p = jnp.exp2(s * scale - top)
        total = jnp.sum(p, axis=0, keepdims=True)
        return top, total, p.astype(BF16)

    def mix(i, top, total, p):
        o = None
        for c in range(n):
            part = mm(x_ref[c, 2 * HD : 3 * HD, :], p[c * tok : (c + 1) * tok], 1, 0)
            o = part if o is None else o + part
        o_ref[0, :, i * width : (i + 1) * width] = (o / total).astype(BF16)
        lse_ref[0, :, i * width : (i + 1) * width] = top + jnp.log2(total)

    scores = [score(0)]
    pending = None
    for i in range(sub):
        if i + 1 < sub:
            scores.append(score(i + 1))
        done = soft(scores[i])
        if pending is not None:
            mix(i - 1, *pending)
        pending = done
    mix(sub - 1, *pending)


def attend(x):
    n, _, tok = x.shape
    length = n * tok
    return pl.pallas_call(
        partial(attend_kernel, n, tok, 2),
        grid=(n,),
        in_specs=[pl.BlockSpec(x.shape, lambda i: (0, 0, 0))],
        out_specs=[
            pl.BlockSpec((1, HD, tok), lambda i: (i, 0, 0)),
            pl.BlockSpec((1, 1, tok), lambda i: (i, 0, 0)),
        ],
        out_shape=[
            jax.ShapeDtypeStruct((n, HD, tok), BF16),
            jax.ShapeDtypeStruct((n, 1, tok), F32),
        ],
        scratch_shapes=[pltpu.VMEM((length, HD), BF16)],
        compiler_params=pltpu.CompilerParams(vmem_limit_bytes=VMEM_LIMIT),
        cost_estimate=pl.CostEstimate(
            flops=16 * length * length * HD, bytes_accessed=8 * length * HD, transcendentals=length * length
        ),
        name="attend",
    )(x)


def attend_back_kernel(
    n, tok, sub, x_ref, g_ref, o_ref, lse_ref, cos_ref, sin_ref, out_ref, k_ref, v_ref, dk_ref, dv_ref
):
    step = pl.program_id(0)
    half = HD // 2

    @pl.when(step == 0)
    def _():
        for c in range(n):
            k_ref[c * tok : (c + 1) * tok, :] = x_ref[c, HD : 2 * HD, :].T
            v_ref[c * tok : (c + 1) * tok, :] = x_ref[c, 2 * HD : 3 * HD, :].T
        dk_ref[...] = jnp.zeros_like(dk_ref)
        dv_ref[...] = jnp.zeros_like(dv_ref)

    scale = LOG2E / math.sqrt(HD)
    width = tok // sub

    def turn_back(grad, cosine, sine):
        a, b = grad[:half], grad[half:]
        return (a * cosine + b * sine).astype(BF16), (b * cosine - a * sine).astype(BF16)

    for i in range(sub):
        cols = slice(i * width, (i + 1) * width)
        q = x_ref[step, 0:HD, cols]
        g = g_ref[step, :, cols]
        o = o_ref[step, :, cols]
        centre = jnp.sum(g.astype(F32) * o.astype(F32), axis=0, keepdims=True)
        s = mm(k_ref[...], q, 1, 0)
        dp = mm(v_ref[...], g, 1, 0)
        p = jnp.exp2(s * scale - lse_ref[step, :, cols])
        p_low = p.astype(BF16)
        ds = (p * (dp - centre)).astype(BF16)
        dv_ref[...] += mm(g, p_low, 1, 1)
        dk_ref[...] += mm(q, ds, 1, 1)
        dq = None
        for c in range(n):
            part = mm(x_ref[c, HD : 2 * HD, :], ds[c * tok : (c + 1) * tok], 1, 0)
            dq = part if dq is None else dq + part
        dq = dq * (1.0 / math.sqrt(HD))
        a, b = turn_back(dq, cos_ref[step, :, cols], sin_ref[step, :, cols])
        out_ref[step, 0:half, cols] = a
        out_ref[step, half:HD, cols] = b

    @pl.when(step == n - 1)
    def _():
        for c in range(n):
            dk = dk_ref[:, c * tok : (c + 1) * tok] * (1.0 / math.sqrt(HD))
            a, b = turn_back(dk, cos_ref[c], sin_ref[c])
            out_ref[c, HD : HD + half, :] = a
            out_ref[c, HD + half : 2 * HD, :] = b
            out_ref[c, 2 * HD : 3 * HD, :] = dv_ref[:, c * tok : (c + 1) * tok].astype(BF16)


def attend_back(x, g, o, lse, cosine, sine):
    n, _, tok = x.shape
    length = n * tok
    whole = lambda a: pl.BlockSpec(a.shape, lambda i: (0,) * a.ndim)
    return pl.pallas_call(
        partial(attend_back_kernel, n, tok, 2),
        grid=(n,),
        in_specs=[whole(a) for a in (x, g, o, lse, cosine, sine)],
        out_specs=whole(x),
        out_shape=jax.ShapeDtypeStruct(x.shape, BF16),
        scratch_shapes=[
            pltpu.VMEM((length, HD), BF16),
            pltpu.VMEM((length, HD), BF16),
            pltpu.VMEM((HD, length), F32),
            pltpu.VMEM((HD, length), F32),
        ],
        compiler_params=pltpu.CompilerParams(vmem_limit_bytes=VMEM_LIMIT),
        cost_estimate=pl.CostEstimate(
            flops=40 * length * length * HD, bytes_accessed=16 * length * HD, transcendentals=length * length
        ),
        name="attend_back",
    )(x, g, o, lse, cosine, sine)


GELU_C = math.sqrt(2.0 / math.pi)
GELU_A = 0.044715


def middle_kernel(
    n,
    slots,
    blocks,
    tokens_ref,
    cot_ref,
    vec_ref,
    bias_ref,
    up_ref,
    down_ref,
    out_w_ref,
    *refs,
):
    mixed_refs, refs = refs[:slots], refs[slots:]
    output_ref, grad_hidden_ref, sums_ref, bias_grad_ref, g_down_ref, g_pack_ref, *refs = refs
    grad_mixed_refs, (mixed_ref, attn_out_ref, mlp_in_ref, low_ref, back_ref) = refs[:slots], refs[slots:]
    j = pl.program_id(0)
    tok, width = tokens_ref.shape
    gate_attn, shift, scale, gate, gain, down_bias = (vec_ref[i : i + 1, :] for i in range(6))
    piece = min(256, tok)
    pieces = tok // piece

    @pl.when(j == 0)
    def _():
        for s in range(slots):
            for c in range(n):
                head = c * slots + s
                mixed_ref[head * HD : (head + 1) * HD, :] = mixed_refs[s][c]
        attn_out_ref[...] = mm(mixed_ref[...], out_w_ref[...], 0, 0)

        def prepare(i, _):
            rows = pl.ds(pl.multiple_of(i * piece, piece), piece)
            hidden = tokens_ref[rows, :] + gate_attn * attn_out_ref[rows, :]
            grad_hidden_ref[rows, :] = hidden
            hat, _ = normalize(hidden)
            mlp_in_ref[rows, :] = (hat * gain * (1.0 + scale) + shift).astype(BF16)
            low_ref[rows, :] = (gate * cot_ref[rows, :]).astype(BF16)
            return 0

        lax.fori_loop(0, pieces, prepare, 0)
        output_ref[...] = jnp.zeros_like(output_ref)
        back_ref[...] = jnp.zeros_like(back_ref)

    @pl.when(j < blocks)
    def _():
        mlp_in, low = mlp_in_ref[...], low_ref[...]
        x = mm(mlp_in, up_ref[...], 1, 0) + bias_ref[0]
        grad_act = mm(low, down_ref[...], 1, 1)
        square = x * x
        t = jnp.tanh(x * (GELU_C + GELU_C * GELU_A * square))
        half = 0.5 + 0.5 * t
        act = (x * half).astype(BF16)
        slope = half + x * (0.5 - 0.5 * t * t) * (GELU_C + 3.0 * GELU_C * GELU_A * square)
        grad_pre = grad_act * slope
        bias_grad_ref[0] = jnp.sum(grad_pre, axis=0, keepdims=True)
        pre_low = grad_pre.astype(BF16)
        output_ref[...] += mm(act, down_ref[...], 1, 0)
        back_ref[...] += mm(pre_low, up_ref[...], 1, 1)
        g_down_ref[...] = mm(act, low, 0, 0).astype(BF16)
        g_pack_ref[...] = mm(mlp_in, pre_low, 0, 0).astype(BF16)

    @pl.when(j == blocks)
    def _():
        def finish(i, sums):
            rows = pl.ds(pl.multiple_of(i * piece, piece), piece)
            cot = cot_ref[rows, :]
            branch = output_ref[rows, :] + down_bias
            hidden = grad_hidden_ref[rows, :]
            output_ref[rows, :] = hidden + gate * branch
            hat, inv = normalize(hidden)
            back = back_ref[rows, :]
            grad_hidden = cot + norm_back(back * ((1.0 + scale) * gain), hat, inv)
            grad_hidden_ref[rows, :] = grad_hidden
            low_ref[rows, :] = (gate_attn * grad_hidden).astype(BF16)
            adds = (grad_hidden * attn_out_ref[rows, :], back, back * hat, cot * branch, cot)
            return tuple(a + jnp.sum(v, axis=0, keepdims=True) for a, v in zip(sums, adds))

        zero = jnp.zeros((1, width), F32)
        sums = lax.fori_loop(0, pieces, finish, (zero,) * 5)
        for i in range(5):
            sums_ref[i : i + 1, :] = sums[i]
        attn_low = low_ref[...]
        g_pack_ref[...] = mm(mixed_ref[...], attn_low, 1, 0).astype(BF16)
        grad_mixed = mm(out_w_ref[...], attn_low, 1, 1).astype(BF16)
        for s in range(slots):
            for c in range(n):
                head = c * slots + s
                grad_mixed_refs[s][c] = grad_mixed[head * HD : (head + 1) * HD]


def middle(tokens, cot, vectors, up_bias, w_pack, w_down, mixed):
    tok, width = tokens.shape
    ff = w_down.shape[0]
    blocks = ff // width
    slots = len(mixed)
    n = mixed[0].shape[0]
    whole = lambda shape: pl.BlockSpec(shape, lambda j: (0,) * len(shape), pipeline_mode=pl.Buffered(1))
    fixed = lambda shape: pl.BlockSpec(shape, lambda j: (0,) * len(shape))
    last = blocks - 1
    head_shape = mixed[0].shape
    flops = 2 * tok * width * (6 * ff + 3 * width)
    return pl.pallas_call(
        partial(middle_kernel, n, slots, blocks),
        grid=(blocks + 1,),
        in_specs=[
            whole(tokens.shape),
            whole(cot.shape),
            whole(vectors.shape),
            pl.BlockSpec((1, 1, width), lambda j: (jnp.minimum(j, last), 0, 0)),
            pl.BlockSpec((width, width), lambda j: (0, jnp.minimum(j, last))),
            pl.BlockSpec((width, width), lambda j: (jnp.minimum(j, last), 0)),
            pl.BlockSpec((width, width), lambda j: (0, blocks), pipeline_mode=pl.Buffered(1)),
        ]
        + [whole(head_shape)] * slots,
        out_specs=[
            fixed((tok, width)),
            fixed((tok, width)),
            fixed((8, width)),
            pl.BlockSpec((1, 1, width), lambda j: (jnp.minimum(j, last), 0, 0)),
            pl.BlockSpec((width, width), lambda j: (jnp.minimum(j, last), 0)),
            pl.BlockSpec((width, width), lambda j: (0, j)),
        ]
        + [fixed(head_shape)] * slots,
        out_shape=[
            jax.ShapeDtypeStruct((tok, width), F32),
            jax.ShapeDtypeStruct((tok, width), F32),
            jax.ShapeDtypeStruct((8, width), F32),
            jax.ShapeDtypeStruct((blocks, 1, width), F32),
            jax.ShapeDtypeStruct((ff, width), BF16),
            jax.ShapeDtypeStruct((width, ff + width), BF16),
        ]
        + [jax.ShapeDtypeStruct(head_shape, BF16)] * slots,
        scratch_shapes=[
            pltpu.VMEM((width, tok), BF16),
            pltpu.VMEM((tok, width), F32),
            pltpu.VMEM((tok, width), BF16),
            pltpu.VMEM((tok, width), BF16),
            pltpu.VMEM((tok, width), F32),
        ],
        compiler_params=pltpu.CompilerParams(vmem_limit_bytes=VMEM_LIMIT),
        cost_estimate=pl.CostEstimate(flops=flops, bytes_accessed=6 * ff * width * 2, transcendentals=tok * ff),
        name="middle",
    )(tokens, cot, vectors, up_bias.reshape(blocks, 1, width), w_pack, w_down, w_pack, *mixed)


def per_device(
    inputs,
    conditioning,
    cotangent,
    attn_gain,
    mlp_gain,
    qkv_weight,
    out_weight,
    up_weight,
    up_bias,
    down_weight,
    down_bias,
    mod_weight,
    mod_bias,
):
    n = lax.axis_size("seq")
    fs = lax.axis_size("fsdp")
    z = lax.axis_index("seq")
    me = lax.axis_index("fsdp")
    tokens = inputs[0]
    tok, width = tokens.shape
    slots = H // n
    gather = lambda a: lax.all_gather(a, "fsdp", axis=0, tiled=True)

    smalls = [attn_gain, mlp_gain, up_bias, down_bias, conditioning[0]]
    sizes = [a.shape[0] for a in smalls]
    packed = lax.all_gather(jnp.concatenate(smalls), "fsdp", axis=0)
    offsets = [sum(sizes[:i]) for i in range(len(sizes))]
    attn_gain_full, mlp_gain_full, up_bias_full, down_bias_full = (
        packed[:, o : o + s].reshape(-1) for o, s in zip(offsets[:4], sizes[:4])
    )
    cond_all = packed[:, offsets[4] :]
    cond_act_all = jax.nn.silu(cond_all)
    cond_low_all = cond_act_all.astype(BF16)
    mod_low = mod_weight.astype(BF16)
    mod_own = mm(cond_low_all, mod_low, 1, 0) + mod_bias[None, :]
    modulation = lax.all_to_all(mod_own, "fsdp", split_axis=0, concat_axis=0, tiled=True).reshape(-1)
    shift_attn, scale_attn, gate_attn, shift_mlp, scale_mlp, gate_mlp = jnp.split(modulation, 6)

    shard = qkv_weight.shape[0]
    qkv_low = qkv_weight.astype(BF16).reshape(shard, 3, n, slots, HD)
    qkv_slots = [
        gather(qkv_low[:, :, :, s].transpose(0, 2, 1, 3).reshape(shard, n * 3 * HD)) for s in range(slots)
    ]
    w_pack = gather(jnp.concatenate([up_weight.astype(BF16), out_weight.astype(BF16)], axis=1))
    down_full = gather(down_weight.astype(BF16))

    inv_freq = jnp.exp(-math.log(10000.0) * jnp.arange(HD // 2, dtype=F32) * (2.0 / HD))
    angles = inv_freq[:, None] * jnp.arange(tok * n, dtype=F32)[None, :]
    cos_all = jnp.cos(angles).reshape(HD // 2, n, tok).transpose(1, 0, 2)
    sin_all = jnp.sin(angles).reshape(HD // 2, n, tok).transpose(1, 0, 2)
    cos_own = lax.dynamic_index_in_dim(cos_all, z, 0, keepdims=False)
    sin_own = lax.dynamic_index_in_dim(sin_all, z, 0, keepdims=False)

    hat_attn, inv_attn = normalize(tokens)
    normed_attn = hat_attn * attn_gain_full
    attn_in = (normed_attn * (1.0 + scale_attn) + shift_attn).astype(BF16)
    swap = lambda a: lax.all_to_all(a, "seq", split_axis=0, concat_axis=0, tiled=True)
    heads = [swap(project(w, attn_in, cos_own, sin_own, n)) for w in qkv_slots]
    mixed_heads, log_totals, mixed_back = [], [], []
    for x in heads:
        o, lse = attend(x)
        mixed_heads.append(o)
        log_totals.append(lse)
        mixed_back.append(swap(o))
    vectors = jnp.stack(
        [gate_attn, shift_mlp, scale_mlp, gate_mlp, mlp_gain_full, down_bias_full, gate_mlp, gate_mlp], axis=0
    )
    output, grad_hidden, sums, up_bias_sum, g_down, g_pack, *grad_mixed = middle(
        tokens, cotangent[0], vectors, up_bias_full, w_pack, down_full, mixed_back
    )
    scatter = lambda a: lax.psum_scatter(a, "fsdp", scatter_dimension=0, tiled=True)
    part_pack = scatter(g_pack)
    part_down = scatter(g_down)

    grad_slots = []
    for s in range(slots):
        g = swap(grad_mixed[s])
        grad_slots.append(swap(attend_back(heads[s], g, mixed_heads[s], log_totals[s], cos_all, sin_all)))

    qkv_parts = []
    grad_attn_in = None
    for s in range(slots):
        rows = grad_slots[s].reshape(n * 3 * HD, tok)
        qkv_parts.append(mm(attn_in, rows, 0, 1).astype(BF16))
        part = mm(rows, qkv_slots[s], 0, 1)
        grad_attn_in = part if grad_attn_in is None else grad_attn_in + part
    grad_normed_attn = grad_attn_in * (1.0 + scale_attn)
    inputs_grad = grad_hidden + norm_back(grad_normed_attn * attn_gain_full, hat_attn, inv_attn)

    part_qkv = scatter(jnp.concatenate(qkv_parts, axis=1))
    back_sum = jnp.sum(grad_attn_in, axis=0)
    hat_sum = jnp.sum(grad_attn_in * hat_attn, axis=0)
    vectors = jnp.concatenate(
        [
            back_sum,
            hat_sum * attn_gain_full,
            sums[0],
            sums[1],
            sums[2] * mlp_gain_full,
            sums[3],
            hat_sum * (1.0 + scale_attn),
            sums[2] * (1.0 + scale_mlp),
            up_bias_sum.reshape(-1),
            sums[4] * gate_mlp,
        ]
    )
    summed = lax.all_gather(lax.psum(vectors, "seq"), "fsdp", axis=0)
    ff = up_bias.shape[0] * fs
    total = jnp.sum(summed, axis=0)
    own = lambda v: lax.dynamic_index_in_dim(v.reshape(fs, -1), me, 0, keepdims=False)
    mods = 6 * width
    attn_gain_grad = own(total[mods : mods + width])
    mlp_gain_grad = own(total[mods + width : mods + 2 * width])
    up_bias_grad = own(total[mods + 2 * width : mods + 2 * width + ff])
    down_bias_grad = own(total[mods + 2 * width + ff :])
    mod_bias_grad = own(total[:mods])
    own_mod = lax.dynamic_slice_in_dim(summed[:, :mods], me * (mods // fs), mods // fs, axis=1)
    mod_weight_grad = lax.dot_general(
        cond_low_all.astype(F32), own_mod, (((0,), (0,)), ((), ())), precision=lax.Precision.HIGHEST
    )
    cond_part = lax.dot_general(
        own_mod, mod_low.astype(F32), (((1,), (1,)), ((), ())), precision=lax.Precision.HIGHEST
    )
    grad_cond_act = lax.psum_scatter(cond_part, "fsdp", scatter_dimension=0, tiled=True)
    _, silu_pull = jax.vjp(jax.nn.silu, conditioning)
    conditioning_grad = silu_pull(grad_cond_act)[0]

    qkv_sum = lax.psum(part_qkv, "seq").astype(F32)
    qkv_weight_grad = (
        qkv_sum.reshape(shard, slots, n, 3, HD).transpose(0, 3, 2, 1, 4).reshape(shard, 3 * width)
    )
    pack_sum = lax.psum(part_pack, "seq").astype(F32)
    down_sum = lax.psum(part_down, "seq").astype(F32)
    out_sum, up_sum = pack_sum[:, ff:], pack_sum[:, :ff]
    return (
        output[None],
        inputs_grad[None],
        conditioning_grad,
        attn_gain_grad,
        mlp_gain_grad,
        qkv_weight_grad,
        out_sum,
        up_sum,
        up_bias_grad,
        down_sum,
        down_bias_grad,
        mod_weight_grad,
        mod_bias_grad,
    )


def solution(mesh):
    specs = (
        P("fsdp", "seq", None),
        P("fsdp", None),
        P("fsdp", "seq", None),
        P("fsdp"),
        P("fsdp"),
        P("fsdp", None),
        P("fsdp", None),
        P("fsdp", None),
        P("fsdp"),
        P("fsdp", None),
        P("fsdp"),
        P(None, "fsdp"),
        P("fsdp"),
    )
    out_specs = (specs[0], specs[0], specs[1]) + specs[3:]
    return jax.shard_map(per_device, mesh=mesh, in_specs=specs, out_specs=out_specs, check_vma=False)
```

```python
from functools import partial
import math

import jax
import jax.numpy as jnp
from jax import lax
from jax.experimental import pallas as pl
from jax.experimental.pallas import tpu as pltpu
from jax.sharding import PartitionSpec as P

H = 12
HD = 64
EPSILON = 1e-05
BF16 = jnp.bfloat16
F32 = jnp.float32
LOG2E = math.log2(math.e)
VMEM_LIMIT = 60 * 1024 * 1024


def mm(a, b, ca, cb):
    return lax.dot_general(a, b, (((ca,), (cb,)), ((), ())), preferred_element_type=F32)


def normalize(values):
    centre = jnp.mean(values, axis=-1, keepdims=True)
    shifted = values - centre
    variance = jnp.mean(shifted * shifted, axis=-1, keepdims=True)
    inv_std = lax.rsqrt(variance + EPSILON)
    return (shifted * inv_std, inv_std)


def norm_back(grad_hat, normed_hat, inv_std):
    mean_grad = jnp.mean(grad_hat, axis=-1, keepdims=True)
    mean_mixed = jnp.mean(grad_hat * normed_hat, axis=-1, keepdims=True)
    return inv_std * (grad_hat - mean_grad - normed_hat * mean_mixed)


def project_kernel(seq_count, w_ref, x_ref, cos_ref, sin_ref, out_ref):
    rows = mm(w_ref[...], x_ref[...], 0, 1).astype(BF16)
    cosine, sine = cos_ref[...], sin_ref[...]
    half = HD // 2
    for z in range(seq_count):
        for part in range(3):
            base = (z * 3 + part) * HD
            if part == 2:
                out_ref[z, part * HD : (part + 1) * HD, :] = rows[base : base + HD]
            else:
                a = rows[base : base + half].astype(F32)
                b = rows[base + half : base + HD].astype(F32)
                out_ref[z, part * HD : part * HD + half, :] = (a * cosine - b * sine).astype(BF16)
                out_ref[z, part * HD + half : (part + 1) * HD, :] = (b * cosine + a * sine).astype(BF16)


def project(weight, attn_in, cosine, sine, seq_count):
    tok = attn_in.shape[0]
    return pl.pallas_call(
        partial(project_kernel, seq_count),
        out_shape=jax.ShapeDtypeStruct((seq_count, 3 * HD, tok), BF16),
        compiler_params=pltpu.CompilerParams(vmem_limit_bytes=VMEM_LIMIT),
        cost_estimate=pl.CostEstimate(
            flops=2 * tok * weight.size, bytes_accessed=2 * weight.size * 3, transcendentals=0
        ),
        name="project",
    )(weight, attn_in, cosine, sine)


def attend_kernel(n, tok, sub, x_ref, o_ref, lse_ref, k_ref):
    step = pl.program_id(0)

    @pl.when(step == 0)
    def _():
        for c in range(n):
            k_ref[c * tok : (c + 1) * tok, :] = x_ref[c, HD : 2 * HD, :].T

    scale = LOG2E / math.sqrt(HD)
    width = tok // sub

    def score(i):
        q = x_ref[step, 0:HD, i * width : (i + 1) * width]
        return mm(k_ref[...], q, 1, 0)

    def soft(s):
        top = jnp.max(s, axis=0, keepdims=True) * scale
        p = jnp.exp2(s * scale - top)
        total = jnp.sum(p, axis=0, keepdims=True)
        return top, total, p.astype(BF16)

    def mix(i, top, total, p):
        o = None
        for c in range(n):
            part = mm(x_ref[c, 2 * HD : 3 * HD, :], p[c * tok : (c + 1) * tok], 1, 0)
            o = part if o is None else o + part
        o_ref[0, :, i * width : (i + 1) * width] = (o / total).astype(BF16)
        lse_ref[0, :, i * width : (i + 1) * width] = top + jnp.log2(total)

    scores = [score(0)]
    pending = None
    for i in range(sub):
        if i + 1 < sub:
            scores.append(score(i + 1))
        done = soft(scores[i])
        if pending is not None:
            mix(i - 1, *pending)
        pending = done
    mix(sub - 1, *pending)


def attend(x):
    n, _, tok = x.shape
    length = n * tok
    return pl.pallas_call(
        partial(attend_kernel, n, tok, 2),
        grid=(n,),
        in_specs=[pl.BlockSpec(x.shape, lambda i: (0, 0, 0))],
        out_specs=[
            pl.BlockSpec((1, HD, tok), lambda i: (i, 0, 0)),
            pl.BlockSpec((1, 1, tok), lambda i: (i, 0, 0)),
        ],
        out_shape=[
            jax.ShapeDtypeStruct((n, HD, tok), BF16),
            jax.ShapeDtypeStruct((n, 1, tok), F32),
        ],
        scratch_shapes=[pltpu.VMEM((length, HD), BF16)],
        compiler_params=pltpu.CompilerParams(vmem_limit_bytes=VMEM_LIMIT),
        cost_estimate=pl.CostEstimate(
            flops=16 * length * length * HD, bytes_accessed=8 * length * HD, transcendentals=length * length
        ),
        name="attend",
    )(x)


def attend_back_kernel(
    n, tok, sub, x_ref, g_ref, o_ref, lse_ref, cos_ref, sin_ref, out_ref, k_ref, v_ref, dk_ref, dv_ref
):
    step = pl.program_id(0)
    half = HD // 2

    @pl.when(step == 0)
    def _():
        for c in range(n):
            k_ref[c * tok : (c + 1) * tok, :] = x_ref[c, HD : 2 * HD, :].T
            v_ref[c * tok : (c + 1) * tok, :] = x_ref[c, 2 * HD : 3 * HD, :].T
        dk_ref[...] = jnp.zeros_like(dk_ref)
        dv_ref[...] = jnp.zeros_like(dv_ref)

    scale = LOG2E / math.sqrt(HD)
    width = tok // sub

    def turn_back(grad, cosine, sine):
        a, b = grad[:half], grad[half:]
        return (a * cosine + b * sine).astype(BF16), (b * cosine - a * sine).astype(BF16)

    for i in range(sub):
        cols = slice(i * width, (i + 1) * width)
        q = x_ref[step, 0:HD, cols]
        g = g_ref[step, :, cols]
        o = o_ref[step, :, cols]
        centre = jnp.sum(g.astype(F32) * o.astype(F32), axis=0, keepdims=True)
        s = mm(k_ref[...], q, 1, 0)
        dp = mm(v_ref[...], g, 1, 0)
        p = jnp.exp2(s * scale - lse_ref[step, :, cols])
        p_low = p.astype(BF16)
        ds = (p * (dp - centre)).astype(BF16)
        dv_ref[...] += mm(g, p_low, 1, 1)
        dk_ref[...] += mm(q, ds, 1, 1)
        dq = None
        for c in range(n):
            part = mm(x_ref[c, HD : 2 * HD, :], ds[c * tok : (c + 1) * tok], 1, 0)
            dq = part if dq is None else dq + part
        dq = dq * (1.0 / math.sqrt(HD))
        a, b = turn_back(dq, cos_ref[step, :, cols], sin_ref[step, :, cols])
        out_ref[step, 0:half, cols] = a
        out_ref[step, half:HD, cols] = b

    @pl.when(step == n - 1)
    def _():
        for c in range(n):
            dk = dk_ref[:, c * tok : (c + 1) * tok] * (1.0 / math.sqrt(HD))
            a, b = turn_back(dk, cos_ref[c], sin_ref[c])
            out_ref[c, HD : HD + half, :] = a
            out_ref[c, HD + half : 2 * HD, :] = b
            out_ref[c, 2 * HD : 3 * HD, :] = dv_ref[:, c * tok : (c + 1) * tok].astype(BF16)


def attend_back(x, g, o, lse, cosine, sine):
    n, _, tok = x.shape
    length = n * tok
    whole = lambda a: pl.BlockSpec(a.shape, lambda i: (0,) * a.ndim)
    return pl.pallas_call(
        partial(attend_back_kernel, n, tok, 2),
        grid=(n,),
        in_specs=[whole(a) for a in (x, g, o, lse, cosine, sine)],
        out_specs=whole(x),
        out_shape=jax.ShapeDtypeStruct(x.shape, BF16),
        scratch_shapes=[
            pltpu.VMEM((length, HD), BF16),
            pltpu.VMEM((length, HD), BF16),
            pltpu.VMEM((HD, length), F32),
            pltpu.VMEM((HD, length), F32),
        ],
        compiler_params=pltpu.CompilerParams(vmem_limit_bytes=VMEM_LIMIT),
        cost_estimate=pl.CostEstimate(
            flops=40 * length * length * HD, bytes_accessed=16 * length * HD, transcendentals=length * length
        ),
        name="attend_back",
    )(x, g, o, lse, cosine, sine)


GELU_C = math.sqrt(2.0 / math.pi)
GELU_A = 0.044715


def middle_kernel(
    n,
    slots,
    blocks,
    tokens_ref,
    cot_ref,
    vec_ref,
    bias_ref,
    up_ref,
    down_ref,
    out_w_ref,
    *refs,
):
    mixed_refs, refs = refs[:slots], refs[slots:]
    output_ref, grad_hidden_ref, sums_ref, bias_grad_ref, g_down_ref, g_pack_ref, *refs = refs
    grad_mixed_refs, (mixed_ref, attn_out_ref, mlp_in_ref, low_ref, back_ref) = refs[:slots], refs[slots:]
    j = pl.program_id(0)
    tok, width = tokens_ref.shape
    gate_attn, shift, scale, gate, gain, down_bias = (vec_ref[i : i + 1, :] for i in range(6))
    piece = min(256, tok)
    pieces = tok // piece

    @pl.when(j == 0)
    def _():
        for s in range(slots):
            for c in range(n):
                head = c * slots + s
                mixed_ref[head * HD : (head + 1) * HD, :] = mixed_refs[s][c]
        attn_out_ref[...] = mm(mixed_ref[...], out_w_ref[...], 0, 0)

        def prepare(i, _):
            rows = pl.ds(pl.multiple_of(i * piece, piece), piece)
            hidden = tokens_ref[rows, :] + gate_attn * attn_out_ref[rows, :]
            grad_hidden_ref[rows, :] = hidden
            hat, _ = normalize(hidden)
            mlp_in_ref[rows, :] = (hat * gain * (1.0 + scale) + shift).astype(BF16)
            low_ref[rows, :] = (gate * cot_ref[rows, :]).astype(BF16)
            return 0

        lax.fori_loop(0, pieces, prepare, 0)
        output_ref[...] = jnp.zeros_like(output_ref)
        back_ref[...] = jnp.zeros_like(back_ref)

    @pl.when(j < blocks)
    def _():
        mlp_in, low = mlp_in_ref[...], low_ref[...]
        x = mm(mlp_in, up_ref[...], 1, 0) + bias_ref[0]
        grad_act = mm(low, down_ref[...], 1, 1)
        square = x * x
        t = jnp.tanh(x * (GELU_C + GELU_C * GELU_A * square))
        half = 0.5 + 0.5 * t
        act = (x * half).astype(BF16)
        slope = half + x * (0.5 - 0.5 * t * t) * (GELU_C + 3.0 * GELU_C * GELU_A * square)
        grad_pre = grad_act * slope
        bias_grad_ref[0] = jnp.sum(grad_pre, axis=0, keepdims=True)
        pre_low = grad_pre.astype(BF16)
        output_ref[...] += mm(act, down_ref[...], 1, 0)
        back_ref[...] += mm(pre_low, up_ref[...], 1, 1)
        g_down_ref[...] = mm(act, low, 0, 0).astype(BF16)
        g_pack_ref[...] = mm(mlp_in, pre_low, 0, 0).astype(BF16)

    @pl.when(j == blocks)
    def _():
        def finish(i, sums):
            rows = pl.ds(pl.multiple_of(i * piece, piece), piece)
            cot = cot_ref[rows, :]
            branch = output_ref[rows, :] + down_bias
            hidden = grad_hidden_ref[rows, :]
            output_ref[rows, :] = hidden + gate * branch
            hat, inv = normalize(hidden)
            back = back_ref[rows, :]
            grad_hidden = cot + norm_back(back * ((1.0 + scale) * gain), hat, inv)
            grad_hidden_ref[rows, :] = grad_hidden
            low_ref[rows, :] = (gate_attn * grad_hidden).astype(BF16)
            adds = (grad_hidden * attn_out_ref[rows, :], back, back * hat, cot * branch, cot)
            return tuple(a + jnp.sum(v, axis=0, keepdims=True) for a, v in zip(sums, adds))

        zero = jnp.zeros((1, width), F32)
        sums = lax.fori_loop(0, pieces, finish, (zero,) * 5)
        for i in range(5):
            sums_ref[i : i + 1, :] = sums[i]
        attn_low = low_ref[...]
        g_pack_ref[...] = mm(mixed_ref[...], attn_low, 1, 0).astype(BF16)
        grad_mixed = mm(out_w_ref[...], attn_low, 1, 1).astype(BF16)
        for s in range(slots):
            for c in range(n):
                head = c * slots + s
                grad_mixed_refs[s][c] = grad_mixed[head * HD : (head + 1) * HD]


def middle(tokens, cot, vectors, up_bias, w_pack, w_down, mixed):
    tok, width = tokens.shape
    ff = w_down.shape[0]
    blocks = ff // width
    slots = len(mixed)
    n = mixed[0].shape[0]
    whole = lambda shape: pl.BlockSpec(shape, lambda j: (0,) * len(shape), pipeline_mode=pl.Buffered(1))
    fixed = lambda shape: pl.BlockSpec(shape, lambda j: (0,) * len(shape))
    last = blocks - 1
    head_shape = mixed[0].shape
    flops = 2 * tok * width * (6 * ff + 3 * width)
    return pl.pallas_call(
        partial(middle_kernel, n, slots, blocks),
        grid=(blocks + 1,),
        in_specs=[
            whole(tokens.shape),
            whole(cot.shape),
            whole(vectors.shape),
            pl.BlockSpec((1, 1, width), lambda j: (jnp.minimum(j, last), 0, 0)),
            pl.BlockSpec((width, width), lambda j: (0, jnp.minimum(j, last))),
            pl.BlockSpec((width, width), lambda j: (jnp.minimum(j, last), 0)),
            pl.BlockSpec((width, width), lambda j: (0, blocks), pipeline_mode=pl.Buffered(1)),
        ]
        + [whole(head_shape)] * slots,
        out_specs=[
            fixed((tok, width)),
            fixed((tok, width)),
            fixed((8, width)),
            pl.BlockSpec((1, 1, width), lambda j: (jnp.minimum(j, last), 0, 0)),
            pl.BlockSpec((width, width), lambda j: (jnp.minimum(j, last), 0)),
            pl.BlockSpec((width, width), lambda j: (0, j)),
        ]
        + [fixed(head_shape)] * slots,
        out_shape=[
            jax.ShapeDtypeStruct((tok, width), F32),
            jax.ShapeDtypeStruct((tok, width), F32),
            jax.ShapeDtypeStruct((8, width), F32),
            jax.ShapeDtypeStruct((blocks, 1, width), F32),
            jax.ShapeDtypeStruct((ff, width), BF16),
            jax.ShapeDtypeStruct((width, ff + width), BF16),
        ]
        + [jax.ShapeDtypeStruct(head_shape, BF16)] * slots,
        scratch_shapes=[
            pltpu.VMEM((width, tok), BF16),
            pltpu.VMEM((tok, width), F32),
            pltpu.VMEM((tok, width), BF16),
            pltpu.VMEM((tok, width), BF16),
            pltpu.VMEM((tok, width), F32),
        ],
        compiler_params=pltpu.CompilerParams(vmem_limit_bytes=VMEM_LIMIT),
        cost_estimate=pl.CostEstimate(flops=flops, bytes_accessed=6 * ff * width * 2, transcendentals=tok * ff),
        name="middle",
    )(tokens, cot, vectors, up_bias.reshape(blocks, 1, width), w_pack, w_down, w_pack, *mixed)


MESH = pl.DeviceIdType.MESH
HIGHEST = lax.Precision.HIGHEST


def add_low(a, b):
    return (a.astype(F32) + b.astype(F32)).astype(BF16)


def remote(src, dst, s, r, **where):
    return pltpu.make_async_remote_copy(
        src_ref=src, dst_ref=dst, send_sem=s, recv_sem=r, device_id=where, device_id_type=MESH
    )


def each(count, body):
    lax.fori_loop(0, count, lambda i, _: (body(i), 0)[1], 0)


def greet(me, z, fs, nz):
    barrier = pltpu.get_barrier_semaphore()

    def hello_fsdp(i):
        peer = {"fsdp": lax.rem(me + 1 + i, fs)}
        pl.semaphore_signal(barrier, inc=1, device_id=peer, device_id_type=MESH)

    def hello_seq(i):
        peer = {"seq": lax.rem(z + 1 + i, nz)}
        pl.semaphore_signal(barrier, inc=1, device_id=peer, device_id_type=MESH)

    each(fs - 1, hello_fsdp)
    each(nz - 1, hello_seq)
    pl.semaphore_wait(barrier, fs + nz - 2)


def reduce_kernel(fs, nz, slots, counts, lengths, *refs):
    row_refs, w_refs, refs = refs[:slots], refs[slots : 2 * slots], refs[2 * slots :]
    attn_in_ref, tokens_hbm, hidden_hbm, vec_in_ref, sums_ref, up_bias_ref, *refs = refs
    bulk_refs, (mod_t_ref, cond_ref), refs = refs[:2], refs[2:4], refs[4:]
    inputs_out, qkv_out, pack_out, down_out, total_out, mod_w_out, cond_out = refs[:7]
    (
        w_buf,
        tokens_buf,
        hidden_buf,
        g_buf,
        pair_buf,
        sum_buf,
        recv_buf,
        own_buf,
        up_pack,
        up_down,
        up_qkv,
        part_pack,
        part_down,
        part_qkv,
        twin_pack,
        twin_down,
        twin_qkv,
        tot_pack,
        tot_down,
        tot_qkv,
        vec_buf,
        vec_z,
        vec_own,
        vec_all,
        cond_send,
        cond_recv,
        local_s,
        pair_s,
        pair_r,
        peer_s,
        peer_r,
        up_s,
        up_r,
        twin_s,
        twin_r,
        tot_s,
        tot_r,
        vecz_s,
        vecz_r,
        vec_s,
        vec_r,
        cond_s,
        cond_r,
    ) = refs[7:]
    me = lax.axis_index("fsdp")
    z = lax.axis_index("seq")
    pairs = fs // 2
    k, c = me // 2, lax.rem(me, 2)
    partner = me + 1 - 2 * c
    inner = jnp.logical_or(z == nz // 2 - 1, z == nz // 2)
    outer = jnp.logical_not(inner)
    twin = nz - 1 - z
    mate = z + 1 - 2 * lax.rem(z, 2)
    tok, width = tokens_buf.shape
    shard = g_buf.shape[3]
    groups = width // 128

    loads = [pltpu.make_async_copy(w_refs[s], w_buf.at[s], local_s.at[s]) for s in range(slots)]
    loads.append(pltpu.make_async_copy(tokens_hbm, tokens_buf, local_s.at[slots]))
    loads.append(pltpu.make_async_copy(hidden_hbm, hidden_buf, local_s.at[slots + 1]))
    for load in loads:
        load.start()
    greet(me, z, fs, nz)

    bulk = [
        (src, up, part, other, tot, i)
        for src, up, part, other, tot, count in (
            (bulk_refs[0], up_pack, part_pack, twin_pack, tot_pack, counts[0]),
            (bulk_refs[1], up_down, part_down, twin_down, tot_down, counts[1]),
        )
        for i in range(count)
    ]
    last = [(own_buf, up_qkv, part_qkv, twin_qkv, tot_qkv, s) for s in range(slots)]
    chain = list(enumerate(bulk + last))
    early, late = chain[: len(bulk)], chain[len(bulk) :]

    def up_copy(n, item):
        src, up, _, _, _, i = item
        return remote(src.at[i], up.at[i], up_s.at[n], up_r.at[n], seq=mate)

    def twin_copy(n, item):
        _, _, part, other, _, i = item
        return remote(part.at[i], other.at[i], twin_s.at[n], twin_r.at[n], seq=twin)

    def tot_copy(n, item):
        tot, i = item[4], item[5]
        return remote(tot.at[i], tot.at[i], tot_s.at[n], tot_r.at[n], seq=mate)

    def chain_in(n, item):
        src, up, part, _, _, i = item
        up_copy(n, item).wait_recv()
        part[i] = add_low(src[i], up[i])
        twin_copy(n, item).start()

    def chain_out(n, item):
        _, _, part, other, tot, i = item
        twin_copy(n, item).wait_recv()
        tot[i] = add_low(part[i], other[i])
        tot_copy(n, item).start()

    def plan(items):
        steps = [(chain_in, items[0])]
        for before, item in zip(items[:-1], items[1:]):
            steps += [(chain_in, item), (chain_out, before)]
        return steps + [(chain_out, items[-1])]

    steps = plan(early)

    def advance(count):
        todo = [steps.pop(0) for _ in range(min(count, len(steps)))]
        if todo:

            @pl.when(inner)
            def _():
                for step, (n, item) in todo:
                    step(n, item)

    half = len(early) // 2

    @pl.when(outer)
    def _():
        for n, item in early[:half]:
            up_copy(n, item).start()

    def pair_copy(s, j):
        return remote(g_buf.at[s, j, 1 - c], pair_buf.at[s, j], pair_s.at[s, j], pair_r.at[s, j], fsdp=partner)

    def peer_copy(s, j):
        return remote(sum_buf.at[s, j], recv_buf.at[s, k], peer_s.at[s, j], peer_r.at[s, k], fsdp=2 * j + c)

    def peer_arrival(s, j):
        return remote(sum_buf.at[s, j], recv_buf.at[s, j], peer_s.at[s, j], peer_r.at[s, j], fsdp=2 * j + c)

    for s in range(slots):
        grad = mm(attn_in_ref[...], row_refs[s][...], 0, 1).astype(BF16)
        for i in range(fs):
            g_buf[s, i // 2, i % 2] = grad[i * shard : (i + 1) * shard]
        each(pairs, lambda i: pair_copy(s, lax.rem(k + 1 + i, pairs)).start())

    advance(1)

    def forward(i):
        j = lax.rem(k + 1 + i, pairs)
        for s in range(slots):
            pair_copy(s, j).wait_recv()
            sum_buf[s, j] = add_low(g_buf[s, j, c], pair_buf[s, j])
            peer_copy(s, j).start()

    each(pairs - 1, forward)
    for load in loads:
        load.wait()

    scale_mlp, gate_mlp, mlp_gain = (vec_in_ref[i : i + 1, :] for i in (2, 3, 4))
    attn_gain, scale_attn = (vec_in_ref[i : i + 1, :] for i in (6, 7))
    piece = min(256, tok)
    back_sum = hat_sum = jnp.zeros((1, width), F32)
    for i in range(tok // piece):
        rows = slice(i * piece, (i + 1) * piece)
        grad = None
        for s in range(slots):
            part = mm(row_refs[s][:, rows], w_buf[s], 0, 1)
            grad = part if grad is None else grad + part
        hat, inv = normalize(tokens_buf[rows, :])
        scaled = grad * ((1.0 + scale_attn) * attn_gain)
        inputs_out[rows, :] = hidden_buf[rows, :] + norm_back(scaled, hat, inv)
        back_sum = back_sum + jnp.sum(grad, axis=0, keepdims=True)
        hat_sum = hat_sum + jnp.sum(grad * hat, axis=0, keepdims=True)
        advance(2)

    sums = [sums_ref[i : i + 1, :] for i in range(5)]
    vectors = [back_sum, hat_sum * attn_gain, sums[0], sums[1], sums[2] * mlp_gain, sums[3]]
    vectors += [hat_sum * (1.0 + scale_attn), sums[2] * (1.0 + scale_mlp)]
    vectors += [up_bias_ref[i] for i in range(up_bias_ref.shape[0])]
    vectors.append(sums[4] * gate_mlp)
    for p, v in enumerate(vectors):
        for i in range(groups):
            vec_buf[p * groups + i : p * groups + i + 1, :] = v[:, i * 128 : (i + 1) * 128]
    used = len(vectors) * groups
    vec_buf[used:, :] = jnp.zeros((vec_buf.shape[0] - used, 128), F32)
    vec_z[z] = vec_buf[...]

    def vecz_copy(i):
        return remote(vec_buf, vec_z.at[z], vecz_s.at[i], vecz_r.at[z], seq=lax.rem(z + 1 + i, nz))

    def vecz_arrival(i):
        peer = lax.rem(z + 1 + i, nz)
        return remote(vec_buf, vec_z.at[peer], vecz_s.at[i], vecz_r.at[peer], seq=peer)

    each(nz - 1, lambda i: vecz_copy(i).start())

    @pl.when(outer)
    def _():
        for n, item in early[half:]:
            up_copy(n, item).start()

    advance(2)
    each(nz - 1, lambda i: vecz_arrival(i).wait_recv())
    summed = vec_z[0]
    for i in range(1, nz):
        summed = summed + vec_z[i]
    vec_own[...] = summed
    vec_all[me] = summed

    def vec_copy(i):
        return remote(vec_own, vec_all.at[me], vec_s.at[i], vec_r.at[me], fsdp=lax.rem(me + 1 + i, fs))

    def vec_arrival(i):
        peer = lax.rem(me + 1 + i, fs)
        return remote(vec_own, vec_all.at[peer], vec_s.at[i], vec_r.at[peer], fsdp=peer)

    each(fs - 1, lambda i: vec_copy(i).start())
    advance(len(steps))

    for s in range(slots):
        pair_copy(s, k).wait_recv()
        own = g_buf[s, k, c].astype(F32) + pair_buf[s, k].astype(F32)

        def gather_in(i, acc):
            j = lax.rem(k + 1 + i, pairs)
            peer_arrival(s, j).wait_recv()
            return acc + recv_buf[s, j].astype(F32)

        own_buf[s] = lax.fori_loop(0, pairs - 1, gather_in, own).astype(BF16)

        @pl.when(outer)
        def _():
            up_copy(*late[s]).start()

    each(fs - 1, lambda i: vec_arrival(i).wait_recv())
    lane_from = lax.broadcasted_iota(jnp.int32, (256, 128), 0)
    lane_to = lax.broadcasted_iota(jnp.int32, (256, 128), 1)
    part, first, place = None, 0, 0
    for which, length in enumerate(lengths):
        block = length // fs
        for i in range(-(-block // 128)):
            offset = me * block + 128 * i
            row = first + offset // 128
            select = (lane_from == lane_to + lax.rem(offset, 128)).astype(F32)
            both = jnp.concatenate([vec_all[:, pl.ds(row, 1), :][:, 0], vec_all[:, pl.ds(row + 1, 1), :][:, 0]], axis=1)
            rows = lax.dot_general(
                both, select, (((1,), (0,)), ((), ())), precision=HIGHEST, preferred_element_type=F32
            )
            total_out[place : place + 1, :] = jnp.sum(rows, axis=0, keepdims=True)
            place += 1
            if which > 0:
                continue
            share = lax.dot_general(
                rows, mod_t_ref[i], (((1,), (0,)), ((), ())), precision=HIGHEST, preferred_element_type=F32
            )
            part = share if part is None else part + share
            outer_product = lax.dot_general(
                cond_ref[...], rows, (((0,), (0,)), ((), ())), precision=HIGHEST, preferred_element_type=F32
            )
            wide = min(128, block - i * 128)
            mod_w_out[:, i * 128 : i * 128 + wide] = outer_product[:, :wide]
        first += length // 128
    cond_send[...] = jnp.broadcast_to(part[:, None, :], cond_send.shape)

    def cond_copy(i):
        peer = lax.rem(me + 1 + i, fs)
        return remote(cond_send.at[peer], cond_recv.at[me], cond_s.at[i], cond_r.at[me], fsdp=peer)

    def cond_arrival(i):
        peer = lax.rem(me + 1 + i, fs)
        return remote(cond_send.at[peer], cond_recv.at[peer], cond_s.at[i], cond_r.at[peer], fsdp=peer)

    each(fs - 1, lambda i: cond_copy(i).start())
    steps.extend(plan(late))
    advance(len(steps))
    cond_recv[me] = cond_send[me]
    each(fs - 1, lambda i: cond_arrival(i).wait_recv())
    cond_out[...] = jnp.sum(cond_recv[...], axis=0)

    @pl.when(outer)
    def _():
        for n, item in chain:
            tot_copy(n, item).wait_recv()
            up_copy(n, item).wait_send()

    pack_out[...] = tot_pack[...]
    down_out[...] = tot_down[...]
    qkv_out[...] = tot_qkv[...]

    @pl.when(inner)
    def _():
        for n, item in chain:
            twin_copy(n, item).wait_send()
            tot_copy(n, item).wait_send()

    def drain_peers(i):
        vec_copy(i).wait_send()
        cond_copy(i).wait_send()

    def drain_pairs(i):
        for s in range(slots):
            pair_copy(s, i).wait_send()

    def drain_sums(i):
        for s in range(slots):
            peer_copy(s, lax.rem(k + 1 + i, pairs)).wait_send()

    each(fs - 1, drain_peers)
    each(pairs, drain_pairs)
    each(pairs - 1, drain_sums)
    each(nz - 1, lambda i: vecz_copy(i).wait_send())


def reduce_all(
    grad_rows, weights, attn_in, tokens, grad_hidden, vectors, sums, up_bias_sum, part_pack, part_down, mod_t, cond, mod_cols, fs, nz
):
    slots = len(grad_rows)
    tok, width = tokens.shape
    shard = width // fs
    count = lambda a: 3 if a.shape[0] % 48 == 0 else 1
    counts = (count(part_pack), count(part_down))
    split = lambda a, n: a.reshape(n, a.shape[0] // n, a.shape[1])
    pack, down = split(part_pack, counts[0]), split(part_down, counts[1])
    pairs = fs // 2
    items = sum(counts) + slots
    ff = up_bias_sum.size
    lengths = (6 * width, width, width, ff, width)
    rows = sum(lengths) // 128 + 2
    places = sum(-(-v // fs // 128) for v in lengths)
    vmem = pl.BlockSpec(memory_space=pltpu.VMEM)
    hbm = pl.BlockSpec(memory_space=pl.ANY)
    low = lambda *shape: pltpu.VMEM(shape, BF16)
    wide = lambda *shape: pltpu.VMEM(shape, F32)
    dma = lambda *shape: pltpu.SemaphoreType.DMA(shape)
    qkv_shape = (slots, shard, width)
    triple = [low(*pack.shape), low(*down.shape), low(*qkv_shape)]
    cols = grad_rows[0].shape[0]
    inputs_grad, qkv_sum, pack_sum, down_sum, total, mod_w, cond_grad = pl.pallas_call(
        partial(reduce_kernel, fs, nz, slots, counts, lengths),
        in_specs=[vmem] * slots + [hbm] * slots + [vmem, hbm, hbm] + [vmem] * 7,
        out_specs=[vmem] * 7,
        out_shape=[
            jax.ShapeDtypeStruct((tok, width), F32),
            jax.ShapeDtypeStruct(qkv_shape, BF16),
            jax.ShapeDtypeStruct(pack.shape, BF16),
            jax.ShapeDtypeStruct(down.shape, BF16),
            jax.ShapeDtypeStruct((places, 128), F32),
            jax.ShapeDtypeStruct((cond.shape[1], mod_cols), F32),
            jax.ShapeDtypeStruct((8, 128), F32),
        ],
        scratch_shapes=[
            low(slots, width, cols),
            wide(tok, width),
            wide(tok, width),
            low(slots, pairs, 2, shard, width),
            low(slots, pairs, shard, width),
            low(slots, pairs, shard, width),
            low(slots, pairs, shard, width),
            low(*qkv_shape),
        ]
        + triple * 4
        + [
            wide(rows, 128),
            wide(nz, rows, 128),
            wide(rows, 128),
            wide(fs, rows, 128),
            wide(fs, 8, 128),
            wide(fs, 8, 128),
            dma(slots + 2),
            dma(slots, pairs),
            dma(slots, pairs),
            dma(slots, pairs),
            dma(slots, pairs),
        ]
        + [dma(items)] * 6
        + [dma(nz - 1), dma(nz), dma(fs - 1), dma(fs), dma(fs - 1), dma(fs)],
        compiler_params=pltpu.CompilerParams(vmem_limit_bytes=VMEM_LIMIT, collective_id=1, has_side_effects=True),
        cost_estimate=pl.CostEstimate(flops=12 * tok * width * cols, bytes_accessed=10**8, transcendentals=0),
        name="reduce_all",
    )(*grad_rows, *weights, attn_in, tokens, grad_hidden, vectors, sums, up_bias_sum, pack, down, mod_t, cond)
    blocks, place = [], 0
    for v in lengths:
        n = -(-v // fs // 128)
        blocks.append(total[place : place + n].reshape(-1)[: v // fs])
        place += n
    return (
        inputs_grad, qkv_sum, pack_sum.reshape(part_pack.shape), down_sum.reshape(part_down.shape), blocks, mod_w, cond_grad
    )


def per_device(
    inputs,
    conditioning,
    cotangent,
    attn_gain,
    mlp_gain,
    qkv_weight,
    out_weight,
    up_weight,
    up_bias,
    down_weight,
    down_bias,
    mod_weight,
    mod_bias,
):
    n = lax.axis_size("seq")
    fs = lax.axis_size("fsdp")
    z = lax.axis_index("seq")
    me = lax.axis_index("fsdp")
    tokens = inputs[0]
    tok, width = tokens.shape
    slots = H // n
    gather = lambda a: lax.all_gather(a, "fsdp", axis=0, tiled=True)

    smalls = [attn_gain, mlp_gain, up_bias, down_bias, conditioning[0]]
    sizes = [a.shape[0] for a in smalls]
    packed = lax.all_gather(jnp.concatenate(smalls), "fsdp", axis=0)
    offsets = [sum(sizes[:i]) for i in range(len(sizes))]
    attn_gain_full, mlp_gain_full, up_bias_full, down_bias_full = (
        packed[:, o : o + s].reshape(-1) for o, s in zip(offsets[:4], sizes[:4])
    )
    cond_all = packed[:, offsets[4] :]
    cond_act_all = jax.nn.silu(cond_all)
    cond_low_all = cond_act_all.astype(BF16)
    mod_low = mod_weight.astype(BF16)
    mod_own = mm(cond_low_all, mod_low, 1, 0) + mod_bias[None, :]
    modulation = lax.all_to_all(mod_own, "fsdp", split_axis=0, concat_axis=0, tiled=True).reshape(-1)
    shift_attn, scale_attn, gate_attn, shift_mlp, scale_mlp, gate_mlp = jnp.split(modulation, 6)

    shard = qkv_weight.shape[0]
    qkv_low = qkv_weight.astype(BF16).reshape(shard, 3, n, slots, HD)
    qkv_slots = [
        gather(qkv_low[:, :, :, s].transpose(0, 2, 1, 3).reshape(shard, n * 3 * HD)) for s in range(slots)
    ]
    w_pack = gather(jnp.concatenate([up_weight.astype(BF16), out_weight.astype(BF16)], axis=1))
    down_full = gather(down_weight.astype(BF16))

    inv_freq = jnp.exp(-math.log(10000.0) * jnp.arange(HD // 2, dtype=F32) * (2.0 / HD))
    angles = inv_freq[:, None] * jnp.arange(tok * n, dtype=F32)[None, :]
    cos_all = jnp.cos(angles).reshape(HD // 2, n, tok).transpose(1, 0, 2)
    sin_all = jnp.sin(angles).reshape(HD // 2, n, tok).transpose(1, 0, 2)
    cos_own = lax.dynamic_index_in_dim(cos_all, z, 0, keepdims=False)
    sin_own = lax.dynamic_index_in_dim(sin_all, z, 0, keepdims=False)

    hat_attn, inv_attn = normalize(tokens)
    normed_attn = hat_attn * attn_gain_full
    attn_in = (normed_attn * (1.0 + scale_attn) + shift_attn).astype(BF16)
    swap = lambda a: lax.all_to_all(a, "seq", split_axis=0, concat_axis=0, tiled=True)
    heads = [swap(project(w, attn_in, cos_own, sin_own, n)) for w in qkv_slots]
    mixed_heads, log_totals, mixed_back = [], [], []
    for x in heads:
        o, lse = attend(x)
        mixed_heads.append(o)
        log_totals.append(lse)
        mixed_back.append(swap(o))
    vectors = jnp.stack(
        [gate_attn, shift_mlp, scale_mlp, gate_mlp, mlp_gain_full, down_bias_full, attn_gain_full, scale_attn], axis=0
    )
    output, grad_hidden, sums, up_bias_sum, g_down, g_pack, *grad_mixed = middle(
        tokens, cotangent[0], vectors, up_bias_full, w_pack, down_full, mixed_back
    )
    scatter = lambda a: lax.psum_scatter(a, "fsdp", scatter_dimension=0, tiled=True)
    part_down = scatter(g_down)
    part_pack = scatter(g_pack)

    grad_slots = []
    for s in range(slots):
        g = swap(grad_mixed[s])
        if s == 1:
            g, part_down = lax.optimization_barrier((g, part_down))
        grad_slots.append(swap(attend_back(heads[s], g, mixed_heads[s], log_totals[s], cos_all, sin_all)))
    grad_slots[-1], part_pack = lax.optimization_barrier((grad_slots[-1], part_pack))

    mod_cols = mod_weight.shape[1]
    mod_t = jnp.pad(mod_low.T.astype(F32), ((0, -mod_cols % 128), (0, 0))).reshape(-1, 128, mod_weight.shape[0])
    inputs_grad, qkv_sum, pack_sum, down_sum, blocks, mod_weight_grad, cond_grad = reduce_all(
        [g.reshape(n * 3 * HD, tok) for g in grad_slots],
        qkv_slots,
        attn_in,
        tokens,
        grad_hidden,
        vectors,
        sums,
        up_bias_sum,
        part_pack,
        part_down,
        mod_t,
        cond_low_all.astype(F32),
        mod_cols,
        fs,
        n,
    )
    mod_bias_grad, attn_gain_grad, mlp_gain_grad, up_bias_grad, down_bias_grad = blocks
    _, silu_pull = jax.vjp(jax.nn.silu, conditioning)
    conditioning_grad = silu_pull(cond_grad[:1])[0]
    qkv_weight_grad = (
        qkv_sum.astype(F32).reshape(slots, shard, n, 3, HD).transpose(1, 3, 2, 0, 4).reshape(shard, 3 * width)
    )
    pack_sum, down_sum = pack_sum.astype(F32), down_sum.astype(F32)
    ff = up_bias.shape[0] * fs
    out_sum, up_sum = pack_sum[:, ff:], pack_sum[:, :ff]
    return (
        output[None],
        inputs_grad[None],
        conditioning_grad,
        attn_gain_grad,
        mlp_gain_grad,
        qkv_weight_grad,
        out_sum,
        up_sum,
        up_bias_grad,
        down_sum,
        down_bias_grad,
        mod_weight_grad,
        mod_bias_grad,
    )


def solution(mesh):
    specs = (
        P("fsdp", "seq", None),
        P("fsdp", None),
        P("fsdp", "seq", None),
        P("fsdp"),
        P("fsdp"),
        P("fsdp", None),
        P("fsdp", None),
        P("fsdp", None),
        P("fsdp"),
        P("fsdp", None),
        P("fsdp"),
        P(None, "fsdp"),
        P("fsdp"),
    )
    out_specs = (specs[0], specs[0], specs[1]) + specs[3:]
    return jax.shard_map(per_device, mesh=mesh, in_specs=specs, out_specs=out_specs, check_vma=False)
```

```python
from functools import partial
import math

import jax
import jax.numpy as jnp
from jax import lax
from jax.experimental import pallas as pl
from jax.experimental.pallas import tpu as pltpu
from jax.sharding import PartitionSpec as P

H = 12
HD = 64
EPSILON = 1e-05
BF16 = jnp.bfloat16
F32 = jnp.float32
LOG2E = math.log2(math.e)
VMEM_LIMIT = 60 * 1024 * 1024


def mm(a, b, ca, cb):
    return lax.dot_general(a, b, (((ca,), (cb,)), ((), ())), preferred_element_type=F32)


def normalize(values):
    centre = jnp.mean(values, axis=-1, keepdims=True)
    shifted = values - centre
    variance = jnp.mean(shifted * shifted, axis=-1, keepdims=True)
    inv_std = lax.rsqrt(variance + EPSILON)
    return (shifted * inv_std, inv_std)


def norm_back(grad_hat, normed_hat, inv_std):
    mean_grad = jnp.mean(grad_hat, axis=-1, keepdims=True)
    mean_mixed = jnp.mean(grad_hat * normed_hat, axis=-1, keepdims=True)
    return inv_std * (grad_hat - mean_grad - normed_hat * mean_mixed)


MESH = pl.DeviceIdType.MESH
HIGHEST = lax.Precision.HIGHEST


def add_low(a, b):
    return (a.astype(F32) + b.astype(F32)).astype(BF16)


def remote(src, dst, s, r, **where):
    return pltpu.make_async_remote_copy(
        src_ref=src, dst_ref=dst, send_sem=s, recv_sem=r, device_id=where, device_id_type=MESH
    )


def each(count, body):
    lax.fori_loop(0, count, lambda i, _: (body(i), 0)[1], 0)


def greet(me, z, fs, nz):
    barrier = pltpu.get_barrier_semaphore()

    def hello_fsdp(i):
        peer = {"fsdp": lax.rem(me + 1 + i, fs)}
        pl.semaphore_signal(barrier, inc=1, device_id=peer, device_id_type=MESH)

    def hello_seq(i):
        peer = {"seq": lax.rem(z + 1 + i, nz)}
        pl.semaphore_signal(barrier, inc=1, device_id=peer, device_id_type=MESH)

    each(fs - 1, hello_fsdp)
    each(nz - 1, hello_seq)
    pl.semaphore_wait(barrier, fs + nz - 2)


def start_kernel(fs, nz, slots, *refs):
    (
        qkv_ref,
        tokens_hbm,
        attn_gain_ref,
        mlp_gain_ref,
        up_bias_ref,
        down_bias_ref,
        cond_ref,
        mod_w_ref,
        mod_b_ref,
        cos_ref,
        sin_ref,
    ) = refs[:11]
    refs = refs[11:]
    heads_ref, rest_refs, refs = refs[0], refs[1:slots], refs[slots:]
    w_ref, attn_in_ref, vec_ref, bias_ref, cond_out = refs[:5]
    (
        tokens_buf,
        w_own,
        z_send,
        narrow,
        spread,
        mod_wide,
        small_send,
        small_all,
        mod_send,
        mod_recv,
        w_full,
        local_s,
        small_s,
        small_r,
        mod_s,
        mod_r,
        w_s,
        w_f,
        w_r,
        z_s,
        z_r,
    ) = refs[5:]
    me = lax.axis_index("fsdp")
    z = lax.axis_index("seq")
    pairs = fs // 2
    k, c = me // 2, lax.rem(me, 2)
    partner = me + 1 - 2 * c
    tok, width = tokens_buf.shape
    shard = w_own.shape[1]
    ff = spread.shape[1]
    block = nz * HD

    load = pltpu.make_async_copy(tokens_hbm, tokens_buf, local_s)
    load.start()
    greet(me, z, fs, nz)

    narrow[...] = jnp.zeros_like(narrow)
    for i, piece in enumerate((attn_gain_ref, mlp_gain_ref, down_bias_ref)):
        narrow[i : i + 1, :shard] = piece[...]
    spread[...] = jnp.zeros_like(spread)
    spread[0:1, : up_bias_ref.shape[1]] = up_bias_ref[...]
    placed = pltpu.roll(narrow[...], me * shard, 1)
    for i in range(3):
        small_send[:, i * width : (i + 1) * width] = placed[i : i + 1]
    placed = pltpu.roll(spread[...], me * up_bias_ref.shape[1], 1)
    small_send[:, 3 * width : 3 * width + ff] = placed[0:1]
    small_send[:, 3 * width + ff :] = cond_ref[...]
    small_all[me] = small_send[...]

    def small_copy(i):
        return remote(small_send, small_all.at[me], small_s.at[i], small_r.at[me], fsdp=lax.rem(me + 1 + i, fs))

    def small_arrival(i):
        peer = lax.rem(me + 1 + i, fs)
        return remote(small_send, small_all.at[peer], small_s.at[i], small_r.at[peer], fsdp=peer)

    each(fs - 1, lambda i: small_copy(i).start())

    for s in range(slots):
        for part in range(3):
            columns = slice(part * width + s * block, part * width + (s + 1) * block)
            w_own[s, :, part * block : (part + 1) * block] = qkv_ref[:, columns].astype(BF16)
        w_ref[s, me] = w_own[s]

    def w_peer(s, i):
        j = lax.rem(k + 1 + i, pairs)
        return remote(w_own.at[s], w_ref.at[s, me], w_s.at[s, i], w_r.at[s, me], fsdp=2 * j + c)

    def w_partner(s):
        return remote(w_own.at[s], w_ref.at[s, me], w_s.at[s, pairs - 1], w_r.at[s, me], fsdp=partner)

    def w_arrival(s, j):
        return remote(w_own.at[s], w_ref.at[s, j], w_s.at[s, 0], w_r.at[s, j], fsdp=partner)

    def w_pass(s, i):
        j = 2 * lax.rem(k + 1 + i, pairs) + c
        return remote(w_ref.at[s, j], w_ref.at[s, j], w_f.at[s, i], w_r.at[s, j], fsdp=partner)

    def send_weight(s):
        each(pairs - 1, lambda i: w_peer(s, i).start())
        w_partner(s).start()

    def pass_weight(s):
        def step(i):
            w_arrival(s, 2 * lax.rem(k + 1 + i, pairs) + c).wait_recv()
            w_pass(s, i).start()

        each(pairs - 1, step)

    send_weight(0)
    for s in range(1, slots - 1):
        send_weight(s)

    each(fs - 1, lambda i: small_arrival(i).wait_recv())
    small_sum = jnp.sum(small_all[:, :, : 3 * width + ff], axis=0)
    cond_all = small_all[:, 0, 3 * width + ff :]
    cond_low = (cond_all / (1.0 + jnp.exp(-cond_all))).astype(BF16)
    cond_out[...] = cond_low.astype(F32)
    own_mod = mm(cond_low, mod_w_ref[...].astype(BF16), 1, 0) + mod_b_ref[...]
    mod_wide[...] = jnp.zeros_like(mod_wide)
    mod_wide[:, : own_mod.shape[1]] = own_mod
    placed = pltpu.roll(mod_wide[...], me * own_mod.shape[1], 1)
    for i in range(fs):
        mod_send[i] = placed[i : i + 1]
    mod_recv[me] = mod_send[me]

    def mod_copy(i):
        peer = lax.rem(me + 1 + i, fs)
        return remote(mod_send.at[peer], mod_recv.at[me], mod_s.at[i], mod_r.at[me], fsdp=peer)

    def mod_arrival(i):
        peer = lax.rem(me + 1 + i, fs)
        return remote(mod_send.at[peer], mod_recv.at[peer], mod_s.at[i], mod_r.at[peer], fsdp=peer)

    each(fs - 1, lambda i: mod_copy(i).start())
    send_weight(slots - 1)
    pass_weight(0)

    attn_gain, mlp_gain, down_bias = (small_sum[:, i * width : (i + 1) * width] for i in range(3))
    for i in range(ff // width):
        bias_ref[i] = small_sum[:, (3 + i) * width : (4 + i) * width]
    load.wait()
    piece = min(256, tok)
    each(fs - 1, lambda i: mod_arrival(i).wait_recv())
    modulation = jnp.sum(mod_recv[...], axis=0)
    shift_attn, scale_attn, gate_attn, shift_mlp, scale_mlp, gate_mlp = (
        modulation[:, i * width : (i + 1) * width] for i in range(6)
    )
    kept = (gate_attn, shift_mlp, scale_mlp, gate_mlp, mlp_gain, down_bias, attn_gain, scale_attn)
    for i, v in enumerate(kept):
        vec_ref[i : i + 1, :] = v
    for i in range(tok // piece):
        rows = slice(i * piece, (i + 1) * piece)
        hat, _ = normalize(tokens_buf[rows, :])
        attn_in_ref[rows, :] = (hat * attn_gain * (1.0 + scale_attn) + shift_attn).astype(BF16)

    cosine, sine = cos_ref[...], sin_ref[...]
    half = HD // 2

    def project(s, out_ref):
        each(pairs, lambda j: w_arrival(s, 2 * j + 1 - c).wait_recv())
        if shard % 16 == 0:
            weight = w_ref[s].reshape(fs * shard, 3 * block)
        else:
            for i in range(fs):
                w_full[i * shard : (i + 1) * shard, :] = w_ref[s, i].astype(F32)
            weight = w_full[...].astype(BF16)
        rows = mm(weight, attn_in_ref[...], 0, 1).astype(BF16)
        for shard_of in range(nz):
            for part in range(3):
                base = (part * nz + shard_of) * HD
                if part == 2:
                    out_ref[shard_of, part * HD : (part + 1) * HD, :] = rows[base : base + HD]
                else:
                    a = rows[base : base + half].astype(F32)
                    b = rows[base + half : base + HD].astype(F32)
                    out_ref[shard_of, part * HD : part * HD + half, :] = (a * cosine - b * sine).astype(BF16)
                    out_ref[shard_of, part * HD + half : (part + 1) * HD, :] = (b * cosine + a * sine).astype(BF16)

    def z_copy(i):
        peer = lax.rem(z + 1 + i, nz)
        return remote(z_send.at[peer], heads_ref.at[z], z_s.at[i], z_r.at[z], seq=peer)

    def z_arrival(i):
        peer = lax.rem(z + 1 + i, nz)
        return remote(z_send.at[peer], heads_ref.at[peer], z_s.at[i], z_r.at[peer], seq=peer)

    project(0, z_send)
    each(nz - 1, lambda i: z_copy(i).start())
    heads_ref[z] = z_send[z]
    for s in range(1, slots):
        pass_weight(s)
        project(s, rest_refs[s - 1])

    each(nz - 1, lambda i: z_arrival(i).wait_recv())
    each(nz - 1, lambda i: z_copy(i).wait_send())

    def drain_peers(i):
        small_copy(i).wait_send()
        mod_copy(i).wait_send()

    def drain_weights(i):
        for s in range(slots):
            w_peer(s, i).wait_send()
            w_pass(s, i).wait_send()

    each(fs - 1, drain_peers)
    each(pairs - 1, drain_weights)
    for s in range(slots):
        w_partner(s).wait_send()


def start(qkv_weight, tokens, gains, cond, mod_weight, mod_bias, cosine, sine, fs, nz):
    slots = H // nz
    tok, width = tokens.shape
    shard = qkv_weight.shape[0]
    pairs = fs // 2
    row = lambda v: v.reshape(1, -1)
    ff = gains[2].shape[0] * fs
    vmem = pl.BlockSpec(memory_space=pltpu.VMEM)
    hbm = pl.BlockSpec(memory_space=pl.ANY)
    low = lambda *shape: pltpu.VMEM(shape, BF16)
    wide = lambda *shape: pltpu.VMEM(shape, F32)
    dma = lambda *shape: pltpu.SemaphoreType.DMA(shape)
    head_shape = (nz, 3 * HD, tok)
    cols = 3 * nz * HD
    small = 3 * width + ff + cond.shape[-1]
    outs = pl.pallas_call(
        partial(start_kernel, fs, nz, slots),
        in_specs=[vmem, hbm] + [vmem] * 9,
        out_specs=[vmem] * (slots + 5),
        out_shape=[jax.ShapeDtypeStruct(head_shape, BF16)] * slots
        + [
            jax.ShapeDtypeStruct((slots, fs, shard, cols), BF16),
            jax.ShapeDtypeStruct((tok, width), BF16),
            jax.ShapeDtypeStruct((8, width), F32),
            jax.ShapeDtypeStruct((ff // width, 1, width), F32),
            jax.ShapeDtypeStruct((fs, cond.shape[-1]), F32),
        ],
        scratch_shapes=[
            wide(tok, width),
            low(slots, shard, cols),
            low(*head_shape),
            wide(8, width),
            wide(8, ff),
            wide(fs, 6 * width),
            wide(1, small),
            wide(fs, 1, small),
            wide(fs, 1, 6 * width),
            wide(fs, 1, 6 * width),
            wide(*((8, 128) if shard % 16 == 0 else (width, cols))),
            pltpu.SemaphoreType.DMA,
            dma(fs - 1),
            dma(fs),
            dma(fs - 1),
            dma(fs),
            dma(slots, pairs),
            dma(slots, pairs),
            dma(slots, fs),
            dma(nz - 1),
            dma(nz),
        ],
        compiler_params=pltpu.CompilerParams(vmem_limit_bytes=VMEM_LIMIT, collective_id=2, has_side_effects=True),
        cost_estimate=pl.CostEstimate(flops=6 * tok * width * cols, bytes_accessed=10**8, transcendentals=0),
        name="start",
    )(
        qkv_weight,
        tokens,
        row(gains[0]),
        row(gains[1]),
        row(gains[2]),
        row(gains[3]),
        cond.reshape(1, -1),
        mod_weight,
        row(mod_bias),
        cosine,
        sine,
    )
    return outs[:slots], *outs[slots:]


def attend_kernel(n, tok, sub, x_ref, o_ref, lse_ref, k_ref):
    step = pl.program_id(0)

    @pl.when(step == 0)
    def _():
        for c in range(n):
            k_ref[c * tok : (c + 1) * tok, :] = x_ref[c, HD : 2 * HD, :].T

    scale = LOG2E / math.sqrt(HD)
    width = tok // sub

    def score(i):
        q = x_ref[step, 0:HD, i * width : (i + 1) * width]
        return mm(k_ref[...], q, 1, 0)

    def soft(s):
        top = jnp.max(s, axis=0, keepdims=True) * scale
        p = jnp.exp2(s * scale - top)
        total = jnp.sum(p, axis=0, keepdims=True)
        return top, total, p.astype(BF16)

    def mix(i, top, total, p):
        o = None
        for c in range(n):
            part = mm(x_ref[c, 2 * HD : 3 * HD, :], p[c * tok : (c + 1) * tok], 1, 0)
            o = part if o is None else o + part
        o_ref[0, :, i * width : (i + 1) * width] = (o / total).astype(BF16)
        lse_ref[0, :, i * width : (i + 1) * width] = top + jnp.log2(total)

    scores = [score(0)]
    pending = None
    for i in range(sub):
        if i + 1 < sub:
            scores.append(score(i + 1))
        done = soft(scores[i])
        if pending is not None:
            mix(i - 1, *pending)
        pending = done
    mix(sub - 1, *pending)


def attend(x):
    n, _, tok = x.shape
    length = n * tok
    return pl.pallas_call(
        partial(attend_kernel, n, tok, 2),
        grid=(n,),
        in_specs=[pl.BlockSpec(x.shape, lambda i: (0, 0, 0))],
        out_specs=[
            pl.BlockSpec((1, HD, tok), lambda i: (i, 0, 0)),
            pl.BlockSpec((1, 1, tok), lambda i: (i, 0, 0)),
        ],
        out_shape=[
            jax.ShapeDtypeStruct((n, HD, tok), BF16),
            jax.ShapeDtypeStruct((n, 1, tok), F32),
        ],
        scratch_shapes=[pltpu.VMEM((length, HD), BF16)],
        compiler_params=pltpu.CompilerParams(vmem_limit_bytes=VMEM_LIMIT),
        cost_estimate=pl.CostEstimate(
            flops=16 * length * length * HD, bytes_accessed=8 * length * HD, transcendentals=length * length
        ),
        name="attend",
    )(x)


def attend_back_kernel(
    n, tok, sub, x_ref, g_ref, o_ref, lse_ref, cos_ref, sin_ref, out_ref, k_ref, v_ref, dk_ref, dv_ref
):
    step = pl.program_id(0)
    half = HD // 2

    @pl.when(step == 0)
    def _():
        for c in range(n):
            k_ref[c * tok : (c + 1) * tok, :] = x_ref[c, HD : 2 * HD, :].T
            v_ref[c * tok : (c + 1) * tok, :] = x_ref[c, 2 * HD : 3 * HD, :].T
        dk_ref[...] = jnp.zeros_like(dk_ref)
        dv_ref[...] = jnp.zeros_like(dv_ref)

    scale = LOG2E / math.sqrt(HD)
    width = tok // sub

    def turn_back(grad, cosine, sine):
        a, b = grad[:half], grad[half:]
        return (a * cosine + b * sine).astype(BF16), (b * cosine - a * sine).astype(BF16)

    for i in range(sub):
        cols = slice(i * width, (i + 1) * width)
        q = x_ref[step, 0:HD, cols]
        g = g_ref[step, :, cols]
        o = o_ref[step, :, cols]
        centre = jnp.sum(g.astype(F32) * o.astype(F32), axis=0, keepdims=True)
        s = mm(k_ref[...], q, 1, 0)
        dp = mm(v_ref[...], g, 1, 0)
        p = jnp.exp2(s * scale - lse_ref[step, :, cols])
        p_low = p.astype(BF16)
        ds = (p * (dp - centre)).astype(BF16)
        dv_ref[...] += mm(g, p_low, 1, 1)
        dk_ref[...] += mm(q, ds, 1, 1)
        dq = None
        for c in range(n):
            part = mm(x_ref[c, HD : 2 * HD, :], ds[c * tok : (c + 1) * tok], 1, 0)
            dq = part if dq is None else dq + part
        dq = dq * (1.0 / math.sqrt(HD))
        a, b = turn_back(dq, cos_ref[step, :, cols], sin_ref[step, :, cols])
        out_ref[step, 0:half, cols] = a
        out_ref[step, half:HD, cols] = b

    @pl.when(step == n - 1)
    def _():
        for c in range(n):
            dk = dk_ref[:, c * tok : (c + 1) * tok] * (1.0 / math.sqrt(HD))
            a, b = turn_back(dk, cos_ref[c], sin_ref[c])
            out_ref[c, HD : HD + half, :] = a
            out_ref[c, HD + half : 2 * HD, :] = b
            out_ref[c, 2 * HD : 3 * HD, :] = dv_ref[:, c * tok : (c + 1) * tok].astype(BF16)


def attend_back(x, g, o, lse, cosine, sine):
    n, _, tok = x.shape
    length = n * tok
    whole = lambda a: pl.BlockSpec(a.shape, lambda i: (0,) * a.ndim)
    return pl.pallas_call(
        partial(attend_back_kernel, n, tok, 2),
        grid=(n,),
        in_specs=[whole(a) for a in (x, g, o, lse, cosine, sine)],
        out_specs=whole(x),
        out_shape=jax.ShapeDtypeStruct(x.shape, BF16),
        scratch_shapes=[
            pltpu.VMEM((length, HD), BF16),
            pltpu.VMEM((length, HD), BF16),
            pltpu.VMEM((HD, length), F32),
            pltpu.VMEM((HD, length), F32),
        ],
        compiler_params=pltpu.CompilerParams(vmem_limit_bytes=VMEM_LIMIT),
        cost_estimate=pl.CostEstimate(
            flops=40 * length * length * HD, bytes_accessed=16 * length * HD, transcendentals=length * length
        ),
        name="attend_back",
    )(x, g, o, lse, cosine, sine)


GELU_C = math.sqrt(2.0 / math.pi)
GELU_A = 0.044715


def middle_kernel(
    n,
    slots,
    blocks,
    tokens_ref,
    cot_ref,
    vec_ref,
    bias_ref,
    up_ref,
    down_ref,
    out_w_ref,
    *refs,
):
    mixed_refs, refs = refs[:slots], refs[slots:]
    output_ref, grad_hidden_ref, sums_ref, bias_grad_ref, g_down_ref, g_pack_ref, *refs = refs
    grad_mixed_refs, (mixed_ref, attn_out_ref, mlp_in_ref, low_ref, back_ref) = refs[:slots], refs[slots:]
    j = pl.program_id(0)
    tok, width = tokens_ref.shape
    gate_attn, shift, scale, gate, gain, down_bias = (vec_ref[i : i + 1, :] for i in range(6))
    piece = min(256, tok)
    pieces = tok // piece

    @pl.when(j == 0)
    def _():
        for s in range(slots):
            for c in range(n):
                head = s * n + c
                mixed_ref[head * HD : (head + 1) * HD, :] = mixed_refs[s][c]
        attn_out_ref[...] = mm(mixed_ref[...], out_w_ref[...], 0, 0)

        def prepare(i, _):
            rows = pl.ds(pl.multiple_of(i * piece, piece), piece)
            hidden = tokens_ref[rows, :] + gate_attn * attn_out_ref[rows, :]
            grad_hidden_ref[rows, :] = hidden
            hat, _ = normalize(hidden)
            mlp_in_ref[rows, :] = (hat * gain * (1.0 + scale) + shift).astype(BF16)
            low_ref[rows, :] = (gate * cot_ref[rows, :]).astype(BF16)
            return 0

        lax.fori_loop(0, pieces, prepare, 0)
        output_ref[...] = jnp.zeros_like(output_ref)
        back_ref[...] = jnp.zeros_like(back_ref)

    @pl.when(j < blocks)
    def _():
        mlp_in, low = mlp_in_ref[...], low_ref[...]
        x = mm(mlp_in, up_ref[...], 1, 0) + bias_ref[0]
        grad_act = mm(low, down_ref[...], 1, 1)
        square = x * x
        t = jnp.tanh(x * (GELU_C + GELU_C * GELU_A * square))
        half = 0.5 + 0.5 * t
        act = (x * half).astype(BF16)
        slope = half + x * (0.5 - 0.5 * t * t) * (GELU_C + 3.0 * GELU_C * GELU_A * square)
        grad_pre = grad_act * slope
        bias_grad_ref[0] = jnp.sum(grad_pre, axis=0, keepdims=True)
        pre_low = grad_pre.astype(BF16)
        output_ref[...] += mm(act, down_ref[...], 1, 0)
        back_ref[...] += mm(pre_low, up_ref[...], 1, 1)
        g_down_ref[...] = mm(act, low, 0, 0).astype(BF16)
        g_pack_ref[...] = mm(mlp_in, pre_low, 0, 0).astype(BF16)

    @pl.when(j == blocks)
    def _():
        def finish(i, sums):
            rows = pl.ds(pl.multiple_of(i * piece, piece), piece)
            cot = cot_ref[rows, :]
            branch = output_ref[rows, :] + down_bias
            hidden = grad_hidden_ref[rows, :]
            output_ref[rows, :] = hidden + gate * branch
            hat, inv = normalize(hidden)
            back = back_ref[rows, :]
            grad_hidden = cot + norm_back(back * ((1.0 + scale) * gain), hat, inv)
            grad_hidden_ref[rows, :] = grad_hidden
            low_ref[rows, :] = (gate_attn * grad_hidden).astype(BF16)
            adds = (grad_hidden * attn_out_ref[rows, :], back, back * hat, cot * branch, cot)
            return tuple(a + jnp.sum(v, axis=0, keepdims=True) for a, v in zip(sums, adds))

        zero = jnp.zeros((1, width), F32)
        sums = lax.fori_loop(0, pieces, finish, (zero,) * 5)
        for i in range(5):
            sums_ref[i : i + 1, :] = sums[i]
        attn_low = low_ref[...]
        g_pack_ref[...] = mm(mixed_ref[...], attn_low, 1, 0).astype(BF16)
        grad_mixed = mm(out_w_ref[...], attn_low, 1, 1).astype(BF16)
        for s in range(slots):
            for c in range(n):
                head = s * n + c
                grad_mixed_refs[s][c] = grad_mixed[head * HD : (head + 1) * HD]


def middle(tokens, cot, vectors, up_bias, w_pack, w_down, mixed):
    tok, width = tokens.shape
    ff = w_down.shape[0]
    blocks = ff // width
    slots = len(mixed)
    n = mixed[0].shape[0]
    whole = lambda shape: pl.BlockSpec(shape, lambda j: (0,) * len(shape), pipeline_mode=pl.Buffered(1))
    fixed = lambda shape: pl.BlockSpec(shape, lambda j: (0,) * len(shape))
    last = blocks - 1
    head_shape = mixed[0].shape
    flops = 2 * tok * width * (6 * ff + 3 * width)
    return pl.pallas_call(
        partial(middle_kernel, n, slots, blocks),
        grid=(blocks + 1,),
        in_specs=[
            whole(tokens.shape),
            whole(cot.shape),
            whole(vectors.shape),
            pl.BlockSpec((1, 1, width), lambda j: (jnp.minimum(j, last), 0, 0)),
            pl.BlockSpec((width, width), lambda j: (0, jnp.minimum(j, last))),
            pl.BlockSpec((width, width), lambda j: (jnp.minimum(j, last), 0)),
            pl.BlockSpec((width, width), lambda j: (0, blocks), pipeline_mode=pl.Buffered(1)),
        ]
        + [whole(head_shape)] * slots,
        out_specs=[
            fixed((tok, width)),
            fixed((tok, width)),
            fixed((8, width)),
            pl.BlockSpec((1, 1, width), lambda j: (jnp.minimum(j, last), 0, 0)),
            pl.BlockSpec((width, width), lambda j: (jnp.minimum(j, last), 0)),
            pl.BlockSpec((width, width), lambda j: (0, j)),
        ]
        + [fixed(head_shape)] * slots,
        out_shape=[
            jax.ShapeDtypeStruct((tok, width), F32),
            jax.ShapeDtypeStruct((tok, width), F32),
            jax.ShapeDtypeStruct((8, width), F32),
            jax.ShapeDtypeStruct((blocks, 1, width), F32),
            jax.ShapeDtypeStruct((ff, width), BF16),
            jax.ShapeDtypeStruct((width, ff + width), BF16),
        ]
        + [jax.ShapeDtypeStruct(head_shape, BF16)] * slots,
        scratch_shapes=[
            pltpu.VMEM((width, tok), BF16),
            pltpu.VMEM((tok, width), F32),
            pltpu.VMEM((tok, width), BF16),
            pltpu.VMEM((tok, width), BF16),
            pltpu.VMEM((tok, width), F32),
        ],
        compiler_params=pltpu.CompilerParams(vmem_limit_bytes=VMEM_LIMIT),
        cost_estimate=pl.CostEstimate(flops=flops, bytes_accessed=6 * ff * width * 2, transcendentals=tok * ff),
        name="middle",
    )(tokens, cot, vectors, up_bias, w_pack, w_down, w_pack, *mixed)


def reduce_kernel(fs, nz, slots, counts, lengths, *refs):
    swapped_refs, w_refs, refs = refs[:slots], refs[slots : 2 * slots], refs[2 * slots :]
    attn_in_ref, tokens_hbm, hidden_hbm, vec_in_ref, sums_ref, up_bias_ref, *refs = refs
    bulk_refs, (mod_t_ref, cond_ref), refs = refs[:2], refs[2:4], refs[4:]
    inputs_out, qkv_out, up_out, out_out, down_out, total_out, mod_w_out, cond_out = refs[:8]
    (
        row_buf,
        w_buf,
        tokens_buf,
        hidden_buf,
        g_buf,
        pair_buf,
        sum_buf,
        recv_buf,
        own_buf,
        up_pack,
        up_down,
        up_qkv,
        part_pack,
        part_down,
        part_qkv,
        twin_pack,
        twin_down,
        twin_qkv,
        tot_pack,
        tot_down,
        tot_qkv,
        vec_buf,
        vec_z,
        vec_own,
        vec_all,
        cond_send,
        cond_recv,
        local_s,
        pair_s,
        pair_r,
        peer_s,
        peer_r,
        up_s,
        up_r,
        twin_s,
        twin_r,
        tot_s,
        tot_r,
        vecz_s,
        vecz_r,
        vec_s,
        vec_r,
        cond_s,
        cond_r,
    ) = refs[8:]
    me = lax.axis_index("fsdp")
    z = lax.axis_index("seq")
    pairs = fs // 2
    k, c = me // 2, lax.rem(me, 2)
    partner = me + 1 - 2 * c
    inner = jnp.logical_or(z == nz // 2 - 1, z == nz // 2)
    outer = jnp.logical_not(inner)
    twin = nz - 1 - z
    mate = z + 1 - 2 * lax.rem(z, 2)
    tok, width = tokens_buf.shape
    shard = g_buf.shape[3]
    groups = width // 128

    loads = [pltpu.make_async_copy(w_refs[s], w_buf.at[s], local_s.at[s]) for s in range(slots)]
    loads.append(pltpu.make_async_copy(tokens_hbm, tokens_buf, local_s.at[slots]))
    loads.append(pltpu.make_async_copy(hidden_hbm, hidden_buf, local_s.at[slots + 1]))
    for load in loads:
        load.start()
    greet(me, z, fs, nz)

    bulk = [
        (src, up, part, other, tot, i)
        for src, up, part, other, tot, count in (
            (bulk_refs[0], up_pack, part_pack, twin_pack, tot_pack, counts[0]),
            (bulk_refs[1], up_down, part_down, twin_down, tot_down, counts[1]),
        )
        for i in range(count)
    ]
    last = [(own_buf, up_qkv, part_qkv, twin_qkv, tot_qkv, s) for s in range(slots)]
    chain = list(enumerate(bulk + last))
    early, late = chain[: len(bulk)], chain[len(bulk) :]

    def up_copy(n, item):
        src, up, _, _, _, i = item
        return remote(src.at[i], up.at[i], up_s.at[n], up_r.at[n], seq=mate)

    def twin_copy(n, item):
        _, _, part, other, _, i = item
        return remote(part.at[i], other.at[i], twin_s.at[n], twin_r.at[n], seq=twin)

    def tot_copy(n, item):
        tot, i = item[4], item[5]
        return remote(tot.at[i], tot.at[i], tot_s.at[n], tot_r.at[n], seq=mate)

    def chain_in(n, item):
        src, up, part, _, _, i = item
        up_copy(n, item).wait_recv()
        part[i] = add_low(src[i], up[i])
        twin_copy(n, item).start()

    def chain_out(n, item):
        _, _, part, other, tot, i = item
        twin_copy(n, item).wait_recv()
        tot[i] = add_low(part[i], other[i])
        tot_copy(n, item).start()

    def plan(items):
        steps = [(chain_in, items[0])]
        for before, item in zip(items[:-1], items[1:]):
            steps += [(chain_in, item), (chain_out, before)]
        return steps + [(chain_out, items[-1])]

    steps = plan(early)

    def advance(count):
        todo = [steps.pop(0) for _ in range(min(count, len(steps)))]
        if todo:

            @pl.when(inner)
            def _():
                for step, (n, item) in todo:
                    step(n, item)

    half = len(early) // 2

    @pl.when(outer)
    def _():
        for n, item in early[:half]:
            up_copy(n, item).start()

    def pair_copy(s, j):
        return remote(g_buf.at[s, j, 1 - c], pair_buf.at[s, j], pair_s.at[s, j], pair_r.at[s, j], fsdp=partner)

    def peer_copy(s, j):
        return remote(sum_buf.at[s, j], recv_buf.at[s, k], peer_s.at[s, j], peer_r.at[s, k], fsdp=2 * j + c)

    def peer_arrival(s, j):
        return remote(sum_buf.at[s, j], recv_buf.at[s, j], peer_s.at[s, j], peer_r.at[s, j], fsdp=2 * j + c)

    for s in range(slots):
        for head in range(nz):
            for p in range(3):
                base = (p * nz + head) * HD
                row_buf[s, base : base + HD, :] = swapped_refs[s][head, p * HD : (p + 1) * HD, :]
        grad = mm(attn_in_ref[...], row_buf[s], 0, 1).astype(BF16)
        for i in range(fs):
            g_buf[s, i // 2, i % 2] = grad[i * shard : (i + 1) * shard]
        each(pairs, lambda i: pair_copy(s, lax.rem(k + 1 + i, pairs)).start())

    advance(1)

    def forward(i):
        j = lax.rem(k + 1 + i, pairs)
        for s in range(slots):
            pair_copy(s, j).wait_recv()
            sum_buf[s, j] = add_low(g_buf[s, j, c], pair_buf[s, j])
            peer_copy(s, j).start()

    each(pairs - 1, forward)
    for load in loads:
        load.wait()

    scale_mlp, gate_mlp, mlp_gain = (vec_in_ref[i : i + 1, :] for i in (2, 3, 4))
    attn_gain, scale_attn = (vec_in_ref[i : i + 1, :] for i in (6, 7))
    piece = min(256, tok)
    back_sum = hat_sum = jnp.zeros((1, width), F32)
    for i in range(tok // piece):
        rows = slice(i * piece, (i + 1) * piece)
        grad = None
        for s in range(slots):
            part = mm(row_buf[s, :, rows], w_buf[s], 0, 1)
            grad = part if grad is None else grad + part
        hat, inv = normalize(tokens_buf[rows, :])
        scaled = grad * ((1.0 + scale_attn) * attn_gain)
        inputs_out[rows, :] = hidden_buf[rows, :] + norm_back(scaled, hat, inv)
        back_sum = back_sum + jnp.sum(grad, axis=0, keepdims=True)
        hat_sum = hat_sum + jnp.sum(grad * hat, axis=0, keepdims=True)
        advance(2)

    sums = [sums_ref[i : i + 1, :] for i in range(5)]
    vectors = [back_sum, hat_sum * attn_gain, sums[0], sums[1], sums[2] * mlp_gain, sums[3]]
    vectors += [hat_sum * (1.0 + scale_attn), sums[2] * (1.0 + scale_mlp)]
    vectors += [up_bias_ref[i] for i in range(up_bias_ref.shape[0])]
    vectors.append(sums[4] * gate_mlp)
    for p, v in enumerate(vectors):
        for i in range(groups):
            vec_buf[p * groups + i : p * groups + i + 1, :] = v[:, i * 128 : (i + 1) * 128]
    used = len(vectors) * groups
    vec_buf[used:, :] = jnp.zeros((vec_buf.shape[0] - used, 128), F32)
    vec_z[z] = vec_buf[...]

    def vecz_copy(i):
        return remote(vec_buf, vec_z.at[z], vecz_s.at[i], vecz_r.at[z], seq=lax.rem(z + 1 + i, nz))

    def vecz_arrival(i):
        peer = lax.rem(z + 1 + i, nz)
        return remote(vec_buf, vec_z.at[peer], vecz_s.at[i], vecz_r.at[peer], seq=peer)

    each(nz - 1, lambda i: vecz_copy(i).start())

    @pl.when(outer)
    def _():
        for n, item in early[half:]:
            up_copy(n, item).start()

    advance(2)
    each(nz - 1, lambda i: vecz_arrival(i).wait_recv())
    summed = vec_z[0]
    for i in range(1, nz):
        summed = summed + vec_z[i]
    vec_own[...] = summed
    vec_all[me] = summed

    def vec_copy(i):
        return remote(vec_own, vec_all.at[me], vec_s.at[i], vec_r.at[me], fsdp=lax.rem(me + 1 + i, fs))

    def vec_arrival(i):
        peer = lax.rem(me + 1 + i, fs)
        return remote(vec_own, vec_all.at[peer], vec_s.at[i], vec_r.at[peer], fsdp=peer)

    each(fs - 1, lambda i: vec_copy(i).start())
    advance(len(steps))

    for s in range(slots):
        pair_copy(s, k).wait_recv()
        own = g_buf[s, k, c].astype(F32) + pair_buf[s, k].astype(F32)

        def gather_in(i, acc):
            j = lax.rem(k + 1 + i, pairs)
            peer_arrival(s, j).wait_recv()
            return acc + recv_buf[s, j].astype(F32)

        own_buf[s] = lax.fori_loop(0, pairs - 1, gather_in, own).astype(BF16)

        @pl.when(outer)
        def _():
            up_copy(*late[s]).start()

    each(fs - 1, lambda i: vec_arrival(i).wait_recv())
    lane_from = lax.broadcasted_iota(jnp.int32, (256, 128), 0)
    lane_to = lax.broadcasted_iota(jnp.int32, (256, 128), 1)
    part, first, place = None, 0, 0
    for which, length in enumerate(lengths):
        block = length // fs
        for i in range(-(-block // 128)):
            offset = me * block + 128 * i
            row = first + offset // 128
            select = (lane_from == lane_to + lax.rem(offset, 128)).astype(F32)
            both = jnp.concatenate([vec_all[:, pl.ds(row, 1), :][:, 0], vec_all[:, pl.ds(row + 1, 1), :][:, 0]], axis=1)
            rows = lax.dot_general(
                both, select, (((1,), (0,)), ((), ())), precision=HIGHEST, preferred_element_type=F32
            )
            total_out[place : place + 1, :] = jnp.sum(rows, axis=0, keepdims=True)
            place += 1
            if which > 0:
                continue
            share = lax.dot_general(
                rows, mod_t_ref[i], (((1,), (0,)), ((), ())), precision=HIGHEST, preferred_element_type=F32
            )
            part = share if part is None else part + share
            outer_product = lax.dot_general(
                cond_ref[...], rows, (((0,), (0,)), ((), ())), precision=HIGHEST, preferred_element_type=F32
            )
            wide = min(128, block - i * 128)
            mod_w_out[:, i * 128 : i * 128 + wide] = outer_product[:, :wide]
        first += length // 128
    cond_send[...] = jnp.broadcast_to(part[:, None, :], cond_send.shape)

    def cond_copy(i):
        peer = lax.rem(me + 1 + i, fs)
        return remote(cond_send.at[peer], cond_recv.at[me], cond_s.at[i], cond_r.at[me], fsdp=peer)

    def cond_arrival(i):
        peer = lax.rem(me + 1 + i, fs)
        return remote(cond_send.at[peer], cond_recv.at[peer], cond_s.at[i], cond_r.at[peer], fsdp=peer)

    each(fs - 1, lambda i: cond_copy(i).start())
    steps.extend(plan(late))
    advance(len(steps))
    cond_recv[me] = cond_send[me]
    each(fs - 1, lambda i: cond_arrival(i).wait_recv())
    cond_out[...] = jnp.sum(cond_recv[...], axis=0)

    @pl.when(outer)
    def _():
        for n, item in chain:
            tot_copy(n, item).wait_recv()
            up_copy(n, item).wait_send()

    block = nz * HD
    ff = up_out.shape[1]
    for i in range(counts[0]):
        rows = slice(i * tot_pack.shape[1], (i + 1) * tot_pack.shape[1])
        up_out[rows, :] = tot_pack[i, :, :ff].astype(F32)
        out_out[rows, :] = tot_pack[i, :, ff:].astype(F32)
    for i in range(counts[1]):
        down_out[i * tot_down.shape[1] : (i + 1) * tot_down.shape[1], :] = tot_down[i].astype(F32)
    for s in range(slots):
        for p in range(3):
            columns = slice(p * width + s * block, p * width + (s + 1) * block)
            qkv_out[:, columns] = tot_qkv[s, :, p * block : (p + 1) * block].astype(F32)

    @pl.when(inner)
    def _():
        for n, item in chain:
            twin_copy(n, item).wait_send()
            tot_copy(n, item).wait_send()

    def drain_peers(i):
        vec_copy(i).wait_send()
        cond_copy(i).wait_send()

    def drain_pairs(i):
        for s in range(slots):
            pair_copy(s, i).wait_send()

    def drain_sums(i):
        for s in range(slots):
            peer_copy(s, lax.rem(k + 1 + i, pairs)).wait_send()

    each(fs - 1, drain_peers)
    each(pairs, drain_pairs)
    each(pairs - 1, drain_sums)
    each(nz - 1, lambda i: vecz_copy(i).wait_send())


def reduce_all(
    grad_rows, weights, attn_in, tokens, grad_hidden, vectors, sums, up_bias_sum, part_pack, part_down, mod_t, cond, mod_cols, fs, nz
):
    slots = len(grad_rows)
    tok, width = tokens.shape
    shard = width // fs
    count = lambda a: 3 if a.shape[0] % 48 == 0 else 1
    counts = (count(part_pack), count(part_down))
    split = lambda a, n: a.reshape(n, a.shape[0] // n, a.shape[1])
    pack, down = split(part_pack, counts[0]), split(part_down, counts[1])
    pairs = fs // 2
    items = sum(counts) + slots
    ff = up_bias_sum.size
    lengths = (6 * width, width, width, ff, width)
    rows = sum(lengths) // 128 + 2
    places = sum(-(-v // fs // 128) for v in lengths)
    vmem = pl.BlockSpec(memory_space=pltpu.VMEM)
    hbm = pl.BlockSpec(memory_space=pl.ANY)
    low = lambda *shape: pltpu.VMEM(shape, BF16)
    wide = lambda *shape: pltpu.VMEM(shape, F32)
    dma = lambda *shape: pltpu.SemaphoreType.DMA(shape)
    qkv_shape = (slots, shard, width)
    triple = [low(*pack.shape), low(*down.shape), low(*qkv_shape)]
    cols = grad_rows[0].shape[0] * grad_rows[0].shape[1]
    inputs_grad, qkv_sum, up_sum, out_sum, down_sum, total, mod_w, cond_grad = pl.pallas_call(
        partial(reduce_kernel, fs, nz, slots, counts, lengths),
        in_specs=[vmem] * slots + [hbm] * slots + [vmem, hbm, hbm] + [vmem] * 7,
        out_specs=[vmem] * 8,
        out_shape=[
            jax.ShapeDtypeStruct((tok, width), F32),
            jax.ShapeDtypeStruct((shard, 3 * width), F32),
            jax.ShapeDtypeStruct((shard, ff), F32),
            jax.ShapeDtypeStruct((shard, part_pack.shape[1] - ff), F32),
            jax.ShapeDtypeStruct(part_down.shape, F32),
            jax.ShapeDtypeStruct((places, 128), F32),
            jax.ShapeDtypeStruct((cond.shape[1], mod_cols), F32),
            jax.ShapeDtypeStruct((8, 128), F32),
        ],
        scratch_shapes=[
            low(slots, cols, tok),
            low(slots, width, cols),
            wide(tok, width),
            wide(tok, width),
            low(slots, pairs, 2, shard, width),
            low(slots, pairs, shard, width),
            low(slots, pairs, shard, width),
            low(slots, pairs, shard, width),
            low(*qkv_shape),
        ]
        + triple * 4
        + [
            wide(rows, 128),
            wide(nz, rows, 128),
            wide(rows, 128),
            wide(fs, rows, 128),
            wide(fs, 8, 128),
            wide(fs, 8, 128),
            dma(slots + 2),
            dma(slots, pairs),
            dma(slots, pairs),
            dma(slots, pairs),
            dma(slots, pairs),
        ]
        + [dma(items)] * 6
        + [dma(nz - 1), dma(nz), dma(fs - 1), dma(fs), dma(fs - 1), dma(fs)],
        compiler_params=pltpu.CompilerParams(vmem_limit_bytes=VMEM_LIMIT, collective_id=1, has_side_effects=True),
        cost_estimate=pl.CostEstimate(flops=12 * tok * width * cols, bytes_accessed=10**8, transcendentals=0),
        name="reduce_all",
    )(*grad_rows, *weights, attn_in, tokens, grad_hidden, vectors, sums, up_bias_sum, pack, down, mod_t, cond)
    blocks, place = [], 0
    for v in lengths:
        n = -(-v // fs // 128)
        blocks.append(total[place : place + n].reshape(-1)[: v // fs])
        place += n
    return inputs_grad, qkv_sum, up_sum, out_sum, down_sum, blocks, mod_w, cond_grad


def per_device(
    inputs,
    conditioning,
    cotangent,
    attn_gain,
    mlp_gain,
    qkv_weight,
    out_weight,
    up_weight,
    up_bias,
    down_weight,
    down_bias,
    mod_weight,
    mod_bias,
):
    n = lax.axis_size("seq")
    fs = lax.axis_size("fsdp")
    z = lax.axis_index("seq")
    tokens = inputs[0]
    tok, width = tokens.shape
    slots = H // n
    gather = lambda a: lax.all_gather(a, "fsdp", axis=0, tiled=True)

    inv_freq = jnp.exp(-math.log(10000.0) * jnp.arange(HD // 2, dtype=F32) * (2.0 / HD))
    positions = jnp.arange(tok, dtype=F32)
    own_angles = inv_freq[:, None] * (positions + (z * tok).astype(F32))[None, :]
    starts = (jnp.arange(n) * tok).astype(F32)
    all_angles = inv_freq[None, :, None] * (positions[None, :] + starts[:, None])[:, None, :]
    cos_all, sin_all = jnp.cos(all_angles), jnp.sin(all_angles)

    sent, qkv_slots, attn_in, vectors, up_bias_full, cond_low_all = start(
        qkv_weight,
        tokens,
        (attn_gain, mlp_gain, up_bias, down_bias),
        conditioning,
        mod_weight,
        mod_bias,
        jnp.cos(own_angles),
        jnp.sin(own_angles),
        fs,
        n,
    )
    swap = lambda a: lax.all_to_all(a, "seq", split_axis=0, concat_axis=0, tiled=True)
    heads = [sent[0]] + [swap(a) for a in sent[1:]]
    pack_own = jnp.concatenate([up_weight.astype(BF16), out_weight.astype(BF16)], axis=1)
    down_own = down_weight.astype(BF16)
    attn_in, pack_own, down_own = lax.optimization_barrier((attn_in, pack_own, down_own))
    w_pack, down_full = gather(pack_own), gather(down_own)

    mixed_heads, log_totals, mixed_back = [], [], []
    for x in heads:
        o, lse = attend(x)
        mixed_heads.append(o)
        log_totals.append(lse)
        mixed_back.append(swap(o))
    output, grad_hidden, sums, up_bias_sum, g_down, g_pack, *grad_mixed = middle(
        tokens, cotangent[0], vectors, up_bias_full, w_pack, down_full, mixed_back
    )
    scatter = lambda a: lax.psum_scatter(a, "fsdp", scatter_dimension=0, tiled=True)
    part_down = scatter(g_down)
    part_pack = scatter(g_pack)

    grad_slots = []
    for s in range(slots):
        g = swap(grad_mixed[s])
        if s == 1:
            g, part_down = lax.optimization_barrier((g, part_down))
        grad_slots.append(swap(attend_back(heads[s], g, mixed_heads[s], log_totals[s], cos_all, sin_all)))
    grad_slots[-1], part_pack = lax.optimization_barrier((grad_slots[-1], part_pack))

    mod_cols = mod_weight.shape[1]
    mod_t = jnp.pad(mod_weight.astype(BF16).T.astype(F32), ((0, -mod_cols % 128), (0, 0)))
    inputs_grad, qkv_weight_grad, up_sum, out_sum, down_sum, blocks, mod_weight_grad, cond_grad = reduce_all(
        grad_slots,
        [qkv_slots[s].reshape(width, -1) for s in range(slots)],
        attn_in,
        tokens,
        grad_hidden,
        vectors,
        sums,
        up_bias_sum,
        part_pack,
        part_down,
        mod_t.reshape(-1, 128, mod_weight.shape[0]),
        cond_low_all,
        mod_cols,
        fs,
        n,
    )
    mod_bias_grad, attn_gain_grad, mlp_gain_grad, up_bias_grad, down_bias_grad = blocks
    _, silu_pull = jax.vjp(jax.nn.silu, conditioning)
    conditioning_grad = silu_pull(cond_grad[:1])[0]
    return (
        output[None],
        inputs_grad[None],
        conditioning_grad,
        attn_gain_grad,
        mlp_gain_grad,
        qkv_weight_grad,
        out_sum,
        up_sum,
        up_bias_grad,
        down_sum,
        down_bias_grad,
        mod_weight_grad,
        mod_bias_grad,
    )


def solution(mesh):
    specs = (
        P("fsdp", "seq", None),
        P("fsdp", None),
        P("fsdp", "seq", None),
        P("fsdp"),
        P("fsdp"),
        P("fsdp", None),
        P("fsdp", None),
        P("fsdp", None),
        P("fsdp"),
        P("fsdp", None),
        P("fsdp"),
        P(None, "fsdp"),
        P("fsdp"),
    )
    out_specs = (specs[0], specs[0], specs[1]) + specs[3:]
    return jax.shard_map(per_device, mesh=mesh, in_specs=specs, out_specs=out_specs, check_vma=False)
```

```python
from functools import partial
import math

import jax
import jax.numpy as jnp
from jax import lax
from jax.experimental import pallas as pl
from jax.experimental.pallas import tpu as pltpu
from jax.sharding import PartitionSpec as P

H = 12
HD = 64
EPSILON = 1e-05
BF16 = jnp.bfloat16
F32 = jnp.float32
LOG2E = math.log2(math.e)
VMEM_LIMIT = 60 * 1024 * 1024


def mm(a, b, ca, cb):
    return lax.dot_general(a, b, (((ca,), (cb,)), ((), ())), preferred_element_type=F32)


def normalize(values):
    centre = jnp.mean(values, axis=-1, keepdims=True)
    shifted = values - centre
    variance = jnp.mean(shifted * shifted, axis=-1, keepdims=True)
    inv_std = lax.rsqrt(variance + EPSILON)
    return (shifted * inv_std, inv_std)


def norm_back(grad_hat, normed_hat, inv_std):
    mean_grad = jnp.mean(grad_hat, axis=-1, keepdims=True)
    mean_mixed = jnp.mean(grad_hat * normed_hat, axis=-1, keepdims=True)
    return inv_std * (grad_hat - mean_grad - normed_hat * mean_mixed)


MESH = pl.DeviceIdType.MESH
HIGHEST = lax.Precision.HIGHEST


def add_low(a, b):
    return (a.astype(F32) + b.astype(F32)).astype(BF16)


def remote(src, dst, s, r, **where):
    return pltpu.make_async_remote_copy(
        src_ref=src, dst_ref=dst, send_sem=s, recv_sem=r, device_id=where, device_id_type=MESH
    )


def each(count, body):
    lax.fori_loop(0, count, lambda i, _: (body(i), 0)[1], 0)


def greet(me, z, fs, nz):
    barrier = pltpu.get_barrier_semaphore()

    def hello_fsdp(i):
        peer = {"fsdp": lax.rem(me + 1 + i, fs)}
        pl.semaphore_signal(barrier, inc=1, device_id=peer, device_id_type=MESH)

    def hello_seq(i):
        peer = {"seq": lax.rem(z + 1 + i, nz)}
        pl.semaphore_signal(barrier, inc=1, device_id=peer, device_id_type=MESH)

    each(fs - 1, hello_fsdp)
    each(nz - 1, hello_seq)
    pl.semaphore_wait(barrier, fs + nz - 2)


def start_kernel(fs, nz, slots, *refs):
    (
        qkv_ref,
        tokens_hbm,
        attn_gain_ref,
        mlp_gain_ref,
        up_bias_ref,
        down_bias_ref,
        cond_ref,
        mod_w_ref,
        mod_b_ref,
        cos_ref,
        sin_ref,
        up_hbm,
        out_hbm,
        down_hbm,
        heads_ref,
        rest_ref,
        w_ref,
        attn_in_ref,
        vec_ref,
        bias_ref,
        cond_out,
        pack_out,
        down_out,
    ) = refs[:23]
    (
        tokens_buf,
        up_buf,
        out_buf,
        down_buf,
        w_own,
        z_send,
        narrow,
        spread,
        mod_wide,
        small_send,
        small_all,
        mod_send,
        mod_recv,
        w_full,
        local_s,
        small_s,
        small_r,
        mod_s,
        mod_r,
        w_s,
        w_f,
        w_r,
        z_s,
        z_r,
    ) = refs[23:]
    me = lax.axis_index("fsdp")
    z = lax.axis_index("seq")
    pairs = fs // 2
    k, c = me // 2, lax.rem(me, 2)
    partner = me + 1 - 2 * c
    tok, width = tokens_buf.shape
    shard = w_own.shape[1]
    ff = spread.shape[1]
    block = nz * HD

    fetch = ((tokens_hbm, tokens_buf), (up_hbm, up_buf), (out_hbm, out_buf), (down_hbm, down_buf))
    loads = [pltpu.make_async_copy(src, dst, local_s.at[i]) for i, (src, dst) in enumerate(fetch)]
    for load in loads:
        load.start()
    greet(me, z, fs, nz)

    narrow[...] = jnp.zeros_like(narrow)
    for i, piece in enumerate((attn_gain_ref, mlp_gain_ref, down_bias_ref)):
        narrow[i : i + 1, :shard] = piece[...].reshape(1, -1)
    spread[...] = jnp.zeros_like(spread)
    spread[0:1, : up_bias_ref.shape[0]] = up_bias_ref[...].reshape(1, -1)
    placed = pltpu.roll(narrow[...], me * shard, 1)
    for i in range(3):
        small_send[:, i * width : (i + 1) * width] = placed[i : i + 1]
    placed = pltpu.roll(spread[...], me * up_bias_ref.shape[0], 1)
    small_send[:, 3 * width : 3 * width + ff] = placed[0:1]
    small_send[:, 3 * width + ff :] = cond_ref[...]
    small_all[me] = small_send[...]

    def small_copy(i):
        return remote(small_send, small_all.at[me], small_s.at[i], small_r.at[me], fsdp=lax.rem(me + 1 + i, fs))

    def small_arrival(i):
        peer = lax.rem(me + 1 + i, fs)
        return remote(small_send, small_all.at[peer], small_s.at[i], small_r.at[peer], fsdp=peer)

    each(fs - 1, lambda i: small_copy(i).start())

    for s in range(slots):
        for part in range(3):
            columns = slice(part * width + s * block, part * width + (s + 1) * block)
            w_own[s, :, part * block : (part + 1) * block] = qkv_ref[:, columns].astype(BF16)
        w_ref[s, me] = w_own[s]

    def w_peer(s, i):
        j = lax.rem(k + 1 + i, pairs)
        return remote(w_own.at[s], w_ref.at[s, me], w_s.at[s, i], w_r.at[s, me], fsdp=2 * j + c)

    def w_partner(s):
        return remote(w_own.at[s], w_ref.at[s, me], w_s.at[s, pairs - 1], w_r.at[s, me], fsdp=partner)

    def w_arrival(s, j):
        return remote(w_own.at[s], w_ref.at[s, j], w_s.at[s, 0], w_r.at[s, j], fsdp=partner)

    def w_pass(s, i):
        j = 2 * lax.rem(k + 1 + i, pairs) + c
        return remote(w_ref.at[s, j], w_ref.at[s, j], w_f.at[s, i], w_r.at[s, j], fsdp=partner)

    def send_weight(s):
        each(pairs - 1, lambda i: w_peer(s, i).start())
        w_partner(s).start()

    def pass_weight(s):
        def step(i):
            w_arrival(s, 2 * lax.rem(k + 1 + i, pairs) + c).wait_recv()
            w_pass(s, i).start()

        each(pairs - 1, step)

    send_weight(0)
    for s in range(1, slots - 1):
        send_weight(s)

    each(fs - 1, lambda i: small_arrival(i).wait_recv())
    small_sum = jnp.sum(small_all[:, :, : 3 * width + ff], axis=0)
    cond_all = small_all[:, 0, 3 * width + ff :]
    cond_low = (cond_all / (1.0 + jnp.exp(-cond_all))).astype(BF16)
    cond_out[...] = cond_low.astype(F32)
    own_mod = mm(cond_low, mod_w_ref[...].astype(BF16), 1, 1) + mod_b_ref[...].reshape(1, -1)
    mod_wide[...] = jnp.zeros_like(mod_wide)
    mod_wide[:, : own_mod.shape[1]] = own_mod
    placed = pltpu.roll(mod_wide[...], me * own_mod.shape[1], 1)
    for i in range(fs):
        mod_send[i] = placed[i : i + 1]
    mod_recv[me] = mod_send[me]

    def mod_copy(i):
        peer = lax.rem(me + 1 + i, fs)
        return remote(mod_send.at[peer], mod_recv.at[me], mod_s.at[i], mod_r.at[me], fsdp=peer)

    def mod_arrival(i):
        peer = lax.rem(me + 1 + i, fs)
        return remote(mod_send.at[peer], mod_recv.at[peer], mod_s.at[i], mod_r.at[peer], fsdp=peer)

    each(fs - 1, lambda i: mod_copy(i).start())
    send_weight(slots - 1)
    pass_weight(0)

    attn_gain, mlp_gain, down_bias = (small_sum[:, i * width : (i + 1) * width] for i in range(3))
    for i in range(ff // width):
        bias_ref[i] = small_sum[:, (3 + i) * width : (4 + i) * width]
    for load in loads:
        load.wait()
    piece = min(256, tok)
    each(fs - 1, lambda i: mod_arrival(i).wait_recv())
    modulation = jnp.sum(mod_recv[...], axis=0)
    shift_attn, scale_attn, gate_attn, shift_mlp, scale_mlp, gate_mlp = (
        modulation[:, i * width : (i + 1) * width] for i in range(6)
    )
    kept = (gate_attn, shift_mlp, scale_mlp, gate_mlp, mlp_gain, down_bias, attn_gain, scale_attn)
    for i, v in enumerate(kept):
        vec_ref[i : i + 1, :] = v
    for i in range(tok // piece):
        rows = slice(i * piece, (i + 1) * piece)
        hat, _ = normalize(tokens_buf[rows, :])
        attn_in_ref[rows, :] = (hat * attn_gain * (1.0 + scale_attn) + shift_attn).astype(BF16)

    cosine, sine = cos_ref[...], sin_ref[...]
    half = HD // 2

    def project(s, out_ref):
        each(pairs, lambda j: w_arrival(s, 2 * j + 1 - c).wait_recv())
        if shard % 16 == 0:
            weight = w_ref[s].reshape(fs * shard, 3 * block)
        else:
            for i in range(fs):
                w_full[i * shard : (i + 1) * shard, :] = w_ref[s, i].astype(F32)
            weight = w_full[...].astype(BF16)
        rows = mm(weight, attn_in_ref[...], 0, 1).astype(BF16)
        for shard_of in range(nz):
            for part in range(3):
                base = (part * nz + shard_of) * HD
                if part == 2:
                    out_ref[shard_of, part * HD : (part + 1) * HD, :] = rows[base : base + HD]
                else:
                    a = rows[base : base + half].astype(F32)
                    b = rows[base + half : base + HD].astype(F32)
                    out_ref[shard_of, part * HD : part * HD + half, :] = (a * cosine - b * sine).astype(BF16)
                    out_ref[shard_of, part * HD + half : (part + 1) * HD, :] = (b * cosine + a * sine).astype(BF16)

    def z_copy(i):
        peer = lax.rem(z + 1 + i, nz)
        return remote(z_send.at[peer], heads_ref.at[z], z_s.at[i], z_r.at[z], seq=peer)

    def z_arrival(i):
        peer = lax.rem(z + 1 + i, nz)
        return remote(z_send.at[peer], heads_ref.at[peer], z_s.at[i], z_r.at[peer], seq=peer)

    project(0, z_send)
    each(nz - 1, lambda i: z_copy(i).start())
    heads_ref[z] = z_send[z]
    for s in range(1, slots):
        pass_weight(s)
        project(s, rest_ref.at[s - 1])

    pack_out[:, :ff] = up_buf[...].astype(BF16)
    pack_out[:, ff:] = out_buf[...].astype(BF16)
    down_out[...] = down_buf[...].astype(BF16)
    each(nz - 1, lambda i: z_arrival(i).wait_recv())
    each(nz - 1, lambda i: z_copy(i).wait_send())

    def drain_peers(i):
        small_copy(i).wait_send()
        mod_copy(i).wait_send()

    def drain_weights(i):
        for s in range(slots):
            w_peer(s, i).wait_send()
            w_pass(s, i).wait_send()

    each(fs - 1, drain_peers)
    each(pairs - 1, drain_weights)
    for s in range(slots):
        w_partner(s).wait_send()


def start(qkv_weight, tokens, gains, cond, mod_weight, mod_bias, cosine, sine, feed, fs, nz):
    slots = H // nz
    tok, width = tokens.shape
    shard = qkv_weight.shape[0]
    pairs = fs // 2
    up, out, down = feed
    ff = gains[2].shape[0] * fs
    vmem = pl.BlockSpec(memory_space=pltpu.VMEM)
    hbm = pl.BlockSpec(memory_space=pl.ANY)
    low = lambda *shape: pltpu.VMEM(shape, BF16)
    wide = lambda *shape: pltpu.VMEM(shape, F32)
    dma = lambda *shape: pltpu.SemaphoreType.DMA(shape)
    head_shape = (nz, 3 * HD, tok)
    cols = 3 * nz * HD
    small = 3 * width + ff + cond.shape[-1]
    return pl.pallas_call(
        partial(start_kernel, fs, nz, slots),
        in_specs=[vmem, hbm] + [vmem] * 9 + [hbm] * 3,
        out_specs=[vmem] * 9,
        out_shape=[
            jax.ShapeDtypeStruct(head_shape, BF16),
            jax.ShapeDtypeStruct((slots - 1, *head_shape), BF16),
            jax.ShapeDtypeStruct((slots, fs, shard, cols), BF16),
            jax.ShapeDtypeStruct((tok, width), BF16),
            jax.ShapeDtypeStruct((8, width), F32),
            jax.ShapeDtypeStruct((ff // width, 1, width), F32),
            jax.ShapeDtypeStruct((fs, cond.shape[-1]), F32),
            jax.ShapeDtypeStruct((shard, up.shape[1] + out.shape[1]), BF16),
            jax.ShapeDtypeStruct(down.shape, BF16),
        ],
        scratch_shapes=[
            wide(tok, width),
            wide(*up.shape),
            wide(*out.shape),
            wide(*down.shape),
            low(slots, shard, cols),
            low(*head_shape),
            wide(8, width),
            wide(8, ff),
            wide(fs, 6 * width),
            wide(1, small),
            wide(fs, 1, small),
            wide(fs, 1, 6 * width),
            wide(fs, 1, 6 * width),
            wide(*((8, 128) if shard % 16 == 0 else (width, cols))),
            dma(4),
            dma(fs - 1),
            dma(fs),
            dma(fs - 1),
            dma(fs),
            dma(slots, pairs),
            dma(slots, pairs),
            dma(slots, fs),
            dma(nz - 1),
            dma(nz),
        ],
        compiler_params=pltpu.CompilerParams(vmem_limit_bytes=VMEM_LIMIT, collective_id=2, has_side_effects=True),
        cost_estimate=pl.CostEstimate(flops=6 * tok * width * cols, bytes_accessed=10**8, transcendentals=0),
        name="start",
    )(
        qkv_weight,
        tokens,
        *gains,
        cond,
        mod_weight.T,
        mod_bias,
        cosine,
        sine,
        *feed,
    )


def greet_seq(z, nz):
    barrier = pltpu.get_barrier_semaphore()

    def hello(i):
        peer = {"seq": lax.rem(z + 1 + i, nz)}
        pl.semaphore_signal(barrier, inc=1, device_id=peer, device_id_type=MESH)

    each(nz - 1, hello)
    pl.semaphore_wait(barrier, nz - 1)


def attend_kernel(n, slots, tok, sub, first_ref, rest_ref, x_ref, o_ref, mixed_ref, lse_ref, k_ref, x_s, x_r, o_s, o_r):
    z = lax.axis_index("seq")
    greet_seq(z, n)

    def x_copy(s, i):
        peer = lax.rem(z + 1 + i, n)
        return remote(rest_ref.at[s - 1, peer], x_ref.at[s, z], x_s.at[s - 1, i], x_r.at[s - 1, z], seq=peer)

    def x_arrival(s, i):
        peer = lax.rem(z + 1 + i, n)
        return remote(rest_ref.at[s - 1, peer], x_ref.at[s, peer], x_s.at[s - 1, i], x_r.at[s - 1, peer], seq=peer)

    def o_copy(s, i):
        peer = lax.rem(z + 1 + i, n)
        return remote(o_ref.at[s, peer], mixed_ref.at[s, z], o_s.at[s, i], o_r.at[s, z], seq=peer)

    def o_arrival(s, i):
        peer = lax.rem(z + 1 + i, n)
        return remote(o_ref.at[s, peer], mixed_ref.at[s, peer], o_s.at[s, i], o_r.at[s, peer], seq=peer)

    for s in range(1, slots):
        each(n - 1, lambda i: x_copy(s, i).start())
    x_ref[0] = first_ref[...]
    for s in range(1, slots):
        x_ref[s, z] = rest_ref[s - 1, z]

    scale = LOG2E / math.sqrt(HD)
    width = tok // sub

    def soft(s):
        top = jnp.max(s, axis=0, keepdims=True) * scale
        p = jnp.exp2(s * scale - top)
        total = jnp.sum(p, axis=0, keepdims=True)
        return top, total, p.astype(BF16)

    def slot(s):
        @pl.when(s > 0)
        def _():
            each(n - 1, lambda i: x_arrival(s, i).wait_recv())

        for c in range(n):
            k_ref[c * tok : (c + 1) * tok, :] = x_ref[s, c, HD : 2 * HD, :].T

        def shard(i):
            step = lax.rem(z + 1 + i, n)

            def score(j):
                q = x_ref[s, step, 0:HD, j * width : (j + 1) * width]
                return mm(k_ref[...], q, 1, 0)

            def mix(j, top, total, p):
                o = None
                for c in range(n):
                    part = mm(x_ref[s, c, 2 * HD : 3 * HD, :], p[c * tok : (c + 1) * tok], 1, 0)
                    o = part if o is None else o + part
                o_ref[s, step, :, j * width : (j + 1) * width] = (o / total).astype(BF16)
                lse_ref[s, step, :, j * width : (j + 1) * width] = top + jnp.log2(total)

            scores = [score(0)]
            pending = None
            for j in range(sub):
                if j + 1 < sub:
                    scores.append(score(j + 1))
                done = soft(scores[j])
                if pending is not None:
                    mix(j - 1, *pending)
                pending = done
            mix(sub - 1, *pending)

            @pl.when(i < n - 1)
            def _():
                o_copy(s, i).start()

        each(n, shard)
        mixed_ref[s, z] = o_ref[s, z]

    each(slots, slot)

    def drain(s):
        each(n - 1, lambda i: o_arrival(s, i).wait_recv())
        each(n - 1, lambda i: o_copy(s, i).wait_send())

    each(slots, drain)
    for s in range(1, slots):
        each(n - 1, lambda i: x_copy(s, i).wait_send())


def attend(first, rest):
    n, _, tok = first.shape
    slots = rest.shape[0] + 1
    length = n * tok
    vmem = pl.BlockSpec(memory_space=pltpu.VMEM)
    dma = lambda *shape: pltpu.SemaphoreType.DMA(shape)
    head_shape = (slots, n, HD, tok)
    return pl.pallas_call(
        partial(attend_kernel, n, slots, tok, 2),
        in_specs=[vmem] * 2,
        out_specs=[vmem] * 4,
        out_shape=[
            jax.ShapeDtypeStruct((slots, n, 3 * HD, tok), BF16),
            jax.ShapeDtypeStruct(head_shape, BF16),
            jax.ShapeDtypeStruct(head_shape, BF16),
            jax.ShapeDtypeStruct((slots, n, 1, tok), F32),
        ],
        scratch_shapes=[
            pltpu.VMEM((length, HD), BF16),
            dma(slots - 1, n - 1),
            dma(slots - 1, n),
            dma(slots, n - 1),
            dma(slots, n),
        ],
        compiler_params=pltpu.CompilerParams(vmem_limit_bytes=VMEM_LIMIT, collective_id=3, has_side_effects=True),
        cost_estimate=pl.CostEstimate(
            flops=16 * slots * length * length * HD, bytes_accessed=10**7, transcendentals=slots * length * length
        ),
        name="attend",
    )(first, rest)


def attend_back_kernel(
    n,
    slots,
    tok,
    sub,
    x_ref,
    sent_ref,
    o_ref,
    lse_ref,
    cos_ref,
    sin_ref,
    out_ref,
    g_ref,
    d_ref,
    k_ref,
    v_ref,
    dk_ref,
    dv_ref,
    g_s,
    g_r,
    q_s,
    q_r,
    kv_s,
    kv_r,
):
    z = lax.axis_index("seq")
    half = HD // 2
    greet_seq(z, n)

    def g_copy(s, i):
        peer = lax.rem(z + 1 + i, n)
        return remote(sent_ref.at[s, peer], g_ref.at[s, z], g_s.at[s, i], g_r.at[s, z], seq=peer)

    def g_arrival(s, i):
        peer = lax.rem(z + 1 + i, n)
        return remote(sent_ref.at[s, peer], g_ref.at[s, peer], g_s.at[s, i], g_r.at[s, peer], seq=peer)

    def part_copy(s, i, rows, send, recv, arrival):
        peer = lax.rem(z + 1 + i, n)
        slot = peer if arrival else z
        return remote(
            d_ref.at[s, peer, rows], out_ref.at[s, slot, rows], send.at[s, i], recv.at[s, slot], seq=peer
        )

    q_rows, kv_rows = pl.ds(0, HD), pl.ds(HD, 2 * HD)
    q_copy = lambda s, i, arrival=False: part_copy(s, i, q_rows, q_s, q_r, arrival)
    kv_copy = lambda s, i, arrival=False: part_copy(s, i, kv_rows, kv_s, kv_r, arrival)

    for s in range(slots):
        each(n - 1, lambda i: g_copy(s, i).start())
        g_ref[s, z] = sent_ref[s, z]

    scale = LOG2E / math.sqrt(HD)
    width = tok // sub

    def turn_back(grad, cosine, sine):
        a, b = grad[:half], grad[half:]
        return (a * cosine + b * sine).astype(BF16), (b * cosine - a * sine).astype(BF16)

    def slot(s):
        for c in range(n):
            k_ref[c * tok : (c + 1) * tok, :] = x_ref[s, c, HD : 2 * HD, :].T
            v_ref[c * tok : (c + 1) * tok, :] = x_ref[s, c, 2 * HD : 3 * HD, :].T
        dk_ref[...] = jnp.zeros_like(dk_ref)
        dv_ref[...] = jnp.zeros_like(dv_ref)
        each(n - 1, lambda i: g_arrival(s, i).wait_recv())

        def shard(i):
            step = lax.rem(z + 1 + i, n)
            for j in range(sub):
                cols = slice(j * width, (j + 1) * width)
                q = x_ref[s, step, 0:HD, cols]
                g = g_ref[s, step, :, cols]
                o = o_ref[s, step, :, cols]
                centre = jnp.sum(g.astype(F32) * o.astype(F32), axis=0, keepdims=True)
                score = mm(k_ref[...], q, 1, 0)
                dp = mm(v_ref[...], g, 1, 0)
                p = jnp.exp2(score * scale - lse_ref[s, step, :, cols])
                p_low = p.astype(BF16)
                ds = (p * (dp - centre)).astype(BF16)
                dv_ref[...] += mm(g, p_low, 1, 1)
                dk_ref[...] += mm(q, ds, 1, 1)
                dq = None
                for c in range(n):
                    part = mm(x_ref[s, c, HD : 2 * HD, :], ds[c * tok : (c + 1) * tok], 1, 0)
                    dq = part if dq is None else dq + part
                dq = dq * (1.0 / math.sqrt(HD))
                a, b = turn_back(dq, cos_ref[step, :, cols], sin_ref[step, :, cols])
                d_ref[s, step, 0:half, cols] = a
                d_ref[s, step, half:HD, cols] = b

            @pl.when(i < n - 1)
            def _():
                q_copy(s, i).start()

        each(n, shard)
        for c in range(n):
            dk = dk_ref[:, c * tok : (c + 1) * tok] * (1.0 / math.sqrt(HD))
            a, b = turn_back(dk, cos_ref[c], sin_ref[c])
            d_ref[s, c, HD : HD + half, :] = a
            d_ref[s, c, HD + half : 2 * HD, :] = b
            d_ref[s, c, 2 * HD : 3 * HD, :] = dv_ref[:, c * tok : (c + 1) * tok].astype(BF16)
        each(n - 1, lambda i: kv_copy(s, i).start())
        out_ref[s, z] = d_ref[s, z]

    each(slots, slot)

    def drain(s):
        def one(i):
            q_copy(s, i, True).wait_recv()
            kv_copy(s, i, True).wait_recv()
            g_copy(s, i).wait_send()
            q_copy(s, i).wait_send()
            kv_copy(s, i).wait_send()

        each(n - 1, one)

    each(slots, drain)


def attend_back(x, g, o, lse, cosine, sine):
    slots, n, _, tok = x.shape
    length = n * tok
    vmem = pl.BlockSpec(memory_space=pltpu.VMEM)
    dma = lambda *shape: pltpu.SemaphoreType.DMA(shape)
    return pl.pallas_call(
        partial(attend_back_kernel, n, slots, tok, 2),
        in_specs=[vmem] * 6,
        out_specs=vmem,
        out_shape=jax.ShapeDtypeStruct(x.shape, BF16),
        scratch_shapes=[
            pltpu.VMEM(g.shape, BF16),
            pltpu.VMEM(x.shape, BF16),
            pltpu.VMEM((length, HD), BF16),
            pltpu.VMEM((length, HD), BF16),
            pltpu.VMEM((HD, length), F32),
            pltpu.VMEM((HD, length), F32),
        ]
        + [dma(slots, n - 1), dma(slots, n)] * 3,
        compiler_params=pltpu.CompilerParams(vmem_limit_bytes=VMEM_LIMIT, collective_id=4, has_side_effects=True),
        cost_estimate=pl.CostEstimate(
            flops=40 * slots * length * length * HD, bytes_accessed=10**7, transcendentals=slots * length * length
        ),
        name="attend_back",
    )(x, g, o, lse, cosine, sine)


GELU_C = math.sqrt(2.0 / math.pi)
GELU_A = 0.044715


def middle_kernel(
    blocks,
    tokens_ref,
    cot_ref,
    vec_ref,
    bias_ref,
    up_ref,
    down_ref,
    out_w_ref,
    mixed_ref,
    output_ref,
    grad_hidden_ref,
    sums_ref,
    bias_grad_ref,
    g_down_ref,
    g_pack_ref,
    grad_mixed_ref,
    attn_out_ref,
    mlp_in_ref,
    low_ref,
    back_ref,
):
    j = pl.program_id(0)
    tok, width = tokens_ref.shape
    gate_attn, shift, scale, gate, gain, down_bias = (vec_ref[i : i + 1, :] for i in range(6))
    piece = min(256, tok)
    pieces = tok // piece

    @pl.when(j == 0)
    def _():
        attn_out_ref[...] = mm(mixed_ref[...], out_w_ref[...], 0, 0)

        def prepare(i, _):
            rows = pl.ds(pl.multiple_of(i * piece, piece), piece)
            hidden = tokens_ref[rows, :] + gate_attn * attn_out_ref[rows, :]
            grad_hidden_ref[rows, :] = hidden
            hat, _ = normalize(hidden)
            mlp_in_ref[rows, :] = (hat * gain * (1.0 + scale) + shift).astype(BF16)
            low_ref[rows, :] = (gate * cot_ref[rows, :]).astype(BF16)
            return 0

        lax.fori_loop(0, pieces, prepare, 0)
        output_ref[...] = jnp.zeros_like(output_ref)
        back_ref[...] = jnp.zeros_like(back_ref)

    @pl.when(j < blocks)
    def _():
        mlp_in, low = mlp_in_ref[...], low_ref[...]
        x = mm(mlp_in, up_ref[...], 1, 0) + bias_ref[0]
        grad_act = mm(low, down_ref[...], 1, 1)
        square = x * x
        t = jnp.tanh(x * (GELU_C + GELU_C * GELU_A * square))
        half = 0.5 + 0.5 * t
        act = (x * half).astype(BF16)
        slope = half + x * (0.5 - 0.5 * t * t) * (GELU_C + 3.0 * GELU_C * GELU_A * square)
        grad_pre = grad_act * slope
        bias_grad_ref[0] = jnp.sum(grad_pre, axis=0, keepdims=True)
        pre_low = grad_pre.astype(BF16)
        output_ref[...] += mm(act, down_ref[...], 1, 0)
        back_ref[...] += mm(pre_low, up_ref[...], 1, 1)
        g_down_ref[...] = mm(act, low, 0, 0).astype(BF16)
        g_pack_ref[...] = mm(mlp_in, pre_low, 0, 0).astype(BF16)

    @pl.when(j == blocks)
    def _():
        def finish(i, sums):
            rows = pl.ds(pl.multiple_of(i * piece, piece), piece)
            cot = cot_ref[rows, :]
            branch = output_ref[rows, :] + down_bias
            hidden = grad_hidden_ref[rows, :]
            output_ref[rows, :] = hidden + gate * branch
            hat, inv = normalize(hidden)
            back = back_ref[rows, :]
            grad_hidden = cot + norm_back(back * ((1.0 + scale) * gain), hat, inv)
            grad_hidden_ref[rows, :] = grad_hidden
            low_ref[rows, :] = (gate_attn * grad_hidden).astype(BF16)
            adds = (grad_hidden * attn_out_ref[rows, :], back, back * hat, cot * branch, cot)
            return tuple(a + jnp.sum(v, axis=0, keepdims=True) for a, v in zip(sums, adds))

        zero = jnp.zeros((1, width), F32)
        sums = lax.fori_loop(0, pieces, finish, (zero,) * 5)
        for i in range(5):
            sums_ref[i : i + 1, :] = sums[i]
        attn_low = low_ref[...]
        g_pack_ref[...] = mm(mixed_ref[...], attn_low, 1, 0).astype(BF16)
        grad_mixed_ref[...] = mm(out_w_ref[...], attn_low, 1, 1).astype(BF16)


def middle(tokens, cot, vectors, up_bias, w_pack, w_down, mixed):
    tok, width = tokens.shape
    ff = w_down.shape[0]
    blocks = ff // width
    whole = lambda shape: pl.BlockSpec(shape, lambda j: (0,) * len(shape), pipeline_mode=pl.Buffered(1))
    fixed = lambda shape: pl.BlockSpec(shape, lambda j: (0,) * len(shape))
    last = blocks - 1
    flops = 2 * tok * width * (6 * ff + 3 * width)
    return pl.pallas_call(
        partial(middle_kernel, blocks),
        grid=(blocks + 1,),
        in_specs=[
            whole(tokens.shape),
            whole(cot.shape),
            whole(vectors.shape),
            pl.BlockSpec((1, 1, width), lambda j: (jnp.minimum(j, last), 0, 0)),
            pl.BlockSpec((width, width), lambda j: (0, jnp.minimum(j, last))),
            pl.BlockSpec((width, width), lambda j: (jnp.minimum(j, last), 0)),
            pl.BlockSpec((width, width), lambda j: (0, blocks), pipeline_mode=pl.Buffered(1)),
        ]
        + [whole(mixed.shape)],
        out_specs=[
            fixed((tok, width)),
            fixed((tok, width)),
            fixed((8, width)),
            pl.BlockSpec((1, 1, width), lambda j: (jnp.minimum(j, last), 0, 0)),
            pl.BlockSpec((width, width), lambda j: (jnp.minimum(j, last), 0)),
            pl.BlockSpec((width, width), lambda j: (0, j)),
        ]
        + [fixed(mixed.shape)],
        out_shape=[
            jax.ShapeDtypeStruct((tok, width), F32),
            jax.ShapeDtypeStruct((tok, width), F32),
            jax.ShapeDtypeStruct((8, width), F32),
            jax.ShapeDtypeStruct((blocks, 1, width), F32),
            jax.ShapeDtypeStruct((ff, width), BF16),
            jax.ShapeDtypeStruct((width, ff + width), BF16),
        ]
        + [jax.ShapeDtypeStruct(mixed.shape, BF16)],
        scratch_shapes=[
            pltpu.VMEM((tok, width), F32),
            pltpu.VMEM((tok, width), BF16),
            pltpu.VMEM((tok, width), BF16),
            pltpu.VMEM((tok, width), F32),
        ],
        compiler_params=pltpu.CompilerParams(vmem_limit_bytes=VMEM_LIMIT),
        cost_estimate=pl.CostEstimate(flops=flops, bytes_accessed=6 * ff * width * 2, transcendentals=tok * ff),
        name="middle",
    )(tokens, cot, vectors, up_bias, w_pack, w_down, w_pack, mixed)


def reduce_kernel(fs, nz, slots, counts, lengths, *refs):
    swapped_ref, w_refs, refs = refs[0], refs[1 : 1 + slots], refs[1 + slots :]
    attn_in_ref, tokens_hbm, hidden_hbm, vec_in_ref, sums_ref, up_bias_ref, *refs = refs
    bulk_refs, (mod_t_ref, cond_ref), refs = refs[:2], refs[2:4], refs[4:]
    inputs_out, qkv_out, up_out, out_out, down_out, total_out, mod_w_out, cond_out = refs[:8]
    (
        row_buf,
        w_buf,
        tokens_buf,
        hidden_buf,
        g_buf,
        pair_buf,
        sum_buf,
        recv_buf,
        own_buf,
        up_pack,
        up_down,
        up_qkv,
        part_pack,
        part_down,
        part_qkv,
        twin_pack,
        twin_down,
        twin_qkv,
        tot_pack,
        tot_down,
        tot_qkv,
        vec_buf,
        vec_z,
        vec_own,
        vec_all,
        cond_send,
        cond_recv,
        local_s,
        pair_s,
        pair_r,
        peer_s,
        peer_r,
        up_s,
        up_r,
        twin_s,
        twin_r,
        tot_s,
        tot_r,
        vecz_s,
        vecz_r,
        vec_s,
        vec_r,
        cond_s,
        cond_r,
    ) = refs[8:]
    me = lax.axis_index("fsdp")
    z = lax.axis_index("seq")
    pairs = fs // 2
    k, c = me // 2, lax.rem(me, 2)
    partner = me + 1 - 2 * c
    inner = jnp.logical_or(z == nz // 2 - 1, z == nz // 2)
    outer = jnp.logical_not(inner)
    twin = nz - 1 - z
    mate = z + 1 - 2 * lax.rem(z, 2)
    tok, width = tokens_buf.shape
    shard = g_buf.shape[3]
    groups = width // 128

    loads = [pltpu.make_async_copy(w_refs[s], w_buf.at[s], local_s.at[s]) for s in range(slots)]
    loads.append(pltpu.make_async_copy(tokens_hbm, tokens_buf, local_s.at[slots]))
    loads.append(pltpu.make_async_copy(hidden_hbm, hidden_buf, local_s.at[slots + 1]))
    for load in loads:
        load.start()
    greet(me, z, fs, nz)

    bulk = [
        (src, up, part, other, tot, i)
        for src, up, part, other, tot, count in (
            (bulk_refs[0], up_pack, part_pack, twin_pack, tot_pack, counts[0]),
            (bulk_refs[1], up_down, part_down, twin_down, tot_down, counts[1]),
        )
        for i in range(count)
    ]
    last = [(own_buf, up_qkv, part_qkv, twin_qkv, tot_qkv, s) for s in range(slots)]
    chain = list(enumerate(bulk + last))
    early, late = chain[: len(bulk)], chain[len(bulk) :]

    def up_copy(n, item):
        src, up, _, _, _, i = item
        return remote(src.at[i], up.at[i], up_s.at[n], up_r.at[n], seq=mate)

    def twin_copy(n, item):
        _, _, part, other, _, i = item
        return remote(part.at[i], other.at[i], twin_s.at[n], twin_r.at[n], seq=twin)

    def tot_copy(n, item):
        tot, i = item[4], item[5]
        return remote(tot.at[i], tot.at[i], tot_s.at[n], tot_r.at[n], seq=mate)

    def chain_in(n, item):
        src, up, part, _, _, i = item
        up_copy(n, item).wait_recv()
        part[i] = add_low(src[i], up[i])
        twin_copy(n, item).start()

    def chain_out(n, item):
        _, _, part, other, tot, i = item
        twin_copy(n, item).wait_recv()
        tot[i] = add_low(part[i], other[i])
        tot_copy(n, item).start()

    def plan(items):
        steps = [(chain_in, items[0])]
        for before, item in zip(items[:-1], items[1:]):
            steps += [(chain_in, item), (chain_out, before)]
        return steps + [(chain_out, items[-1])]

    steps = plan(early)

    def advance(count):
        todo = [steps.pop(0) for _ in range(min(count, len(steps)))]
        if todo:

            @pl.when(inner)
            def _():
                for step, (n, item) in todo:
                    step(n, item)

    half = len(early) // 2

    @pl.when(outer)
    def _():
        for n, item in early[:half]:
            up_copy(n, item).start()

    def pair_copy(s, j):
        return remote(g_buf.at[s, j, 1 - c], pair_buf.at[s, j], pair_s.at[s, j], pair_r.at[s, j], fsdp=partner)

    def peer_copy(s, j):
        return remote(sum_buf.at[s, j], recv_buf.at[s, k], peer_s.at[s, j], peer_r.at[s, k], fsdp=2 * j + c)

    def peer_arrival(s, j):
        return remote(sum_buf.at[s, j], recv_buf.at[s, j], peer_s.at[s, j], peer_r.at[s, j], fsdp=2 * j + c)

    for s in range(slots):
        for head in range(nz):
            for p in range(3):
                base = (p * nz + head) * HD
                row_buf[s, base : base + HD, :] = swapped_ref[s, head, p * HD : (p + 1) * HD, :]
        grad = mm(attn_in_ref[...], row_buf[s], 0, 1).astype(BF16)
        for i in range(fs):
            g_buf[s, i // 2, i % 2] = grad[i * shard : (i + 1) * shard]
        each(pairs, lambda i: pair_copy(s, lax.rem(k + 1 + i, pairs)).start())

    advance(1)

    def forward(i):
        j = lax.rem(k + 1 + i, pairs)
        for s in range(slots):
            pair_copy(s, j).wait_recv()
            sum_buf[s, j] = add_low(g_buf[s, j, c], pair_buf[s, j])
            peer_copy(s, j).start()

    each(pairs - 1, forward)
    for load in loads:
        load.wait()

    scale_mlp, gate_mlp, mlp_gain = (vec_in_ref[i : i + 1, :] for i in (2, 3, 4))
    attn_gain, scale_attn = (vec_in_ref[i : i + 1, :] for i in (6, 7))
    piece = min(256, tok)
    back_sum = hat_sum = jnp.zeros((1, width), F32)
    for i in range(tok // piece):
        rows = slice(i * piece, (i + 1) * piece)
        grad = None
        for s in range(slots):
            part = mm(row_buf[s, :, rows], w_buf[s], 0, 1)
            grad = part if grad is None else grad + part
        hat, inv = normalize(tokens_buf[rows, :])
        scaled = grad * ((1.0 + scale_attn) * attn_gain)
        inputs_out[rows, :] = hidden_buf[rows, :] + norm_back(scaled, hat, inv)
        back_sum = back_sum + jnp.sum(grad, axis=0, keepdims=True)
        hat_sum = hat_sum + jnp.sum(grad * hat, axis=0, keepdims=True)
        advance(2)

    sums = [sums_ref[i : i + 1, :] for i in range(5)]
    vectors = [back_sum, hat_sum * attn_gain, sums[0], sums[1], sums[2] * mlp_gain, sums[3]]
    vectors += [hat_sum * (1.0 + scale_attn), sums[2] * (1.0 + scale_mlp)]
    vectors += [up_bias_ref[i] for i in range(up_bias_ref.shape[0])]
    vectors.append(sums[4] * gate_mlp)
    for p, v in enumerate(vectors):
        for i in range(groups):
            vec_buf[p * groups + i : p * groups + i + 1, :] = v[:, i * 128 : (i + 1) * 128]
    used = len(vectors) * groups
    vec_buf[used:, :] = jnp.zeros((vec_buf.shape[0] - used, 128), F32)
    vec_z[z] = vec_buf[...]

    def vecz_copy(i):
        return remote(vec_buf, vec_z.at[z], vecz_s.at[i], vecz_r.at[z], seq=lax.rem(z + 1 + i, nz))

    def vecz_arrival(i):
        peer = lax.rem(z + 1 + i, nz)
        return remote(vec_buf, vec_z.at[peer], vecz_s.at[i], vecz_r.at[peer], seq=peer)

    each(nz - 1, lambda i: vecz_copy(i).start())

    @pl.when(outer)
    def _():
        for n, item in early[half:]:
            up_copy(n, item).start()

    advance(2)
    each(nz - 1, lambda i: vecz_arrival(i).wait_recv())
    summed = vec_z[0]
    for i in range(1, nz):
        summed = summed + vec_z[i]
    vec_own[...] = summed
    vec_all[me] = summed

    def vec_copy(i):
        return remote(vec_own, vec_all.at[me], vec_s.at[i], vec_r.at[me], fsdp=lax.rem(me + 1 + i, fs))

    def vec_arrival(i):
        peer = lax.rem(me + 1 + i, fs)
        return remote(vec_own, vec_all.at[peer], vec_s.at[i], vec_r.at[peer], fsdp=peer)

    each(fs - 1, lambda i: vec_copy(i).start())
    advance(len(steps))

    for s in range(slots):
        pair_copy(s, k).wait_recv()
        own = g_buf[s, k, c].astype(F32) + pair_buf[s, k].astype(F32)

        def gather_in(i, acc):
            j = lax.rem(k + 1 + i, pairs)
            peer_arrival(s, j).wait_recv()
            return acc + recv_buf[s, j].astype(F32)

        own_buf[s] = lax.fori_loop(0, pairs - 1, gather_in, own).astype(BF16)

        @pl.when(outer)
        def _():
            up_copy(*late[s]).start()

    each(fs - 1, lambda i: vec_arrival(i).wait_recv())
    lane_from = lax.broadcasted_iota(jnp.int32, (256, 128), 0)
    lane_to = lax.broadcasted_iota(jnp.int32, (256, 128), 1)
    part, first, place = None, 0, 0
    for which, length in enumerate(lengths):
        block = length // fs
        for i in range(-(-block // 128)):
            offset = me * block + 128 * i
            row = first + offset // 128
            select = (lane_from == lane_to + lax.rem(offset, 128)).astype(F32)
            both = jnp.concatenate([vec_all[:, pl.ds(row, 1), :][:, 0], vec_all[:, pl.ds(row + 1, 1), :][:, 0]], axis=1)
            rows = lax.dot_general(
                both, select, (((1,), (0,)), ((), ())), precision=HIGHEST, preferred_element_type=F32
            )
            total_out[place : place + 1, :] = jnp.sum(rows, axis=0, keepdims=True)
            place += 1
            if which > 0:
                continue
            share = lax.dot_general(
                rows, mod_t_ref[i], (((1,), (0,)), ((), ())), precision=HIGHEST, preferred_element_type=F32
            )
            part = share if part is None else part + share
            outer_product = lax.dot_general(
                cond_ref[...], rows, (((0,), (0,)), ((), ())), precision=HIGHEST, preferred_element_type=F32
            )
            wide = min(128, block - i * 128)
            mod_w_out[:, i * 128 : i * 128 + wide] = outer_product[:, :wide]
        first += length // 128
    cond_send[...] = jnp.broadcast_to(part[:, None, :], cond_send.shape)

    def cond_copy(i):
        peer = lax.rem(me + 1 + i, fs)
        return remote(cond_send.at[peer], cond_recv.at[me], cond_s.at[i], cond_r.at[me], fsdp=peer)

    def cond_arrival(i):
        peer = lax.rem(me + 1 + i, fs)
        return remote(cond_send.at[peer], cond_recv.at[peer], cond_s.at[i], cond_r.at[peer], fsdp=peer)

    each(fs - 1, lambda i: cond_copy(i).start())
    steps.extend(plan(late))
    advance(len(steps))
    cond_recv[me] = cond_send[me]
    each(fs - 1, lambda i: cond_arrival(i).wait_recv())
    cond_out[...] = jnp.sum(cond_recv[...], axis=0)

    @pl.when(outer)
    def _():
        for n, item in chain:
            tot_copy(n, item).wait_recv()
            up_copy(n, item).wait_send()

    block = nz * HD
    ff = up_out.shape[1]
    for i in range(counts[0]):
        rows = slice(i * tot_pack.shape[1], (i + 1) * tot_pack.shape[1])
        up_out[rows, :] = tot_pack[i, :, :ff].astype(F32)
        out_out[rows, :] = tot_pack[i, :, ff:].astype(F32)
    for i in range(counts[1]):
        down_out[i * tot_down.shape[1] : (i + 1) * tot_down.shape[1], :] = tot_down[i].astype(F32)
    for s in range(slots):
        for p in range(3):
            columns = slice(p * width + s * block, p * width + (s + 1) * block)
            qkv_out[:, columns] = tot_qkv[s, :, p * block : (p + 1) * block].astype(F32)

    @pl.when(inner)
    def _():
        for n, item in chain:
            twin_copy(n, item).wait_send()
            tot_copy(n, item).wait_send()

    def drain_peers(i):
        vec_copy(i).wait_send()
        cond_copy(i).wait_send()

    def drain_pairs(i):
        for s in range(slots):
            pair_copy(s, i).wait_send()

    def drain_sums(i):
        for s in range(slots):
            peer_copy(s, lax.rem(k + 1 + i, pairs)).wait_send()

    each(fs - 1, drain_peers)
    each(pairs, drain_pairs)
    each(pairs - 1, drain_sums)
    each(nz - 1, lambda i: vecz_copy(i).wait_send())


def reduce_all(
    grad_rows, weights, attn_in, tokens, grad_hidden, vectors, sums, up_bias_sum, part_pack, part_down, mod_t, cond, mod_cols, fs, nz
):
    slots = grad_rows.shape[0]
    tok, width = tokens.shape
    shard = width // fs
    count = lambda a: 3 if a.shape[0] % 48 == 0 else 1
    counts = (count(part_pack), count(part_down))
    split = lambda a, n: a.reshape(n, a.shape[0] // n, a.shape[1])
    pack, down = split(part_pack, counts[0]), split(part_down, counts[1])
    pairs = fs // 2
    items = sum(counts) + slots
    ff = up_bias_sum.size
    lengths = (6 * width, width, width, ff, width)
    rows = sum(lengths) // 128 + 2
    places = sum(-(-v // fs // 128) for v in lengths)
    vmem = pl.BlockSpec(memory_space=pltpu.VMEM)
    hbm = pl.BlockSpec(memory_space=pl.ANY)
    low = lambda *shape: pltpu.VMEM(shape, BF16)
    wide = lambda *shape: pltpu.VMEM(shape, F32)
    dma = lambda *shape: pltpu.SemaphoreType.DMA(shape)
    qkv_shape = (slots, shard, width)
    triple = [low(*pack.shape), low(*down.shape), low(*qkv_shape)]
    cols = grad_rows.shape[1] * grad_rows.shape[2]
    inputs_grad, qkv_sum, up_sum, out_sum, down_sum, total, mod_w, cond_grad = pl.pallas_call(
        partial(reduce_kernel, fs, nz, slots, counts, lengths),
        in_specs=[vmem] + [hbm] * slots + [vmem, hbm, hbm] + [vmem] * 7,
        out_specs=[vmem] * 8,
        out_shape=[
            jax.ShapeDtypeStruct((tok, width), F32),
            jax.ShapeDtypeStruct((shard, 3 * width), F32),
            jax.ShapeDtypeStruct((shard, ff), F32),
            jax.ShapeDtypeStruct((shard, part_pack.shape[1] - ff), F32),
            jax.ShapeDtypeStruct(part_down.shape, F32),
            jax.ShapeDtypeStruct((places, 128), F32),
            jax.ShapeDtypeStruct((cond.shape[1], mod_cols), F32),
            jax.ShapeDtypeStruct((8, 128), F32),
        ],
        scratch_shapes=[
            low(slots, cols, tok),
            low(slots, width, cols),
            wide(tok, width),
            wide(tok, width),
            low(slots, pairs, 2, shard, width),
            low(slots, pairs, shard, width),
            low(slots, pairs, shard, width),
            low(slots, pairs, shard, width),
            low(*qkv_shape),
        ]
        + triple * 4
        + [
            wide(rows, 128),
            wide(nz, rows, 128),
            wide(rows, 128),
            wide(fs, rows, 128),
            wide(fs, 8, 128),
            wide(fs, 8, 128),
            dma(slots + 2),
            dma(slots, pairs),
            dma(slots, pairs),
            dma(slots, pairs),
            dma(slots, pairs),
        ]
        + [dma(items)] * 6
        + [dma(nz - 1), dma(nz), dma(fs - 1), dma(fs), dma(fs - 1), dma(fs)],
        compiler_params=pltpu.CompilerParams(vmem_limit_bytes=VMEM_LIMIT, collective_id=1, has_side_effects=True),
        cost_estimate=pl.CostEstimate(flops=12 * tok * width * cols, bytes_accessed=10**8, transcendentals=0),
        name="reduce_all",
    )(grad_rows, *weights, attn_in, tokens, grad_hidden, vectors, sums, up_bias_sum, pack, down, mod_t, cond)
    blocks, place = [], 0
    for v in lengths:
        n = -(-v // fs // 128)
        blocks.append(total[place : place + n].reshape(-1)[: v // fs])
        place += n
    return inputs_grad, qkv_sum, up_sum, out_sum, down_sum, blocks, mod_w, cond_grad


def per_device(
    inputs,
    conditioning,
    cotangent,
    attn_gain,
    mlp_gain,
    qkv_weight,
    out_weight,
    up_weight,
    up_bias,
    down_weight,
    down_bias,
    mod_weight,
    mod_bias,
):
    n = lax.axis_size("seq")
    fs = lax.axis_size("fsdp")
    z = lax.axis_index("seq")
    tokens = inputs[0]
    tok, width = tokens.shape
    slots = H // n
    gather = lambda a: lax.all_gather(a, "fsdp", axis=0, tiled=True)

    inv_freq = jnp.exp(-math.log(10000.0) * jnp.arange(HD // 2, dtype=F32) * (2.0 / HD))
    positions = jnp.arange(tok, dtype=F32)
    own_angles = inv_freq[:, None] * (positions + (z * tok).astype(F32))[None, :]
    starts = (jnp.arange(n) * tok).astype(F32)
    all_angles = inv_freq[None, :, None] * (positions[None, :] + starts[:, None])[:, None, :]
    cos_all, sin_all = jnp.cos(all_angles), jnp.sin(all_angles)

    first, rest, qkv_slots, attn_in, vectors, up_bias_full, cond_low_all, pack_own, down_own = start(
        qkv_weight,
        tokens,
        (attn_gain, mlp_gain, up_bias, down_bias),
        conditioning,
        mod_weight,
        mod_bias,
        jnp.cos(own_angles),
        jnp.sin(own_angles),
        (up_weight, out_weight, down_weight),
        fs,
        n,
    )
    down_full, w_pack = gather(down_own), gather(pack_own)
    x, heads_out, mixed, log_totals = attend(first, rest)
    output, grad_hidden, sums, up_bias_sum, g_down, g_pack, grad_mixed = middle(
        tokens, cotangent[0], vectors, up_bias_full, w_pack, down_full, mixed.reshape(width, tok)
    )
    scatter = lambda a: lax.psum_scatter(a, "fsdp", scatter_dimension=0, tiled=True)
    part_down, part_pack = scatter(g_down), scatter(g_pack)
    grad_slots = attend_back(x, grad_mixed.reshape(heads_out.shape), heads_out, log_totals, cos_all, sin_all)
    mod_cols = mod_weight.shape[1]
    mod_t = jnp.pad(mod_weight.astype(BF16).T.astype(F32), ((0, -mod_cols % 128), (0, 0)))
    inputs_grad, qkv_weight_grad, up_sum, out_sum, down_sum, blocks, mod_weight_grad, cond_grad = reduce_all(
        grad_slots,
        [qkv_slots[s].reshape(width, -1) for s in range(slots)],
        attn_in,
        tokens,
        grad_hidden,
        vectors,
        sums,
        up_bias_sum,
        part_pack,
        part_down,
        mod_t.reshape(-1, 128, mod_weight.shape[0]),
        cond_low_all,
        mod_cols,
        fs,
        n,
    )
    mod_bias_grad, attn_gain_grad, mlp_gain_grad, up_bias_grad, down_bias_grad = blocks
    _, silu_pull = jax.vjp(jax.nn.silu, conditioning)
    conditioning_grad = silu_pull(cond_grad[:1])[0]
    return (
        output[None],
        inputs_grad[None],
        conditioning_grad,
        attn_gain_grad,
        mlp_gain_grad,
        qkv_weight_grad,
        out_sum,
        up_sum,
        up_bias_grad,
        down_sum,
        down_bias_grad,
        mod_weight_grad,
        mod_bias_grad,
    )


def solution(mesh):
    specs = (
        P("fsdp", "seq", None),
        P("fsdp", None),
        P("fsdp", "seq", None),
        P("fsdp"),
        P("fsdp"),
        P("fsdp", None),
        P("fsdp", None),
        P("fsdp", None),
        P("fsdp"),
        P("fsdp", None),
        P("fsdp"),
        P(None, "fsdp"),
        P("fsdp"),
    )
    out_specs = (specs[0], specs[0], specs[1]) + specs[3:]
    return jax.shard_map(per_device, mesh=mesh, in_specs=specs, out_specs=out_specs, check_vma=False)
```

```python
from functools import partial
import math

import jax
import jax.numpy as jnp
from jax import lax
from jax.experimental import pallas as pl
from jax.experimental.pallas import tpu as pltpu
from jax.sharding import PartitionSpec as P

H = 12
HD = 64
EPSILON = 1e-05
BF16 = jnp.bfloat16
F32 = jnp.float32
LOG2E = math.log2(math.e)
VMEM_LIMIT = 60 * 1024 * 1024


def mm(a, b, ca, cb):
    return lax.dot_general(a, b, (((ca,), (cb,)), ((), ())), preferred_element_type=F32)


def normalize(values):
    centre = jnp.mean(values, axis=-1, keepdims=True)
    shifted = values - centre
    variance = jnp.mean(shifted * shifted, axis=-1, keepdims=True)
    inv_std = lax.rsqrt(variance + EPSILON)
    return (shifted * inv_std, inv_std)


def norm_back(grad_hat, normed_hat, inv_std):
    mean_grad = jnp.mean(grad_hat, axis=-1, keepdims=True)
    mean_mixed = jnp.mean(grad_hat * normed_hat, axis=-1, keepdims=True)
    return inv_std * (grad_hat - mean_grad - normed_hat * mean_mixed)


MESH = pl.DeviceIdType.MESH
HIGHEST = lax.Precision.HIGHEST


def add_low(a, b):
    return (a.astype(F32) + b.astype(F32)).astype(BF16)


def remote(src, dst, s, r, **where):
    return pltpu.make_async_remote_copy(
        src_ref=src, dst_ref=dst, send_sem=s, recv_sem=r, device_id=where, device_id_type=MESH
    )


def each(count, body):
    lax.fori_loop(0, count, lambda i, _: (body(i), 0)[1], 0)


def greet(me, z, fs, nz):
    barrier = pltpu.get_barrier_semaphore()

    def hello_fsdp(i):
        peer = {"fsdp": lax.rem(me + 1 + i, fs)}
        pl.semaphore_signal(barrier, inc=1, device_id=peer, device_id_type=MESH)

    def hello_seq(i):
        peer = {"seq": lax.rem(z + 1 + i, nz)}
        pl.semaphore_signal(barrier, inc=1, device_id=peer, device_id_type=MESH)

    each(fs - 1, hello_fsdp)
    each(nz - 1, hello_seq)
    pl.semaphore_wait(barrier, fs + nz - 2)


def start_kernel(fs, nz, slots, *refs):
    (
        qkv_ref,
        tokens_hbm,
        attn_gain_ref,
        mlp_gain_ref,
        up_bias_ref,
        down_bias_ref,
        cond_ref,
        mod_w_ref,
        mod_b_ref,
        cos_ref,
        sin_ref,
        up_hbm,
        out_hbm,
        down_hbm,
        heads_ref,
        rest_ref,
        w_ref,
        attn_in_ref,
        vec_ref,
        bias_ref,
        cond_out,
        pack_out,
        down_out,
    ) = refs[:23]
    (
        tokens_buf,
        up_buf,
        out_buf,
        down_buf,
        w_own,
        z_send,
        narrow,
        spread,
        mod_wide,
        small_send,
        small_all,
        mod_send,
        mod_recv,
        w_full,
        local_s,
        small_s,
        small_r,
        mod_s,
        mod_r,
        w_s,
        w_f,
        w_r,
        z_s,
        z_r,
    ) = refs[23:]
    me = lax.axis_index("fsdp")
    z = lax.axis_index("seq")
    pairs = fs // 2
    k, c = me // 2, lax.rem(me, 2)
    partner = me + 1 - 2 * c
    tok, width = tokens_buf.shape
    shard = w_own.shape[1]
    ff = spread.shape[1]
    block = nz * HD

    fetch = ((tokens_hbm, tokens_buf), (up_hbm, up_buf), (out_hbm, out_buf), (down_hbm, down_buf))
    loads = [pltpu.make_async_copy(src, dst, local_s.at[i]) for i, (src, dst) in enumerate(fetch)]
    for load in loads:
        load.start()
    greet(me, z, fs, nz)

    narrow[...] = jnp.zeros_like(narrow)
    for i, piece in enumerate((attn_gain_ref, mlp_gain_ref, down_bias_ref)):
        narrow[i : i + 1, :shard] = piece[...].reshape(1, -1)
    spread[...] = jnp.zeros_like(spread)
    spread[0:1, : up_bias_ref.shape[0]] = up_bias_ref[...].reshape(1, -1)
    placed = pltpu.roll(narrow[...], me * shard, 1)
    for i in range(3):
        small_send[:, i * width : (i + 1) * width] = placed[i : i + 1]
    placed = pltpu.roll(spread[...], me * up_bias_ref.shape[0], 1)
    small_send[:, 3 * width : 3 * width + ff] = placed[0:1]
    small_send[:, 3 * width + ff :] = cond_ref[...]
    small_all[me] = small_send[...]

    def small_copy(i):
        return remote(small_send, small_all.at[me], small_s.at[i], small_r.at[me], fsdp=lax.rem(me + 1 + i, fs))

    def small_arrival(i):
        peer = lax.rem(me + 1 + i, fs)
        return remote(small_send, small_all.at[peer], small_s.at[i], small_r.at[peer], fsdp=peer)

    each(fs - 1, lambda i: small_copy(i).start())

    for s in range(slots):
        for part in range(3):
            columns = slice(part * width + s * block, part * width + (s + 1) * block)
            w_own[s, :, part * block : (part + 1) * block] = qkv_ref[:, columns].astype(BF16)
        w_ref[s, me] = w_own[s]

    def w_peer(s, i):
        j = lax.rem(k + 1 + i, pairs)
        return remote(w_own.at[s], w_ref.at[s, me], w_s.at[s, i], w_r.at[s, me], fsdp=2 * j + c)

    def w_partner(s):
        return remote(w_own.at[s], w_ref.at[s, me], w_s.at[s, pairs - 1], w_r.at[s, me], fsdp=partner)

    def w_arrival(s, j):
        return remote(w_own.at[s], w_ref.at[s, j], w_s.at[s, 0], w_r.at[s, j], fsdp=partner)

    def w_pass(s, i):
        j = 2 * lax.rem(k + 1 + i, pairs) + c
        return remote(w_ref.at[s, j], w_ref.at[s, j], w_f.at[s, i], w_r.at[s, j], fsdp=partner)

    def send_weight(s):
        each(pairs - 1, lambda i: w_peer(s, i).start())
        w_partner(s).start()

    def pass_weight(s):
        def step(i):
            w_arrival(s, 2 * lax.rem(k + 1 + i, pairs) + c).wait_recv()
            w_pass(s, i).start()

        each(pairs - 1, step)

    send_weight(0)

    each(fs - 1, lambda i: small_arrival(i).wait_recv())
    small_sum = jnp.sum(small_all[:, :, : 3 * width + ff], axis=0)
    cond_all = small_all[:, 0, 3 * width + ff :]
    cond_low = (cond_all / (1.0 + jnp.exp(-cond_all))).astype(BF16)
    cond_out[...] = cond_low.astype(F32)
    own_mod = mm(cond_low, mod_w_ref[...].astype(BF16), 1, 1) + mod_b_ref[...].reshape(1, -1)
    mod_wide[...] = jnp.zeros_like(mod_wide)
    mod_wide[:, : own_mod.shape[1]] = own_mod
    placed = pltpu.roll(mod_wide[...], me * own_mod.shape[1], 1)
    for i in range(fs):
        mod_send[i] = placed[i : i + 1]
    mod_recv[me] = mod_send[me]

    def mod_copy(i):
        peer = lax.rem(me + 1 + i, fs)
        return remote(mod_send.at[peer], mod_recv.at[me], mod_s.at[i], mod_r.at[me], fsdp=peer)

    def mod_arrival(i):
        peer = lax.rem(me + 1 + i, fs)
        return remote(mod_send.at[peer], mod_recv.at[peer], mod_s.at[i], mod_r.at[peer], fsdp=peer)

    each(fs - 1, lambda i: mod_copy(i).start())
    for s in range(1, slots):
        send_weight(s)
    pass_weight(0)

    attn_gain, mlp_gain, down_bias = (small_sum[:, i * width : (i + 1) * width] for i in range(3))
    for i in range(ff // width):
        bias_ref[i] = small_sum[:, (3 + i) * width : (4 + i) * width]
    for load in loads:
        load.wait()
    piece = min(256, tok)
    each(fs - 1, lambda i: mod_arrival(i).wait_recv())
    modulation = jnp.sum(mod_recv[...], axis=0)
    shift_attn, scale_attn, gate_attn, shift_mlp, scale_mlp, gate_mlp = (
        modulation[:, i * width : (i + 1) * width] for i in range(6)
    )
    kept = (gate_attn, shift_mlp, scale_mlp, gate_mlp, mlp_gain, down_bias, attn_gain, scale_attn)
    for i, v in enumerate(kept):
        vec_ref[i : i + 1, :] = v
    for i in range(tok // piece):
        rows = slice(i * piece, (i + 1) * piece)
        hat, _ = normalize(tokens_buf[rows, :])
        attn_in_ref[rows, :] = (hat * attn_gain * (1.0 + scale_attn) + shift_attn).astype(BF16)

    cosine, sine = cos_ref[...], sin_ref[...]
    half = HD // 2

    def project(s, out_ref):
        each(pairs, lambda j: w_arrival(s, 2 * j + 1 - c).wait_recv())
        if shard % 16 == 0:
            weight = w_ref[s].reshape(fs * shard, 3 * block)
        else:
            for i in range(fs):
                w_full[i * shard : (i + 1) * shard, :] = w_ref[s, i].astype(F32)
            weight = w_full[...].astype(BF16)
        rows = mm(weight, attn_in_ref[...], 0, 1).astype(BF16)
        for shard_of in range(nz):
            for part in range(3):
                base = (part * nz + shard_of) * HD
                if part == 2:
                    out_ref[shard_of, part * HD : (part + 1) * HD, :] = rows[base : base + HD]
                else:
                    a = rows[base : base + half].astype(F32)
                    b = rows[base + half : base + HD].astype(F32)
                    out_ref[shard_of, part * HD : part * HD + half, :] = (a * cosine - b * sine).astype(BF16)
                    out_ref[shard_of, part * HD + half : (part + 1) * HD, :] = (b * cosine + a * sine).astype(BF16)

    def z_copy(i):
        peer = lax.rem(z + 1 + i, nz)
        return remote(z_send.at[peer], heads_ref.at[z], z_s.at[i], z_r.at[z], seq=peer)

    def z_arrival(i):
        peer = lax.rem(z + 1 + i, nz)
        return remote(z_send.at[peer], heads_ref.at[peer], z_s.at[i], z_r.at[peer], seq=peer)

    project(0, z_send)
    each(nz - 1, lambda i: z_copy(i).start())
    heads_ref[z] = z_send[z]

    def later(i):
        pass_weight(i + 1)
        project(i + 1, rest_ref.at[i])

    each(slots - 1, later)

    pack_out[:, :ff] = up_buf[...].astype(BF16)
    pack_out[:, ff:] = out_buf[...].astype(BF16)
    down_out[...] = down_buf[...].astype(BF16)
    each(nz - 1, lambda i: z_arrival(i).wait_recv())
    each(nz - 1, lambda i: z_copy(i).wait_send())

    def drain_peers(i):
        small_copy(i).wait_send()
        mod_copy(i).wait_send()

    def drain_weights(i):
        for s in range(slots):
            w_peer(s, i).wait_send()
            w_pass(s, i).wait_send()

    each(fs - 1, drain_peers)
    each(pairs - 1, drain_weights)
    for s in range(slots):
        w_partner(s).wait_send()


def start(qkv_weight, tokens, gains, cond, mod_weight, mod_bias, cosine, sine, feed, fs, nz):
    slots = H // nz
    tok, width = tokens.shape
    shard = qkv_weight.shape[0]
    pairs = fs // 2
    up, out, down = feed
    ff = gains[2].shape[0] * fs
    vmem = pl.BlockSpec(memory_space=pltpu.VMEM)
    hbm = pl.BlockSpec(memory_space=pl.ANY)
    low = lambda *shape: pltpu.VMEM(shape, BF16)
    wide = lambda *shape: pltpu.VMEM(shape, F32)
    dma = lambda *shape: pltpu.SemaphoreType.DMA(shape)
    head_shape = (nz, 3 * HD, tok)
    cols = 3 * nz * HD
    small = 3 * width + ff + cond.shape[-1]
    return pl.pallas_call(
        partial(start_kernel, fs, nz, slots),
        in_specs=[vmem, hbm] + [vmem] * 9 + [hbm] * 3,
        out_specs=[vmem] * 9,
        out_shape=[
            jax.ShapeDtypeStruct(head_shape, BF16),
            jax.ShapeDtypeStruct((slots - 1, *head_shape), BF16),
            jax.ShapeDtypeStruct((slots, fs, shard, cols), BF16),
            jax.ShapeDtypeStruct((tok, width), BF16),
            jax.ShapeDtypeStruct((8, width), F32),
            jax.ShapeDtypeStruct((ff // width, 1, width), F32),
            jax.ShapeDtypeStruct((fs, cond.shape[-1]), F32),
            jax.ShapeDtypeStruct((shard, up.shape[1] + out.shape[1]), BF16),
            jax.ShapeDtypeStruct(down.shape, BF16),
        ],
        scratch_shapes=[
            wide(tok, width),
            wide(*up.shape),
            wide(*out.shape),
            wide(*down.shape),
            low(slots, shard, cols),
            low(*head_shape),
            wide(8, width),
            wide(8, ff),
            wide(fs, 6 * width),
            wide(1, small),
            wide(fs, 1, small),
            wide(fs, 1, 6 * width),
            wide(fs, 1, 6 * width),
            wide(*((8, 128) if shard % 16 == 0 else (width, cols))),
            dma(4),
            dma(fs - 1),
            dma(fs),
            dma(fs - 1),
            dma(fs),
            dma(slots, pairs),
            dma(slots, pairs),
            dma(slots, fs),
            dma(nz - 1),
            dma(nz),
        ],
        compiler_params=pltpu.CompilerParams(vmem_limit_bytes=VMEM_LIMIT, collective_id=2, has_side_effects=True),
        cost_estimate=pl.CostEstimate(flops=6 * tok * width * cols, bytes_accessed=10**8, transcendentals=0),
        name="start",
    )(
        qkv_weight,
        tokens,
        *gains,
        cond,
        mod_weight.T,
        mod_bias,
        cosine,
        sine,
        *feed,
    )


def greet_seq(z, nz):
    barrier = pltpu.get_barrier_semaphore()

    def hello(i):
        peer = {"seq": lax.rem(z + 1 + i, nz)}
        pl.semaphore_signal(barrier, inc=1, device_id=peer, device_id_type=MESH)

    each(nz - 1, hello)
    pl.semaphore_wait(barrier, nz - 1)


def attend_kernel(n, slots, tok, sub, first_ref, rest_ref, x_ref, o_ref, mixed_ref, lse_ref, k_ref, x_s, x_r, o_s, o_r):
    z = lax.axis_index("seq")
    greet_seq(z, n)

    def x_copy(s, i):
        peer = lax.rem(z + 1 + i, n)
        return remote(rest_ref.at[s - 1, peer], x_ref.at[s, z], x_s.at[s - 1, i], x_r.at[s - 1, z], seq=peer)

    def x_arrival(s, i):
        peer = lax.rem(z + 1 + i, n)
        return remote(rest_ref.at[s - 1, peer], x_ref.at[s, peer], x_s.at[s - 1, i], x_r.at[s - 1, peer], seq=peer)

    def o_copy(s, i):
        peer = lax.rem(z + 1 + i, n)
        return remote(o_ref.at[s, peer], mixed_ref.at[s, z], o_s.at[s, i], o_r.at[s, z], seq=peer)

    def o_arrival(s, i):
        peer = lax.rem(z + 1 + i, n)
        return remote(o_ref.at[s, peer], mixed_ref.at[s, peer], o_s.at[s, i], o_r.at[s, peer], seq=peer)

    for s in range(1, slots):
        each(n - 1, lambda i: x_copy(s, i).start())
    x_ref[0] = first_ref[...]
    for s in range(1, slots):
        x_ref[s, z] = rest_ref[s - 1, z]

    scale = LOG2E / math.sqrt(HD)
    width = tok // sub

    def soft(s):
        top = jnp.max(s, axis=0, keepdims=True) * scale
        p = jnp.exp2(s * scale - top)
        total = jnp.sum(p, axis=0, keepdims=True)
        return top, total, p.astype(BF16)

    def slot(s):
        @pl.when(s > 0)
        def _():
            each(n - 1, lambda i: x_arrival(s, i).wait_recv())

        for c in range(n):
            k_ref[c * tok : (c + 1) * tok, :] = x_ref[s, c, HD : 2 * HD, :].T

        def shard(i):
            step = lax.rem(z + 1 + i, n)

            def score(j):
                q = x_ref[s, step, 0:HD, j * width : (j + 1) * width]
                return mm(k_ref[...], q, 1, 0)

            def mix(j, top, total, p):
                o = None
                for c in range(n):
                    part = mm(x_ref[s, c, 2 * HD : 3 * HD, :], p[c * tok : (c + 1) * tok], 1, 0)
                    o = part if o is None else o + part
                o_ref[s, step, :, j * width : (j + 1) * width] = (o / total).astype(BF16)
                lse_ref[s, step, :, j * width : (j + 1) * width] = top + jnp.log2(total)

            scores = [score(0)]
            pending = None
            for j in range(sub):
                if j + 1 < sub:
                    scores.append(score(j + 1))
                done = soft(scores[j])
                if pending is not None:
                    mix(j - 1, *pending)
                pending = done
            mix(sub - 1, *pending)

            @pl.when(i < n - 1)
            def _():
                o_copy(s, i).start()

        each(n, shard)
        mixed_ref[s, z] = o_ref[s, z]

    each(slots, slot)

    def drain(s):
        each(n - 1, lambda i: o_arrival(s, i).wait_recv())
        each(n - 1, lambda i: o_copy(s, i).wait_send())

    each(slots, drain)
    for s in range(1, slots):
        each(n - 1, lambda i: x_copy(s, i).wait_send())


def attend(first, rest):
    n, _, tok = first.shape
    slots = rest.shape[0] + 1
    length = n * tok
    vmem = pl.BlockSpec(memory_space=pltpu.VMEM)
    dma = lambda *shape: pltpu.SemaphoreType.DMA(shape)
    head_shape = (slots, n, HD, tok)
    return pl.pallas_call(
        partial(attend_kernel, n, slots, tok, 2),
        in_specs=[vmem] * 2,
        out_specs=[vmem] * 4,
        out_shape=[
            jax.ShapeDtypeStruct((slots, n, 3 * HD, tok), BF16),
            jax.ShapeDtypeStruct(head_shape, BF16),
            jax.ShapeDtypeStruct(head_shape, BF16),
            jax.ShapeDtypeStruct((slots, n, 1, tok), F32),
        ],
        scratch_shapes=[
            pltpu.VMEM((length, HD), BF16),
            dma(slots - 1, n - 1),
            dma(slots - 1, n),
            dma(slots, n - 1),
            dma(slots, n),
        ],
        compiler_params=pltpu.CompilerParams(vmem_limit_bytes=VMEM_LIMIT, collective_id=3, has_side_effects=True),
        cost_estimate=pl.CostEstimate(
            flops=16 * slots * length * length * HD, bytes_accessed=10**7, transcendentals=slots * length * length
        ),
        name="attend",
    )(first, rest)


def attend_back_kernel(
    n,
    slots,
    tok,
    sub,
    x_ref,
    sent_ref,
    o_ref,
    lse_ref,
    cos_ref,
    sin_ref,
    out_ref,
    g_ref,
    d_ref,
    k_ref,
    v_ref,
    dk_ref,
    dv_ref,
    g_s,
    g_r,
    q_s,
    q_r,
    kv_s,
    kv_r,
):
    z = lax.axis_index("seq")
    half = HD // 2
    greet_seq(z, n)

    def g_copy(s, i):
        peer = lax.rem(z + 1 + i, n)
        return remote(sent_ref.at[s, peer], g_ref.at[s, z], g_s.at[s, i], g_r.at[s, z], seq=peer)

    def g_arrival(s, i):
        peer = lax.rem(z + 1 + i, n)
        return remote(sent_ref.at[s, peer], g_ref.at[s, peer], g_s.at[s, i], g_r.at[s, peer], seq=peer)

    def part_copy(s, i, rows, send, recv, arrival):
        peer = lax.rem(z + 1 + i, n)
        slot = peer if arrival else z
        return remote(
            d_ref.at[s, peer, rows], out_ref.at[s, slot, rows], send.at[s, i], recv.at[s, slot], seq=peer
        )

    q_rows, kv_rows = pl.ds(0, HD), pl.ds(HD, 2 * HD)
    q_copy = lambda s, i, arrival=False: part_copy(s, i, q_rows, q_s, q_r, arrival)
    kv_copy = lambda s, i, arrival=False: part_copy(s, i, kv_rows, kv_s, kv_r, arrival)

    for s in range(slots):
        each(n - 1, lambda i: g_copy(s, i).start())
        g_ref[s, z] = sent_ref[s, z]

    scale = LOG2E / math.sqrt(HD)
    width = tok // sub

    def turn_back(grad, cosine, sine):
        a, b = grad[:half], grad[half:]
        return (a * cosine + b * sine).astype(BF16), (b * cosine - a * sine).astype(BF16)

    def slot(s):
        for c in range(n):
            k_ref[c * tok : (c + 1) * tok, :] = x_ref[s, c, HD : 2 * HD, :].T
            v_ref[c * tok : (c + 1) * tok, :] = x_ref[s, c, 2 * HD : 3 * HD, :].T
        dk_ref[...] = jnp.zeros_like(dk_ref)
        dv_ref[...] = jnp.zeros_like(dv_ref)
        each(n - 1, lambda i: g_arrival(s, i).wait_recv())

        def shard(i):
            step = lax.rem(z + 1 + i, n)
            for j in range(sub):
                cols = slice(j * width, (j + 1) * width)
                q = x_ref[s, step, 0:HD, cols]
                g = g_ref[s, step, :, cols]
                o = o_ref[s, step, :, cols]
                centre = jnp.sum(g.astype(F32) * o.astype(F32), axis=0, keepdims=True)
                score = mm(k_ref[...], q, 1, 0)
                dp = mm(v_ref[...], g, 1, 0)
                p = jnp.exp2(score * scale - lse_ref[s, step, :, cols])
                p_low = p.astype(BF16)
                ds = (p * (dp - centre)).astype(BF16)
                dv_ref[...] += mm(g, p_low, 1, 1)
                dk_ref[...] += mm(q, ds, 1, 1)
                dq = None
                for c in range(n):
                    part = mm(x_ref[s, c, HD : 2 * HD, :], ds[c * tok : (c + 1) * tok], 1, 0)
                    dq = part if dq is None else dq + part
                dq = dq * (1.0 / math.sqrt(HD))
                a, b = turn_back(dq, cos_ref[step, :, cols], sin_ref[step, :, cols])
                d_ref[s, step, 0:half, cols] = a
                d_ref[s, step, half:HD, cols] = b

            @pl.when(i < n - 1)
            def _():
                q_copy(s, i).start()

        each(n, shard)
        for c in range(n):
            dk = dk_ref[:, c * tok : (c + 1) * tok] * (1.0 / math.sqrt(HD))
            a, b = turn_back(dk, cos_ref[c], sin_ref[c])
            d_ref[s, c, HD : HD + half, :] = a
            d_ref[s, c, HD + half : 2 * HD, :] = b
            d_ref[s, c, 2 * HD : 3 * HD, :] = dv_ref[:, c * tok : (c + 1) * tok].astype(BF16)
        each(n - 1, lambda i: kv_copy(s, i).start())
        out_ref[s, z] = d_ref[s, z]

    each(slots, slot)

    def drain(s):
        def one(i):
            q_copy(s, i, True).wait_recv()
            kv_copy(s, i, True).wait_recv()
            g_copy(s, i).wait_send()
            q_copy(s, i).wait_send()
            kv_copy(s, i).wait_send()

        each(n - 1, one)

    each(slots, drain)


def attend_back(x, g, o, lse, cosine, sine):
    slots, n, _, tok = x.shape
    length = n * tok
    vmem = pl.BlockSpec(memory_space=pltpu.VMEM)
    dma = lambda *shape: pltpu.SemaphoreType.DMA(shape)
    return pl.pallas_call(
        partial(attend_back_kernel, n, slots, tok, 2),
        in_specs=[vmem] * 6,
        out_specs=vmem,
        out_shape=jax.ShapeDtypeStruct(x.shape, BF16),
        scratch_shapes=[
            pltpu.VMEM(g.shape, BF16),
            pltpu.VMEM(x.shape, BF16),
            pltpu.VMEM((length, HD), BF16),
            pltpu.VMEM((length, HD), BF16),
            pltpu.VMEM((HD, length), F32),
            pltpu.VMEM((HD, length), F32),
        ]
        + [dma(slots, n - 1), dma(slots, n)] * 3,
        compiler_params=pltpu.CompilerParams(vmem_limit_bytes=VMEM_LIMIT, collective_id=4, has_side_effects=True),
        cost_estimate=pl.CostEstimate(
            flops=40 * slots * length * length * HD, bytes_accessed=10**7, transcendentals=slots * length * length
        ),
        name="attend_back",
    )(x, g, o, lse, cosine, sine)


GELU_C = math.sqrt(2.0 / math.pi)
GELU_A = 0.044715


def middle_kernel(
    blocks,
    tokens_ref,
    cot_ref,
    vec_ref,
    bias_ref,
    up_ref,
    down_ref,
    out_w_ref,
    mixed_ref,
    output_ref,
    grad_hidden_ref,
    sums_ref,
    bias_grad_ref,
    g_down_ref,
    g_pack_ref,
    grad_mixed_ref,
    attn_out_ref,
    mlp_in_ref,
    low_ref,
    back_ref,
):
    j = pl.program_id(0)
    tok, width = tokens_ref.shape
    gate_attn, shift, scale, gate, gain, down_bias = (vec_ref[i : i + 1, :] for i in range(6))
    piece = min(256, tok)
    pieces = tok // piece

    @pl.when(j == 0)
    def _():
        attn_out_ref[...] = mm(mixed_ref[...], out_w_ref[...], 0, 0)

        def prepare(i, _):
            rows = pl.ds(pl.multiple_of(i * piece, piece), piece)
            hidden = tokens_ref[rows, :] + gate_attn * attn_out_ref[rows, :]
            grad_hidden_ref[rows, :] = hidden
            hat, _ = normalize(hidden)
            mlp_in_ref[rows, :] = (hat * gain * (1.0 + scale) + shift).astype(BF16)
            low_ref[rows, :] = (gate * cot_ref[rows, :]).astype(BF16)
            return 0

        lax.fori_loop(0, pieces, prepare, 0)
        output_ref[...] = jnp.zeros_like(output_ref)
        back_ref[...] = jnp.zeros_like(back_ref)

    @pl.when(j < blocks)
    def _():
        mlp_in, low = mlp_in_ref[...], low_ref[...]
        x = mm(mlp_in, up_ref[...], 1, 0) + bias_ref[0]
        grad_act = mm(low, down_ref[...], 1, 1)
        square = x * x
        t = jnp.tanh(x * (GELU_C + GELU_C * GELU_A * square))
        half = 0.5 + 0.5 * t
        act = (x * half).astype(BF16)
        slope = half + x * (0.5 - 0.5 * t * t) * (GELU_C + 3.0 * GELU_C * GELU_A * square)
        grad_pre = grad_act * slope
        bias_grad_ref[0] = jnp.sum(grad_pre, axis=0, keepdims=True)
        pre_low = grad_pre.astype(BF16)
        output_ref[...] += mm(act, down_ref[...], 1, 0)
        back_ref[...] += mm(pre_low, up_ref[...], 1, 1)
        g_down_ref[...] = mm(act, low, 0, 0).astype(BF16)
        g_pack_ref[...] = mm(mlp_in, pre_low, 0, 0).astype(BF16)

    @pl.when(j == blocks)
    def _():
        def finish(i, sums):
            rows = pl.ds(pl.multiple_of(i * piece, piece), piece)
            cot = cot_ref[rows, :]
            branch = output_ref[rows, :] + down_bias
            hidden = grad_hidden_ref[rows, :]
            output_ref[rows, :] = hidden + gate * branch
            hat, inv = normalize(hidden)
            back = back_ref[rows, :]
            grad_hidden = cot + norm_back(back * ((1.0 + scale) * gain), hat, inv)
            grad_hidden_ref[rows, :] = grad_hidden
            low_ref[rows, :] = (gate_attn * grad_hidden).astype(BF16)
            adds = (grad_hidden * attn_out_ref[rows, :], back, back * hat, cot * branch, cot)
            return tuple(a + jnp.sum(v, axis=0, keepdims=True) for a, v in zip(sums, adds))

        zero = jnp.zeros((1, width), F32)
        sums = lax.fori_loop(0, pieces, finish, (zero,) * 5)
        for i in range(5):
            sums_ref[i : i + 1, :] = sums[i]
        attn_low = low_ref[...]
        g_pack_ref[...] = mm(mixed_ref[...], attn_low, 1, 0).astype(BF16)
        grad_mixed_ref[...] = mm(out_w_ref[...], attn_low, 1, 1).astype(BF16)


def middle(tokens, cot, vectors, up_bias, w_pack, w_down, mixed):
    tok, width = tokens.shape
    ff = w_down.shape[0]
    blocks = ff // width
    whole = lambda shape: pl.BlockSpec(shape, lambda j: (0,) * len(shape), pipeline_mode=pl.Buffered(1))
    fixed = lambda shape: pl.BlockSpec(shape, lambda j: (0,) * len(shape))
    last = blocks - 1
    flops = 2 * tok * width * (6 * ff + 3 * width)
    return pl.pallas_call(
        partial(middle_kernel, blocks),
        grid=(blocks + 1,),
        in_specs=[
            whole(tokens.shape),
            whole(cot.shape),
            whole(vectors.shape),
            pl.BlockSpec((1, 1, width), lambda j: (jnp.minimum(j, last), 0, 0)),
            pl.BlockSpec((width, width), lambda j: (0, jnp.minimum(j, last))),
            pl.BlockSpec((width, width), lambda j: (jnp.minimum(j, last), 0)),
            pl.BlockSpec((width, width), lambda j: (0, blocks), pipeline_mode=pl.Buffered(1)),
        ]
        + [whole(mixed.shape)],
        out_specs=[
            fixed((tok, width)),
            fixed((tok, width)),
            fixed((8, width)),
            pl.BlockSpec((1, 1, width), lambda j: (jnp.minimum(j, last), 0, 0)),
            pl.BlockSpec((width, width), lambda j: (jnp.minimum(j, last), 0)),
            pl.BlockSpec((width, width), lambda j: (0, j)),
        ]
        + [fixed(mixed.shape)],
        out_shape=[
            jax.ShapeDtypeStruct((tok, width), F32),
            jax.ShapeDtypeStruct((tok, width), F32),
            jax.ShapeDtypeStruct((8, width), F32),
            jax.ShapeDtypeStruct((blocks, 1, width), F32),
            jax.ShapeDtypeStruct((ff, width), BF16),
            jax.ShapeDtypeStruct((width, ff + width), BF16),
        ]
        + [jax.ShapeDtypeStruct(mixed.shape, BF16)],
        scratch_shapes=[
            pltpu.VMEM((tok, width), F32),
            pltpu.VMEM((tok, width), BF16),
            pltpu.VMEM((tok, width), BF16),
            pltpu.VMEM((tok, width), F32),
        ],
        compiler_params=pltpu.CompilerParams(vmem_limit_bytes=VMEM_LIMIT),
        cost_estimate=pl.CostEstimate(flops=flops, bytes_accessed=6 * ff * width * 2, transcendentals=tok * ff),
        name="middle",
    )(tokens, cot, vectors, up_bias, w_pack, w_down, w_pack, mixed)


def reduce_kernel(fs, nz, slots, counts, lengths, *refs):
    swapped_ref, w_hbm, attn_in_ref, tokens_hbm, hidden_hbm, vec_in_ref, sums_ref, up_bias_ref, *refs = refs
    bulk_refs, (mod_t_ref, cond_ref), refs = refs[:2], refs[2:4], refs[4:]
    inputs_out, qkv_out, up_out, out_out, down_out, total_out, mod_w_out, cond_out = refs[:8]
    (
        row_buf,
        w_buf,
        tokens_buf,
        hidden_buf,
        g_buf,
        pair_buf,
        sum_buf,
        recv_buf,
        own_buf,
        up_pack,
        up_down,
        up_qkv,
        part_pack,
        part_down,
        part_qkv,
        twin_pack,
        twin_down,
        twin_qkv,
        tot_pack,
        tot_down,
        tot_qkv,
        vec_buf,
        vec_z,
        vec_own,
        vec_all,
        cond_send,
        cond_recv,
        local_s,
        pair_s,
        pair_r,
        peer_s,
        peer_r,
        up_s,
        up_r,
        twin_s,
        twin_r,
        tot_s,
        tot_r,
        vecz_s,
        vecz_r,
        vec_s,
        vec_r,
        cond_s,
        cond_r,
    ) = refs[8:]
    me = lax.axis_index("fsdp")
    z = lax.axis_index("seq")
    pairs = fs // 2
    k, c = me // 2, lax.rem(me, 2)
    partner = me + 1 - 2 * c
    inner = jnp.logical_or(z == nz // 2 - 1, z == nz // 2)
    outer = jnp.logical_not(inner)
    twin = nz - 1 - z
    mate = z + 1 - 2 * lax.rem(z, 2)
    tok, width = tokens_buf.shape
    shard = g_buf.shape[3]
    groups = width // 128

    fetch = ((w_hbm, w_buf), (tokens_hbm, tokens_buf), (hidden_hbm, hidden_buf))
    loads = [pltpu.make_async_copy(src, dst, local_s.at[i]) for i, (src, dst) in enumerate(fetch)]
    for load in loads:
        load.start()
    greet(me, z, fs, nz)

    bulk = [
        (src, up, part, other, tot, i)
        for src, up, part, other, tot, count in (
            (bulk_refs[0], up_pack, part_pack, twin_pack, tot_pack, counts[0]),
            (bulk_refs[1], up_down, part_down, twin_down, tot_down, counts[1]),
        )
        for i in range(count)
    ]
    last = [(own_buf, up_qkv, part_qkv, twin_qkv, tot_qkv, s) for s in range(slots)]
    chain = list(enumerate(bulk + last))
    early, late = chain[: len(bulk)], chain[len(bulk) :]

    def up_copy(n, item):
        src, up, _, _, _, i = item
        return remote(src.at[i], up.at[i], up_s.at[n], up_r.at[n], seq=mate)

    def twin_copy(n, item):
        _, _, part, other, _, i = item
        return remote(part.at[i], other.at[i], twin_s.at[n], twin_r.at[n], seq=twin)

    def tot_copy(n, item):
        tot, i = item[4], item[5]
        return remote(tot.at[i], tot.at[i], tot_s.at[n], tot_r.at[n], seq=mate)

    def chain_in(n, item):
        src, up, part, _, _, i = item
        up_copy(n, item).wait_recv()
        part[i] = add_low(src[i], up[i])
        twin_copy(n, item).start()

    def chain_out(n, item):
        _, _, part, other, tot, i = item
        twin_copy(n, item).wait_recv()
        tot[i] = add_low(part[i], other[i])
        tot_copy(n, item).start()

    def plan(items):
        steps = [(chain_in, items[0])]
        for before, item in zip(items[:-1], items[1:]):
            steps += [(chain_in, item), (chain_out, before)]
        return steps + [(chain_out, items[-1])]

    steps = plan(early)

    def advance(count):
        todo = [steps.pop(0) for _ in range(min(count, len(steps)))]
        if todo:

            @pl.when(inner)
            def _():
                for step, (n, item) in todo:
                    step(n, item)

    @pl.when(outer)
    def _():
        for n, item in early:
            up_copy(n, item).start()

    def pair_copy(s, j):
        return remote(g_buf.at[s, j, 1 - c], pair_buf.at[s, j], pair_s.at[s, j], pair_r.at[s, j], fsdp=partner)

    def peer_copy(s, j):
        return remote(sum_buf.at[s, j], recv_buf.at[s, k], peer_s.at[s, j], peer_r.at[s, k], fsdp=2 * j + c)

    def peer_arrival(s, j):
        return remote(sum_buf.at[s, j], recv_buf.at[s, j], peer_s.at[s, j], peer_r.at[s, j], fsdp=2 * j + c)

    def project_grad(s):
        for head in range(nz):
            for p in range(3):
                base = (p * nz + head) * HD
                row_buf[s, base : base + HD, :] = swapped_ref[s, head, p * HD : (p + 1) * HD, :]
        grad = mm(attn_in_ref[...], row_buf[s], 0, 1).astype(BF16)
        for i in range(fs):
            g_buf[s, i // 2, i % 2] = grad[i * shard : (i + 1) * shard]
        each(pairs, lambda i: pair_copy(s, lax.rem(k + 1 + i, pairs)).start())

    each(slots, project_grad)

    advance(1)

    def forward(i):
        j = lax.rem(k + 1 + i, pairs)
        for s in range(slots):
            pair_copy(s, j).wait_recv()
            sum_buf[s, j] = add_low(g_buf[s, j, c], pair_buf[s, j])
            peer_copy(s, j).start()

    each(pairs - 1, forward)
    for load in loads:
        load.wait()

    scale_mlp, gate_mlp, mlp_gain = (vec_in_ref[i : i + 1, :] for i in (2, 3, 4))
    attn_gain, scale_attn = (vec_in_ref[i : i + 1, :] for i in (6, 7))
    piece = min(256, tok)

    def norm_piece(i, kept):
        back_sum, hat_sum = kept
        rows = pl.ds(pl.multiple_of(i * piece, piece), piece)
        grad = None
        for s in range(slots):
            part = mm(row_buf[s, :, rows], w_buf[s], 0, 1)
            grad = part if grad is None else grad + part
        hat, inv = normalize(tokens_buf[rows, :])
        scaled = grad * ((1.0 + scale_attn) * attn_gain)
        inputs_out[rows, :] = hidden_buf[rows, :] + norm_back(scaled, hat, inv)
        back_sum = back_sum + jnp.sum(grad, axis=0, keepdims=True)
        hat_sum = hat_sum + jnp.sum(grad * hat, axis=0, keepdims=True)
        return back_sum, hat_sum

    zero = jnp.zeros((1, width), F32)
    back_sum, hat_sum = lax.fori_loop(0, tok // piece, norm_piece, (zero, zero))

    sums = [sums_ref[i : i + 1, :] for i in range(5)]
    vectors = [back_sum, hat_sum * attn_gain, sums[0], sums[1], sums[2] * mlp_gain, sums[3]]
    vectors += [hat_sum * (1.0 + scale_attn), sums[2] * (1.0 + scale_mlp)]
    vectors += [up_bias_ref[i] for i in range(up_bias_ref.shape[0])]
    vectors.append(sums[4] * gate_mlp)
    for p, v in enumerate(vectors):
        for i in range(groups):
            vec_buf[p * groups + i : p * groups + i + 1, :] = v[:, i * 128 : (i + 1) * 128]
    used = len(vectors) * groups
    vec_buf[used:, :] = jnp.zeros((vec_buf.shape[0] - used, 128), F32)
    vec_z[z] = vec_buf[...]

    def vecz_copy(i):
        return remote(vec_buf, vec_z.at[z], vecz_s.at[i], vecz_r.at[z], seq=lax.rem(z + 1 + i, nz))

    def vecz_arrival(i):
        peer = lax.rem(z + 1 + i, nz)
        return remote(vec_buf, vec_z.at[peer], vecz_s.at[i], vecz_r.at[peer], seq=peer)

    each(nz - 1, lambda i: vecz_copy(i).start())

    advance(len(steps))
    for s in range(slots):
        pair_copy(s, k).wait_recv()
        own = g_buf[s, k, c].astype(F32) + pair_buf[s, k].astype(F32)

        def gather_in(i, acc):
            j = lax.rem(k + 1 + i, pairs)
            peer_arrival(s, j).wait_recv()
            return acc + recv_buf[s, j].astype(F32)

        own_buf[s] = lax.fori_loop(0, pairs - 1, gather_in, own).astype(BF16)

        @pl.when(outer)
        def _():
            up_copy(*late[s]).start()

    steps.extend(plan(late))
    each(nz - 1, lambda i: vecz_arrival(i).wait_recv())
    summed = vec_z[0]
    for i in range(1, nz):
        summed = summed + vec_z[i]
    vec_own[...] = summed
    vec_all[me] = summed

    def vec_copy(i):
        return remote(vec_own, vec_all.at[me], vec_s.at[i], vec_r.at[me], fsdp=lax.rem(me + 1 + i, fs))

    def vec_arrival(i):
        peer = lax.rem(me + 1 + i, fs)
        return remote(vec_own, vec_all.at[peer], vec_s.at[i], vec_r.at[peer], fsdp=peer)

    each(fs - 1, lambda i: vec_copy(i).start())
    advance(3)

    each(fs - 1, lambda i: vec_arrival(i).wait_recv())
    lane_from = lax.broadcasted_iota(jnp.int32, (256, 128), 0)
    lane_to = lax.broadcasted_iota(jnp.int32, (256, 128), 1)
    part, first, place = None, 0, 0
    for which, length in enumerate(lengths):
        block = length // fs
        for i in range(-(-block // 128)):
            offset = me * block + 128 * i
            row = first + offset // 128
            select = (lane_from == lane_to + lax.rem(offset, 128)).astype(F32)
            both = jnp.concatenate([vec_all[:, pl.ds(row, 1), :][:, 0], vec_all[:, pl.ds(row + 1, 1), :][:, 0]], axis=1)
            rows = lax.dot_general(
                both, select, (((1,), (0,)), ((), ())), precision=HIGHEST, preferred_element_type=F32
            )
            total_out[place : place + 1, :] = jnp.sum(rows, axis=0, keepdims=True)
            place += 1
            if which > 0:
                continue
            wide = min(128, block - i * 128)
            columns = slice(i * 128, i * 128 + wide)
            mod_rows = mod_t_ref[columns, :].astype(BF16).astype(F32)
            share = lax.dot_general(
                rows[:, :wide], mod_rows, (((1,), (0,)), ((), ())), precision=HIGHEST, preferred_element_type=F32
            )
            part = share if part is None else part + share
            outer_product = lax.dot_general(
                rows, cond_ref[...], (((0,), (0,)), ((), ())), precision=HIGHEST, preferred_element_type=F32
            )
            mod_w_out[columns, :] = outer_product[:wide]
        first += length // 128
    cond_send[...] = jnp.broadcast_to(part[:, None, :], cond_send.shape)

    def cond_copy(i):
        peer = lax.rem(me + 1 + i, fs)
        return remote(cond_send.at[peer], cond_recv.at[me], cond_s.at[i], cond_r.at[me], fsdp=peer)

    def cond_arrival(i):
        peer = lax.rem(me + 1 + i, fs)
        return remote(cond_send.at[peer], cond_recv.at[peer], cond_s.at[i], cond_r.at[peer], fsdp=peer)

    each(fs - 1, lambda i: cond_copy(i).start())
    advance(len(steps))
    cond_recv[me] = cond_send[me]
    each(fs - 1, lambda i: cond_arrival(i).wait_recv())
    cond_out[...] = jnp.sum(cond_recv[...], axis=0)

    @pl.when(outer)
    def _():
        for n, item in chain:
            tot_copy(n, item).wait_recv()
            up_copy(n, item).wait_send()

    block = nz * HD
    ff = up_out.shape[1]

    def write_pack(i):
        rows = pl.ds(i * tot_pack.shape[1], tot_pack.shape[1])
        up_out[rows, :] = tot_pack[i, :, :ff].astype(F32)
        out_out[rows, :] = tot_pack[i, :, ff:].astype(F32)

    def write_down(i):
        down_out[pl.ds(i * tot_down.shape[1], tot_down.shape[1]), :] = tot_down[i].astype(F32)

    each(counts[0], write_pack)
    each(counts[1], write_down)
    for s in range(slots):
        for p in range(3):
            columns = slice(p * width + s * block, p * width + (s + 1) * block)
            qkv_out[:, columns] = tot_qkv[s, :, p * block : (p + 1) * block].astype(F32)

    @pl.when(inner)
    def _():
        for n, item in chain:
            twin_copy(n, item).wait_send()
            tot_copy(n, item).wait_send()

    def drain_peers(i):
        vec_copy(i).wait_send()
        cond_copy(i).wait_send()

    def drain_pairs(i):
        for s in range(slots):
            pair_copy(s, i).wait_send()

    def drain_sums(i):
        for s in range(slots):
            peer_copy(s, lax.rem(k + 1 + i, pairs)).wait_send()

    each(fs - 1, drain_peers)
    each(pairs, drain_pairs)
    each(pairs - 1, drain_sums)
    each(nz - 1, lambda i: vecz_copy(i).wait_send())


def reduce_all(
    grad_rows, weights, attn_in, tokens, grad_hidden, vectors, sums, up_bias_sum, part_pack, part_down, mod_t, cond, fs, nz
):
    slots = grad_rows.shape[0]
    tok, width = tokens.shape
    shard = width // fs
    count = lambda a: 3 if a.shape[0] % 48 == 0 else 1
    counts = (count(part_pack), count(part_down))
    split = lambda a, n: a.reshape(n, a.shape[0] // n, a.shape[1])
    pack, down = split(part_pack, counts[0]), split(part_down, counts[1])
    pairs = fs // 2
    items = sum(counts) + slots
    ff = up_bias_sum.size
    lengths = (6 * width, width, width, ff, width)
    rows = sum(lengths) // 128 + 2
    places = sum(-(-v // fs // 128) for v in lengths)
    vmem = pl.BlockSpec(memory_space=pltpu.VMEM)
    hbm = pl.BlockSpec(memory_space=pl.ANY)
    low = lambda *shape: pltpu.VMEM(shape, BF16)
    wide = lambda *shape: pltpu.VMEM(shape, F32)
    dma = lambda *shape: pltpu.SemaphoreType.DMA(shape)
    qkv_shape = (slots, shard, width)
    triple = [low(*pack.shape), low(*down.shape), low(*qkv_shape)]
    cols = grad_rows.shape[1] * grad_rows.shape[2]
    inputs_grad, qkv_sum, up_sum, out_sum, down_sum, total, mod_w, cond_grad = pl.pallas_call(
        partial(reduce_kernel, fs, nz, slots, counts, lengths),
        in_specs=[vmem, hbm, vmem, hbm, hbm] + [vmem] * 7,
        out_specs=[vmem] * 8,
        out_shape=[
            jax.ShapeDtypeStruct((tok, width), F32),
            jax.ShapeDtypeStruct((shard, 3 * width), F32),
            jax.ShapeDtypeStruct((shard, ff), F32),
            jax.ShapeDtypeStruct((shard, part_pack.shape[1] - ff), F32),
            jax.ShapeDtypeStruct(part_down.shape, F32),
            jax.ShapeDtypeStruct((places, 128), F32),
            jax.ShapeDtypeStruct(mod_t.shape, F32),
            jax.ShapeDtypeStruct((8, 128), F32),
        ],
        scratch_shapes=[
            low(slots, cols, tok),
            low(slots, width, cols),
            wide(tok, width),
            wide(tok, width),
            low(slots, pairs, 2, shard, width),
            low(slots, pairs, shard, width),
            low(slots, pairs, shard, width),
            low(slots, pairs, shard, width),
            low(*qkv_shape),
        ]
        + triple * 4
        + [
            wide(rows, 128),
            wide(nz, rows, 128),
            wide(rows, 128),
            wide(fs, rows, 128),
            wide(fs, 8, 128),
            wide(fs, 8, 128),
            dma(3),
            dma(slots, pairs),
            dma(slots, pairs),
            dma(slots, pairs),
            dma(slots, pairs),
        ]
        + [dma(items)] * 6
        + [dma(nz - 1), dma(nz), dma(fs - 1), dma(fs), dma(fs - 1), dma(fs)],
        compiler_params=pltpu.CompilerParams(vmem_limit_bytes=VMEM_LIMIT, collective_id=1, has_side_effects=True),
        cost_estimate=pl.CostEstimate(flops=12 * tok * width * cols, bytes_accessed=10**8, transcendentals=0),
        name="reduce_all",
    )(grad_rows, weights, attn_in, tokens, grad_hidden, vectors, sums, up_bias_sum, pack, down, mod_t, cond)
    blocks, place = [], 0
    for v in lengths:
        n = -(-v // fs // 128)
        blocks.append(total[place : place + n].reshape(-1)[: v // fs])
        place += n
    return inputs_grad, qkv_sum, up_sum, out_sum, down_sum, blocks, mod_w.T, cond_grad


def per_device(
    inputs,
    conditioning,
    cotangent,
    attn_gain,
    mlp_gain,
    qkv_weight,
    out_weight,
    up_weight,
    up_bias,
    down_weight,
    down_bias,
    mod_weight,
    mod_bias,
):
    n = lax.axis_size("seq")
    fs = lax.axis_size("fsdp")
    z = lax.axis_index("seq")
    tokens = inputs[0]
    tok, width = tokens.shape
    slots = H // n
    gather = lambda a: lax.all_gather(a, "fsdp", axis=0, tiled=True)

    inv_freq = jnp.exp(-math.log(10000.0) * jnp.arange(HD // 2, dtype=F32) * (2.0 / HD))
    positions = jnp.arange(tok, dtype=F32)
    own_angles = inv_freq[:, None] * (positions + (z * tok).astype(F32))[None, :]
    starts = (jnp.arange(n) * tok).astype(F32)
    all_angles = inv_freq[None, :, None] * (positions[None, :] + starts[:, None])[:, None, :]
    cos_all, sin_all = jnp.cos(all_angles), jnp.sin(all_angles)

    first, rest, qkv_slots, attn_in, vectors, up_bias_full, cond_low_all, pack_own, down_own = start(
        qkv_weight,
        tokens,
        (attn_gain, mlp_gain, up_bias, down_bias),
        conditioning,
        mod_weight,
        mod_bias,
        jnp.cos(own_angles),
        jnp.sin(own_angles),
        (up_weight, out_weight, down_weight),
        fs,
        n,
    )
    down_full, w_pack = gather(down_own), gather(pack_own)
    x, heads_out, mixed, log_totals = attend(first, rest)
    output, grad_hidden, sums, up_bias_sum, g_down, g_pack, grad_mixed = middle(
        tokens, cotangent[0], vectors, up_bias_full, w_pack, down_full, mixed.reshape(width, tok)
    )
    scatter = lambda a: lax.psum_scatter(a, "fsdp", scatter_dimension=0, tiled=True)
    part_down, part_pack = scatter(g_down), scatter(g_pack)
    grad_slots = attend_back(x, grad_mixed.reshape(heads_out.shape), heads_out, log_totals, cos_all, sin_all)
    inputs_grad, qkv_weight_grad, up_sum, out_sum, down_sum, blocks, mod_weight_grad, cond_grad = reduce_all(
        grad_slots,
        qkv_slots.reshape(slots, width, -1),
        attn_in,
        tokens,
        grad_hidden,
        vectors,
        sums,
        up_bias_sum,
        part_pack,
        part_down,
        mod_weight.T,
        cond_low_all,
        fs,
        n,
    )
    mod_bias_grad, attn_gain_grad, mlp_gain_grad, up_bias_grad, down_bias_grad = blocks
    _, silu_pull = jax.vjp(jax.nn.silu, conditioning)
    conditioning_grad = silu_pull(cond_grad[:1])[0]
    return (
        output[None],
        inputs_grad[None],
        conditioning_grad,
        attn_gain_grad,
        mlp_gain_grad,
        qkv_weight_grad,
        out_sum,
        up_sum,
        up_bias_grad,
        down_sum,
        down_bias_grad,
        mod_weight_grad,
        mod_bias_grad,
    )


def solution(mesh):
    specs = (
        P("fsdp", "seq", None),
        P("fsdp", None),
        P("fsdp", "seq", None),
        P("fsdp"),
        P("fsdp"),
        P("fsdp", None),
        P("fsdp", None),
        P("fsdp", None),
        P("fsdp"),
        P("fsdp", None),
        P("fsdp"),
        P(None, "fsdp"),
        P("fsdp"),
    )
    out_specs = (specs[0], specs[0], specs[1]) + specs[3:]
    return jax.shard_map(per_device, mesh=mesh, in_specs=specs, out_specs=out_specs, check_vma=False)
```

```python
from functools import partial
import math

import jax
import jax.numpy as jnp
from jax import lax
from jax.experimental import pallas as pl
from jax.experimental.pallas import tpu as pltpu
from jax.sharding import PartitionSpec as P

H = 12
HD = 64
EPSILON = 1e-05
BF16 = jnp.bfloat16
F32 = jnp.float32
LOG2E = math.log2(math.e)
VMEM_LIMIT = 60 * 1024 * 1024


def mm(a, b, ca, cb):
    return lax.dot_general(a, b, (((ca,), (cb,)), ((), ())), preferred_element_type=F32)


def normalize(values):
    centre = jnp.mean(values, axis=-1, keepdims=True)
    shifted = values - centre
    variance = jnp.mean(shifted * shifted, axis=-1, keepdims=True)
    inv_std = lax.rsqrt(variance + EPSILON)
    return (shifted * inv_std, inv_std)


def norm_back(grad_hat, normed_hat, inv_std):
    mean_grad = jnp.mean(grad_hat, axis=-1, keepdims=True)
    mean_mixed = jnp.mean(grad_hat * normed_hat, axis=-1, keepdims=True)
    return inv_std * (grad_hat - mean_grad - normed_hat * mean_mixed)


MESH = pl.DeviceIdType.MESH
HIGHEST = lax.Precision.HIGHEST


def add_low(a, b):
    return (a.astype(F32) + b.astype(F32)).astype(BF16)


def remote(src, dst, s, r, **where):
    return pltpu.make_async_remote_copy(
        src_ref=src, dst_ref=dst, send_sem=s, recv_sem=r, device_id=where, device_id_type=MESH
    )


def each(count, body):
    lax.fori_loop(0, count, lambda i, _: (body(i), 0)[1], 0)


def greet(me, z, fs, nz):
    barrier = pltpu.get_barrier_semaphore()

    def hello_fsdp(i):
        peer = {"fsdp": lax.rem(me + 1 + i, fs)}
        pl.semaphore_signal(barrier, inc=1, device_id=peer, device_id_type=MESH)

    def hello_seq(i):
        peer = {"seq": lax.rem(z + 1 + i, nz)}
        pl.semaphore_signal(barrier, inc=1, device_id=peer, device_id_type=MESH)

    each(fs - 1, hello_fsdp)
    each(nz - 1, hello_seq)
    pl.semaphore_wait(barrier, fs + nz - 2)


def forward_kernel(fs, nz, slots, sub, *refs):
    (
        qkv_ref,
        tokens_hbm,
        attn_gain_ref,
        mlp_gain_ref,
        up_bias_ref,
        down_bias_ref,
        cond_ref,
        mod_w_ref,
        mod_b_ref,
        cos_ref,
        sin_ref,
        up_hbm,
        out_hbm,
        down_hbm,
        x_ref,
        o_ref,
        mixed_ref,
        lse_ref,
        w_ref,
        attn_in_ref,
        vec_ref,
        bias_ref,
        cond_out,
        pack_hbm,
        feed_hbm,
    ) = refs[:25]
    (
        tokens_buf,
        up_buf,
        out_buf,
        down_buf,
        w_own,
        z_send,
        narrow,
        spread,
        mod_wide,
        small_send,
        small_all,
        mod_send,
        mod_recv,
        w_full,
        local_s,
        small_s,
        small_r,
        mod_s,
        mod_r,
        w_s,
        w_f,
        w_r,
        pack_own,
        feed_own,
        k_ref,
        x_s,
        x_r,
        o_s,
        o_r,
        p_s,
        p_f,
        p_r,
        own_s,
    ) = refs[25:]
    me = lax.axis_index("fsdp")
    z = lax.axis_index("seq")
    pairs = fs // 2
    k, c = me // 2, lax.rem(me, 2)
    partner = me + 1 - 2 * c
    tok, width = tokens_buf.shape
    shard = w_own.shape[1]
    ff = spread.shape[1]
    block = nz * HD

    fetch = ((tokens_hbm, tokens_buf), (up_hbm, up_buf), (out_hbm, out_buf), (down_hbm, down_buf))
    loads = [pltpu.make_async_copy(src, dst, local_s.at[i]) for i, (src, dst) in enumerate(fetch)]
    for load in loads:
        load.start()
    greet(me, z, fs, nz)

    narrow[...] = jnp.zeros_like(narrow)
    for i, piece in enumerate((attn_gain_ref, mlp_gain_ref, down_bias_ref)):
        narrow[i : i + 1, :shard] = piece[...].reshape(1, -1)
    spread[...] = jnp.zeros_like(spread)
    spread[0:1, : up_bias_ref.shape[0]] = up_bias_ref[...].reshape(1, -1)
    placed = pltpu.roll(narrow[...], me * shard, 1)
    for i in range(3):
        small_send[:, i * width : (i + 1) * width] = placed[i : i + 1]
    placed = pltpu.roll(spread[...], me * up_bias_ref.shape[0], 1)
    small_send[:, 3 * width : 3 * width + ff] = placed[0:1]
    small_send[:, 3 * width + ff :] = cond_ref[...]
    small_all[me] = small_send[...]

    def small_copy(i):
        return remote(small_send, small_all.at[me], small_s.at[i], small_r.at[me], fsdp=lax.rem(me + 1 + i, fs))

    def small_arrival(i):
        peer = lax.rem(me + 1 + i, fs)
        return remote(small_send, small_all.at[peer], small_s.at[i], small_r.at[peer], fsdp=peer)

    each(fs - 1, lambda i: small_copy(i).start())

    for s in range(slots):
        for part in range(3):
            columns = slice(part * width + s * block, part * width + (s + 1) * block)
            w_own[s, :, part * block : (part + 1) * block] = qkv_ref[:, columns].astype(BF16)
        w_ref[s, me] = w_own[s]

    def w_peer(s, i):
        j = lax.rem(k + 1 + i, pairs)
        return remote(w_own.at[s], w_ref.at[s, me], w_s.at[s, i], w_r.at[s, me], fsdp=2 * j + c)

    def w_partner(s):
        return remote(w_own.at[s], w_ref.at[s, me], w_s.at[s, pairs - 1], w_r.at[s, me], fsdp=partner)

    def w_arrival(s, j):
        return remote(w_own.at[s], w_ref.at[s, j], w_s.at[s, 0], w_r.at[s, j], fsdp=partner)

    def w_pass(s, i):
        j = 2 * lax.rem(k + 1 + i, pairs) + c
        return remote(w_ref.at[s, j], w_ref.at[s, j], w_f.at[s, i], w_r.at[s, j], fsdp=partner)

    def send_weight(s):
        each(pairs - 1, lambda i: w_peer(s, i).start())
        w_partner(s).start()

    def pass_weight(s):
        def step(i):
            w_arrival(s, 2 * lax.rem(k + 1 + i, pairs) + c).wait_recv()
            w_pass(s, i).start()

        each(pairs - 1, step)

    send_weight(0)

    each(fs - 1, lambda i: small_arrival(i).wait_recv())
    small_sum = jnp.sum(small_all[:, :, : 3 * width + ff], axis=0)
    cond_all = small_all[:, 0, 3 * width + ff :]
    cond_low = (cond_all / (1.0 + jnp.exp(-cond_all))).astype(BF16)
    cond_out[...] = cond_low.astype(F32)
    own_mod = mm(cond_low, mod_w_ref[...].astype(BF16), 1, 1) + mod_b_ref[...].reshape(1, -1)
    mod_wide[...] = jnp.zeros_like(mod_wide)
    mod_wide[:, : own_mod.shape[1]] = own_mod
    placed = pltpu.roll(mod_wide[...], me * own_mod.shape[1], 1)
    for i in range(fs):
        mod_send[i] = placed[i : i + 1]
    mod_recv[me] = mod_send[me]

    def mod_copy(i):
        peer = lax.rem(me + 1 + i, fs)
        return remote(mod_send.at[peer], mod_recv.at[me], mod_s.at[i], mod_r.at[me], fsdp=peer)

    def mod_arrival(i):
        peer = lax.rem(me + 1 + i, fs)
        return remote(mod_send.at[peer], mod_recv.at[peer], mod_s.at[i], mod_r.at[peer], fsdp=peer)

    each(fs - 1, lambda i: mod_copy(i).start())
    for s in range(1, slots):
        send_weight(s)
    pass_weight(0)

    attn_gain, mlp_gain, down_bias = (small_sum[:, i * width : (i + 1) * width] for i in range(3))
    for i in range(ff // width):
        bias_ref[i] = small_sum[:, (3 + i) * width : (4 + i) * width]
    for load in loads:
        load.wait()
    piece = min(256, tok)
    each(fs - 1, lambda i: mod_arrival(i).wait_recv())
    modulation = jnp.sum(mod_recv[...], axis=0)
    shift_attn, scale_attn, gate_attn, shift_mlp, scale_mlp, gate_mlp = (
        modulation[:, i * width : (i + 1) * width] for i in range(6)
    )
    kept = (gate_attn, shift_mlp, scale_mlp, gate_mlp, mlp_gain, down_bias, attn_gain, scale_attn)
    for i, v in enumerate(kept):
        vec_ref[i : i + 1, :] = v
    for i in range(tok // piece):
        rows = slice(i * piece, (i + 1) * piece)
        hat, _ = normalize(tokens_buf[rows, :])
        attn_in_ref[rows, :] = (hat * attn_gain * (1.0 + scale_attn) + shift_attn).astype(BF16)

    cosine, sine = cos_ref[...], sin_ref[...]
    half = HD // 2

    def project(s, out_ref):
        each(pairs, lambda j: w_arrival(s, 2 * j + 1 - c).wait_recv())
        if shard % 16 == 0:
            weight = w_ref[s].reshape(fs * shard, 3 * block)
        else:
            for i in range(fs):
                w_full[i * shard : (i + 1) * shard, :] = w_ref[s, i].astype(F32)
            weight = w_full[...].astype(BF16)
        rows = mm(weight, attn_in_ref[...], 0, 1).astype(BF16)
        for shard_of in range(nz):
            for part in range(3):
                base = (part * nz + shard_of) * HD
                if part == 2:
                    out_ref[shard_of, part * HD : (part + 1) * HD, :] = rows[base : base + HD]
                else:
                    a = rows[base : base + half].astype(F32)
                    b = rows[base + half : base + HD].astype(F32)
                    out_ref[shard_of, part * HD : part * HD + half, :] = (a * cosine - b * sine).astype(BF16)
                    out_ref[shard_of, part * HD + half : (part + 1) * HD, :] = (b * cosine + a * sine).astype(BF16)

    def x_copy(s, i):
        peer = lax.rem(z + 1 + i, nz)
        return remote(z_send.at[s, peer], x_ref.at[s, z], x_s.at[s, i], x_r.at[s, z], seq=peer)

    def x_arrival(s, i):
        peer = lax.rem(z + 1 + i, nz)
        return remote(z_send.at[s, peer], x_ref.at[s, peer], x_s.at[s, i], x_r.at[s, peer], seq=peer)

    def o_copy(s, i):
        peer = lax.rem(z + 1 + i, nz)
        return remote(o_ref.at[s, peer], mixed_ref.at[s, z], o_s.at[s, i], o_r.at[s, z], seq=peer)

    def o_arrival(s, i):
        peer = lax.rem(z + 1 + i, nz)
        return remote(o_ref.at[s, peer], mixed_ref.at[s, peer], o_s.at[s, i], o_r.at[s, peer], seq=peer)

    def send_slot(s):
        project(s, z_send.at[s])
        each(nz - 1, lambda i: x_copy(s, i).start())
        x_ref[s, z] = z_send[s, z]

    send_slot(0)

    def later(i):
        pass_weight(i + 1)
        send_slot(i + 1)

    each(slots - 1, later)

    pack_own[:, :ff] = up_buf[...].astype(BF16)
    pack_own[:, ff:] = out_buf[...].astype(BF16)
    feed_own[...] = down_buf[...].astype(BF16)
    bulk = ((pack_own, pack_hbm), (feed_own, feed_hbm))

    def p_peer(a, i):
        j = lax.rem(k + 1 + i, pairs)
        own, whole = bulk[a]
        return remote(own, whole.at[me], p_s.at[a, i], p_r.at[a, me], fsdp=2 * j + c)

    def p_partner(a):
        own, whole = bulk[a]
        return remote(own, whole.at[me], p_s.at[a, pairs - 1], p_r.at[a, me], fsdp=partner)

    def p_arrival(a, j):
        own, whole = bulk[a]
        return remote(own, whole.at[j], p_s.at[a, 0], p_r.at[a, j], fsdp=partner)

    def p_pass(a, i):
        j = 2 * lax.rem(k + 1 + i, pairs) + c
        whole = bulk[a][1]
        return remote(whole.at[j], whole.at[j], p_f.at[a, i], p_r.at[a, j], fsdp=partner)

    def p_own(a):
        own, whole = bulk[a]
        return pltpu.make_async_copy(own, whole.at[me], own_s.at[a])

    for a in range(2):
        each(pairs - 1, lambda i: p_peer(a, i).start())
        p_partner(a).start()
        p_own(a).start()

    def pass_bulk(a):
        def step(i):
            p_arrival(a, 2 * lax.rem(k + 1 + i, pairs) + c).wait_recv()
            p_pass(a, i).start()

        each(pairs - 1, step)

    scale = LOG2E / math.sqrt(HD)
    part_width = tok // sub

    def soft(s):
        top = jnp.max(s, axis=0, keepdims=True) * scale
        p = jnp.exp2(s * scale - top)
        total = jnp.sum(p, axis=0, keepdims=True)
        return top, total, p.astype(BF16)

    def slot(s):
        each(nz - 1, lambda i: x_arrival(s, i).wait_recv())
        for shard_of in range(nz):
            k_ref[shard_of * tok : (shard_of + 1) * tok, :] = x_ref[s, shard_of, HD : 2 * HD, :].T

        def one_shard(i):
            step = lax.rem(z + 1 + i, nz)

            def score(j):
                q = x_ref[s, step, 0:HD, j * part_width : (j + 1) * part_width]
                return mm(k_ref[...], q, 1, 0)

            def mix(j, top, total, p):
                o = None
                for shard_of in range(nz):
                    part = mm(x_ref[s, shard_of, 2 * HD : 3 * HD, :], p[shard_of * tok : (shard_of + 1) * tok], 1, 0)
                    o = part if o is None else o + part
                o_ref[s, step, :, j * part_width : (j + 1) * part_width] = (o / total).astype(BF16)
                lse_ref[s, step, :, j * part_width : (j + 1) * part_width] = top + jnp.log2(total)

            scores = [score(0)]
            pending = None
            for j in range(sub):
                if j + 1 < sub:
                    scores.append(score(j + 1))
                done = soft(scores[j])
                if pending is not None:
                    mix(j - 1, *pending)
                pending = done
            mix(sub - 1, *pending)

            @pl.when(i < nz - 1)
            def _():
                o_copy(s, i).start()

        each(nz, one_shard)
        mixed_ref[s, z] = o_ref[s, z]

        @pl.when(s == slots - 2)
        def _():
            pass_bulk(0)

    each(slots, slot)
    pass_bulk(1)

    def drain_slots(s):
        each(nz - 1, lambda i: o_arrival(s, i).wait_recv())
        each(nz - 1, lambda i: o_copy(s, i).wait_send())
        each(nz - 1, lambda i: x_copy(s, i).wait_send())

    each(slots, drain_slots)
    for a in range(2):
        each(pairs, lambda j: p_arrival(a, 2 * j + 1 - c).wait_recv())
        each(pairs - 1, lambda i: p_peer(a, i).wait_send())
        each(pairs - 1, lambda i: p_pass(a, i).wait_send())
        p_partner(a).wait_send()
        p_own(a).wait()

    def drain_peers(i):
        small_copy(i).wait_send()
        mod_copy(i).wait_send()

    def drain_weights(i):
        for s in range(slots):
            w_peer(s, i).wait_send()
            w_pass(s, i).wait_send()

    each(fs - 1, drain_peers)
    each(pairs - 1, drain_weights)
    for s in range(slots):
        w_partner(s).wait_send()


def forward(qkv_weight, tokens, gains, cond, mod_weight, mod_bias, cosine, sine, feed, fs, nz):
    slots = H // nz
    tok, width = tokens.shape
    shard = qkv_weight.shape[0]
    pairs = fs // 2
    up, out, down = feed
    ff = gains[2].shape[0] * fs
    vmem = pl.BlockSpec(memory_space=pltpu.VMEM)
    hbm = pl.BlockSpec(memory_space=pl.ANY)
    low = lambda *shape: pltpu.VMEM(shape, BF16)
    wide = lambda *shape: pltpu.VMEM(shape, F32)
    dma = lambda *shape: pltpu.SemaphoreType.DMA(shape)
    head_shape = (slots, nz, 3 * HD, tok)
    pack_shape = (shard, up.shape[1] + out.shape[1])
    length = nz * tok
    cols = 3 * nz * HD
    small = 3 * width + ff + cond.shape[-1]
    return pl.pallas_call(
        partial(forward_kernel, fs, nz, slots, 2),
        in_specs=[vmem, hbm] + [vmem] * 9 + [hbm] * 3,
        out_specs=[vmem] * 9 + [hbm] * 2,
        out_shape=[
            jax.ShapeDtypeStruct(head_shape, BF16),
            jax.ShapeDtypeStruct((slots, nz, HD, tok), BF16),
            jax.ShapeDtypeStruct((slots, nz, HD, tok), BF16),
            jax.ShapeDtypeStruct((slots, nz, 1, tok), F32),
            jax.ShapeDtypeStruct((slots, fs, shard, cols), BF16),
            jax.ShapeDtypeStruct((tok, width), BF16),
            jax.ShapeDtypeStruct((8, width), F32),
            jax.ShapeDtypeStruct((ff // width, 1, width), F32),
            jax.ShapeDtypeStruct((fs, cond.shape[-1]), F32),
            jax.ShapeDtypeStruct((fs, *pack_shape), BF16),
            jax.ShapeDtypeStruct((fs, *down.shape), BF16),
        ],
        scratch_shapes=[
            wide(tok, width),
            wide(*up.shape),
            wide(*out.shape),
            wide(*down.shape),
            low(slots, shard, cols),
            low(*head_shape),
            wide(8, width),
            wide(8, ff),
            wide(fs, 6 * width),
            wide(1, small),
            wide(fs, 1, small),
            wide(fs, 1, 6 * width),
            wide(fs, 1, 6 * width),
            wide(*((8, 128) if shard % 16 == 0 else (width, cols))),
            dma(4),
            dma(fs - 1),
            dma(fs),
            dma(fs - 1),
            dma(fs),
            dma(slots, pairs),
            dma(slots, pairs),
            dma(slots, fs),
            low(*pack_shape),
            low(*down.shape),
            low(length, HD),
            dma(slots, nz - 1),
            dma(slots, nz),
            dma(slots, nz - 1),
            dma(slots, nz),
            dma(2, pairs),
            dma(2, pairs),
            dma(2, fs),
            dma(2),
        ],
        compiler_params=pltpu.CompilerParams(vmem_limit_bytes=VMEM_LIMIT, collective_id=2, has_side_effects=True),
        cost_estimate=pl.CostEstimate(
            flops=16 * slots * length * length * HD, bytes_accessed=10**7, transcendentals=slots * length * length
        ),
        name="forward",
    )(
        qkv_weight,
        tokens,
        *gains,
        cond,
        mod_weight.T,
        mod_bias,
        cosine,
        sine,
        *feed,
    )


def greet_seq(z, nz):
    barrier = pltpu.get_barrier_semaphore()

    def hello(i):
        peer = {"seq": lax.rem(z + 1 + i, nz)}
        pl.semaphore_signal(barrier, inc=1, device_id=peer, device_id_type=MESH)

    each(nz - 1, hello)
    pl.semaphore_wait(barrier, nz - 1)


def attend_back_kernel(
    n,
    slots,
    tok,
    sub,
    x_ref,
    sent_ref,
    o_ref,
    lse_ref,
    cos_ref,
    sin_ref,
    out_ref,
    g_ref,
    d_ref,
    k_ref,
    v_ref,
    dk_ref,
    dv_ref,
    g_s,
    g_r,
    q_s,
    q_r,
    kv_s,
    kv_r,
):
    z = lax.axis_index("seq")
    half = HD // 2
    greet_seq(z, n)

    def g_copy(s, i):
        peer = lax.rem(z + 1 + i, n)
        return remote(sent_ref.at[s, peer], g_ref.at[s, z], g_s.at[s, i], g_r.at[s, z], seq=peer)

    def g_arrival(s, i):
        peer = lax.rem(z + 1 + i, n)
        return remote(sent_ref.at[s, peer], g_ref.at[s, peer], g_s.at[s, i], g_r.at[s, peer], seq=peer)

    def part_copy(s, i, rows, send, recv, arrival):
        peer = lax.rem(z + 1 + i, n)
        slot = peer if arrival else z
        return remote(
            d_ref.at[s, peer, rows], out_ref.at[s, slot, rows], send.at[s, i], recv.at[s, slot], seq=peer
        )

    q_rows, kv_rows = pl.ds(0, HD), pl.ds(HD, 2 * HD)
    q_copy = lambda s, i, arrival=False: part_copy(s, i, q_rows, q_s, q_r, arrival)
    kv_copy = lambda s, i, arrival=False: part_copy(s, i, kv_rows, kv_s, kv_r, arrival)

    for s in range(slots):
        each(n - 1, lambda i: g_copy(s, i).start())
        g_ref[s, z] = sent_ref[s, z]

    scale = LOG2E / math.sqrt(HD)
    width = tok // sub

    def turn_back(grad, cosine, sine):
        a, b = grad[:half], grad[half:]
        return (a * cosine + b * sine).astype(BF16), (b * cosine - a * sine).astype(BF16)

    def slot(s):
        for c in range(n):
            k_ref[c * tok : (c + 1) * tok, :] = x_ref[s, c, HD : 2 * HD, :].T
            v_ref[c * tok : (c + 1) * tok, :] = x_ref[s, c, 2 * HD : 3 * HD, :].T
        dk_ref[...] = jnp.zeros_like(dk_ref)
        dv_ref[...] = jnp.zeros_like(dv_ref)
        each(n - 1, lambda i: g_arrival(s, i).wait_recv())

        def shard(i):
            step = lax.rem(z + 1 + i, n)
            for j in range(sub):
                cols = slice(j * width, (j + 1) * width)
                q = x_ref[s, step, 0:HD, cols]
                g = g_ref[s, step, :, cols]
                o = o_ref[s, step, :, cols]
                centre = jnp.sum(g.astype(F32) * o.astype(F32), axis=0, keepdims=True)
                score = mm(k_ref[...], q, 1, 0)
                dp = mm(v_ref[...], g, 1, 0)
                p = jnp.exp2(score * scale - lse_ref[s, step, :, cols])
                p_low = p.astype(BF16)
                ds = (p * (dp - centre)).astype(BF16)
                dv_ref[...] += mm(g, p_low, 1, 1)
                dk_ref[...] += mm(q, ds, 1, 1)
                dq = None
                for c in range(n):
                    part = mm(x_ref[s, c, HD : 2 * HD, :], ds[c * tok : (c + 1) * tok], 1, 0)
                    dq = part if dq is None else dq + part
                dq = dq * (1.0 / math.sqrt(HD))
                a, b = turn_back(dq, cos_ref[step, :, cols], sin_ref[step, :, cols])
                d_ref[s, step, 0:half, cols] = a
                d_ref[s, step, half:HD, cols] = b

            @pl.when(i < n - 1)
            def _():
                q_copy(s, i).start()

        each(n, shard)
        for c in range(n):
            dk = dk_ref[:, c * tok : (c + 1) * tok] * (1.0 / math.sqrt(HD))
            a, b = turn_back(dk, cos_ref[c], sin_ref[c])
            d_ref[s, c, HD : HD + half, :] = a
            d_ref[s, c, HD + half : 2 * HD, :] = b
            d_ref[s, c, 2 * HD : 3 * HD, :] = dv_ref[:, c * tok : (c + 1) * tok].astype(BF16)
        each(n - 1, lambda i: kv_copy(s, i).start())
        out_ref[s, z] = d_ref[s, z]

    each(slots, slot)

    def drain(s):
        def one(i):
            q_copy(s, i, True).wait_recv()
            kv_copy(s, i, True).wait_recv()
            g_copy(s, i).wait_send()
            q_copy(s, i).wait_send()
            kv_copy(s, i).wait_send()

        each(n - 1, one)

    each(slots, drain)


def attend_back(x, g, o, lse, cosine, sine):
    slots, n, _, tok = x.shape
    length = n * tok
    vmem = pl.BlockSpec(memory_space=pltpu.VMEM)
    dma = lambda *shape: pltpu.SemaphoreType.DMA(shape)
    return pl.pallas_call(
        partial(attend_back_kernel, n, slots, tok, 2),
        in_specs=[vmem] * 6,
        out_specs=vmem,
        out_shape=jax.ShapeDtypeStruct(x.shape, BF16),
        scratch_shapes=[
            pltpu.VMEM(g.shape, BF16),
            pltpu.VMEM(x.shape, BF16),
            pltpu.VMEM((length, HD), BF16),
            pltpu.VMEM((length, HD), BF16),
            pltpu.VMEM((HD, length), F32),
            pltpu.VMEM((HD, length), F32),
        ]
        + [dma(slots, n - 1), dma(slots, n)] * 3,
        compiler_params=pltpu.CompilerParams(vmem_limit_bytes=VMEM_LIMIT, collective_id=4, has_side_effects=True),
        cost_estimate=pl.CostEstimate(
            flops=40 * slots * length * length * HD, bytes_accessed=10**7, transcendentals=slots * length * length
        ),
        name="attend_back",
    )(x, g, o, lse, cosine, sine)


GELU_C = math.sqrt(2.0 / math.pi)
GELU_A = 0.044715


def middle_kernel(
    blocks,
    tokens_ref,
    cot_ref,
    vec_ref,
    bias_ref,
    up_ref,
    down_ref,
    out_w_ref,
    mixed_ref,
    output_ref,
    grad_hidden_ref,
    sums_ref,
    bias_grad_ref,
    g_down_ref,
    g_pack_ref,
    grad_mixed_ref,
    attn_out_ref,
    mlp_in_ref,
    low_ref,
    back_ref,
):
    j = pl.program_id(0)
    tok, width = tokens_ref.shape
    gate_attn, shift, scale, gate, gain, down_bias = (vec_ref[i : i + 1, :] for i in range(6))
    piece = min(256, tok)
    pieces = tok // piece

    @pl.when(j == 0)
    def _():
        attn_out_ref[...] = mm(mixed_ref[...], out_w_ref[...], 0, 0)

        def prepare(i, _):
            rows = pl.ds(pl.multiple_of(i * piece, piece), piece)
            hidden = tokens_ref[rows, :] + gate_attn * attn_out_ref[rows, :]
            grad_hidden_ref[rows, :] = hidden
            hat, _ = normalize(hidden)
            mlp_in_ref[rows, :] = (hat * gain * (1.0 + scale) + shift).astype(BF16)
            low_ref[rows, :] = (gate * cot_ref[rows, :]).astype(BF16)
            return 0

        lax.fori_loop(0, pieces, prepare, 0)
        output_ref[...] = jnp.zeros_like(output_ref)
        back_ref[...] = jnp.zeros_like(back_ref)

    @pl.when(j < blocks)
    def _():
        mlp_in, low = mlp_in_ref[...], low_ref[...]
        x = mm(mlp_in, up_ref[...], 1, 0) + bias_ref[0]
        grad_act = mm(low, down_ref[...], 1, 1)
        square = x * x
        t = jnp.tanh(x * (GELU_C + GELU_C * GELU_A * square))
        half = 0.5 + 0.5 * t
        act = (x * half).astype(BF16)
        slope = half + x * (0.5 - 0.5 * t * t) * (GELU_C + 3.0 * GELU_C * GELU_A * square)
        grad_pre = grad_act * slope
        bias_grad_ref[0] = jnp.sum(grad_pre, axis=0, keepdims=True)
        pre_low = grad_pre.astype(BF16)
        output_ref[...] += mm(act, down_ref[...], 1, 0)
        back_ref[...] += mm(pre_low, up_ref[...], 1, 1)
        g_down_ref[...] = mm(act, low, 0, 0).astype(BF16)
        g_pack_ref[...] = mm(mlp_in, pre_low, 0, 0).astype(BF16)

    @pl.when(j == blocks)
    def _():
        def finish(i, sums):
            rows = pl.ds(pl.multiple_of(i * piece, piece), piece)
            cot = cot_ref[rows, :]
            branch = output_ref[rows, :] + down_bias
            hidden = grad_hidden_ref[rows, :]
            output_ref[rows, :] = hidden + gate * branch
            hat, inv = normalize(hidden)
            back = back_ref[rows, :]
            grad_hidden = cot + norm_back(back * ((1.0 + scale) * gain), hat, inv)
            grad_hidden_ref[rows, :] = grad_hidden
            low_ref[rows, :] = (gate_attn * grad_hidden).astype(BF16)
            adds = (grad_hidden * attn_out_ref[rows, :], back, back * hat, cot * branch, cot)
            return tuple(a + jnp.sum(v, axis=0, keepdims=True) for a, v in zip(sums, adds))

        zero = jnp.zeros((1, width), F32)
        sums = lax.fori_loop(0, pieces, finish, (zero,) * 5)
        for i in range(5):
            sums_ref[i : i + 1, :] = sums[i]
        attn_low = low_ref[...]
        g_pack_ref[...] = mm(mixed_ref[...], attn_low, 1, 0).astype(BF16)
        grad_mixed_ref[...] = mm(out_w_ref[...], attn_low, 1, 1).astype(BF16)


def middle(tokens, cot, vectors, up_bias, w_pack, w_down, mixed):
    tok, width = tokens.shape
    ff = w_down.shape[0]
    blocks = ff // width
    whole = lambda shape: pl.BlockSpec(shape, lambda j: (0,) * len(shape), pipeline_mode=pl.Buffered(1))
    fixed = lambda shape: pl.BlockSpec(shape, lambda j: (0,) * len(shape))
    last = blocks - 1
    flops = 2 * tok * width * (6 * ff + 3 * width)
    return pl.pallas_call(
        partial(middle_kernel, blocks),
        grid=(blocks + 1,),
        in_specs=[
            whole(tokens.shape),
            whole(cot.shape),
            whole(vectors.shape),
            pl.BlockSpec((1, 1, width), lambda j: (jnp.minimum(j, last), 0, 0)),
            pl.BlockSpec((width, width), lambda j: (0, jnp.minimum(j, last))),
            pl.BlockSpec((width, width), lambda j: (jnp.minimum(j, last), 0)),
            pl.BlockSpec((width, width), lambda j: (0, blocks), pipeline_mode=pl.Buffered(1)),
        ]
        + [whole(mixed.shape)],
        out_specs=[
            fixed((tok, width)),
            fixed((tok, width)),
            fixed((8, width)),
            pl.BlockSpec((1, 1, width), lambda j: (jnp.minimum(j, last), 0, 0)),
            pl.BlockSpec((width, width), lambda j: (jnp.minimum(j, last), 0)),
            pl.BlockSpec((width, width), lambda j: (0, j)),
        ]
        + [fixed(mixed.shape)],
        out_shape=[
            jax.ShapeDtypeStruct((tok, width), F32),
            jax.ShapeDtypeStruct((tok, width), F32),
            jax.ShapeDtypeStruct((8, width), F32),
            jax.ShapeDtypeStruct((blocks, 1, width), F32),
            jax.ShapeDtypeStruct((ff, width), BF16),
            jax.ShapeDtypeStruct((width, ff + width), BF16),
        ]
        + [jax.ShapeDtypeStruct(mixed.shape, BF16)],
        scratch_shapes=[
            pltpu.VMEM((tok, width), F32),
            pltpu.VMEM((tok, width), BF16),
            pltpu.VMEM((tok, width), BF16),
            pltpu.VMEM((tok, width), F32),
        ],
        compiler_params=pltpu.CompilerParams(vmem_limit_bytes=VMEM_LIMIT),
        cost_estimate=pl.CostEstimate(flops=flops, bytes_accessed=6 * ff * width * 2, transcendentals=tok * ff),
        name="middle",
    )(tokens, cot, vectors, up_bias, w_pack, w_down, w_pack, mixed)


def reduce_kernel(fs, nz, slots, counts, lengths, *refs):
    swapped_hbm, w_hbm, attn_in_hbm, tokens_hbm, hidden_hbm, vec_in_ref, sums_ref, up_bias_ref, *refs = refs
    bulk_refs, (mod_t_ref, cond_ref), refs = refs[:2], refs[2:4], refs[4:]
    inputs_out, qkv_out, up_out, out_out, down_out, total_out, mod_w_out, cond_out = refs[:8]
    (
        swapped_ref,
        attn_in_ref,
        swap_s,
        row_buf,
        w_buf,
        tokens_buf,
        hidden_buf,
        g_buf,
        pair_buf,
        sum_buf,
        recv_buf,
        own_buf,
        up_pack,
        up_down,
        up_qkv,
        part_pack,
        part_down,
        part_qkv,
        twin_pack,
        twin_down,
        twin_qkv,
        tot_pack,
        tot_down,
        tot_qkv,
        vec_buf,
        vec_z,
        vec_own,
        vec_all,
        cond_send,
        cond_recv,
        local_s,
        pair_s,
        pair_r,
        peer_s,
        peer_r,
        up_s,
        up_r,
        twin_s,
        twin_r,
        tot_s,
        tot_r,
        vecz_s,
        vecz_r,
        vec_s,
        vec_r,
        cond_s,
        cond_r,
    ) = refs[8:]
    me = lax.axis_index("fsdp")
    z = lax.axis_index("seq")
    pairs = fs // 2
    k, c = me // 2, lax.rem(me, 2)
    partner = me + 1 - 2 * c
    inner = jnp.logical_or(z == nz // 2 - 1, z == nz // 2)
    outer = jnp.logical_not(inner)
    twin = nz - 1 - z
    mate = z + 1 - 2 * lax.rem(z, 2)
    tok, width = tokens_buf.shape
    shard = g_buf.shape[3]
    groups = width // 128

    def swap_load(s):
        return pltpu.make_async_copy(swapped_hbm.at[s], swapped_ref.at[s], swap_s.at[s])

    first_load = pltpu.make_async_copy(attn_in_hbm, attn_in_ref, local_s.at[3])
    first_load.start()
    for s in range(slots):
        swap_load(s).start()
    fetch = ((w_hbm, w_buf), (tokens_hbm, tokens_buf), (hidden_hbm, hidden_buf))
    loads = [pltpu.make_async_copy(src, dst, local_s.at[i]) for i, (src, dst) in enumerate(fetch)]
    for load in loads:
        load.start()
    greet(me, z, fs, nz)

    bulk = [
        (src, up, part, other, tot, i)
        for src, up, part, other, tot, count in (
            (bulk_refs[0], up_pack, part_pack, twin_pack, tot_pack, counts[0]),
            (bulk_refs[1], up_down, part_down, twin_down, tot_down, counts[1]),
        )
        for i in range(count)
    ]
    last = [(own_buf, up_qkv, part_qkv, twin_qkv, tot_qkv, s) for s in range(slots)]
    chain = list(enumerate(bulk + last))
    early, late = chain[: len(bulk)], chain[len(bulk) :]

    def up_copy(n, item):
        src, up, _, _, _, i = item
        return remote(src.at[i], up.at[i], up_s.at[n], up_r.at[n], seq=mate)

    def twin_copy(n, item):
        _, _, part, other, _, i = item
        return remote(part.at[i], other.at[i], twin_s.at[n], twin_r.at[n], seq=twin)

    def tot_copy(n, item):
        tot, i = item[4], item[5]
        return remote(tot.at[i], tot.at[i], tot_s.at[n], tot_r.at[n], seq=mate)

    def chain_in(n, item):
        src, up, part, _, _, i = item
        up_copy(n, item).wait_recv()
        part[i] = add_low(src[i], up[i])
        twin_copy(n, item).start()

    def chain_out(n, item):
        _, _, part, other, tot, i = item
        twin_copy(n, item).wait_recv()
        tot[i] = add_low(part[i], other[i])
        tot_copy(n, item).start()

    def plan(items):
        steps = [(chain_in, items[0])]
        for before, item in zip(items[:-1], items[1:]):
            steps += [(chain_in, item), (chain_out, before)]
        return steps + [(chain_out, items[-1])]

    steps = plan(early)

    def advance(count):
        todo = [steps.pop(0) for _ in range(min(count, len(steps)))]
        if todo:

            @pl.when(inner)
            def _():
                for step, (n, item) in todo:
                    step(n, item)

    @pl.when(outer)
    def _():
        for n, item in early:
            up_copy(n, item).start()

    def pair_copy(s, j):
        return remote(g_buf.at[s, j, 1 - c], pair_buf.at[s, j], pair_s.at[s, j], pair_r.at[s, j], fsdp=partner)

    def peer_copy(s, j):
        return remote(sum_buf.at[s, j], recv_buf.at[s, k], peer_s.at[s, j], peer_r.at[s, k], fsdp=2 * j + c)

    def peer_arrival(s, j):
        return remote(sum_buf.at[s, j], recv_buf.at[s, j], peer_s.at[s, j], peer_r.at[s, j], fsdp=2 * j + c)

    first_load.wait()

    def project_grad(s):
        swap_load(s).wait()
        for head in range(nz):
            for p in range(3):
                base = (p * nz + head) * HD
                row_buf[s, base : base + HD, :] = swapped_ref[s, head, p * HD : (p + 1) * HD, :]
        grad = mm(attn_in_ref[...], row_buf[s], 0, 1).astype(BF16)
        for i in range(fs):
            g_buf[s, i // 2, i % 2] = grad[i * shard : (i + 1) * shard]
        each(pairs, lambda i: pair_copy(s, lax.rem(k + 1 + i, pairs)).start())


    def forward(s, i):
        j = lax.rem(k + 1 + i, pairs)
        pair_copy(s, j).wait_recv()
        sum_buf[s, j] = add_low(g_buf[s, j, c], pair_buf[s, j])
        peer_copy(s, j).start()

    def stage(s):
        @pl.when(s < slots)
        def _():
            project_grad(s)

        @pl.when(s > 0)
        def _():
            each(pairs - 1, lambda i: forward(s - 1, i))

    each(slots + 1, stage)
    advance(1)
    for load in loads:
        load.wait()

    scale_mlp, gate_mlp, mlp_gain = (vec_in_ref[i : i + 1, :] for i in (2, 3, 4))
    attn_gain, scale_attn = (vec_in_ref[i : i + 1, :] for i in (6, 7))
    piece = min(256, tok)

    def norm_piece(i, kept):
        back_sum, hat_sum = kept
        rows = pl.ds(pl.multiple_of(i * piece, piece), piece)
        grad = None
        for s in range(slots):
            part = mm(row_buf[s, :, rows], w_buf[s], 0, 1)
            grad = part if grad is None else grad + part
        hat, inv = normalize(tokens_buf[rows, :])
        scaled = grad * ((1.0 + scale_attn) * attn_gain)
        inputs_out[rows, :] = hidden_buf[rows, :] + norm_back(scaled, hat, inv)
        back_sum = back_sum + jnp.sum(grad, axis=0, keepdims=True)
        hat_sum = hat_sum + jnp.sum(grad * hat, axis=0, keepdims=True)
        return back_sum, hat_sum

    zero = jnp.zeros((1, width), F32)
    back_sum, hat_sum = lax.fori_loop(0, tok // piece, norm_piece, (zero, zero))

    sums = [sums_ref[i : i + 1, :] for i in range(5)]
    vectors = [back_sum, hat_sum * attn_gain, sums[0], sums[1], sums[2] * mlp_gain, sums[3]]
    vectors += [hat_sum * (1.0 + scale_attn), sums[2] * (1.0 + scale_mlp)]
    vectors += [up_bias_ref[i] for i in range(up_bias_ref.shape[0])]
    vectors.append(sums[4] * gate_mlp)
    for p, v in enumerate(vectors):
        for i in range(groups):
            vec_buf[p * groups + i : p * groups + i + 1, :] = v[:, i * 128 : (i + 1) * 128]
    used = len(vectors) * groups
    vec_buf[used:, :] = jnp.zeros((vec_buf.shape[0] - used, 128), F32)
    vec_z[z] = vec_buf[...]

    def vecz_copy(i):
        return remote(vec_buf, vec_z.at[z], vecz_s.at[i], vecz_r.at[z], seq=lax.rem(z + 1 + i, nz))

    def vecz_arrival(i):
        peer = lax.rem(z + 1 + i, nz)
        return remote(vec_buf, vec_z.at[peer], vecz_s.at[i], vecz_r.at[peer], seq=peer)

    each(nz - 1, lambda i: vecz_copy(i).start())

    advance(len(steps))
    for s in range(slots):
        pair_copy(s, k).wait_recv()
        own = g_buf[s, k, c].astype(F32) + pair_buf[s, k].astype(F32)

        def gather_in(i, acc):
            j = lax.rem(k + 1 + i, pairs)
            peer_arrival(s, j).wait_recv()
            return acc + recv_buf[s, j].astype(F32)

        own_buf[s] = lax.fori_loop(0, pairs - 1, gather_in, own).astype(BF16)

        @pl.when(outer)
        def _():
            up_copy(*late[s]).start()

    steps.extend(plan(late))
    each(nz - 1, lambda i: vecz_arrival(i).wait_recv())
    summed = vec_z[0]
    for i in range(1, nz):
        summed = summed + vec_z[i]
    vec_own[...] = summed
    vec_all[me] = summed

    def vec_copy(i):
        return remote(vec_own, vec_all.at[me], vec_s.at[i], vec_r.at[me], fsdp=lax.rem(me + 1 + i, fs))

    def vec_arrival(i):
        peer = lax.rem(me + 1 + i, fs)
        return remote(vec_own, vec_all.at[peer], vec_s.at[i], vec_r.at[peer], fsdp=peer)

    each(fs - 1, lambda i: vec_copy(i).start())
    advance(3)

    each(fs - 1, lambda i: vec_arrival(i).wait_recv())
    lane_from = lax.broadcasted_iota(jnp.int32, (256, 128), 0)
    lane_to = lax.broadcasted_iota(jnp.int32, (256, 128), 1)
    part, first, place = None, 0, 0
    for which, length in enumerate(lengths):
        block = length // fs
        for i in range(-(-block // 128)):
            offset = me * block + 128 * i
            row = first + offset // 128
            select = (lane_from == lane_to + lax.rem(offset, 128)).astype(F32)
            both = jnp.concatenate([vec_all[:, pl.ds(row, 1), :][:, 0], vec_all[:, pl.ds(row + 1, 1), :][:, 0]], axis=1)
            rows = lax.dot_general(
                both, select, (((1,), (0,)), ((), ())), precision=HIGHEST, preferred_element_type=F32
            )
            total_out[place : place + 1, :] = jnp.sum(rows, axis=0, keepdims=True)
            place += 1
            if which > 0:
                continue
            wide = min(128, block - i * 128)
            columns = slice(i * 128, i * 128 + wide)
            mod_rows = mod_t_ref[columns, :].astype(BF16).astype(F32)
            share = lax.dot_general(
                rows[:, :wide], mod_rows, (((1,), (0,)), ((), ())), precision=HIGHEST, preferred_element_type=F32
            )
            part = share if part is None else part + share
            outer_product = lax.dot_general(
                rows, cond_ref[...], (((0,), (0,)), ((), ())), precision=HIGHEST, preferred_element_type=F32
            )
            mod_w_out[columns, :] = outer_product[:wide]
        first += length // 128
    cond_send[...] = jnp.broadcast_to(part[:, None, :], cond_send.shape)

    def cond_copy(i):
        peer = lax.rem(me + 1 + i, fs)
        return remote(cond_send.at[peer], cond_recv.at[me], cond_s.at[i], cond_r.at[me], fsdp=peer)

    def cond_arrival(i):
        peer = lax.rem(me + 1 + i, fs)
        return remote(cond_send.at[peer], cond_recv.at[peer], cond_s.at[i], cond_r.at[peer], fsdp=peer)

    each(fs - 1, lambda i: cond_copy(i).start())
    advance(len(steps))
    cond_recv[me] = cond_send[me]
    each(fs - 1, lambda i: cond_arrival(i).wait_recv())
    cond_out[...] = jnp.sum(cond_recv[...], axis=0)

    @pl.when(outer)
    def _():
        for n, item in chain:
            tot_copy(n, item).wait_recv()
            up_copy(n, item).wait_send()

    block = nz * HD
    ff = up_out.shape[1]

    def write_pack(i):
        rows = pl.ds(i * tot_pack.shape[1], tot_pack.shape[1])
        up_out[rows, :] = tot_pack[i, :, :ff].astype(F32)
        out_out[rows, :] = tot_pack[i, :, ff:].astype(F32)

    def write_down(i):
        down_out[pl.ds(i * tot_down.shape[1], tot_down.shape[1]), :] = tot_down[i].astype(F32)

    each(counts[0], write_pack)
    each(counts[1], write_down)
    for s in range(slots):
        for p in range(3):
            columns = slice(p * width + s * block, p * width + (s + 1) * block)
            qkv_out[:, columns] = tot_qkv[s, :, p * block : (p + 1) * block].astype(F32)

    @pl.when(inner)
    def _():
        for n, item in chain:
            twin_copy(n, item).wait_send()
            tot_copy(n, item).wait_send()

    def drain_peers(i):
        vec_copy(i).wait_send()
        cond_copy(i).wait_send()

    def drain_pairs(i):
        for s in range(slots):
            pair_copy(s, i).wait_send()

    def drain_sums(i):
        for s in range(slots):
            peer_copy(s, lax.rem(k + 1 + i, pairs)).wait_send()

    each(fs - 1, drain_peers)
    each(pairs, drain_pairs)
    each(pairs - 1, drain_sums)
    each(nz - 1, lambda i: vecz_copy(i).wait_send())


def reduce_all(
    grad_rows, weights, attn_in, tokens, grad_hidden, vectors, sums, up_bias_sum, part_pack, part_down, mod_t, cond, fs, nz
):
    slots = grad_rows.shape[0]
    tok, width = tokens.shape
    shard = width // fs
    count = lambda a: 3 if a.shape[0] % 48 == 0 else 1
    counts = (count(part_pack), count(part_down))
    split = lambda a, n: a.reshape(n, a.shape[0] // n, a.shape[1])
    pack, down = split(part_pack, counts[0]), split(part_down, counts[1])
    pairs = fs // 2
    items = sum(counts) + slots
    ff = up_bias_sum.size
    lengths = (6 * width, width, width, ff, width)
    rows = sum(lengths) // 128 + 2
    places = sum(-(-v // fs // 128) for v in lengths)
    vmem = pl.BlockSpec(memory_space=pltpu.VMEM)
    hbm = pl.BlockSpec(memory_space=pl.ANY)
    low = lambda *shape: pltpu.VMEM(shape, BF16)
    wide = lambda *shape: pltpu.VMEM(shape, F32)
    dma = lambda *shape: pltpu.SemaphoreType.DMA(shape)
    qkv_shape = (slots, shard, width)
    triple = [low(*pack.shape), low(*down.shape), low(*qkv_shape)]
    cols = grad_rows.shape[1] * grad_rows.shape[2]
    inputs_grad, qkv_sum, up_sum, out_sum, down_sum, total, mod_w, cond_grad = pl.pallas_call(
        partial(reduce_kernel, fs, nz, slots, counts, lengths),
        in_specs=[hbm] * 5 + [vmem] * 7,
        out_specs=[vmem] * 8,
        out_shape=[
            jax.ShapeDtypeStruct((tok, width), F32),
            jax.ShapeDtypeStruct((shard, 3 * width), F32),
            jax.ShapeDtypeStruct((shard, ff), F32),
            jax.ShapeDtypeStruct((shard, part_pack.shape[1] - ff), F32),
            jax.ShapeDtypeStruct(part_down.shape, F32),
            jax.ShapeDtypeStruct((places, 128), F32),
            jax.ShapeDtypeStruct(mod_t.shape, F32),
            jax.ShapeDtypeStruct((8, 128), F32),
        ],
        scratch_shapes=[
            low(*grad_rows.shape),
            low(tok, width),
            dma(slots),
            low(slots, cols, tok),
            low(slots, width, cols),
            wide(tok, width),
            wide(tok, width),
            low(slots, pairs, 2, shard, width),
            low(slots, pairs, shard, width),
            low(slots, pairs, shard, width),
            low(slots, pairs, shard, width),
            low(*qkv_shape),
        ]
        + triple * 4
        + [
            wide(rows, 128),
            wide(nz, rows, 128),
            wide(rows, 128),
            wide(fs, rows, 128),
            wide(fs, 8, 128),
            wide(fs, 8, 128),
            dma(4),
            dma(slots, pairs),
            dma(slots, pairs),
            dma(slots, pairs),
            dma(slots, pairs),
        ]
        + [dma(items)] * 6
        + [dma(nz - 1), dma(nz), dma(fs - 1), dma(fs), dma(fs - 1), dma(fs)],
        compiler_params=pltpu.CompilerParams(vmem_limit_bytes=VMEM_LIMIT, collective_id=1, has_side_effects=True),
        cost_estimate=pl.CostEstimate(flops=12 * tok * width * cols, bytes_accessed=10**8, transcendentals=0),
        name="reduce_all",
    )(grad_rows, weights, attn_in, tokens, grad_hidden, vectors, sums, up_bias_sum, pack, down, mod_t, cond)
    blocks, place = [], 0
    for v in lengths:
        n = -(-v // fs // 128)
        blocks.append(total[place : place + n].reshape(-1)[: v // fs])
        place += n
    return inputs_grad, qkv_sum, up_sum, out_sum, down_sum, blocks, mod_w.T, cond_grad


def per_device(
    inputs,
    conditioning,
    cotangent,
    attn_gain,
    mlp_gain,
    qkv_weight,
    out_weight,
    up_weight,
    up_bias,
    down_weight,
    down_bias,
    mod_weight,
    mod_bias,
):
    n = lax.axis_size("seq")
    fs = lax.axis_size("fsdp")
    z = lax.axis_index("seq")
    tokens = inputs[0]
    tok, width = tokens.shape
    slots = H // n

    inv_freq = jnp.exp(-math.log(10000.0) * jnp.arange(HD // 2, dtype=F32) * (2.0 / HD))
    positions = jnp.arange(tok, dtype=F32)
    own_angles = inv_freq[:, None] * (positions + (z * tok).astype(F32))[None, :]
    starts = (jnp.arange(n) * tok).astype(F32)
    all_angles = inv_freq[None, :, None] * (positions[None, :] + starts[:, None])[:, None, :]
    cos_all, sin_all = jnp.cos(all_angles), jnp.sin(all_angles)

    x, heads_out, mixed, log_totals, qkv_slots, attn_in, vectors, up_bias_full, cond_low_all, pack, down = forward(
        qkv_weight,
        tokens,
        (attn_gain, mlp_gain, up_bias, down_bias),
        conditioning,
        mod_weight,
        mod_bias,
        jnp.cos(own_angles),
        jnp.sin(own_angles),
        (up_weight, out_weight, down_weight),
        fs,
        n,
    )
    w_pack, down_full = pack.reshape(width, -1), down.reshape(-1, width)
    output, grad_hidden, sums, up_bias_sum, g_down, g_pack, grad_mixed = middle(
        tokens, cotangent[0], vectors, up_bias_full, w_pack, down_full, mixed.reshape(width, tok)
    )
    scatter = lambda a: lax.psum_scatter(a, "fsdp", scatter_dimension=0, tiled=True)
    part_down, part_pack = scatter(g_down), scatter(g_pack)
    grad_slots = attend_back(x, grad_mixed.reshape(heads_out.shape), heads_out, log_totals, cos_all, sin_all)
    inputs_grad, qkv_weight_grad, up_sum, out_sum, down_sum, blocks, mod_weight_grad, cond_grad = reduce_all(
        grad_slots,
        qkv_slots.reshape(slots, width, -1),
        attn_in,
        tokens,
        grad_hidden,
        vectors,
        sums,
        up_bias_sum,
        part_pack,
        part_down,
        mod_weight.T,
        cond_low_all,
        fs,
        n,
    )
    mod_bias_grad, attn_gain_grad, mlp_gain_grad, up_bias_grad, down_bias_grad = blocks
    _, silu_pull = jax.vjp(jax.nn.silu, conditioning)
    conditioning_grad = silu_pull(cond_grad[:1])[0]
    return (
        output[None],
        inputs_grad[None],
        conditioning_grad,
        attn_gain_grad,
        mlp_gain_grad,
        qkv_weight_grad,
        out_sum,
        up_sum,
        up_bias_grad,
        down_sum,
        down_bias_grad,
        mod_weight_grad,
        mod_bias_grad,
    )


def solution(mesh):
    specs = (
        P("fsdp", "seq", None),
        P("fsdp", None),
        P("fsdp", "seq", None),
        P("fsdp"),
        P("fsdp"),
        P("fsdp", None),
        P("fsdp", None),
        P("fsdp", None),
        P("fsdp"),
        P("fsdp", None),
        P("fsdp"),
        P(None, "fsdp"),
        P("fsdp"),
    )
    out_specs = (specs[0], specs[0], specs[1]) + specs[3:]
    return jax.shard_map(per_device, mesh=mesh, in_specs=specs, out_specs=out_specs, check_vma=False)
```

```python
from functools import partial
import math

import jax
import jax.numpy as jnp
from jax import lax
from jax.experimental import pallas as pl
from jax.experimental.pallas import tpu as pltpu
from jax.sharding import PartitionSpec as P

H = 12
HD = 64
EPSILON = 1e-05
BF16 = jnp.bfloat16
F32 = jnp.float32
LOG2E = math.log2(math.e)
VMEM_LIMIT = 60 * 1024 * 1024


def mm(a, b, ca, cb):
    return lax.dot_general(a, b, (((ca,), (cb,)), ((), ())), preferred_element_type=F32)


def normalize(values):
    centre = jnp.mean(values, axis=-1, keepdims=True)
    shifted = values - centre
    variance = jnp.mean(shifted * shifted, axis=-1, keepdims=True)
    inv_std = lax.rsqrt(variance + EPSILON)
    return (shifted * inv_std, inv_std)


def norm_back(grad_hat, normed_hat, inv_std):
    mean_grad = jnp.mean(grad_hat, axis=-1, keepdims=True)
    mean_mixed = jnp.mean(grad_hat * normed_hat, axis=-1, keepdims=True)
    return inv_std * (grad_hat - mean_grad - normed_hat * mean_mixed)


MESH = pl.DeviceIdType.MESH
HIGHEST = lax.Precision.HIGHEST


def add_low(a, b):
    return (a.astype(F32) + b.astype(F32)).astype(BF16)


def remote(src, dst, s, r, **where):
    return pltpu.make_async_remote_copy(
        src_ref=src, dst_ref=dst, send_sem=s, recv_sem=r, device_id=where, device_id_type=MESH
    )


def each(count, body):
    lax.fori_loop(0, count, lambda i, _: (body(i), 0)[1], 0)


def greet(me, z, fs, nz):
    barrier = pltpu.get_barrier_semaphore()

    def hello_fsdp(i):
        peer = {"fsdp": lax.rem(me + 1 + i, fs)}
        pl.semaphore_signal(barrier, inc=1, device_id=peer, device_id_type=MESH)

    def hello_seq(i):
        peer = {"seq": lax.rem(z + 1 + i, nz)}
        pl.semaphore_signal(barrier, inc=1, device_id=peer, device_id_type=MESH)

    each(fs - 1, hello_fsdp)
    each(nz - 1, hello_seq)
    pl.semaphore_wait(barrier, fs + nz - 2)


def forward_kernel(fs, nz, slots, sub, *refs):
    (
        qkv_ref,
        tokens_hbm,
        attn_gain_ref,
        mlp_gain_ref,
        up_bias_ref,
        down_bias_ref,
        cond_ref,
        mod_w_ref,
        mod_b_ref,
        cos_ref,
        sin_ref,
        up_hbm,
        out_hbm,
        down_hbm,
        x_ref,
        o_ref,
        mixed_ref,
        lse_ref,
        w_ref,
        attn_in_ref,
        vec_ref,
        bias_ref,
        cond_out,
        pack_hbm,
        feed_hbm,
    ) = refs[:25]
    (
        tokens_buf,
        up_buf,
        out_buf,
        down_buf,
        w_own,
        z_send,
        narrow,
        spread,
        mod_wide,
        small_send,
        small_all,
        mod_send,
        mod_recv,
        w_full,
        local_s,
        small_s,
        small_r,
        mod_s,
        mod_r,
        w_s,
        w_f,
        w_r,
        pack_own,
        feed_own,
        k_ref,
        x_s,
        x_r,
        o_s,
        o_r,
        p_s,
        p_f,
        p_r,
        own_s,
    ) = refs[25:]
    me = lax.axis_index("fsdp")
    z = lax.axis_index("seq")
    pairs = fs // 2
    k, c = me // 2, lax.rem(me, 2)
    partner = me + 1 - 2 * c
    tok, width = tokens_buf.shape
    shard = w_own.shape[1]
    ff = spread.shape[1]
    block = nz * HD

    fetch = ((tokens_hbm, tokens_buf), (up_hbm, up_buf), (out_hbm, out_buf), (down_hbm, down_buf))
    loads = [pltpu.make_async_copy(src, dst, local_s.at[i]) for i, (src, dst) in enumerate(fetch)]
    for load in loads:
        load.start()
    greet(me, z, fs, nz)

    narrow[...] = jnp.zeros_like(narrow)
    for i, piece in enumerate((attn_gain_ref, mlp_gain_ref, down_bias_ref)):
        narrow[i : i + 1, :shard] = piece[...].reshape(1, -1)
    spread[...] = jnp.zeros_like(spread)
    spread[0:1, : up_bias_ref.shape[0]] = up_bias_ref[...].reshape(1, -1)
    placed = pltpu.roll(narrow[...], me * shard, 1)
    for i in range(3):
        small_send[:, i * width : (i + 1) * width] = placed[i : i + 1]
    placed = pltpu.roll(spread[...], me * up_bias_ref.shape[0], 1)
    small_send[:, 3 * width : 3 * width + ff] = placed[0:1]
    small_send[:, 3 * width + ff :] = cond_ref[...]
    small_all[me] = small_send[...]

    def small_copy(i):
        return remote(small_send, small_all.at[me], small_s.at[i], small_r.at[me], fsdp=lax.rem(me + 1 + i, fs))

    def small_arrival(i):
        peer = lax.rem(me + 1 + i, fs)
        return remote(small_send, small_all.at[peer], small_s.at[i], small_r.at[peer], fsdp=peer)

    each(fs - 1, lambda i: small_copy(i).start())

    for s in range(slots):
        for part in range(3):
            columns = slice(part * width + s * block, part * width + (s + 1) * block)
            w_own[s, :, part * block : (part + 1) * block] = qkv_ref[:, columns].astype(BF16)
        w_ref[s, me] = w_own[s]

    def w_peer(s, i):
        j = lax.rem(k + 1 + i, pairs)
        return remote(w_own.at[s], w_ref.at[s, me], w_s.at[s, i], w_r.at[s, me], fsdp=2 * j + c)

    def w_partner(s):
        return remote(w_own.at[s], w_ref.at[s, me], w_s.at[s, pairs - 1], w_r.at[s, me], fsdp=partner)

    def w_arrival(s, j):
        return remote(w_own.at[s], w_ref.at[s, j], w_s.at[s, 0], w_r.at[s, j], fsdp=partner)

    def w_pass(s, i):
        j = 2 * lax.rem(k + 1 + i, pairs) + c
        return remote(w_ref.at[s, j], w_ref.at[s, j], w_f.at[s, i], w_r.at[s, j], fsdp=partner)

    def send_weight(s):
        each(pairs - 1, lambda i: w_peer(s, i).start())
        w_partner(s).start()

    def pass_weight(s):
        def step(i):
            w_arrival(s, 2 * lax.rem(k + 1 + i, pairs) + c).wait_recv()
            w_pass(s, i).start()

        each(pairs - 1, step)

    send_weight(0)

    each(fs - 1, lambda i: small_arrival(i).wait_recv())
    small_sum = jnp.sum(small_all[:, :, : 3 * width + ff], axis=0)
    cond_all = small_all[:, 0, 3 * width + ff :]
    cond_low = (cond_all / (1.0 + jnp.exp(-cond_all))).astype(BF16)
    cond_out[...] = cond_low.astype(F32)
    own_mod = mm(cond_low, mod_w_ref[...].astype(BF16), 1, 1) + mod_b_ref[...].reshape(1, -1)
    mod_wide[...] = jnp.zeros_like(mod_wide)
    mod_wide[:, : own_mod.shape[1]] = own_mod
    placed = pltpu.roll(mod_wide[...], me * own_mod.shape[1], 1)
    for i in range(fs):
        mod_send[i] = placed[i : i + 1]
    mod_recv[me] = mod_send[me]

    def mod_copy(i):
        peer = lax.rem(me + 1 + i, fs)
        return remote(mod_send.at[peer], mod_recv.at[me], mod_s.at[i], mod_r.at[me], fsdp=peer)

    def mod_arrival(i):
        peer = lax.rem(me + 1 + i, fs)
        return remote(mod_send.at[peer], mod_recv.at[peer], mod_s.at[i], mod_r.at[peer], fsdp=peer)

    each(fs - 1, lambda i: mod_copy(i).start())
    for s in range(1, slots):
        send_weight(s)
    pass_weight(0)

    attn_gain, mlp_gain, down_bias = (small_sum[:, i * width : (i + 1) * width] for i in range(3))
    for i in range(ff // width):
        bias_ref[i] = small_sum[:, (3 + i) * width : (4 + i) * width]
    for load in loads:
        load.wait()
    piece = min(256, tok)
    each(fs - 1, lambda i: mod_arrival(i).wait_recv())
    modulation = jnp.sum(mod_recv[...], axis=0)
    shift_attn, scale_attn, gate_attn, shift_mlp, scale_mlp, gate_mlp = (
        modulation[:, i * width : (i + 1) * width] for i in range(6)
    )
    kept = (gate_attn, shift_mlp, scale_mlp, gate_mlp, mlp_gain, down_bias, attn_gain, scale_attn)
    for i, v in enumerate(kept):
        vec_ref[i : i + 1, :] = v
    for i in range(tok // piece):
        rows = slice(i * piece, (i + 1) * piece)
        hat, _ = normalize(tokens_buf[rows, :])
        attn_in_ref[rows, :] = (hat * attn_gain * (1.0 + scale_attn) + shift_attn).astype(BF16)

    cosine, sine = cos_ref[...], sin_ref[...]
    half = HD // 2

    def project(s, out_ref):
        each(pairs, lambda j: w_arrival(s, 2 * j + 1 - c).wait_recv())
        if shard % 16 == 0:
            weight = w_ref[s].reshape(fs * shard, 3 * block)
        else:
            for i in range(fs):
                w_full[i * shard : (i + 1) * shard, :] = w_ref[s, i].astype(F32)
            weight = w_full[...].astype(BF16)
        rows = mm(weight, attn_in_ref[...], 0, 1).astype(BF16)
        for shard_of in range(nz):
            for part in range(3):
                base = (part * nz + shard_of) * HD
                if part == 2:
                    out_ref[shard_of, part * HD : (part + 1) * HD, :] = rows[base : base + HD]
                else:
                    a = rows[base : base + half].astype(F32)
                    b = rows[base + half : base + HD].astype(F32)
                    out_ref[shard_of, part * HD : part * HD + half, :] = (a * cosine - b * sine).astype(BF16)
                    out_ref[shard_of, part * HD + half : (part + 1) * HD, :] = (b * cosine + a * sine).astype(BF16)

    def x_copy(s, i):
        peer = lax.rem(z + 1 + i, nz)
        return remote(z_send.at[s, peer], x_ref.at[s, z], x_s.at[s, i], x_r.at[s, z], seq=peer)

    def x_arrival(s, i):
        peer = lax.rem(z + 1 + i, nz)
        return remote(z_send.at[s, peer], x_ref.at[s, peer], x_s.at[s, i], x_r.at[s, peer], seq=peer)

    def o_copy(s, i):
        peer = lax.rem(z + 1 + i, nz)
        return remote(o_ref.at[s, peer], mixed_ref.at[s, z], o_s.at[s, i], o_r.at[s, z], seq=peer)

    def o_arrival(s, i):
        peer = lax.rem(z + 1 + i, nz)
        return remote(o_ref.at[s, peer], mixed_ref.at[s, peer], o_s.at[s, i], o_r.at[s, peer], seq=peer)

    def send_slot(s):
        project(s, z_send.at[s])
        each(nz - 1, lambda i: x_copy(s, i).start())
        x_ref[s, z] = z_send[s, z]

    def next_slot(s):
        @pl.when(s > 0)
        def _():
            pass_weight(s)

        send_slot(s)

    each(slots, next_slot)

    pack_own[:, :ff] = up_buf[...].astype(BF16)
    pack_own[:, ff:] = out_buf[...].astype(BF16)
    feed_own[...] = down_buf[...].astype(BF16)
    bulk = ((pack_own, pack_hbm), (feed_own, feed_hbm))

    def p_peer(a, i):
        j = lax.rem(k + 1 + i, pairs)
        own, whole = bulk[a]
        return remote(own, whole.at[me], p_s.at[a, i], p_r.at[a, me], fsdp=2 * j + c)

    def p_partner(a):
        own, whole = bulk[a]
        return remote(own, whole.at[me], p_s.at[a, pairs - 1], p_r.at[a, me], fsdp=partner)

    def p_arrival(a, j):
        own, whole = bulk[a]
        return remote(own, whole.at[j], p_s.at[a, 0], p_r.at[a, j], fsdp=partner)

    def p_pass(a, i):
        j = 2 * lax.rem(k + 1 + i, pairs) + c
        whole = bulk[a][1]
        return remote(whole.at[j], whole.at[j], p_f.at[a, i], p_r.at[a, j], fsdp=partner)

    def p_own(a):
        own, whole = bulk[a]
        return pltpu.make_async_copy(own, whole.at[me], own_s.at[a])

    for a in range(2):
        each(pairs - 1, lambda i: p_peer(a, i).start())
        p_partner(a).start()
        p_own(a).start()

    def pass_bulk(a):
        def step(i):
            p_arrival(a, 2 * lax.rem(k + 1 + i, pairs) + c).wait_recv()
            p_pass(a, i).start()

        each(pairs - 1, step)

    scale = LOG2E / math.sqrt(HD)
    part_width = tok // sub

    def soft(s):
        top = jnp.max(s, axis=0, keepdims=True) * scale
        p = jnp.exp2(s * scale - top)
        total = jnp.sum(p, axis=0, keepdims=True)
        return top, total, p.astype(BF16)

    def slot(s):
        each(nz - 1, lambda i: x_arrival(s, i).wait_recv())
        for shard_of in range(nz):
            k_ref[shard_of * tok : (shard_of + 1) * tok, :] = x_ref[s, shard_of, HD : 2 * HD, :].T

        def one_shard(i):
            step = lax.rem(z + 1 + i, nz)

            def score(j):
                q = x_ref[s, step, 0:HD, j * part_width : (j + 1) * part_width]
                return mm(k_ref[...], q, 1, 0)

            def mix(j, top, total, p):
                o = None
                for shard_of in range(nz):
                    part = mm(x_ref[s, shard_of, 2 * HD : 3 * HD, :], p[shard_of * tok : (shard_of + 1) * tok], 1, 0)
                    o = part if o is None else o + part
                o_ref[s, step, :, j * part_width : (j + 1) * part_width] = (o / total).astype(BF16)
                lse_ref[s, step, :, j * part_width : (j + 1) * part_width] = top + jnp.log2(total)

            scores = [score(0)]
            pending = None
            for j in range(sub):
                if j + 1 < sub:
                    scores.append(score(j + 1))
                done = soft(scores[j])
                if pending is not None:
                    mix(j - 1, *pending)
                pending = done
            mix(sub - 1, *pending)

            @pl.when(i < nz - 1)
            def _():
                o_copy(s, i).start()

        each(nz, one_shard)
        mixed_ref[s, z] = o_ref[s, z]

        @pl.when(s == slots - 2)
        def _():
            pass_bulk(0)

    each(slots, slot)
    pass_bulk(1)

    def drain_slots(s):
        each(nz - 1, lambda i: o_arrival(s, i).wait_recv())
        each(nz - 1, lambda i: o_copy(s, i).wait_send())
        each(nz - 1, lambda i: x_copy(s, i).wait_send())

    each(slots, drain_slots)
    for a in range(2):
        each(pairs, lambda j: p_arrival(a, 2 * j + 1 - c).wait_recv())
        each(pairs - 1, lambda i: p_peer(a, i).wait_send())
        each(pairs - 1, lambda i: p_pass(a, i).wait_send())
        p_partner(a).wait_send()
        p_own(a).wait()

    def drain_peers(i):
        small_copy(i).wait_send()
        mod_copy(i).wait_send()

    def drain_weights(i):
        for s in range(slots):
            w_peer(s, i).wait_send()
            w_pass(s, i).wait_send()

    each(fs - 1, drain_peers)
    each(pairs - 1, drain_weights)
    for s in range(slots):
        w_partner(s).wait_send()


def forward(qkv_weight, tokens, gains, cond, mod_weight, mod_bias, cosine, sine, feed, fs, nz):
    slots = H // nz
    tok, width = tokens.shape
    shard = qkv_weight.shape[0]
    pairs = fs // 2
    up, out, down = feed
    ff = gains[2].shape[0] * fs
    vmem = pl.BlockSpec(memory_space=pltpu.VMEM)
    hbm = pl.BlockSpec(memory_space=pl.ANY)
    low = lambda *shape: pltpu.VMEM(shape, BF16)
    wide = lambda *shape: pltpu.VMEM(shape, F32)
    dma = lambda *shape: pltpu.SemaphoreType.DMA(shape)
    head_shape = (slots, nz, 3 * HD, tok)
    pack_shape = (shard, up.shape[1] + out.shape[1])
    length = nz * tok
    cols = 3 * nz * HD
    small = 3 * width + ff + cond.shape[-1]
    return pl.pallas_call(
        partial(forward_kernel, fs, nz, slots, 2),
        in_specs=[vmem, hbm] + [vmem] * 9 + [hbm] * 3,
        out_specs=[vmem] * 9 + [hbm] * 2,
        out_shape=[
            jax.ShapeDtypeStruct(head_shape, BF16),
            jax.ShapeDtypeStruct((slots, nz, HD, tok), BF16),
            jax.ShapeDtypeStruct((slots, nz, HD, tok), BF16),
            jax.ShapeDtypeStruct((slots, nz, 1, tok), F32),
            jax.ShapeDtypeStruct((slots, fs, shard, cols), BF16),
            jax.ShapeDtypeStruct((tok, width), BF16),
            jax.ShapeDtypeStruct((8, width), F32),
            jax.ShapeDtypeStruct((ff // width, 1, width), F32),
            jax.ShapeDtypeStruct((fs, cond.shape[-1]), F32),
            jax.ShapeDtypeStruct((fs, *pack_shape), BF16),
            jax.ShapeDtypeStruct((fs, *down.shape), BF16),
        ],
        scratch_shapes=[
            wide(tok, width),
            wide(*up.shape),
            wide(*out.shape),
            wide(*down.shape),
            low(slots, shard, cols),
            low(*head_shape),
            wide(8, width),
            wide(8, ff),
            wide(fs, 6 * width),
            wide(1, small),
            wide(fs, 1, small),
            wide(fs, 1, 6 * width),
            wide(fs, 1, 6 * width),
            wide(*((8, 128) if shard % 16 == 0 else (width, cols))),
            dma(4),
            dma(fs - 1),
            dma(fs),
            dma(fs - 1),
            dma(fs),
            dma(slots, pairs),
            dma(slots, pairs),
            dma(slots, fs),
            low(*pack_shape),
            low(*down.shape),
            low(length, HD),
            dma(slots, nz - 1),
            dma(slots, nz),
            dma(slots, nz - 1),
            dma(slots, nz),
            dma(2, pairs),
            dma(2, pairs),
            dma(2, fs),
            dma(2),
        ],
        compiler_params=pltpu.CompilerParams(vmem_limit_bytes=VMEM_LIMIT, collective_id=2, has_side_effects=True),
        cost_estimate=pl.CostEstimate(
            flops=16 * slots * length * length * HD, bytes_accessed=10**7, transcendentals=slots * length * length
        ),
        name="forward",
    )(
        qkv_weight,
        tokens,
        *gains,
        cond,
        mod_weight.T,
        mod_bias,
        cosine,
        sine,
        *feed,
    )


def attend_back_kernel(
    fs,
    n,
    slots,
    tok,
    sub,
    x_ref,
    sent_ref,
    o_ref,
    lse_ref,
    cos_ref,
    sin_ref,
    pack_hbm,
    down_hbm,
    out_ref,
    part_pack,
    part_down,
    own_pack,
    own_down,
    pair_pack,
    pair_down,
    recv_pack,
    recv_down,
    own_s,
    pair_s,
    pair_r,
    peer_s,
    peer_r,
    g_ref,
    d_ref,
    k_ref,
    v_ref,
    q_all,
    g_all,
    lse_all,
    centre_all,
    dq_ref,
    g_s,
    g_r,
    q_s,
    q_r,
    kv_s,
    kv_r,
):
    z = lax.axis_index("seq")
    half = HD // 2
    me = lax.axis_index("fsdp")
    pairs = fs // 2
    k, c = me // 2, lax.rem(me, 2)
    partner = me + 1 - 2 * c
    bulk = ((pack_hbm, own_pack, pair_pack, recv_pack, part_pack), (down_hbm, own_down, pair_down, recv_down, part_down))

    def own_load(a, j):
        return pltpu.make_async_copy(bulk[a][0].at[j, c], bulk[a][1].at[j], own_s.at[a, j])

    def pair_copy(a, j):
        return remote(bulk[a][0].at[j, 1 - c], bulk[a][2].at[j], pair_s.at[a, j], pair_r.at[a, j], fsdp=partner)

    def peer_copy(a, j):
        return remote(bulk[a][1].at[j], bulk[a][3].at[k], peer_s.at[a, j], peer_r.at[a, k], fsdp=2 * j + c)

    def peer_arrival(a, j):
        return remote(bulk[a][1].at[j], bulk[a][3].at[j], peer_s.at[a, j], peer_r.at[a, j], fsdp=2 * j + c)

    def forward_bulk(a):
        own, pair = bulk[a][1:3]

        def one(i):
            j = lax.rem(k + 1 + i, pairs)
            own_load(a, j).wait()
            pair_copy(a, j).wait_recv()
            own[j] = add_low(own[j], pair[j])
            peer_copy(a, j).start()

        each(pairs - 1, one)

    def finish_bulk(a):
        _, own, pair, recv, part = bulk[a]
        own_load(a, k).wait()
        pair_copy(a, k).wait_recv()
        each(pairs - 1, lambda i: peer_arrival(a, lax.rem(k + 1 + i, pairs)).wait_recv())
        height = part.shape[0]
        block = 32 if height % 32 == 0 else height

        def one(b):
            rows = pl.ds(b * block, block)
            total = own[k, rows].astype(F32) + pair[k, rows].astype(F32)
            for i in range(pairs - 1):
                total = total + recv[lax.rem(k + 1 + i, pairs), rows].astype(F32)
            part[rows, :] = total.astype(BF16)

        each(height // block, one)

    def drain_bulk(a):
        each(pairs, lambda j: pair_copy(a, j).wait_send())
        each(pairs - 1, lambda i: peer_copy(a, lax.rem(k + 1 + i, pairs)).wait_send())

    for a in range(2):
        each(pairs, lambda j: own_load(a, j).start())
    greet(me, z, fs, n)

    def g_copy(s, i):
        peer = lax.rem(z + 1 + i, n)
        return remote(sent_ref.at[s, peer], g_ref.at[s, z], g_s.at[s, i], g_r.at[s, z], seq=peer)

    def g_arrival(s, i):
        peer = lax.rem(z + 1 + i, n)
        return remote(sent_ref.at[s, peer], g_ref.at[s, peer], g_s.at[s, i], g_r.at[s, peer], seq=peer)

    def part_copy(s, i, rows, send, recv, arrival):
        peer = lax.rem(z + 1 + i, n)
        slot = peer if arrival else z
        return remote(
            d_ref.at[s, peer, rows], out_ref.at[s, slot, rows], send.at[s, i], recv.at[s, slot], seq=peer
        )

    q_rows, kv_rows = pl.ds(0, HD), pl.ds(HD, 2 * HD)
    q_copy = lambda s, i, arrival=False: part_copy(s, i, q_rows, q_s, q_r, arrival)
    kv_copy = lambda s, i, arrival=False: part_copy(s, i, kv_rows, kv_s, kv_r, arrival)

    for s in range(slots):
        each(n - 1, lambda i: g_copy(s, i).start())
        g_ref[s, z] = sent_ref[s, z]
    for a in range(2):
        each(pairs, lambda i: pair_copy(a, lax.rem(k + 1 + i, pairs)).start())

    scale = LOG2E / math.sqrt(HD)
    width = tok // sub

    def turn_back(grad, cosine, sine):
        a, b = grad[:half], grad[half:]
        return (a * cosine + b * sine).astype(BF16), (b * cosine - a * sine).astype(BF16)

    def slot(s):
        for owner in range(n):
            cols = slice(owner * tok, (owner + 1) * tok)
            k_ref[cols, :] = x_ref[s, owner, HD : 2 * HD, :].T
            v_ref[cols, :] = x_ref[s, owner, 2 * HD : 3 * HD, :].T
            q_all[:, cols] = x_ref[s, owner, 0:HD, :]
            lse_all[:, cols] = lse_ref[s, owner]
        each(n - 1, lambda i: g_arrival(s, i).wait_recv())
        for owner in range(n):
            cols = slice(owner * tok, (owner + 1) * tok)
            g = g_ref[s, owner]
            g_all[:, cols] = g
            centre_all[:, cols] = jnp.sum(g.astype(F32) * o_ref[s, owner].astype(F32), axis=0, keepdims=True)
        dq_ref[...] = jnp.zeros_like(dq_ref)

        def shard(i):
            step = lax.rem(z + 1 + i, n)
            for j in range(sub):
                cols = slice(j * width, (j + 1) * width)
                rows = pl.ds(pl.multiple_of(step * tok + j * width, width), width)
                score = mm(k_ref[rows, :], q_all[...], 1, 0)
                dp = mm(v_ref[rows, :], g_all[...], 1, 0)
                p = jnp.exp2(score * scale - lse_all[...])
                p_low = p.astype(BF16)
                ds = (p * (dp - centre_all[...])).astype(BF16)
                dv = mm(g_all[...], p_low, 1, 1)
                dk = mm(q_all[...], ds, 1, 1) * (1.0 / math.sqrt(HD))
                dq_ref[...] += mm(x_ref[s, step, HD : 2 * HD, cols], ds, 1, 0)
                a, b = turn_back(dk, cos_ref[step, :, cols], sin_ref[step, :, cols])
                d_ref[s, step, HD : HD + half, cols] = a
                d_ref[s, step, HD + half : 2 * HD, cols] = b
                d_ref[s, step, 2 * HD : 3 * HD, cols] = dv.astype(BF16)

            @pl.when(i < n - 1)
            def _():
                kv_copy(s, i).start()

        each(n, shard)
        for owner in range(n):
            dq = dq_ref[:, owner * tok : (owner + 1) * tok] * (1.0 / math.sqrt(HD))
            a, b = turn_back(dq, cos_ref[owner], sin_ref[owner])
            d_ref[s, owner, 0:half, :] = a
            d_ref[s, owner, half:HD, :] = b
        each(n - 1, lambda i: q_copy(s, i).start())
        out_ref[s, z] = d_ref[s, z]

        @pl.when(s == 0)
        def _():
            for a in range(2):
                forward_bulk(a)

    each(slots, slot)
    for a in range(2):
        finish_bulk(a)
        drain_bulk(a)

    def drain(s):
        def one(i):
            q_copy(s, i, True).wait_recv()
            kv_copy(s, i, True).wait_recv()
            g_copy(s, i).wait_send()
            q_copy(s, i).wait_send()
            kv_copy(s, i).wait_send()

        each(n - 1, one)

    each(slots, drain)


def attend_back(x, g, o, lse, cosine, sine, g_pack, g_down, fs):
    slots, n, _, tok = x.shape
    length = n * tok
    vmem = pl.BlockSpec(memory_space=pltpu.VMEM)
    dma = lambda *shape: pltpu.SemaphoreType.DMA(shape)
    pairs = fs // 2
    shards = [(v.shape[0] // fs, v.shape[1]) for v in (g_pack, g_down)]
    split = lambda v: v.reshape(pairs, 2, v.shape[0] // fs, v.shape[1])
    return pl.pallas_call(
        partial(attend_back_kernel, fs, n, slots, tok, 2),
        in_specs=[vmem] * 6 + [pl.BlockSpec(memory_space=pl.ANY)] * 2,
        out_specs=[vmem] * 3,
        out_shape=[
            jax.ShapeDtypeStruct(x.shape, BF16),
            jax.ShapeDtypeStruct(shards[0], BF16),
            jax.ShapeDtypeStruct(shards[1], BF16),
        ],
        scratch_shapes=[pltpu.VMEM((pairs, *shard), BF16) for shard in shards * 3]
        + [dma(2, pairs)] * 5
        + [
            pltpu.VMEM(g.shape, BF16),
            pltpu.VMEM(x.shape, BF16),
            pltpu.VMEM((length, HD), BF16),
            pltpu.VMEM((length, HD), BF16),
            pltpu.VMEM((HD, length), BF16),
            pltpu.VMEM((HD, length), BF16),
            pltpu.VMEM((1, length), F32),
            pltpu.VMEM((1, length), F32),
            pltpu.VMEM((HD, length), F32),
        ]
        + [dma(slots, n - 1), dma(slots, n)] * 3,
        compiler_params=pltpu.CompilerParams(vmem_limit_bytes=VMEM_LIMIT, collective_id=4, has_side_effects=True),
        cost_estimate=pl.CostEstimate(
            flops=40 * slots * length * length * HD, bytes_accessed=10**7, transcendentals=slots * length * length
        ),
        name="attend_back",
    )(x, g, o, lse, cosine, sine, split(g_pack), split(g_down))


GELU_C = math.sqrt(2.0 / math.pi)
GELU_A = 0.044715


def middle_kernel(
    blocks,
    tokens_ref,
    cot_ref,
    vec_ref,
    bias_ref,
    up_ref,
    down_ref,
    out_w_ref,
    mixed_ref,
    output_ref,
    grad_hidden_ref,
    sums_ref,
    bias_grad_ref,
    g_down_ref,
    g_pack_ref,
    grad_mixed_ref,
    attn_out_ref,
    mlp_in_ref,
    low_ref,
    back_ref,
):
    j = pl.program_id(0)
    tok, width = tokens_ref.shape
    gate_attn, shift, scale, gate, gain, down_bias = (vec_ref[i : i + 1, :] for i in range(6))
    piece = min(256, tok)
    pieces = tok // piece

    @pl.when(j == 0)
    def _():
        attn_out_ref[...] = mm(mixed_ref[...], out_w_ref[...], 0, 0)

        def prepare(i, _):
            rows = pl.ds(pl.multiple_of(i * piece, piece), piece)
            hidden = tokens_ref[rows, :] + gate_attn * attn_out_ref[rows, :]
            grad_hidden_ref[rows, :] = hidden
            hat, _ = normalize(hidden)
            mlp_in_ref[rows, :] = (hat * gain * (1.0 + scale) + shift).astype(BF16)
            low_ref[rows, :] = (gate * cot_ref[rows, :]).astype(BF16)
            return 0

        lax.fori_loop(0, pieces, prepare, 0)
        output_ref[...] = jnp.zeros_like(output_ref)
        back_ref[...] = jnp.zeros_like(back_ref)

    @pl.when(j < blocks)
    def _():
        mlp_in, low = mlp_in_ref[...], low_ref[...]
        x = mm(mlp_in, up_ref[...], 1, 0) + bias_ref[0]
        grad_act = mm(low, down_ref[...], 1, 1)
        square = x * x
        t = jnp.tanh(x * (GELU_C + GELU_C * GELU_A * square))
        half = 0.5 + 0.5 * t
        act = (x * half).astype(BF16)
        slope = half + x * (0.5 - 0.5 * t * t) * (GELU_C + 3.0 * GELU_C * GELU_A * square)
        grad_pre = grad_act * slope
        bias_grad_ref[0] = jnp.sum(grad_pre, axis=0, keepdims=True)
        pre_low = grad_pre.astype(BF16)
        output_ref[...] += mm(act, down_ref[...], 1, 0)
        back_ref[...] += mm(pre_low, up_ref[...], 1, 1)
        g_down_ref[...] = mm(act, low, 0, 0).astype(BF16)
        g_pack_ref[...] = mm(mlp_in, pre_low, 0, 0).astype(BF16)

    @pl.when(j == blocks)
    def _():
        def finish(i, sums):
            rows = pl.ds(pl.multiple_of(i * piece, piece), piece)
            cot = cot_ref[rows, :]
            branch = output_ref[rows, :] + down_bias
            hidden = grad_hidden_ref[rows, :]
            output_ref[rows, :] = hidden + gate * branch
            hat, inv = normalize(hidden)
            back = back_ref[rows, :]
            grad_hidden = cot + norm_back(back * ((1.0 + scale) * gain), hat, inv)
            grad_hidden_ref[rows, :] = grad_hidden
            low_ref[rows, :] = (gate_attn * grad_hidden).astype(BF16)
            adds = (grad_hidden * attn_out_ref[rows, :], back, back * hat, cot * branch, cot)
            return tuple(a + jnp.sum(v, axis=0, keepdims=True) for a, v in zip(sums, adds))

        zero = jnp.zeros((1, width), F32)
        sums = lax.fori_loop(0, pieces, finish, (zero,) * 5)
        for i in range(5):
            sums_ref[i : i + 1, :] = sums[i]
        attn_low = low_ref[...]
        g_pack_ref[...] = mm(mixed_ref[...], attn_low, 1, 0).astype(BF16)
        grad_mixed_ref[...] = mm(out_w_ref[...], attn_low, 1, 1).astype(BF16)


def middle(tokens, cot, vectors, up_bias, w_pack, w_down, mixed):
    tok, width = tokens.shape
    ff = w_down.shape[0]
    blocks = ff // width
    whole = lambda shape: pl.BlockSpec(shape, lambda j: (0,) * len(shape), pipeline_mode=pl.Buffered(1))
    fixed = lambda shape: pl.BlockSpec(shape, lambda j: (0,) * len(shape))
    last = blocks - 1
    flops = 2 * tok * width * (6 * ff + 3 * width)
    return pl.pallas_call(
        partial(middle_kernel, blocks),
        grid=(blocks + 1,),
        in_specs=[
            whole(tokens.shape),
            whole(cot.shape),
            whole(vectors.shape),
            pl.BlockSpec((1, 1, width), lambda j: (jnp.minimum(j, last), 0, 0)),
            pl.BlockSpec((width, width), lambda j: (0, jnp.minimum(j, last))),
            pl.BlockSpec((width, width), lambda j: (jnp.minimum(j, last), 0)),
            pl.BlockSpec((width, width), lambda j: (0, blocks), pipeline_mode=pl.Buffered(1)),
        ]
        + [whole(mixed.shape)],
        out_specs=[
            fixed((tok, width)),
            fixed((tok, width)),
            fixed((8, width)),
            pl.BlockSpec((1, 1, width), lambda j: (jnp.minimum(j, last), 0, 0)),
            pl.BlockSpec((width, width), lambda j: (jnp.minimum(j, last), 0)),
            pl.BlockSpec((width, width), lambda j: (0, j)),
        ]
        + [fixed(mixed.shape)],
        out_shape=[
            jax.ShapeDtypeStruct((tok, width), F32),
            jax.ShapeDtypeStruct((tok, width), F32),
            jax.ShapeDtypeStruct((8, width), F32),
            jax.ShapeDtypeStruct((blocks, 1, width), F32),
            jax.ShapeDtypeStruct((ff, width), BF16),
            jax.ShapeDtypeStruct((width, ff + width), BF16),
        ]
        + [jax.ShapeDtypeStruct(mixed.shape, BF16)],
        scratch_shapes=[
            pltpu.VMEM((tok, width), F32),
            pltpu.VMEM((tok, width), BF16),
            pltpu.VMEM((tok, width), BF16),
            pltpu.VMEM((tok, width), F32),
        ],
        compiler_params=pltpu.CompilerParams(vmem_limit_bytes=VMEM_LIMIT),
        cost_estimate=pl.CostEstimate(flops=flops, bytes_accessed=6 * ff * width * 2, transcendentals=tok * ff),
        name="middle",
    )(tokens, cot, vectors, up_bias, w_pack, w_down, w_pack, mixed)


def reduce_kernel(fs, nz, slots, counts, lengths, *refs):
    swapped_hbm, w_hbm, attn_in_hbm, tokens_hbm, hidden_hbm, vec_in_ref, sums_ref, up_bias_ref, *refs = refs
    bulk_refs, (mod_t_ref, cond_ref), refs = refs[:2], refs[2:4], refs[4:]
    inputs_out, qkv_out, up_out, out_out, down_out, total_out, mod_w_out, cond_out = refs[:8]
    (
        swapped_ref,
        attn_in_ref,
        swap_s,
        row_buf,
        w_buf,
        tokens_buf,
        hidden_buf,
        g_buf,
        pair_buf,
        sum_buf,
        recv_buf,
        own_buf,
        up_pack,
        up_down,
        up_qkv,
        part_pack,
        part_down,
        part_qkv,
        twin_pack,
        twin_down,
        twin_qkv,
        tot_pack,
        tot_down,
        tot_qkv,
        vec_buf,
        vec_z,
        vec_own,
        vec_all,
        cond_send,
        cond_recv,
        local_s,
        pair_s,
        pair_r,
        peer_s,
        peer_r,
        up_s,
        up_r,
        twin_s,
        twin_r,
        tot_s,
        tot_r,
        vecz_s,
        vecz_r,
        vec_s,
        vec_r,
        cond_s,
        cond_r,
    ) = refs[8:]
    me = lax.axis_index("fsdp")
    z = lax.axis_index("seq")
    pairs = fs // 2
    k, c = me // 2, lax.rem(me, 2)
    partner = me + 1 - 2 * c
    inner = jnp.logical_or(z == nz // 2 - 1, z == nz // 2)
    outer = jnp.logical_not(inner)
    twin = nz - 1 - z
    mate = z + 1 - 2 * lax.rem(z, 2)
    tok, width = tokens_buf.shape
    shard = g_buf.shape[3]
    groups = width // 128

    def swap_load(s):
        return pltpu.make_async_copy(swapped_hbm.at[s], swapped_ref.at[s], swap_s.at[s])

    first_load = pltpu.make_async_copy(attn_in_hbm, attn_in_ref, local_s.at[3])
    first_load.start()
    for s in range(slots):
        swap_load(s).start()
    fetch = ((w_hbm, w_buf), (tokens_hbm, tokens_buf), (hidden_hbm, hidden_buf))
    loads = [pltpu.make_async_copy(src, dst, local_s.at[i]) for i, (src, dst) in enumerate(fetch)]
    for load in loads:
        load.start()
    greet(me, z, fs, nz)

    bulk = [
        (src, up, part, other, tot, i)
        for src, up, part, other, tot, count in (
            (bulk_refs[0], up_pack, part_pack, twin_pack, tot_pack, counts[0]),
            (bulk_refs[1], up_down, part_down, twin_down, tot_down, counts[1]),
        )
        for i in range(count)
    ]
    last = [(own_buf, up_qkv, part_qkv, twin_qkv, tot_qkv, s) for s in range(slots)]
    chain = list(enumerate(bulk + last))
    early, late = chain[: len(bulk)], chain[len(bulk) :]

    def up_copy(n, item):
        src, up, _, _, _, i = item
        return remote(src.at[i], up.at[i], up_s.at[n], up_r.at[n], seq=mate)

    def twin_copy(n, item):
        _, _, part, other, _, i = item
        return remote(part.at[i], other.at[i], twin_s.at[n], twin_r.at[n], seq=twin)

    def tot_copy(n, item):
        tot, i = item[4], item[5]
        return remote(tot.at[i], tot.at[i], tot_s.at[n], tot_r.at[n], seq=mate)

    def chain_in(n, item):
        src, up, part, _, _, i = item
        up_copy(n, item).wait_recv()
        part[i] = add_low(src[i], up[i])
        twin_copy(n, item).start()

    def chain_out(n, item):
        _, _, part, other, tot, i = item
        twin_copy(n, item).wait_recv()
        tot[i] = add_low(part[i], other[i])
        tot_copy(n, item).start()

    def plan(items):
        steps = [(chain_in, items[0])]
        for before, item in zip(items[:-1], items[1:]):
            steps += [(chain_in, item), (chain_out, before)]
        return steps + [(chain_out, items[-1])]

    steps = plan(early)

    def advance(count):
        todo = [steps.pop(0) for _ in range(min(count, len(steps)))]
        if todo:

            @pl.when(inner)
            def _():
                for step, (n, item) in todo:
                    step(n, item)

    half = len(early) - 2

    @pl.when(outer)
    def _():
        for n, item in early[:half]:
            up_copy(n, item).start()

    def pair_copy(s, j):
        return remote(g_buf.at[s, j, 1 - c], pair_buf.at[s, j], pair_s.at[s, j], pair_r.at[s, j], fsdp=partner)

    def peer_copy(s, j):
        return remote(sum_buf.at[s, j], recv_buf.at[s, k], peer_s.at[s, j], peer_r.at[s, k], fsdp=2 * j + c)

    def peer_arrival(s, j):
        return remote(sum_buf.at[s, j], recv_buf.at[s, j], peer_s.at[s, j], peer_r.at[s, j], fsdp=2 * j + c)

    first_load.wait()

    def project_grad(s):
        swap_load(s).wait()
        for head in range(nz):
            for p in range(3):
                base = (p * nz + head) * HD
                row_buf[s, base : base + HD, :] = swapped_ref[s, head, p * HD : (p + 1) * HD, :]
        grad = mm(attn_in_ref[...], row_buf[s], 0, 1).astype(BF16)
        for i in range(fs):
            g_buf[s, i // 2, i % 2] = grad[i * shard : (i + 1) * shard]
        each(pairs, lambda i: pair_copy(s, lax.rem(k + 1 + i, pairs)).start())


    def forward(s, i):
        j = lax.rem(k + 1 + i, pairs)
        pair_copy(s, j).wait_recv()
        sum_buf[s, j] = add_low(g_buf[s, j, c], pair_buf[s, j])
        peer_copy(s, j).start()

    def stage(s):
        @pl.when(s < slots)
        def _():
            project_grad(s)

        @pl.when(s > 0)
        def _():
            each(pairs - 1, lambda i: forward(s - 1, i))

    each(slots + 1, stage)
    advance(1)
    for load in loads:
        load.wait()

    scale_mlp, gate_mlp, mlp_gain = (vec_in_ref[i : i + 1, :] for i in (2, 3, 4))
    attn_gain, scale_attn = (vec_in_ref[i : i + 1, :] for i in (6, 7))
    piece = min(256, tok)

    def norm_piece(i, kept):
        back_sum, hat_sum = kept
        rows = pl.ds(pl.multiple_of(i * piece, piece), piece)
        grad = None
        for s in range(slots):
            part = mm(row_buf[s, :, rows], w_buf[s], 0, 1)
            grad = part if grad is None else grad + part
        hat, inv = normalize(tokens_buf[rows, :])
        scaled = grad * ((1.0 + scale_attn) * attn_gain)
        inputs_out[rows, :] = hidden_buf[rows, :] + norm_back(scaled, hat, inv)
        back_sum = back_sum + jnp.sum(grad, axis=0, keepdims=True)
        hat_sum = hat_sum + jnp.sum(grad * hat, axis=0, keepdims=True)
        return back_sum, hat_sum

    zero = jnp.zeros((1, width), F32)
    kept = lax.fori_loop(0, tok // piece - 1, norm_piece, (zero, zero))
    advance(2)
    back_sum, hat_sum = norm_piece(tok // piece - 1, kept)

    sums = [sums_ref[i : i + 1, :] for i in range(5)]
    vectors = [back_sum, hat_sum * attn_gain, sums[0], sums[1], sums[2] * mlp_gain, sums[3]]
    vectors += [hat_sum * (1.0 + scale_attn), sums[2] * (1.0 + scale_mlp)]
    vectors += [up_bias_ref[i] for i in range(up_bias_ref.shape[0])]
    vectors.append(sums[4] * gate_mlp)
    for p, v in enumerate(vectors):
        for i in range(groups):
            vec_buf[p * groups + i : p * groups + i + 1, :] = v[:, i * 128 : (i + 1) * 128]
    used = len(vectors) * groups
    vec_buf[used:, :] = jnp.zeros((vec_buf.shape[0] - used, 128), F32)
    vec_z[z] = vec_buf[...]

    def vecz_copy(i):
        return remote(vec_buf, vec_z.at[z], vecz_s.at[i], vecz_r.at[z], seq=lax.rem(z + 1 + i, nz))

    def vecz_arrival(i):
        peer = lax.rem(z + 1 + i, nz)
        return remote(vec_buf, vec_z.at[peer], vecz_s.at[i], vecz_r.at[peer], seq=peer)

    each(nz - 1, lambda i: vecz_copy(i).start())

    @pl.when(outer)
    def _():
        for n, item in early[half:]:
            up_copy(n, item).start()

    advance(max(0, len(steps) - 3))
    each(nz - 1, lambda i: vecz_arrival(i).wait_recv())
    summed = vec_z[0]
    for i in range(1, nz):
        summed = summed + vec_z[i]
    vec_own[...] = summed
    vec_all[me] = summed

    def vec_copy(i):
        return remote(vec_own, vec_all.at[me], vec_s.at[i], vec_r.at[me], fsdp=lax.rem(me + 1 + i, fs))

    def vec_arrival(i):
        peer = lax.rem(me + 1 + i, fs)
        return remote(vec_own, vec_all.at[peer], vec_s.at[i], vec_r.at[peer], fsdp=peer)

    each(fs - 1, lambda i: vec_copy(i).start())

    def gather_slot(s):
        pair_copy(s, k).wait_recv()
        own = g_buf[s, k, c].astype(F32) + pair_buf[s, k].astype(F32)

        def gather_in(i, acc):
            j = lax.rem(k + 1 + i, pairs)
            peer_arrival(s, j).wait_recv()
            return acc + recv_buf[s, j].astype(F32)

        own_buf[s] = lax.fori_loop(0, pairs - 1, gather_in, own).astype(BF16)

        @pl.when(outer)
        def _():
            up = remote(own_buf.at[s], up_qkv.at[s], up_s.at[len(early) + s], up_r.at[len(early) + s], seq=mate)
            up.start()

    each(slots, gather_slot)
    advance(len(steps))
    steps.extend(plan(late))

    each(fs - 1, lambda i: vec_arrival(i).wait_recv())
    lane_from = lax.broadcasted_iota(jnp.int32, (256, 128), 0)
    lane_to = lax.broadcasted_iota(jnp.int32, (256, 128), 1)
    part, first, place = None, 0, 0
    for which, length in enumerate(lengths):
        block = length // fs
        for i in range(-(-block // 128)):
            offset = me * block + 128 * i
            row = first + offset // 128
            select = (lane_from == lane_to + lax.rem(offset, 128)).astype(F32)
            both = jnp.concatenate([vec_all[:, pl.ds(row, 1), :][:, 0], vec_all[:, pl.ds(row + 1, 1), :][:, 0]], axis=1)
            rows = lax.dot_general(
                both, select, (((1,), (0,)), ((), ())), precision=HIGHEST, preferred_element_type=F32
            )
            total_out[place : place + 1, :] = jnp.sum(rows, axis=0, keepdims=True)
            place += 1
            if which > 0:
                continue
            wide = min(128, block - i * 128)
            columns = slice(i * 128, i * 128 + wide)
            mod_rows = mod_t_ref[columns, :].astype(BF16).astype(F32)
            share = lax.dot_general(
                rows[:, :wide], mod_rows, (((1,), (0,)), ((), ())), precision=HIGHEST, preferred_element_type=F32
            )
            part = share if part is None else part + share
            outer_product = lax.dot_general(
                rows, cond_ref[...], (((0,), (0,)), ((), ())), precision=HIGHEST, preferred_element_type=F32
            )
            mod_w_out[columns, :] = outer_product[:wide]
        first += length // 128
    cond_send[...] = jnp.broadcast_to(part[:, None, :], cond_send.shape)

    def cond_copy(i):
        peer = lax.rem(me + 1 + i, fs)
        return remote(cond_send.at[peer], cond_recv.at[me], cond_s.at[i], cond_r.at[me], fsdp=peer)

    def cond_arrival(i):
        peer = lax.rem(me + 1 + i, fs)
        return remote(cond_send.at[peer], cond_recv.at[peer], cond_s.at[i], cond_r.at[peer], fsdp=peer)

    each(fs - 1, lambda i: cond_copy(i).start())
    advance(3)
    ff = up_out.shape[1]

    def write_pack(i):
        rows = pl.ds(i * tot_pack.shape[1], tot_pack.shape[1])
        up_out[rows, :] = tot_pack[i, :, :ff].astype(F32)
        out_out[rows, :] = tot_pack[i, :, ff:].astype(F32)

    def write_down(i):
        down_out[pl.ds(i * tot_down.shape[1], tot_down.shape[1]), :] = tot_down[i].astype(F32)

    @pl.when(outer)
    def _():
        for n, item in early:
            tot_copy(n, item).wait_recv()

    each(counts[0], write_pack)
    each(counts[1], write_down)
    advance(len(steps))
    cond_recv[me] = cond_send[me]
    each(fs - 1, lambda i: cond_arrival(i).wait_recv())
    cond_out[...] = jnp.sum(cond_recv[...], axis=0)

    @pl.when(outer)
    def _():
        for n, item in late:
            tot_copy(n, item).wait_recv()
        for n, item in chain:
            up_copy(n, item).wait_send()

    block = nz * HD
    for s in range(slots):
        for p in range(3):
            columns = slice(p * width + s * block, p * width + (s + 1) * block)
            qkv_out[:, columns] = tot_qkv[s, :, p * block : (p + 1) * block].astype(F32)

    @pl.when(inner)
    def _():
        for n, item in chain:
            twin_copy(n, item).wait_send()
            tot_copy(n, item).wait_send()

    def drain_peers(i):
        vec_copy(i).wait_send()
        cond_copy(i).wait_send()

    def drain_pairs(i):
        for s in range(slots):
            pair_copy(s, i).wait_send()

    def drain_sums(i):
        for s in range(slots):
            peer_copy(s, lax.rem(k + 1 + i, pairs)).wait_send()

    each(fs - 1, drain_peers)
    each(pairs, drain_pairs)
    each(pairs - 1, drain_sums)
    each(nz - 1, lambda i: vecz_copy(i).wait_send())


def reduce_all(
    grad_rows, weights, attn_in, tokens, grad_hidden, vectors, sums, up_bias_sum, part_pack, part_down, mod_t, cond, fs, nz
):
    slots = grad_rows.shape[0]
    tok, width = tokens.shape
    shard = width // fs
    count = lambda a: 3 if a.shape[0] % 48 == 0 else 1
    counts = (count(part_pack), count(part_down))
    split = lambda a, n: a.reshape(n, a.shape[0] // n, a.shape[1])
    pack, down = split(part_pack, counts[0]), split(part_down, counts[1])
    pairs = fs // 2
    items = sum(counts) + slots
    ff = up_bias_sum.size
    lengths = (6 * width, width, width, ff, width)
    rows = sum(lengths) // 128 + 2
    places = sum(-(-v // fs // 128) for v in lengths)
    vmem = pl.BlockSpec(memory_space=pltpu.VMEM)
    hbm = pl.BlockSpec(memory_space=pl.ANY)
    low = lambda *shape: pltpu.VMEM(shape, BF16)
    wide = lambda *shape: pltpu.VMEM(shape, F32)
    dma = lambda *shape: pltpu.SemaphoreType.DMA(shape)
    qkv_shape = (slots, shard, width)
    triple = [low(*pack.shape), low(*down.shape), low(*qkv_shape)]
    cols = grad_rows.shape[1] * grad_rows.shape[2]
    inputs_grad, qkv_sum, up_sum, out_sum, down_sum, total, mod_w, cond_grad = pl.pallas_call(
        partial(reduce_kernel, fs, nz, slots, counts, lengths),
        in_specs=[hbm] * 5 + [vmem] * 7,
        out_specs=[vmem] * 8,
        out_shape=[
            jax.ShapeDtypeStruct((tok, width), F32),
            jax.ShapeDtypeStruct((shard, 3 * width), F32),
            jax.ShapeDtypeStruct((shard, ff), F32),
            jax.ShapeDtypeStruct((shard, part_pack.shape[1] - ff), F32),
            jax.ShapeDtypeStruct(part_down.shape, F32),
            jax.ShapeDtypeStruct((places, 128), F32),
            jax.ShapeDtypeStruct(mod_t.shape, F32),
            jax.ShapeDtypeStruct((8, 128), F32),
        ],
        scratch_shapes=[
            low(*grad_rows.shape),
            low(tok, width),
            dma(slots),
            low(slots, cols, tok),
            low(slots, width, cols),
            wide(tok, width),
            wide(tok, width),
            low(slots, pairs, 2, shard, width),
            low(slots, pairs, shard, width),
            low(slots, pairs, shard, width),
            low(slots, pairs, shard, width),
            low(*qkv_shape),
        ]
        + triple * 4
        + [
            wide(rows, 128),
            wide(nz, rows, 128),
            wide(rows, 128),
            wide(fs, rows, 128),
            wide(fs, 8, 128),
            wide(fs, 8, 128),
            dma(4),
            dma(slots, pairs),
            dma(slots, pairs),
            dma(slots, pairs),
            dma(slots, pairs),
        ]
        + [dma(items)] * 6
        + [dma(nz - 1), dma(nz), dma(fs - 1), dma(fs), dma(fs - 1), dma(fs)],
        compiler_params=pltpu.CompilerParams(vmem_limit_bytes=VMEM_LIMIT, collective_id=1, has_side_effects=True),
        cost_estimate=pl.CostEstimate(flops=12 * tok * width * cols, bytes_accessed=10**8, transcendentals=0),
        name="reduce_all",
    )(grad_rows, weights, attn_in, tokens, grad_hidden, vectors, sums, up_bias_sum, pack, down, mod_t, cond)
    blocks, place = [], 0
    for v in lengths:
        n = -(-v // fs // 128)
        blocks.append(total[place : place + n].reshape(-1)[: v // fs])
        place += n
    return inputs_grad, qkv_sum, up_sum, out_sum, down_sum, blocks, mod_w.T, cond_grad


def per_device(
    inputs,
    conditioning,
    cotangent,
    attn_gain,
    mlp_gain,
    qkv_weight,
    out_weight,
    up_weight,
    up_bias,
    down_weight,
    down_bias,
    mod_weight,
    mod_bias,
):
    n = lax.axis_size("seq")
    fs = lax.axis_size("fsdp")
    z = lax.axis_index("seq")
    tokens = inputs[0]
    tok, width = tokens.shape
    slots = H // n

    inv_freq = jnp.exp(-math.log(10000.0) * jnp.arange(HD // 2, dtype=F32) * (2.0 / HD))
    positions = jnp.arange(tok, dtype=F32)
    own_angles = inv_freq[:, None] * (positions + (z * tok).astype(F32))[None, :]
    starts = (jnp.arange(n) * tok).astype(F32)
    all_angles = inv_freq[None, :, None] * (positions[None, :] + starts[:, None])[:, None, :]
    cos_all, sin_all = jnp.cos(all_angles), jnp.sin(all_angles)

    x, heads_out, mixed, log_totals, qkv_slots, attn_in, vectors, up_bias_full, cond_low_all, pack, down = forward(
        qkv_weight,
        tokens,
        (attn_gain, mlp_gain, up_bias, down_bias),
        conditioning,
        mod_weight,
        mod_bias,
        jnp.cos(own_angles),
        jnp.sin(own_angles),
        (up_weight, out_weight, down_weight),
        fs,
        n,
    )
    w_pack, down_full = pack.reshape(width, -1), down.reshape(-1, width)
    output, grad_hidden, sums, up_bias_sum, g_down, g_pack, grad_mixed = middle(
        tokens, cotangent[0], vectors, up_bias_full, w_pack, down_full, mixed.reshape(width, tok)
    )
    grad_slots, part_pack, part_down = attend_back(
        x, grad_mixed.reshape(heads_out.shape), heads_out, log_totals, cos_all, sin_all, g_pack, g_down, fs
    )
    inputs_grad, qkv_weight_grad, up_sum, out_sum, down_sum, blocks, mod_weight_grad, cond_grad = reduce_all(
        grad_slots,
        qkv_slots.reshape(slots, width, -1),
        attn_in,
        tokens,
        grad_hidden,
        vectors,
        sums,
        up_bias_sum,
        part_pack,
        part_down,
        mod_weight.T,
        cond_low_all,
        fs,
        n,
    )
    mod_bias_grad, attn_gain_grad, mlp_gain_grad, up_bias_grad, down_bias_grad = blocks
    _, silu_pull = jax.vjp(jax.nn.silu, conditioning)
    conditioning_grad = silu_pull(cond_grad[:1])[0]
    return (
        output[None],
        inputs_grad[None],
        conditioning_grad,
        attn_gain_grad,
        mlp_gain_grad,
        qkv_weight_grad,
        out_sum,
        up_sum,
        up_bias_grad,
        down_sum,
        down_bias_grad,
        mod_weight_grad,
        mod_bias_grad,
    )


def solution(mesh):
    specs = (
        P("fsdp", "seq", None),
        P("fsdp", None),
        P("fsdp", "seq", None),
        P("fsdp"),
        P("fsdp"),
        P("fsdp", None),
        P("fsdp", None),
        P("fsdp", None),
        P("fsdp"),
        P("fsdp", None),
        P("fsdp"),
        P(None, "fsdp"),
        P("fsdp"),
    )
    out_specs = (specs[0], specs[0], specs[1]) + specs[3:]
    return jax.shard_map(per_device, mesh=mesh, in_specs=specs, out_specs=out_specs, check_vma=False)
```

```python
from functools import partial
import math

import jax
import jax.numpy as jnp
from jax import lax
from jax.experimental import pallas as pl
from jax.experimental.pallas import tpu as pltpu
from jax.sharding import PartitionSpec as P

H = 12
HD = 64
EPSILON = 1e-05
BF16 = jnp.bfloat16
F32 = jnp.float32
LOG2E = math.log2(math.e)
VMEM_LIMIT = 60 * 1024 * 1024


def mm(a, b, ca, cb):
    return lax.dot_general(a, b, (((ca,), (cb,)), ((), ())), preferred_element_type=F32)


def normalize(values):
    centre = jnp.mean(values, axis=-1, keepdims=True)
    shifted = values - centre
    variance = jnp.mean(shifted * shifted, axis=-1, keepdims=True)
    inv_std = lax.rsqrt(variance + EPSILON)
    return (shifted * inv_std, inv_std)


def norm_back(grad_hat, normed_hat, inv_std):
    mean_grad = jnp.mean(grad_hat, axis=-1, keepdims=True)
    mean_mixed = jnp.mean(grad_hat * normed_hat, axis=-1, keepdims=True)
    return inv_std * (grad_hat - mean_grad - normed_hat * mean_mixed)


MESH = pl.DeviceIdType.MESH
HIGHEST = lax.Precision.HIGHEST


def add_low(a, b):
    return (a.astype(F32) + b.astype(F32)).astype(BF16)


def remote(src, dst, s, r, **where):
    return pltpu.make_async_remote_copy(
        src_ref=src, dst_ref=dst, send_sem=s, recv_sem=r, device_id=where, device_id_type=MESH
    )


def each(count, body):
    lax.fori_loop(0, count, lambda i, _: (body(i), 0)[1], 0)


def greet(me, z, fs, nz):
    barrier = pltpu.get_barrier_semaphore()

    def hello_fsdp(i):
        peer = {"fsdp": lax.rem(me + 1 + i, fs)}
        pl.semaphore_signal(barrier, inc=1, device_id=peer, device_id_type=MESH)

    def hello_seq(i):
        peer = {"seq": lax.rem(z + 1 + i, nz)}
        pl.semaphore_signal(barrier, inc=1, device_id=peer, device_id_type=MESH)

    each(fs - 1, hello_fsdp)
    each(nz - 1, hello_seq)
    pl.semaphore_wait(barrier, fs + nz - 2)


def forward_kernel(fs, nz, slots, sub, *refs):
    (
        qkv_ref,
        tokens_hbm,
        attn_gain_ref,
        mlp_gain_ref,
        up_bias_ref,
        down_bias_ref,
        cond_ref,
        mod_w_ref,
        mod_b_ref,
        cos_ref,
        sin_ref,
        up_hbm,
        out_hbm,
        down_hbm,
        x_hbm,
        o_hbm,
        mixed_ref,
        lse_ref,
        w_hbm,
        attn_in_hbm,
        vec_ref,
        bias_ref,
        cond_out,
        pack_hbm,
        feed_hbm,
    ) = refs[:25]
    (
        x_ref,
        o_ref,
        w_ref,
        attn_in_ref,
        store_s,
        tokens_buf,
        up_buf,
        out_buf,
        down_buf,
        w_own,
        z_send,
        narrow,
        spread,
        mod_wide,
        small_send,
        small_all,
        mod_send,
        mod_recv,
        w_full,
        local_s,
        small_s,
        small_r,
        mod_s,
        mod_r,
        w_s,
        w_f,
        w_r,
        pack_own,
        feed_own,
        k_ref,
        x_s,
        x_r,
        o_s,
        o_r,
        p_s,
        p_f,
        p_r,
        own_s,
    ) = refs[25:]
    me = lax.axis_index("fsdp")
    z = lax.axis_index("seq")
    pairs = fs // 2
    k, c = me // 2, lax.rem(me, 2)
    partner = me + 1 - 2 * c
    tok, width = tokens_buf.shape
    shard = w_own.shape[1]
    ff = spread.shape[1]
    block = nz * HD

    fetch = ((tokens_hbm, tokens_buf), (up_hbm, up_buf), (out_hbm, out_buf), (down_hbm, down_buf))
    loads = [pltpu.make_async_copy(src, dst, local_s.at[i]) for i, (src, dst) in enumerate(fetch)]
    for load in loads:
        load.start()
    greet(me, z, fs, nz)

    narrow[...] = jnp.zeros_like(narrow)
    for i, piece in enumerate((attn_gain_ref, mlp_gain_ref, down_bias_ref)):
        narrow[i : i + 1, :shard] = piece[...].reshape(1, -1)
    spread[...] = jnp.zeros_like(spread)
    spread[0:1, : up_bias_ref.shape[0]] = up_bias_ref[...].reshape(1, -1)
    placed = pltpu.roll(narrow[...], me * shard, 1)
    for i in range(3):
        small_send[:, i * width : (i + 1) * width] = placed[i : i + 1]
    placed = pltpu.roll(spread[...], me * up_bias_ref.shape[0], 1)
    small_send[:, 3 * width : 3 * width + ff] = placed[0:1]
    small_send[:, 3 * width + ff :] = cond_ref[...]
    small_all[me] = small_send[...]

    def small_copy(i):
        return remote(small_send, small_all.at[me], small_s.at[i], small_r.at[me], fsdp=lax.rem(me + 1 + i, fs))

    def small_arrival(i):
        peer = lax.rem(me + 1 + i, fs)
        return remote(small_send, small_all.at[peer], small_s.at[i], small_r.at[peer], fsdp=peer)

    each(fs - 1, lambda i: small_copy(i).start())

    for s in range(slots):
        for part in range(3):
            columns = slice(part * width + s * block, part * width + (s + 1) * block)
            w_own[s, :, part * block : (part + 1) * block] = qkv_ref[:, columns].astype(BF16)
        w_ref[s, me] = w_own[s]

    def w_peer(s, i):
        j = lax.rem(k + 1 + i, pairs)
        return remote(w_own.at[s], w_ref.at[s, me], w_s.at[s, i], w_r.at[s, me], fsdp=2 * j + c)

    def w_partner(s):
        return remote(w_own.at[s], w_ref.at[s, me], w_s.at[s, pairs - 1], w_r.at[s, me], fsdp=partner)

    def w_arrival(s, j):
        return remote(w_own.at[s], w_ref.at[s, j], w_s.at[s, 0], w_r.at[s, j], fsdp=partner)

    def w_pass(s, i):
        j = 2 * lax.rem(k + 1 + i, pairs) + c
        return remote(w_ref.at[s, j], w_ref.at[s, j], w_f.at[s, i], w_r.at[s, j], fsdp=partner)

    def send_weight(s):
        each(pairs - 1, lambda i: w_peer(s, i).start())
        w_partner(s).start()

    def pass_weight(s):
        def step(i):
            w_arrival(s, 2 * lax.rem(k + 1 + i, pairs) + c).wait_recv()
            w_pass(s, i).start()

        each(pairs - 1, step)

    send_weight(0)

    each(fs - 1, lambda i: small_arrival(i).wait_recv())
    small_sum = jnp.sum(small_all[:, :, : 3 * width + ff], axis=0)
    cond_all = small_all[:, 0, 3 * width + ff :]
    cond_low = (cond_all / (1.0 + jnp.exp(-cond_all))).astype(BF16)
    cond_out[...] = cond_low.astype(F32)
    own_mod = mm(cond_low, mod_w_ref[...].astype(BF16), 1, 1) + mod_b_ref[...].reshape(1, -1)
    mod_wide[...] = jnp.zeros_like(mod_wide)
    mod_wide[:, : own_mod.shape[1]] = own_mod
    placed = pltpu.roll(mod_wide[...], me * own_mod.shape[1], 1)
    for i in range(fs):
        mod_send[i] = placed[i : i + 1]
    mod_recv[me] = mod_send[me]

    def mod_copy(i):
        peer = lax.rem(me + 1 + i, fs)
        return remote(mod_send.at[peer], mod_recv.at[me], mod_s.at[i], mod_r.at[me], fsdp=peer)

    def mod_arrival(i):
        peer = lax.rem(me + 1 + i, fs)
        return remote(mod_send.at[peer], mod_recv.at[peer], mod_s.at[i], mod_r.at[peer], fsdp=peer)

    each(fs - 1, lambda i: mod_copy(i).start())
    for s in range(1, slots):
        send_weight(s)
    pass_weight(0)

    attn_gain, mlp_gain, down_bias = (small_sum[:, i * width : (i + 1) * width] for i in range(3))
    for i in range(ff // width):
        bias_ref[i] = small_sum[:, (3 + i) * width : (4 + i) * width]
    for load in loads:
        load.wait()
    piece = min(256, tok)
    each(fs - 1, lambda i: mod_arrival(i).wait_recv())
    modulation = jnp.sum(mod_recv[...], axis=0)
    shift_attn, scale_attn, gate_attn, shift_mlp, scale_mlp, gate_mlp = (
        modulation[:, i * width : (i + 1) * width] for i in range(6)
    )
    kept = (gate_attn, shift_mlp, scale_mlp, gate_mlp, mlp_gain, down_bias, attn_gain, scale_attn)
    for i, v in enumerate(kept):
        vec_ref[i : i + 1, :] = v
    for i in range(tok // piece):
        rows = slice(i * piece, (i + 1) * piece)
        hat, _ = normalize(tokens_buf[rows, :])
        attn_in_ref[rows, :] = (hat * attn_gain * (1.0 + scale_attn) + shift_attn).astype(BF16)

    cosine, sine = cos_ref[...], sin_ref[...]
    half = HD // 2

    def project(s, out_ref):
        each(pairs, lambda j: w_arrival(s, 2 * j + 1 - c).wait_recv())
        if shard % 16 == 0:
            weight = w_ref[s].reshape(fs * shard, 3 * block)
        else:
            for i in range(fs):
                w_full[i * shard : (i + 1) * shard, :] = w_ref[s, i].astype(F32)
            weight = w_full[...].astype(BF16)
        rows = mm(weight, attn_in_ref[...], 0, 1).astype(BF16)
        for shard_of in range(nz):
            for part in range(3):
                base = (part * nz + shard_of) * HD
                if part == 2:
                    out_ref[shard_of, part * HD : (part + 1) * HD, :] = rows[base : base + HD]
                else:
                    a = rows[base : base + half].astype(F32)
                    b = rows[base + half : base + HD].astype(F32)
                    out_ref[shard_of, part * HD : part * HD + half, :] = (a * cosine - b * sine).astype(BF16)
                    out_ref[shard_of, part * HD + half : (part + 1) * HD, :] = (b * cosine + a * sine).astype(BF16)

    def x_copy(s, i):
        peer = lax.rem(z + 1 + i, nz)
        return remote(z_send.at[s, peer], x_ref.at[s, z], x_s.at[s, i], x_r.at[s, z], seq=peer)

    def x_arrival(s, i):
        peer = lax.rem(z + 1 + i, nz)
        return remote(z_send.at[s, peer], x_ref.at[s, peer], x_s.at[s, i], x_r.at[s, peer], seq=peer)

    def o_copy(s, i):
        peer = lax.rem(z + 1 + i, nz)
        return remote(o_ref.at[s, peer], mixed_ref.at[s, z], o_s.at[s, i], o_r.at[s, z], seq=peer)

    def o_arrival(s, i):
        peer = lax.rem(z + 1 + i, nz)
        return remote(o_ref.at[s, peer], mixed_ref.at[s, peer], o_s.at[s, i], o_r.at[s, peer], seq=peer)

    def send_slot(s):
        project(s, z_send.at[s])
        each(nz - 1, lambda i: x_copy(s, i).start())
        x_ref[s, z] = z_send[s, z]

    def next_slot(s):
        @pl.when(s > 0)
        def _():
            pass_weight(s)

        send_slot(s)

    each(slots, next_slot)
    results = ((w_ref, w_hbm), (attn_in_ref, attn_in_hbm), (x_ref, x_hbm), (o_ref, o_hbm))
    stores = [pltpu.make_async_copy(src, dst, store_s.at[i]) for i, (src, dst) in enumerate(results)]
    for store in stores[:2]:
        store.start()

    pack_own[:, :ff] = up_buf[...].astype(BF16)
    pack_own[:, ff:] = out_buf[...].astype(BF16)
    feed_own[...] = down_buf[...].astype(BF16)
    bulk = ((pack_own, pack_hbm), (feed_own, feed_hbm))

    def p_peer(a, i):
        j = lax.rem(k + 1 + i, pairs)
        own, whole = bulk[a]
        return remote(own, whole.at[me], p_s.at[a, i], p_r.at[a, me], fsdp=2 * j + c)

    def p_partner(a):
        own, whole = bulk[a]
        return remote(own, whole.at[me], p_s.at[a, pairs - 1], p_r.at[a, me], fsdp=partner)

    def p_arrival(a, j):
        own, whole = bulk[a]
        return remote(own, whole.at[j], p_s.at[a, 0], p_r.at[a, j], fsdp=partner)

    def p_pass(a, i):
        j = 2 * lax.rem(k + 1 + i, pairs) + c
        whole = bulk[a][1]
        return remote(whole.at[j], whole.at[j], p_f.at[a, i], p_r.at[a, j], fsdp=partner)

    def p_own(a):
        own, whole = bulk[a]
        return pltpu.make_async_copy(own, whole.at[me], own_s.at[a])

    for a in range(2):
        each(pairs - 1, lambda i: p_peer(a, i).start())
        p_partner(a).start()
        p_own(a).start()

    def pass_bulk(a):
        def step(i):
            p_arrival(a, 2 * lax.rem(k + 1 + i, pairs) + c).wait_recv()
            p_pass(a, i).start()

        each(pairs - 1, step)

    scale = LOG2E / math.sqrt(HD)
    part_width = tok // sub

    def soft(s):
        top = jnp.max(s, axis=0, keepdims=True) * scale
        p = jnp.exp2(s * scale - top)
        total = jnp.sum(p, axis=0, keepdims=True)
        return top, total, p.astype(BF16)

    def slot(s):
        each(nz - 1, lambda i: x_arrival(s, i).wait_recv())
        for shard_of in range(nz):
            k_ref[shard_of * tok : (shard_of + 1) * tok, :] = x_ref[s, shard_of, HD : 2 * HD, :].T

        def one_shard(i):
            step = lax.rem(z + 1 + i, nz)

            def score(j):
                q = x_ref[s, step, 0:HD, j * part_width : (j + 1) * part_width]
                return mm(k_ref[...], q, 1, 0)

            def mix(j, top, total, p):
                o = None
                for shard_of in range(nz):
                    part = mm(x_ref[s, shard_of, 2 * HD : 3 * HD, :], p[shard_of * tok : (shard_of + 1) * tok], 1, 0)
                    o = part if o is None else o + part
                o_ref[s, step, :, j * part_width : (j + 1) * part_width] = (o / total).astype(BF16)
                lse_ref[s, step, :, j * part_width : (j + 1) * part_width] = top + jnp.log2(total)

            scores = [score(0)]
            pending = None
            for j in range(sub):
                if j + 1 < sub:
                    scores.append(score(j + 1))
                done = soft(scores[j])
                if pending is not None:
                    mix(j - 1, *pending)
                pending = done
            mix(sub - 1, *pending)

            @pl.when(i < nz - 1)
            def _():
                o_copy(s, i).start()

        each(nz, one_shard)
        mixed_ref[s, z] = o_ref[s, z]

        @pl.when(s == slots - 2)
        def _():
            pass_bulk(0)

    each(slots, slot)
    for store in stores[2:]:
        store.start()
    pass_bulk(1)

    def drain_slots(s):
        each(nz - 1, lambda i: o_arrival(s, i).wait_recv())
        each(nz - 1, lambda i: o_copy(s, i).wait_send())
        each(nz - 1, lambda i: x_copy(s, i).wait_send())

    each(slots, drain_slots)
    for a in range(2):
        each(pairs, lambda j: p_arrival(a, 2 * j + 1 - c).wait_recv())
        each(pairs - 1, lambda i: p_peer(a, i).wait_send())
        each(pairs - 1, lambda i: p_pass(a, i).wait_send())
        p_partner(a).wait_send()
        p_own(a).wait()
    for store in stores:
        store.wait()

    def drain_peers(i):
        small_copy(i).wait_send()
        mod_copy(i).wait_send()

    def drain_weights(i):
        for s in range(slots):
            w_peer(s, i).wait_send()
            w_pass(s, i).wait_send()

    each(fs - 1, drain_peers)
    each(pairs - 1, drain_weights)
    for s in range(slots):
        w_partner(s).wait_send()


def forward(qkv_weight, tokens, gains, cond, mod_weight, mod_bias, cosine, sine, feed, fs, nz):
    slots = H // nz
    tok, width = tokens.shape
    shard = qkv_weight.shape[0]
    pairs = fs // 2
    up, out, down = feed
    ff = gains[2].shape[0] * fs
    vmem = pl.BlockSpec(memory_space=pltpu.VMEM)
    hbm = pl.BlockSpec(memory_space=pl.ANY)
    low = lambda *shape: pltpu.VMEM(shape, BF16)
    wide = lambda *shape: pltpu.VMEM(shape, F32)
    dma = lambda *shape: pltpu.SemaphoreType.DMA(shape)
    head_shape = (slots, nz, 3 * HD, tok)
    pack_shape = (shard, up.shape[1] + out.shape[1])
    length = nz * tok
    cols = 3 * nz * HD
    small = 3 * width + ff + cond.shape[-1]
    return pl.pallas_call(
        partial(forward_kernel, fs, nz, slots, 2),
        in_specs=[vmem, hbm] + [vmem] * 9 + [hbm] * 3,
        out_specs=[hbm, hbm, vmem, vmem, hbm, hbm, vmem, vmem, vmem, hbm, hbm],
        out_shape=[
            jax.ShapeDtypeStruct(head_shape, BF16),
            jax.ShapeDtypeStruct((slots, nz, HD, tok), BF16),
            jax.ShapeDtypeStruct((slots, nz, HD, tok), BF16),
            jax.ShapeDtypeStruct((slots, nz, 1, tok), F32),
            jax.ShapeDtypeStruct((slots, fs, shard, cols), BF16),
            jax.ShapeDtypeStruct((tok, width), BF16),
            jax.ShapeDtypeStruct((8, width), F32),
            jax.ShapeDtypeStruct((ff // width, 1, width), F32),
            jax.ShapeDtypeStruct((fs, cond.shape[-1]), F32),
            jax.ShapeDtypeStruct((fs, *pack_shape), BF16),
            jax.ShapeDtypeStruct((fs, *down.shape), BF16),
        ],
        scratch_shapes=[
            low(*head_shape),
            low(slots, nz, HD, tok),
            low(slots, fs, shard, cols),
            low(tok, width),
            dma(4),
            wide(tok, width),
            wide(*up.shape),
            wide(*out.shape),
            wide(*down.shape),
            low(slots, shard, cols),
            low(*head_shape),
            wide(8, width),
            wide(8, ff),
            wide(fs, 6 * width),
            wide(1, small),
            wide(fs, 1, small),
            wide(fs, 1, 6 * width),
            wide(fs, 1, 6 * width),
            wide(*((8, 128) if shard % 16 == 0 else (width, cols))),
            dma(4),
            dma(fs - 1),
            dma(fs),
            dma(fs - 1),
            dma(fs),
            dma(slots, pairs),
            dma(slots, pairs),
            dma(slots, fs),
            low(*pack_shape),
            low(*down.shape),
            low(length, HD),
            dma(slots, nz - 1),
            dma(slots, nz),
            dma(slots, nz - 1),
            dma(slots, nz),
            dma(2, pairs),
            dma(2, pairs),
            dma(2, fs),
            dma(2),
        ],
        compiler_params=pltpu.CompilerParams(vmem_limit_bytes=VMEM_LIMIT, collective_id=2, has_side_effects=True),
        cost_estimate=pl.CostEstimate(
            flops=16 * slots * length * length * HD, bytes_accessed=10**7, transcendentals=slots * length * length
        ),
        name="forward",
    )(
        qkv_weight,
        tokens,
        *gains,
        cond,
        mod_weight.T,
        mod_bias,
        cosine,
        sine,
        *feed,
    )


def attend_back_kernel(
    fs,
    n,
    slots,
    tok,
    sub,
    x_hbm,
    sent_ref,
    o_hbm,
    lse_ref,
    cos_hbm,
    sin_hbm,
    pack_hbm,
    down_hbm,
    out_ref,
    part_pack,
    part_down,
    x_ref,
    o_ref,
    cos_ref,
    sin_ref,
    load_s,
    own_pack,
    own_down,
    pair_pack,
    pair_down,
    recv_pack,
    recv_down,
    own_s,
    pair_s,
    pair_r,
    peer_s,
    peer_r,
    g_ref,
    d_ref,
    k_ref,
    v_ref,
    q_all,
    g_all,
    lse_all,
    centre_all,
    dq_ref,
    g_s,
    g_r,
    q_s,
    q_r,
    kv_s,
    kv_r,
):
    z = lax.axis_index("seq")
    half = HD // 2
    me = lax.axis_index("fsdp")
    pairs = fs // 2
    k, c = me // 2, lax.rem(me, 2)
    partner = me + 1 - 2 * c
    bulk = ((pack_hbm, own_pack, pair_pack, recv_pack, part_pack), (down_hbm, own_down, pair_down, recv_down, part_down))

    def own_load(a, j):
        return pltpu.make_async_copy(bulk[a][0].at[j, c], bulk[a][1].at[j], own_s.at[a, j])

    def pair_copy(a, j):
        return remote(bulk[a][0].at[j, 1 - c], bulk[a][2].at[j], pair_s.at[a, j], pair_r.at[a, j], fsdp=partner)

    def peer_copy(a, j):
        return remote(bulk[a][1].at[j], bulk[a][3].at[k], peer_s.at[a, j], peer_r.at[a, k], fsdp=2 * j + c)

    def peer_arrival(a, j):
        return remote(bulk[a][1].at[j], bulk[a][3].at[j], peer_s.at[a, j], peer_r.at[a, j], fsdp=2 * j + c)

    def forward_bulk(a):
        own, pair = bulk[a][1:3]

        def one(i):
            j = lax.rem(k + 1 + i, pairs)
            own_load(a, j).wait()
            pair_copy(a, j).wait_recv()
            own[j] = add_low(own[j], pair[j])
            peer_copy(a, j).start()

        each(pairs - 1, one)

    def finish_bulk(a):
        _, own, pair, recv, part = bulk[a]
        own_load(a, k).wait()
        pair_copy(a, k).wait_recv()
        each(pairs - 1, lambda i: peer_arrival(a, lax.rem(k + 1 + i, pairs)).wait_recv())
        height = part.shape[0]
        block = 32 if height % 32 == 0 else height

        def one(b):
            rows = pl.ds(b * block, block)
            total = own[k, rows].astype(F32) + pair[k, rows].astype(F32)
            for i in range(pairs - 1):
                total = total + recv[lax.rem(k + 1 + i, pairs), rows].astype(F32)
            part[rows, :] = total.astype(BF16)

        each(height // block, one)

    def drain_bulk(a):
        each(pairs, lambda j: pair_copy(a, j).wait_send())
        each(pairs - 1, lambda i: peer_copy(a, lax.rem(k + 1 + i, pairs)).wait_send())

    fetch = ((x_hbm, x_ref), (o_hbm, o_ref), (cos_hbm, cos_ref), (sin_hbm, sin_ref))
    loads = [pltpu.make_async_copy(src, dst, load_s.at[i]) for i, (src, dst) in enumerate(fetch)]
    for load in loads:
        load.start()
    for a in range(2):
        each(pairs, lambda j: own_load(a, j).start())
    greet(me, z, fs, n)

    def g_copy(s, i):
        peer = lax.rem(z + 1 + i, n)
        return remote(sent_ref.at[s, peer], g_ref.at[s, z], g_s.at[s, i], g_r.at[s, z], seq=peer)

    def g_arrival(s, i):
        peer = lax.rem(z + 1 + i, n)
        return remote(sent_ref.at[s, peer], g_ref.at[s, peer], g_s.at[s, i], g_r.at[s, peer], seq=peer)

    def part_copy(s, i, rows, send, recv, arrival):
        peer = lax.rem(z + 1 + i, n)
        slot = peer if arrival else z
        return remote(
            d_ref.at[s, peer, rows], out_ref.at[s, slot, rows], send.at[s, i], recv.at[s, slot], seq=peer
        )

    q_rows, kv_rows = pl.ds(0, HD), pl.ds(HD, 2 * HD)
    q_copy = lambda s, i, arrival=False: part_copy(s, i, q_rows, q_s, q_r, arrival)
    kv_copy = lambda s, i, arrival=False: part_copy(s, i, kv_rows, kv_s, kv_r, arrival)

    for s in range(slots):
        each(n - 1, lambda i: g_copy(s, i).start())
        g_ref[s, z] = sent_ref[s, z]
    for a in range(2):
        each(pairs, lambda i: pair_copy(a, lax.rem(k + 1 + i, pairs)).start())

    scale = LOG2E / math.sqrt(HD)
    width = tok // sub

    def turn_back(grad, cosine, sine):
        a, b = grad[:half], grad[half:]
        return (a * cosine + b * sine).astype(BF16), (b * cosine - a * sine).astype(BF16)

    def slot(s):
        for owner in range(n):
            cols = slice(owner * tok, (owner + 1) * tok)
            k_ref[cols, :] = x_ref[s, owner, HD : 2 * HD, :].T
            v_ref[cols, :] = x_ref[s, owner, 2 * HD : 3 * HD, :].T
            q_all[:, cols] = x_ref[s, owner, 0:HD, :]
            lse_all[:, cols] = lse_ref[s, owner]
        each(n - 1, lambda i: g_arrival(s, i).wait_recv())
        for owner in range(n):
            cols = slice(owner * tok, (owner + 1) * tok)
            g = g_ref[s, owner]
            g_all[:, cols] = g
            centre_all[:, cols] = jnp.sum(g.astype(F32) * o_ref[s, owner].astype(F32), axis=0, keepdims=True)
        dq_ref[...] = jnp.zeros_like(dq_ref)

        def shard(i):
            step = lax.rem(z + 1 + i, n)
            for j in range(sub):
                cols = slice(j * width, (j + 1) * width)
                rows = pl.ds(pl.multiple_of(step * tok + j * width, width), width)
                score = mm(k_ref[rows, :], q_all[...], 1, 0)
                dp = mm(v_ref[rows, :], g_all[...], 1, 0)
                p = jnp.exp2(score * scale - lse_all[...])
                p_low = p.astype(BF16)
                ds = (p * (dp - centre_all[...])).astype(BF16)
                dv = mm(g_all[...], p_low, 1, 1)
                dk = mm(q_all[...], ds, 1, 1) * (1.0 / math.sqrt(HD))
                dq_ref[...] += mm(x_ref[s, step, HD : 2 * HD, cols], ds, 1, 0)
                a, b = turn_back(dk, cos_ref[step, :, cols], sin_ref[step, :, cols])
                d_ref[s, step, HD : HD + half, cols] = a
                d_ref[s, step, HD + half : 2 * HD, cols] = b
                d_ref[s, step, 2 * HD : 3 * HD, cols] = dv.astype(BF16)

            @pl.when(i < n - 1)
            def _():
                kv_copy(s, i).start()

        each(n, shard)
        for owner in range(n):
            dq = dq_ref[:, owner * tok : (owner + 1) * tok] * (1.0 / math.sqrt(HD))
            a, b = turn_back(dq, cos_ref[owner], sin_ref[owner])
            d_ref[s, owner, 0:half, :] = a
            d_ref[s, owner, half:HD, :] = b
        each(n - 1, lambda i: q_copy(s, i).start())
        out_ref[s, z] = d_ref[s, z]

        @pl.when(s == 0)
        def _():
            for a in range(2):
                forward_bulk(a)

    for load in loads:
        load.wait()
    each(slots, slot)
    for a in range(2):
        finish_bulk(a)
        drain_bulk(a)

    def drain(s):
        def one(i):
            q_copy(s, i, True).wait_recv()
            kv_copy(s, i, True).wait_recv()
            g_copy(s, i).wait_send()
            q_copy(s, i).wait_send()
            kv_copy(s, i).wait_send()

        each(n - 1, one)

    each(slots, drain)


def attend_back(x, g, o, lse, cosine, sine, g_pack, g_down, fs):
    slots, n, _, tok = x.shape
    length = n * tok
    vmem, hbm = pl.BlockSpec(memory_space=pltpu.VMEM), pl.BlockSpec(memory_space=pl.ANY)
    dma = lambda *shape: pltpu.SemaphoreType.DMA(shape)
    pairs = fs // 2
    shards = [(v.shape[0] // fs, v.shape[1]) for v in (g_pack, g_down)]
    split = lambda v: v.reshape(pairs, 2, v.shape[0] // fs, v.shape[1])
    return pl.pallas_call(
        partial(attend_back_kernel, fs, n, slots, tok, 2),
        in_specs=[hbm, vmem, hbm, vmem] + [hbm] * 4,
        out_specs=[vmem] * 3,
        out_shape=[
            jax.ShapeDtypeStruct(x.shape, BF16),
            jax.ShapeDtypeStruct(shards[0], BF16),
            jax.ShapeDtypeStruct(shards[1], BF16),
        ],
        scratch_shapes=[pltpu.VMEM(x.shape, BF16), pltpu.VMEM(o.shape, BF16)]
        + [pltpu.VMEM(cosine.shape, F32)] * 2
        + [dma(4)]
        + [pltpu.VMEM((pairs, *shard), BF16) for shard in shards * 3]
        + [dma(2, pairs)] * 5
        + [
            pltpu.VMEM(g.shape, BF16),
            pltpu.VMEM(x.shape, BF16),
            pltpu.VMEM((length, HD), BF16),
            pltpu.VMEM((length, HD), BF16),
            pltpu.VMEM((HD, length), BF16),
            pltpu.VMEM((HD, length), BF16),
            pltpu.VMEM((1, length), F32),
            pltpu.VMEM((1, length), F32),
            pltpu.VMEM((HD, length), F32),
        ]
        + [dma(slots, n - 1), dma(slots, n)] * 3,
        compiler_params=pltpu.CompilerParams(vmem_limit_bytes=VMEM_LIMIT, collective_id=4, has_side_effects=True),
        cost_estimate=pl.CostEstimate(
            flops=40 * slots * length * length * HD, bytes_accessed=10**7, transcendentals=slots * length * length
        ),
        name="attend_back",
    )(x, g, o, lse, cosine, sine, split(g_pack), split(g_down))


GELU_C = math.sqrt(2.0 / math.pi)
GELU_A = 0.044715


def middle_kernel(
    blocks,
    tokens_ref,
    cot_ref,
    vec_ref,
    bias_ref,
    up_ref,
    down_ref,
    out_w_ref,
    mixed_ref,
    output_ref,
    grad_hidden_ref,
    sums_ref,
    bias_grad_ref,
    g_down_ref,
    g_pack_ref,
    grad_mixed_ref,
    attn_out_ref,
    mlp_in_ref,
    low_ref,
    back_ref,
):
    j = pl.program_id(0)
    tok, width = tokens_ref.shape
    gate_attn, shift, scale, gate, gain, down_bias = (vec_ref[i : i + 1, :] for i in range(6))
    piece = min(256, tok)
    pieces = tok // piece

    @pl.when(j == 0)
    def _():
        attn_out_ref[...] = mm(mixed_ref[...], out_w_ref[...], 0, 0)

        def prepare(i, _):
            rows = pl.ds(pl.multiple_of(i * piece, piece), piece)
            hidden = tokens_ref[rows, :] + gate_attn * attn_out_ref[rows, :]
            grad_hidden_ref[rows, :] = hidden
            hat, _ = normalize(hidden)
            mlp_in_ref[rows, :] = (hat * gain * (1.0 + scale) + shift).astype(BF16)
            low_ref[rows, :] = (gate * cot_ref[rows, :]).astype(BF16)
            return 0

        lax.fori_loop(0, pieces, prepare, 0)
        output_ref[...] = jnp.zeros_like(output_ref)
        back_ref[...] = jnp.zeros_like(back_ref)

    @pl.when(j < blocks)
    def _():
        mlp_in, low = mlp_in_ref[...], low_ref[...]
        x = mm(mlp_in, up_ref[...], 1, 0) + bias_ref[0]
        grad_act = mm(low, down_ref[...], 1, 1)
        square = x * x
        t = jnp.tanh(x * (GELU_C + GELU_C * GELU_A * square))
        half = 0.5 + 0.5 * t
        act = (x * half).astype(BF16)
        slope = half + x * (0.5 - 0.5 * t * t) * (GELU_C + 3.0 * GELU_C * GELU_A * square)
        grad_pre = grad_act * slope
        bias_grad_ref[0] = jnp.sum(grad_pre, axis=0, keepdims=True)
        pre_low = grad_pre.astype(BF16)
        output_ref[...] += mm(act, down_ref[...], 1, 0)
        back_ref[...] += mm(pre_low, up_ref[...], 1, 1)
        g_down_ref[...] = mm(act, low, 0, 0).astype(BF16)
        g_pack_ref[...] = mm(mlp_in, pre_low, 0, 0).astype(BF16)

    @pl.when(j == blocks)
    def _():
        def finish(i, sums):
            rows = pl.ds(pl.multiple_of(i * piece, piece), piece)
            cot = cot_ref[rows, :]
            branch = output_ref[rows, :] + down_bias
            hidden = grad_hidden_ref[rows, :]
            output_ref[rows, :] = hidden + gate * branch
            hat, inv = normalize(hidden)
            back = back_ref[rows, :]
            grad_hidden = cot + norm_back(back * ((1.0 + scale) * gain), hat, inv)
            grad_hidden_ref[rows, :] = grad_hidden
            low_ref[rows, :] = (gate_attn * grad_hidden).astype(BF16)
            adds = (grad_hidden * attn_out_ref[rows, :], back, back * hat, cot * branch, cot)
            return tuple(a + jnp.sum(v, axis=0, keepdims=True) for a, v in zip(sums, adds))

        zero = jnp.zeros((1, width), F32)
        sums = lax.fori_loop(0, pieces, finish, (zero,) * 5)
        for i in range(5):
            sums_ref[i : i + 1, :] = sums[i]
        attn_low = low_ref[...]
        g_pack_ref[...] = mm(mixed_ref[...], attn_low, 1, 0).astype(BF16)
        grad_mixed_ref[...] = mm(out_w_ref[...], attn_low, 1, 1).astype(BF16)


def middle(tokens, cot, vectors, up_bias, w_pack, w_down, mixed):
    tok, width = tokens.shape
    ff = w_down.shape[0]
    blocks = ff // width
    whole = lambda shape: pl.BlockSpec(shape, lambda j: (0,) * len(shape), pipeline_mode=pl.Buffered(1))
    fixed = lambda shape: pl.BlockSpec(shape, lambda j: (0,) * len(shape))
    last = blocks - 1
    flops = 2 * tok * width * (6 * ff + 3 * width)
    return pl.pallas_call(
        partial(middle_kernel, blocks),
        grid=(blocks + 1,),
        in_specs=[
            whole(tokens.shape),
            whole(cot.shape),
            whole(vectors.shape),
            pl.BlockSpec((1, 1, width), lambda j: (jnp.minimum(j, last), 0, 0)),
            pl.BlockSpec((width, width), lambda j: (0, jnp.minimum(j, last))),
            pl.BlockSpec((width, width), lambda j: (jnp.minimum(j, last), 0)),
            pl.BlockSpec((width, width), lambda j: (0, blocks), pipeline_mode=pl.Buffered(1)),
        ]
        + [whole(mixed.shape)],
        out_specs=[
            fixed((tok, width)),
            fixed((tok, width)),
            fixed((8, width)),
            pl.BlockSpec((1, 1, width), lambda j: (jnp.minimum(j, last), 0, 0)),
            pl.BlockSpec((width, width), lambda j: (jnp.minimum(j, last), 0)),
            pl.BlockSpec((width, width), lambda j: (0, j)),
        ]
        + [fixed(mixed.shape)],
        out_shape=[
            jax.ShapeDtypeStruct((tok, width), F32),
            jax.ShapeDtypeStruct((tok, width), F32),
            jax.ShapeDtypeStruct((8, width), F32),
            jax.ShapeDtypeStruct((blocks, 1, width), F32),
            jax.ShapeDtypeStruct((ff, width), BF16),
            jax.ShapeDtypeStruct((width, ff + width), BF16),
        ]
        + [jax.ShapeDtypeStruct(mixed.shape, BF16)],
        scratch_shapes=[
            pltpu.VMEM((tok, width), F32),
            pltpu.VMEM((tok, width), BF16),
            pltpu.VMEM((tok, width), BF16),
            pltpu.VMEM((tok, width), F32),
        ],
        compiler_params=pltpu.CompilerParams(vmem_limit_bytes=VMEM_LIMIT),
        cost_estimate=pl.CostEstimate(flops=flops, bytes_accessed=6 * ff * width * 2, transcendentals=tok * ff),
        name="middle",
    )(tokens, cot, vectors, up_bias, w_pack, w_down, w_pack, mixed)


def reduce_kernel(fs, nz, slots, counts, lengths, *refs):
    swapped_hbm, w_hbm, attn_in_hbm, tokens_hbm, hidden_hbm, vec_in_ref, sums_ref, up_bias_ref, *refs = refs
    bulk_refs, (mod_t_ref, cond_ref), refs = refs[:2], refs[2:4], refs[4:]
    inputs_hbm, qkv_out, up_hbm, out_hbm, down_hbm, total_out, mod_w_out, cond_out = refs[:8]
    (
        inputs_out,
        up_out,
        out_out,
        down_out,
        store_s,
        swapped_ref,
        attn_in_ref,
        swap_s,
        row_buf,
        w_buf,
        tokens_buf,
        hidden_buf,
        g_buf,
        pair_buf,
        sum_buf,
        recv_buf,
        own_buf,
        up_pack,
        up_down,
        up_qkv,
        part_pack,
        part_down,
        part_qkv,
        twin_pack,
        twin_down,
        twin_qkv,
        tot_pack,
        tot_down,
        tot_qkv,
        vec_buf,
        vec_z,
        vec_own,
        vec_all,
        cond_send,
        cond_recv,
        local_s,
        pair_s,
        pair_r,
        peer_s,
        peer_r,
        up_s,
        up_r,
        twin_s,
        twin_r,
        tot_s,
        tot_r,
        vecz_s,
        vecz_r,
        vec_s,
        vec_r,
        cond_s,
        cond_r,
    ) = refs[8:]
    me = lax.axis_index("fsdp")
    z = lax.axis_index("seq")
    pairs = fs // 2
    k, c = me // 2, lax.rem(me, 2)
    partner = me + 1 - 2 * c
    inner = jnp.logical_or(z == nz // 2 - 1, z == nz // 2)
    outer = jnp.logical_not(inner)
    twin = nz - 1 - z
    mate = z + 1 - 2 * lax.rem(z, 2)
    tok, width = tokens_buf.shape
    shard = g_buf.shape[3]
    groups = width // 128

    def swap_load(s):
        return pltpu.make_async_copy(swapped_hbm.at[s], swapped_ref.at[s], swap_s.at[s])

    first_load = pltpu.make_async_copy(attn_in_hbm, attn_in_ref, local_s.at[3])
    first_load.start()
    for s in range(slots):
        swap_load(s).start()
    fetch = ((w_hbm, w_buf), (tokens_hbm, tokens_buf), (hidden_hbm, hidden_buf))
    loads = [pltpu.make_async_copy(src, dst, local_s.at[i]) for i, (src, dst) in enumerate(fetch)]
    for load in loads:
        load.start()
    greet(me, z, fs, nz)

    bulk = [
        (src, up, part, other, tot, i)
        for src, up, part, other, tot, count in (
            (bulk_refs[0], up_pack, part_pack, twin_pack, tot_pack, counts[0]),
            (bulk_refs[1], up_down, part_down, twin_down, tot_down, counts[1]),
        )
        for i in range(count)
    ]
    halves = own_buf.shape[0] // slots
    last = [(own_buf, up_qkv, part_qkv, twin_qkv, tot_qkv, i) for i in range(slots * halves)]
    chain = list(enumerate(bulk + last))
    early, late = chain[: len(bulk)], chain[len(bulk) :]

    def up_copy(n, item):
        src, up, _, _, _, i = item
        return remote(src.at[i], up.at[i], up_s.at[n], up_r.at[n], seq=mate)

    def twin_copy(n, item):
        _, _, part, other, _, i = item
        return remote(part.at[i], other.at[i], twin_s.at[n], twin_r.at[n], seq=twin)

    def tot_copy(n, item):
        tot, i = item[4], item[5]
        return remote(tot.at[i], tot.at[i], tot_s.at[n], tot_r.at[n], seq=mate)

    def chain_in(n, item):
        src, up, part, _, _, i = item
        up_copy(n, item).wait_recv()
        part[i] = add_low(src[i], up[i])
        twin_copy(n, item).start()

    def chain_out(n, item):
        _, _, part, other, tot, i = item
        twin_copy(n, item).wait_recv()
        tot[i] = add_low(part[i], other[i])
        tot_copy(n, item).start()

    def plan(items):
        ahead = 2
        steps = [(chain_in, item) for item in items[:ahead]]
        for before, item in zip(items, items[ahead:]):
            steps += [(chain_in, item), (chain_out, before)]
        return steps + [(chain_out, item) for item in items[-ahead:]]

    steps = plan(early)

    def advance(count):
        todo = [steps.pop(0) for _ in range(min(count, len(steps)))]
        if todo:

            @pl.when(inner)
            def _():
                for step, (n, item) in todo:
                    step(n, item)

    half = len(early) - len(early) // 3

    @pl.when(outer)
    def _():
        for n, item in early[:half]:
            up_copy(n, item).start()

    def pair_copy(s, j):
        return remote(g_buf.at[s, j, 1 - c], pair_buf.at[s, j], pair_s.at[s, j], pair_r.at[s, j], fsdp=partner)

    def peer_copy(s, j):
        return remote(sum_buf.at[s, j], recv_buf.at[s, k], peer_s.at[s, j], peer_r.at[s, k], fsdp=2 * j + c)

    def peer_arrival(s, j):
        return remote(sum_buf.at[s, j], recv_buf.at[s, j], peer_s.at[s, j], peer_r.at[s, j], fsdp=2 * j + c)

    first_load.wait()

    def project_grad(s):
        swap_load(s).wait()
        for head in range(nz):
            for p in range(3):
                base = (p * nz + head) * HD
                row_buf[s, base : base + HD, :] = swapped_ref[s, head, p * HD : (p + 1) * HD, :]
        grad = mm(attn_in_ref[...], row_buf[s], 0, 1).astype(BF16)
        for i in range(fs):
            g_buf[s, i // 2, i % 2] = grad[i * shard : (i + 1) * shard]
        each(pairs, lambda i: pair_copy(s, lax.rem(k + 1 + i, pairs)).start())


    def forward(s, i):
        j = lax.rem(k + 1 + i, pairs)
        pair_copy(s, j).wait_recv()
        sum_buf[s, j] = add_low(g_buf[s, j, c], pair_buf[s, j])
        peer_copy(s, j).start()

    def stage(s):
        @pl.when(s < slots)
        def _():
            project_grad(s)

        @pl.when(s > 0)
        def _():
            each(pairs - 1, lambda i: forward(s - 1, i))

    each(slots + 1, stage)
    advance(3)
    for load in loads:
        load.wait()

    scale_mlp, gate_mlp, mlp_gain = (vec_in_ref[i : i + 1, :] for i in (2, 3, 4))
    attn_gain, scale_attn = (vec_in_ref[i : i + 1, :] for i in (6, 7))
    piece = min(256, tok)

    def norm_piece(i, kept):
        back_sum, hat_sum = kept
        rows = pl.ds(pl.multiple_of(i * piece, piece), piece)
        grad = None
        for s in range(slots):
            part = mm(row_buf[s, :, rows], w_buf[s], 0, 1)
            grad = part if grad is None else grad + part
        hat, inv = normalize(tokens_buf[rows, :])
        scaled = grad * ((1.0 + scale_attn) * attn_gain)
        inputs_out[rows, :] = hidden_buf[rows, :] + norm_back(scaled, hat, inv)
        back_sum = back_sum + jnp.sum(grad, axis=0, keepdims=True)
        hat_sum = hat_sum + jnp.sum(grad * hat, axis=0, keepdims=True)
        return back_sum, hat_sum

    zero = jnp.zeros((1, width), F32)
    kept = (zero, zero)
    for i in range(tok // piece):
        kept = norm_piece(i, kept)
        advance(4)
    back_sum, hat_sum = kept
    results = ((inputs_out, inputs_hbm), (up_out, up_hbm), (out_out, out_hbm), (down_out, down_hbm))
    stores = [pltpu.make_async_copy(src, dst, store_s.at[i]) for i, (src, dst) in enumerate(results)]
    stores[0].start()

    sums = [sums_ref[i : i + 1, :] for i in range(5)]
    vectors = [back_sum, hat_sum * attn_gain, sums[0], sums[1], sums[2] * mlp_gain, sums[3]]
    vectors += [hat_sum * (1.0 + scale_attn), sums[2] * (1.0 + scale_mlp)]
    vectors += [up_bias_ref[i] for i in range(up_bias_ref.shape[0])]
    vectors.append(sums[4] * gate_mlp)
    for p, v in enumerate(vectors):
        for i in range(groups):
            vec_buf[p * groups + i : p * groups + i + 1, :] = v[:, i * 128 : (i + 1) * 128]
    used = len(vectors) * groups
    vec_buf[used:, :] = jnp.zeros((vec_buf.shape[0] - used, 128), F32)
    vec_z[z] = vec_buf[...]

    def vecz_copy(i):
        return remote(vec_buf, vec_z.at[z], vecz_s.at[i], vecz_r.at[z], seq=lax.rem(z + 1 + i, nz))

    def vecz_arrival(i):
        peer = lax.rem(z + 1 + i, nz)
        return remote(vec_buf, vec_z.at[peer], vecz_s.at[i], vecz_r.at[peer], seq=peer)

    each(nz - 1, lambda i: vecz_copy(i).start())

    @pl.when(outer)
    def _():
        for n, item in early[half:]:
            up_copy(n, item).start()

    advance(max(0, len(steps) - 5))
    each(nz - 1, lambda i: vecz_arrival(i).wait_recv())
    summed = vec_z[0]
    for i in range(1, nz):
        summed = summed + vec_z[i]
    vec_own[...] = summed
    vec_all[me] = summed

    def vec_copy(i):
        return remote(vec_own, vec_all.at[me], vec_s.at[i], vec_r.at[me], fsdp=lax.rem(me + 1 + i, fs))

    def vec_arrival(i):
        peer = lax.rem(me + 1 + i, fs)
        return remote(vec_own, vec_all.at[peer], vec_s.at[i], vec_r.at[peer], fsdp=peer)

    each(fs - 1, lambda i: vec_copy(i).start())

    def gather_slot(s):
        pair_copy(s, k).wait_recv()
        own = g_buf[s, k, c].astype(F32) + pair_buf[s, k].astype(F32)

        def gather_in(i, acc):
            j = lax.rem(k + 1 + i, pairs)
            peer_arrival(s, j).wait_recv()
            return acc + recv_buf[s, j].astype(F32)

        own = lax.fori_loop(0, pairs - 1, gather_in, own).astype(BF16)
        for h in range(halves):
            i, n = halves * s + h, len(early) + halves * s + h
            own_buf[i] = own[h * own_buf.shape[1] : (h + 1) * own_buf.shape[1]]
            up = remote(own_buf.at[i], up_qkv.at[i], up_s.at[n], up_r.at[n], seq=mate)

            @pl.when(outer)
            def _(up=up):
                up.start()

    each(slots, gather_slot)
    advance(len(steps))
    steps.extend(plan(late))

    each(fs - 1, lambda i: vec_arrival(i).wait_recv())
    lane_from = lax.broadcasted_iota(jnp.int32, (256, 128), 0)
    lane_to = lax.broadcasted_iota(jnp.int32, (256, 128), 1)
    part, first, place = None, 0, 0
    for which, length in enumerate(lengths):
        block = length // fs
        for i in range(-(-block // 128)):
            offset = me * block + 128 * i
            row = first + offset // 128
            select = (lane_from == lane_to + lax.rem(offset, 128)).astype(F32)
            both = jnp.concatenate([vec_all[:, pl.ds(row, 1), :][:, 0], vec_all[:, pl.ds(row + 1, 1), :][:, 0]], axis=1)
            rows = lax.dot_general(
                both, select, (((1,), (0,)), ((), ())), precision=HIGHEST, preferred_element_type=F32
            )
            total_out[place : place + 1, :] = jnp.sum(rows, axis=0, keepdims=True)
            place += 1
            if which > 0:
                continue
            wide = min(128, block - i * 128)
            columns = slice(i * 128, i * 128 + wide)
            mod_rows = mod_t_ref[columns, :].astype(BF16).astype(F32)
            share = lax.dot_general(
                rows[:, :wide], mod_rows, (((1,), (0,)), ((), ())), precision=HIGHEST, preferred_element_type=F32
            )
            part = share if part is None else part + share
            outer_product = lax.dot_general(
                rows, cond_ref[...], (((0,), (0,)), ((), ())), precision=HIGHEST, preferred_element_type=F32
            )
            mod_w_out[columns, :] = outer_product[:wide]
        first += length // 128
    cond_send[...] = jnp.broadcast_to(part[:, None, :], cond_send.shape)

    def cond_copy(i):
        peer = lax.rem(me + 1 + i, fs)
        return remote(cond_send.at[peer], cond_recv.at[me], cond_s.at[i], cond_r.at[me], fsdp=peer)

    def cond_arrival(i):
        peer = lax.rem(me + 1 + i, fs)
        return remote(cond_send.at[peer], cond_recv.at[peer], cond_s.at[i], cond_r.at[peer], fsdp=peer)

    each(fs - 1, lambda i: cond_copy(i).start())
    advance(3)
    ff = up_out.shape[1]

    def write_pack(i):
        rows = pl.ds(i * tot_pack.shape[1], tot_pack.shape[1])
        up_out[rows, :] = tot_pack[i, :, :ff].astype(F32)
        out_out[rows, :] = tot_pack[i, :, ff:].astype(F32)

    def write_down(i):
        down_out[pl.ds(i * tot_down.shape[1], tot_down.shape[1]), :] = tot_down[i].astype(F32)

    @pl.when(outer)
    def _():
        for n, item in early:
            tot_copy(n, item).wait_recv()

    each(counts[0], write_pack)
    each(counts[1], write_down)
    for store in stores[1:]:
        store.start()
    advance(len(steps))
    cond_recv[me] = cond_send[me]
    each(fs - 1, lambda i: cond_arrival(i).wait_recv())
    cond_out[...] = jnp.sum(cond_recv[...], axis=0)

    @pl.when(outer)
    def _():
        for n, item in late:
            tot_copy(n, item).wait_recv()
        for n, item in chain:
            up_copy(n, item).wait_send()

    block = nz * HD
    for i in range(slots * halves):
        s, h = i // halves, i % halves
        rows = slice(h * tot_qkv.shape[1], (h + 1) * tot_qkv.shape[1])
        for p in range(3):
            columns = slice(p * width + s * block, p * width + (s + 1) * block)
            qkv_out[rows, columns] = tot_qkv[i, :, p * block : (p + 1) * block].astype(F32)

    @pl.when(inner)
    def _():
        for n, item in chain:
            twin_copy(n, item).wait_send()
            tot_copy(n, item).wait_send()

    def drain_peers(i):
        vec_copy(i).wait_send()
        cond_copy(i).wait_send()

    def drain_pairs(i):
        for s in range(slots):
            pair_copy(s, i).wait_send()

    def drain_sums(i):
        for s in range(slots):
            peer_copy(s, lax.rem(k + 1 + i, pairs)).wait_send()

    each(fs - 1, drain_peers)
    each(pairs, drain_pairs)
    each(pairs - 1, drain_sums)
    each(nz - 1, lambda i: vecz_copy(i).wait_send())
    for store in stores:
        store.wait()


def reduce_all(
    grad_rows, weights, attn_in, tokens, grad_hidden, vectors, sums, up_bias_sum, part_pack, part_down, mod_t, cond, fs, nz
):
    slots = grad_rows.shape[0]
    tok, width = tokens.shape
    shard = width // fs
    count = lambda a: 6 if a.shape[0] % 96 == 0 else 1
    counts = (count(part_pack), count(part_down))
    split = lambda a, n: a.reshape(n, a.shape[0] // n, a.shape[1])
    pack, down = split(part_pack, counts[0]), split(part_down, counts[1])
    pairs = fs // 2
    halves = 2 if shard % 32 == 0 else 1
    items = sum(counts) + slots * halves
    ff = up_bias_sum.size
    lengths = (6 * width, width, width, ff, width)
    rows = sum(lengths) // 128 + 2
    places = sum(-(-v // fs // 128) for v in lengths)
    vmem = pl.BlockSpec(memory_space=pltpu.VMEM)
    hbm = pl.BlockSpec(memory_space=pl.ANY)
    low = lambda *shape: pltpu.VMEM(shape, BF16)
    wide = lambda *shape: pltpu.VMEM(shape, F32)
    dma = lambda *shape: pltpu.SemaphoreType.DMA(shape)
    qkv_shape = (slots * halves, shard // halves, width)
    triple = [low(*pack.shape), low(*down.shape), low(*qkv_shape)]
    cols = grad_rows.shape[1] * grad_rows.shape[2]
    inputs_grad, qkv_sum, up_sum, out_sum, down_sum, total, mod_w, cond_grad = pl.pallas_call(
        partial(reduce_kernel, fs, nz, slots, counts, lengths),
        in_specs=[hbm] * 5 + [vmem] * 7,
        out_specs=[hbm, vmem, hbm, hbm, hbm, vmem, vmem, vmem],
        out_shape=[
            jax.ShapeDtypeStruct((tok, width), F32),
            jax.ShapeDtypeStruct((shard, 3 * width), F32),
            jax.ShapeDtypeStruct((shard, ff), F32),
            jax.ShapeDtypeStruct((shard, part_pack.shape[1] - ff), F32),
            jax.ShapeDtypeStruct(part_down.shape, F32),
            jax.ShapeDtypeStruct((places, 128), F32),
            jax.ShapeDtypeStruct(mod_t.shape, F32),
            jax.ShapeDtypeStruct((8, 128), F32),
        ],
        scratch_shapes=[
            wide(tok, width),
            wide(shard, ff),
            wide(shard, part_pack.shape[1] - ff),
            wide(*part_down.shape),
            dma(4),
            low(*grad_rows.shape),
            low(tok, width),
            dma(slots),
            low(slots, cols, tok),
            low(slots, width, cols),
            wide(tok, width),
            wide(tok, width),
            low(slots, pairs, 2, shard, width),
            low(slots, pairs, shard, width),
            low(slots, pairs, shard, width),
            low(slots, pairs, shard, width),
            low(*qkv_shape),
        ]
        + triple * 4
        + [
            wide(rows, 128),
            wide(nz, rows, 128),
            wide(rows, 128),
            wide(fs, rows, 128),
            wide(fs, 8, 128),
            wide(fs, 8, 128),
            dma(4),
            dma(slots, pairs),
            dma(slots, pairs),
            dma(slots, pairs),
            dma(slots, pairs),
        ]
        + [dma(items)] * 6
        + [dma(nz - 1), dma(nz), dma(fs - 1), dma(fs), dma(fs - 1), dma(fs)],
        compiler_params=pltpu.CompilerParams(vmem_limit_bytes=VMEM_LIMIT, collective_id=1, has_side_effects=True),
        cost_estimate=pl.CostEstimate(flops=12 * tok * width * cols, bytes_accessed=10**8, transcendentals=0),
        name="reduce_all",
    )(grad_rows, weights, attn_in, tokens, grad_hidden, vectors, sums, up_bias_sum, pack, down, mod_t, cond)
    blocks, place = [], 0
    for v in lengths:
        n = -(-v // fs // 128)
        blocks.append(total[place : place + n].reshape(-1)[: v // fs])
        place += n
    return inputs_grad, qkv_sum, up_sum, out_sum, down_sum, blocks, mod_w.T, cond_grad


def per_device(
    inputs,
    conditioning,
    cotangent,
    attn_gain,
    mlp_gain,
    qkv_weight,
    out_weight,
    up_weight,
    up_bias,
    down_weight,
    down_bias,
    mod_weight,
    mod_bias,
):
    n = lax.axis_size("seq")
    fs = lax.axis_size("fsdp")
    z = lax.axis_index("seq")
    tokens = inputs[0]
    tok, width = tokens.shape
    slots = H // n

    inv_freq = jnp.exp(-math.log(10000.0) * jnp.arange(HD // 2, dtype=F32) * (2.0 / HD))
    positions = jnp.arange(tok, dtype=F32)
    own_angles = inv_freq[:, None] * (positions + (z * tok).astype(F32))[None, :]
    starts = (jnp.arange(n) * tok).astype(F32)
    all_angles = inv_freq[None, :, None] * (positions[None, :] + starts[:, None])[:, None, :]
    cos_all, sin_all = jnp.cos(all_angles), jnp.sin(all_angles)

    x, heads_out, mixed, log_totals, qkv_slots, attn_in, vectors, up_bias_full, cond_low_all, pack, down = forward(
        qkv_weight,
        tokens,
        (attn_gain, mlp_gain, up_bias, down_bias),
        conditioning,
        mod_weight,
        mod_bias,
        jnp.cos(own_angles),
        jnp.sin(own_angles),
        (up_weight, out_weight, down_weight),
        fs,
        n,
    )
    w_pack, down_full = pack.reshape(width, -1), down.reshape(-1, width)
    output, grad_hidden, sums, up_bias_sum, g_down, g_pack, grad_mixed = middle(
        tokens, cotangent[0], vectors, up_bias_full, w_pack, down_full, mixed.reshape(width, tok)
    )
    grad_slots, part_pack, part_down = attend_back(
        x, grad_mixed.reshape(heads_out.shape), heads_out, log_totals, cos_all, sin_all, g_pack, g_down, fs
    )
    inputs_grad, qkv_weight_grad, up_sum, out_sum, down_sum, blocks, mod_weight_grad, cond_grad = reduce_all(
        grad_slots,
        qkv_slots.reshape(slots, width, -1),
        attn_in,
        tokens,
        grad_hidden,
        vectors,
        sums,
        up_bias_sum,
        part_pack,
        part_down,
        mod_weight.T,
        cond_low_all,
        fs,
        n,
    )
    mod_bias_grad, attn_gain_grad, mlp_gain_grad, up_bias_grad, down_bias_grad = blocks
    _, silu_pull = jax.vjp(jax.nn.silu, conditioning)
    conditioning_grad = silu_pull(cond_grad[:1])[0]
    return (
        output[None],
        inputs_grad[None],
        conditioning_grad,
        attn_gain_grad,
        mlp_gain_grad,
        qkv_weight_grad,
        out_sum,
        up_sum,
        up_bias_grad,
        down_sum,
        down_bias_grad,
        mod_weight_grad,
        mod_bias_grad,
    )


def solution(mesh):
    specs = (
        P("fsdp", "seq", None),
        P("fsdp", None),
        P("fsdp", "seq", None),
        P("fsdp"),
        P("fsdp"),
        P("fsdp", None),
        P("fsdp", None),
        P("fsdp", None),
        P("fsdp"),
        P("fsdp", None),
        P("fsdp"),
        P(None, "fsdp"),
        P("fsdp"),
    )
    out_specs = (specs[0], specs[0], specs[1]) + specs[3:]
    return jax.shard_map(per_device, mesh=mesh, in_specs=specs, out_specs=out_specs, check_vma=False)
```

```python
from functools import partial
import math

import jax
import jax.numpy as jnp
from jax import lax
from jax.experimental import pallas as pl
from jax.experimental.pallas import tpu as pltpu
from jax.sharding import PartitionSpec as P

H = 12
HD = 64
EPSILON = 1e-05
BF16 = jnp.bfloat16
F32 = jnp.float32
LOG2E = math.log2(math.e)
VMEM_LIMIT = 60 * 1024 * 1024


def mm(a, b, ca, cb):
    return lax.dot_general(a, b, (((ca,), (cb,)), ((), ())), preferred_element_type=F32)


def normalize(values):
    centre = jnp.mean(values, axis=-1, keepdims=True)
    shifted = values - centre
    variance = jnp.mean(shifted * shifted, axis=-1, keepdims=True)
    inv_std = lax.rsqrt(variance + EPSILON)
    return (shifted * inv_std, inv_std)


def norm_back(grad_hat, normed_hat, inv_std):
    mean_grad = jnp.mean(grad_hat, axis=-1, keepdims=True)
    mean_mixed = jnp.mean(grad_hat * normed_hat, axis=-1, keepdims=True)
    return inv_std * (grad_hat - mean_grad - normed_hat * mean_mixed)


MESH = pl.DeviceIdType.MESH
HIGHEST = lax.Precision.HIGHEST


def add_low(a, b):
    return (a.astype(F32) + b.astype(F32)).astype(BF16)


def remote(src, dst, s, r, **where):
    return pltpu.make_async_remote_copy(
        src_ref=src, dst_ref=dst, send_sem=s, recv_sem=r, device_id=where, device_id_type=MESH
    )


def each(count, body):
    lax.fori_loop(0, count, lambda i, _: (body(i), 0)[1], 0)


def greet(me, z, fs, nz):
    barrier = pltpu.get_barrier_semaphore()

    def hello_fsdp(i):
        peer = {"fsdp": lax.rem(me + 1 + i, fs)}
        pl.semaphore_signal(barrier, inc=1, device_id=peer, device_id_type=MESH)

    def hello_seq(i):
        peer = {"seq": lax.rem(z + 1 + i, nz)}
        pl.semaphore_signal(barrier, inc=1, device_id=peer, device_id_type=MESH)

    each(fs - 1, hello_fsdp)
    each(nz - 1, hello_seq)
    pl.semaphore_wait(barrier, fs + nz - 2)


def forward_kernel(fs, nz, slots, sub, *refs):
    (
        qkv_ref,
        tokens_hbm,
        attn_gain_ref,
        mlp_gain_ref,
        up_bias_ref,
        down_bias_ref,
        cond_ref,
        mod_w_ref,
        mod_b_ref,
        cos_ref,
        sin_ref,
        up_hbm,
        out_hbm,
        down_hbm,
        x_hbm,
        o_hbm,
        mixed_ref,
        lse_ref,
        w_hbm,
        attn_in_hbm,
        vec_ref,
        bias_ref,
        cond_out,
        pack_hbm,
        feed_hbm,
    ) = refs[:25]
    (
        x_ref,
        o_ref,
        w_ref,
        attn_in_ref,
        store_s,
        tokens_buf,
        up_buf,
        out_buf,
        down_buf,
        w_own,
        z_send,
        narrow,
        spread,
        mod_wide,
        small_send,
        small_all,
        mod_send,
        mod_recv,
        w_full,
        local_s,
        small_s,
        small_r,
        mod_s,
        mod_r,
        w_s,
        w_f,
        w_r,
        pack_own,
        feed_own,
        k_ref,
        x_s,
        x_r,
        o_s,
        o_r,
        p_s,
        p_f,
        p_r,
        own_s,
    ) = refs[25:]
    me = lax.axis_index("fsdp")
    z = lax.axis_index("seq")
    pairs = fs // 2
    k, c = me // 2, lax.rem(me, 2)
    partner = me + 1 - 2 * c
    tok, width = tokens_buf.shape
    shard = w_own.shape[1]
    ff = spread.shape[1]
    block = nz * HD

    fetch = ((tokens_hbm, tokens_buf), (up_hbm, up_buf), (out_hbm, out_buf), (down_hbm, down_buf))
    loads = [pltpu.make_async_copy(src, dst, local_s.at[i]) for i, (src, dst) in enumerate(fetch)]
    for load in loads:
        load.start()
    greet(me, z, fs, nz)

    narrow[...] = jnp.zeros_like(narrow)
    for i, piece in enumerate((attn_gain_ref, mlp_gain_ref, down_bias_ref)):
        narrow[i : i + 1, :shard] = piece[...].reshape(1, -1)
    spread[...] = jnp.zeros_like(spread)
    spread[0:1, : up_bias_ref.shape[0]] = up_bias_ref[...].reshape(1, -1)
    placed = pltpu.roll(narrow[...], me * shard, 1)
    for i in range(3):
        small_send[:, i * width : (i + 1) * width] = placed[i : i + 1]
    placed = pltpu.roll(spread[...], me * up_bias_ref.shape[0], 1)
    small_send[:, 3 * width : 3 * width + ff] = placed[0:1]
    small_send[:, 3 * width + ff :] = cond_ref[...]
    small_all[me] = small_send[...]

    def small_copy(i):
        return remote(small_send, small_all.at[me], small_s.at[i], small_r.at[me], fsdp=lax.rem(me + 1 + i, fs))

    def small_arrival(i):
        peer = lax.rem(me + 1 + i, fs)
        return remote(small_send, small_all.at[peer], small_s.at[i], small_r.at[peer], fsdp=peer)

    each(fs - 1, lambda i: small_copy(i).start())

    for s in range(slots):
        for part in range(3):
            columns = slice(part * width + s * block, part * width + (s + 1) * block)
            w_own[s, :, part * block : (part + 1) * block] = qkv_ref[:, columns].astype(BF16)
        w_ref[s, me] = w_own[s]

    def w_peer(s, i):
        j = lax.rem(k + 1 + i, pairs)
        return remote(w_own.at[s], w_ref.at[s, me], w_s.at[s, i], w_r.at[s, me], fsdp=2 * j + c)

    def w_partner(s):
        return remote(w_own.at[s], w_ref.at[s, me], w_s.at[s, pairs - 1], w_r.at[s, me], fsdp=partner)

    def w_arrival(s, j):
        return remote(w_own.at[s], w_ref.at[s, j], w_s.at[s, 0], w_r.at[s, j], fsdp=partner)

    def w_pass(s, i):
        j = 2 * lax.rem(k + 1 + i, pairs) + c
        return remote(w_ref.at[s, j], w_ref.at[s, j], w_f.at[s, i], w_r.at[s, j], fsdp=partner)

    def send_weight(s):
        each(pairs - 1, lambda i: w_peer(s, i).start())
        w_partner(s).start()

    def pass_weight(s):
        def step(i):
            w_arrival(s, 2 * lax.rem(k + 1 + i, pairs) + c).wait_recv()
            w_pass(s, i).start()

        each(pairs - 1, step)

    send_weight(0)

    each(fs - 1, lambda i: small_arrival(i).wait_recv())
    small_sum = jnp.sum(small_all[:, :, : 3 * width + ff], axis=0)
    cond_all = small_all[:, 0, 3 * width + ff :]
    cond_low = (cond_all / (1.0 + jnp.exp(-cond_all))).astype(BF16)
    cond_out[...] = cond_low.astype(F32)
    own_mod = mm(cond_low, mod_w_ref[...].astype(BF16), 1, 1) + mod_b_ref[...].reshape(1, -1)
    mod_wide[...] = jnp.zeros_like(mod_wide)
    mod_wide[:, : own_mod.shape[1]] = own_mod
    placed = pltpu.roll(mod_wide[...], me * own_mod.shape[1], 1)
    for i in range(fs):
        mod_send[i] = placed[i : i + 1]
    mod_recv[me] = mod_send[me]

    def mod_copy(i):
        peer = lax.rem(me + 1 + i, fs)
        return remote(mod_send.at[peer], mod_recv.at[me], mod_s.at[i], mod_r.at[me], fsdp=peer)

    def mod_arrival(i):
        peer = lax.rem(me + 1 + i, fs)
        return remote(mod_send.at[peer], mod_recv.at[peer], mod_s.at[i], mod_r.at[peer], fsdp=peer)

    each(fs - 1, lambda i: mod_copy(i).start())
    for s in range(1, slots):
        send_weight(s)

    attn_gain, mlp_gain, down_bias = (small_sum[:, i * width : (i + 1) * width] for i in range(3))
    for i in range(ff // width):
        bias_ref[i] = small_sum[:, (3 + i) * width : (4 + i) * width]
    for load in loads:
        load.wait()
    piece = min(256, tok)

    def normed_piece(i):
        rows = pl.ds(pl.multiple_of(i * piece, piece), piece)
        tokens_buf[rows, :] = normalize(tokens_buf[rows, :])[0] * attn_gain

    each(tok // piece, normed_piece)
    pass_weight(0)
    each(fs - 1, lambda i: mod_arrival(i).wait_recv())
    modulation = jnp.sum(mod_recv[...], axis=0)
    shift_attn, scale_attn, gate_attn, shift_mlp, scale_mlp, gate_mlp = (
        modulation[:, i * width : (i + 1) * width] for i in range(6)
    )
    kept = (gate_attn, shift_mlp, scale_mlp, gate_mlp, mlp_gain, down_bias, attn_gain, scale_attn)
    for i, v in enumerate(kept):
        vec_ref[i : i + 1, :] = v
    for i in range(tok // piece):
        rows = slice(i * piece, (i + 1) * piece)
        attn_in_ref[rows, :] = (tokens_buf[rows, :] * (1.0 + scale_attn) + shift_attn).astype(BF16)

    cosine, sine = cos_ref[...], sin_ref[...]
    half = HD // 2

    def project(s, out_ref):
        each(pairs, lambda j: w_arrival(s, 2 * j + 1 - c).wait_recv())
        if shard % 16 == 0:
            weight = w_ref[s].reshape(fs * shard, 3 * block)
        else:
            for i in range(fs):
                w_full[i * shard : (i + 1) * shard, :] = w_ref[s, i].astype(F32)
            weight = w_full[...].astype(BF16)
        rows = mm(weight, attn_in_ref[...], 0, 1).astype(BF16)
        for shard_of in range(nz):
            for part in range(3):
                base = (part * nz + shard_of) * HD
                if part == 2:
                    out_ref[shard_of, part * HD : (part + 1) * HD, :] = rows[base : base + HD]
                else:
                    a = rows[base : base + half].astype(F32)
                    b = rows[base + half : base + HD].astype(F32)
                    out_ref[shard_of, part * HD : part * HD + half, :] = (a * cosine - b * sine).astype(BF16)
                    out_ref[shard_of, part * HD + half : (part + 1) * HD, :] = (b * cosine + a * sine).astype(BF16)

    def x_copy(s, i):
        peer = lax.rem(z + 1 + i, nz)
        return remote(z_send.at[s, peer], x_ref.at[s, z], x_s.at[s, i], x_r.at[s, z], seq=peer)

    def x_arrival(s, i):
        peer = lax.rem(z + 1 + i, nz)
        return remote(z_send.at[s, peer], x_ref.at[s, peer], x_s.at[s, i], x_r.at[s, peer], seq=peer)

    def o_copy(s, i):
        peer = lax.rem(z + 1 + i, nz)
        return remote(o_ref.at[s, peer], mixed_ref.at[s, z], o_s.at[s, i], o_r.at[s, z], seq=peer)

    def o_arrival(s, i):
        peer = lax.rem(z + 1 + i, nz)
        return remote(o_ref.at[s, peer], mixed_ref.at[s, peer], o_s.at[s, i], o_r.at[s, peer], seq=peer)

    def send_slot(s):
        project(s, z_send.at[s])
        each(nz - 1, lambda i: x_copy(s, i).start())
        x_ref[s, z] = z_send[s, z]

    def next_slot(s):
        @pl.when(s > 0)
        def _():
            pass_weight(s)

        send_slot(s)

    each(slots, next_slot)
    results = ((w_ref, w_hbm), (attn_in_ref, attn_in_hbm), (x_ref, x_hbm), (o_ref, o_hbm))
    stores = [pltpu.make_async_copy(src, dst, store_s.at[i]) for i, (src, dst) in enumerate(results)]
    for store in stores[:2]:
        store.start()

    pack_own[:, :ff] = up_buf[...].astype(BF16)
    pack_own[:, ff:] = out_buf[...].astype(BF16)
    feed_own[...] = down_buf[...].astype(BF16)
    bulk = ((pack_own, pack_hbm), (feed_own, feed_hbm))

    def p_peer(a, i):
        j = lax.rem(k + 1 + i, pairs)
        own, whole = bulk[a]
        return remote(own, whole.at[me], p_s.at[a, i], p_r.at[a, me], fsdp=2 * j + c)

    def p_partner(a):
        own, whole = bulk[a]
        return remote(own, whole.at[me], p_s.at[a, pairs - 1], p_r.at[a, me], fsdp=partner)

    def p_arrival(a, j):
        own, whole = bulk[a]
        return remote(own, whole.at[j], p_s.at[a, 0], p_r.at[a, j], fsdp=partner)

    def p_pass(a, i):
        j = 2 * lax.rem(k + 1 + i, pairs) + c
        whole = bulk[a][1]
        return remote(whole.at[j], whole.at[j], p_f.at[a, i], p_r.at[a, j], fsdp=partner)

    def p_own(a):
        own, whole = bulk[a]
        return pltpu.make_async_copy(own, whole.at[me], own_s.at[a])

    for a in range(2):
        each(pairs - 1, lambda i: p_peer(a, i).start())
        p_partner(a).start()
        p_own(a).start()

    def pass_bulk(a):
        def step(i):
            p_arrival(a, 2 * lax.rem(k + 1 + i, pairs) + c).wait_recv()
            p_pass(a, i).start()

        each(pairs - 1, step)

    scale = LOG2E / math.sqrt(HD)
    part_width = tok // sub

    def soft(s):
        top = jnp.max(s, axis=0, keepdims=True) * scale
        p = jnp.exp2(s * scale - top)
        total = jnp.sum(p, axis=0, keepdims=True)
        return top, total, p.astype(BF16)

    def slot(s):
        each(nz - 1, lambda i: x_arrival(s, i).wait_recv())
        for shard_of in range(nz):
            k_ref[shard_of * tok : (shard_of + 1) * tok, :] = x_ref[s, shard_of, HD : 2 * HD, :].T

        def one_shard(i):
            step = lax.rem(z + 1 + i, nz)

            def score(j):
                q = x_ref[s, step, 0:HD, j * part_width : (j + 1) * part_width]
                return mm(k_ref[...], q, 1, 0)

            def mix(j, top, total, p):
                o = None
                for shard_of in range(nz):
                    part = mm(x_ref[s, shard_of, 2 * HD : 3 * HD, :], p[shard_of * tok : (shard_of + 1) * tok], 1, 0)
                    o = part if o is None else o + part
                o_ref[s, step, :, j * part_width : (j + 1) * part_width] = (o / total).astype(BF16)
                lse_ref[s, step, :, j * part_width : (j + 1) * part_width] = top + jnp.log2(total)

            scores = [score(0)]
            pending = None
            for j in range(sub):
                if j + 1 < sub:
                    scores.append(score(j + 1))
                done = soft(scores[j])
                if pending is not None:
                    mix(j - 1, *pending)
                pending = done
            mix(sub - 1, *pending)

            @pl.when(i < nz - 1)
            def _():
                o_copy(s, i).start()

        each(nz, one_shard)
        mixed_ref[s, z] = o_ref[s, z]

        @pl.when(s == slots - 2)
        def _():
            pass_bulk(0)

    each(slots, slot)
    for store in stores[2:]:
        store.start()
    pass_bulk(1)

    def drain_slots(s):
        each(nz - 1, lambda i: o_arrival(s, i).wait_recv())
        each(nz - 1, lambda i: o_copy(s, i).wait_send())
        each(nz - 1, lambda i: x_copy(s, i).wait_send())

    each(slots, drain_slots)
    for a in range(2):
        each(pairs, lambda j: p_arrival(a, 2 * j + 1 - c).wait_recv())
        each(pairs - 1, lambda i: p_peer(a, i).wait_send())
        each(pairs - 1, lambda i: p_pass(a, i).wait_send())
        p_partner(a).wait_send()
        p_own(a).wait()
    for store in stores:
        store.wait()

    def drain_peers(i):
        small_copy(i).wait_send()
        mod_copy(i).wait_send()

    def drain_weights(i):
        for s in range(slots):
            w_peer(s, i).wait_send()
            w_pass(s, i).wait_send()

    each(fs - 1, drain_peers)
    each(pairs - 1, drain_weights)
    for s in range(slots):
        w_partner(s).wait_send()


def forward(qkv_weight, tokens, gains, cond, mod_weight, mod_bias, cosine, sine, feed, fs, nz):
    slots = H // nz
    tok, width = tokens.shape
    shard = qkv_weight.shape[0]
    pairs = fs // 2
    up, out, down = feed
    ff = gains[2].shape[0] * fs
    vmem = pl.BlockSpec(memory_space=pltpu.VMEM)
    hbm = pl.BlockSpec(memory_space=pl.ANY)
    low = lambda *shape: pltpu.VMEM(shape, BF16)
    wide = lambda *shape: pltpu.VMEM(shape, F32)
    dma = lambda *shape: pltpu.SemaphoreType.DMA(shape)
    head_shape = (slots, nz, 3 * HD, tok)
    pack_shape = (shard, up.shape[1] + out.shape[1])
    length = nz * tok
    cols = 3 * nz * HD
    small = 3 * width + ff + cond.shape[-1]
    return pl.pallas_call(
        partial(forward_kernel, fs, nz, slots, 2),
        in_specs=[vmem, hbm] + [vmem] * 9 + [hbm] * 3,
        out_specs=[hbm, hbm, vmem, vmem, hbm, hbm, vmem, vmem, vmem, hbm, hbm],
        out_shape=[
            jax.ShapeDtypeStruct(head_shape, BF16),
            jax.ShapeDtypeStruct((slots, nz, HD, tok), BF16),
            jax.ShapeDtypeStruct((slots, nz, HD, tok), BF16),
            jax.ShapeDtypeStruct((slots, nz, 1, tok), F32),
            jax.ShapeDtypeStruct((slots, fs, shard, cols), BF16),
            jax.ShapeDtypeStruct((tok, width), BF16),
            jax.ShapeDtypeStruct((8, width), F32),
            jax.ShapeDtypeStruct((ff // width, 1, width), F32),
            jax.ShapeDtypeStruct((fs, cond.shape[-1]), F32),
            jax.ShapeDtypeStruct((fs, *pack_shape), BF16),
            jax.ShapeDtypeStruct((fs, *down.shape), BF16),
        ],
        scratch_shapes=[
            low(*head_shape),
            low(slots, nz, HD, tok),
            low(slots, fs, shard, cols),
            low(tok, width),
            dma(4),
            wide(tok, width),
            wide(*up.shape),
            wide(*out.shape),
            wide(*down.shape),
            low(slots, shard, cols),
            low(*head_shape),
            wide(8, width),
            wide(8, ff),
            wide(fs, 6 * width),
            wide(1, small),
            wide(fs, 1, small),
            wide(fs, 1, 6 * width),
            wide(fs, 1, 6 * width),
            wide(*((8, 128) if shard % 16 == 0 else (width, cols))),
            dma(4),
            dma(fs - 1),
            dma(fs),
            dma(fs - 1),
            dma(fs),
            dma(slots, pairs),
            dma(slots, pairs),
            dma(slots, fs),
            low(*pack_shape),
            low(*down.shape),
            low(length, HD),
            dma(slots, nz - 1),
            dma(slots, nz),
            dma(slots, nz - 1),
            dma(slots, nz),
            dma(2, pairs),
            dma(2, pairs),
            dma(2, fs),
            dma(2),
        ],
        compiler_params=pltpu.CompilerParams(vmem_limit_bytes=VMEM_LIMIT, collective_id=2, has_side_effects=True),
        cost_estimate=pl.CostEstimate(
            flops=16 * slots * length * length * HD, bytes_accessed=10**7, transcendentals=slots * length * length
        ),
        name="forward",
    )(
        qkv_weight,
        tokens,
        *gains,
        cond,
        mod_weight.T,
        mod_bias,
        cosine,
        sine,
        *feed,
    )


def attend_back_kernel(
    fs,
    n,
    slots,
    tok,
    sub,
    x_hbm,
    sent_ref,
    o_hbm,
    lse_ref,
    cos_hbm,
    sin_hbm,
    pack_hbm,
    down_hbm,
    out_ref,
    part_pack,
    part_down,
    x_ref,
    o_ref,
    cos_ref,
    sin_ref,
    load_s,
    own_pack,
    own_down,
    pair_pack,
    pair_down,
    recv_pack,
    recv_down,
    own_s,
    pair_s,
    pair_r,
    peer_s,
    peer_r,
    g_ref,
    d_ref,
    k_ref,
    v_ref,
    q_all,
    g_all,
    lse_all,
    centre_all,
    dq_ref,
    g_s,
    g_r,
    q_s,
    q_r,
    kv_s,
    kv_r,
):
    z = lax.axis_index("seq")
    half = HD // 2
    me = lax.axis_index("fsdp")
    pairs = fs // 2
    k, c = me // 2, lax.rem(me, 2)
    partner = me + 1 - 2 * c
    bulk = ((pack_hbm, own_pack, pair_pack, recv_pack, part_pack), (down_hbm, own_down, pair_down, recv_down, part_down))

    def own_load(a, j):
        return pltpu.make_async_copy(bulk[a][0].at[j, c], bulk[a][1].at[j], own_s.at[a, j])

    def pair_copy(a, j):
        return remote(bulk[a][0].at[j, 1 - c], bulk[a][2].at[j], pair_s.at[a, j], pair_r.at[a, j], fsdp=partner)

    def peer_copy(a, j):
        return remote(bulk[a][1].at[j], bulk[a][3].at[k], peer_s.at[a, j], peer_r.at[a, k], fsdp=2 * j + c)

    def peer_arrival(a, j):
        return remote(bulk[a][1].at[j], bulk[a][3].at[j], peer_s.at[a, j], peer_r.at[a, j], fsdp=2 * j + c)

    def forward_bulk(a):
        own, pair = bulk[a][1:3]

        def one(i):
            j = lax.rem(k + 1 + i, pairs)
            own_load(a, j).wait()
            pair_copy(a, j).wait_recv()
            own[j] = add_low(own[j], pair[j])
            peer_copy(a, j).start()

        each(pairs - 1, one)

    def finish_bulk(a):
        _, own, pair, recv, part = bulk[a]
        own_load(a, k).wait()
        pair_copy(a, k).wait_recv()
        each(pairs - 1, lambda i: peer_arrival(a, lax.rem(k + 1 + i, pairs)).wait_recv())
        height = part.shape[0]
        block = 32 if height % 32 == 0 else height

        def one(b):
            rows = pl.ds(b * block, block)
            total = own[k, rows].astype(F32) + pair[k, rows].astype(F32)
            for i in range(pairs - 1):
                total = total + recv[lax.rem(k + 1 + i, pairs), rows].astype(F32)
            part[rows, :] = total.astype(BF16)

        each(height // block, one)

    def drain_bulk(a):
        each(pairs, lambda j: pair_copy(a, j).wait_send())
        each(pairs - 1, lambda i: peer_copy(a, lax.rem(k + 1 + i, pairs)).wait_send())

    fetch = ((x_hbm, x_ref), (o_hbm, o_ref), (cos_hbm, cos_ref), (sin_hbm, sin_ref))
    loads = [pltpu.make_async_copy(src, dst, load_s.at[i]) for i, (src, dst) in enumerate(fetch)]
    for load in loads:
        load.start()
    for a in range(2):
        each(pairs, lambda j: own_load(a, j).start())
    greet(me, z, fs, n)

    def g_copy(s, i):
        peer = lax.rem(z + 1 + i, n)
        return remote(sent_ref.at[s, peer], g_ref.at[s, z], g_s.at[s, i], g_r.at[s, z], seq=peer)

    def g_arrival(s, i):
        peer = lax.rem(z + 1 + i, n)
        return remote(sent_ref.at[s, peer], g_ref.at[s, peer], g_s.at[s, i], g_r.at[s, peer], seq=peer)

    def part_copy(s, i, rows, send, recv, arrival):
        peer = lax.rem(z + 1 + i, n)
        slot = peer if arrival else z
        return remote(
            d_ref.at[s, peer, rows], out_ref.at[s, slot, rows], send.at[s, i], recv.at[s, slot], seq=peer
        )

    q_rows, kv_rows = pl.ds(0, HD), pl.ds(HD, 2 * HD)
    q_copy = lambda s, i, arrival=False: part_copy(s, i, q_rows, q_s, q_r, arrival)
    kv_copy = lambda s, i, arrival=False: part_copy(s, i, kv_rows, kv_s, kv_r, arrival)

    for s in range(slots):
        each(n - 1, lambda i: g_copy(s, i).start())
        g_ref[s, z] = sent_ref[s, z]
    for a in range(2):
        each(pairs, lambda i: pair_copy(a, lax.rem(k + 1 + i, pairs)).start())

    scale = LOG2E / math.sqrt(HD)
    width = tok // sub

    def turn_back(grad, cosine, sine):
        a, b = grad[:half], grad[half:]
        return (a * cosine + b * sine).astype(BF16), (b * cosine - a * sine).astype(BF16)

    def slot(s):
        for owner in range(n):
            cols = slice(owner * tok, (owner + 1) * tok)
            k_ref[cols, :] = x_ref[s, owner, HD : 2 * HD, :].T
            v_ref[cols, :] = x_ref[s, owner, 2 * HD : 3 * HD, :].T
            q_all[:, cols] = x_ref[s, owner, 0:HD, :]
            lse_all[:, cols] = lse_ref[s, owner]
        each(n - 1, lambda i: g_arrival(s, i).wait_recv())
        for owner in range(n):
            cols = slice(owner * tok, (owner + 1) * tok)
            g = g_ref[s, owner]
            g_all[:, cols] = g
            centre_all[:, cols] = jnp.sum(g.astype(F32) * o_ref[s, owner].astype(F32), axis=0, keepdims=True)
        dq_ref[...] = jnp.zeros_like(dq_ref)

        def shard(i):
            step = lax.rem(z + 1 + i, n)
            for j in range(sub):
                cols = slice(j * width, (j + 1) * width)
                rows = pl.ds(pl.multiple_of(step * tok + j * width, width), width)
                score = mm(k_ref[rows, :], q_all[...], 1, 0)
                dp = mm(v_ref[rows, :], g_all[...], 1, 0)
                p = jnp.exp2(score * scale - lse_all[...])
                p_low = p.astype(BF16)
                ds = (p * (dp - centre_all[...])).astype(BF16)
                dv = mm(g_all[...], p_low, 1, 1)
                dk = mm(q_all[...], ds, 1, 1) * (1.0 / math.sqrt(HD))
                dq_ref[...] += mm(x_ref[s, step, HD : 2 * HD, cols], ds, 1, 0)
                a, b = turn_back(dk, cos_ref[step, :, cols], sin_ref[step, :, cols])
                d_ref[s, step, HD : HD + half, cols] = a
                d_ref[s, step, HD + half : 2 * HD, cols] = b
                d_ref[s, step, 2 * HD : 3 * HD, cols] = dv.astype(BF16)

            @pl.when(i < n - 1)
            def _():
                kv_copy(s, i).start()

        each(n, shard)
        for owner in range(n):
            dq = dq_ref[:, owner * tok : (owner + 1) * tok] * (1.0 / math.sqrt(HD))
            a, b = turn_back(dq, cos_ref[owner], sin_ref[owner])
            d_ref[s, owner, 0:half, :] = a
            d_ref[s, owner, half:HD, :] = b
        each(n - 1, lambda i: q_copy(s, i).start())
        out_ref[s, z] = d_ref[s, z]

        @pl.when(s == 0)
        def _():
            for a in range(2):
                forward_bulk(a)

    for load in loads:
        load.wait()
    each(slots, slot)
    for a in range(2):
        finish_bulk(a)
        drain_bulk(a)

    def drain(s):
        def one(i):
            q_copy(s, i, True).wait_recv()
            kv_copy(s, i, True).wait_recv()
            g_copy(s, i).wait_send()
            q_copy(s, i).wait_send()
            kv_copy(s, i).wait_send()

        each(n - 1, one)

    each(slots, drain)


def attend_back(x, g, o, lse, cosine, sine, g_pack, g_down, fs):
    slots, n, _, tok = x.shape
    length = n * tok
    vmem, hbm = pl.BlockSpec(memory_space=pltpu.VMEM), pl.BlockSpec(memory_space=pl.ANY)
    dma = lambda *shape: pltpu.SemaphoreType.DMA(shape)
    pairs = fs // 2
    shards = [(v.shape[0] // fs, v.shape[1]) for v in (g_pack, g_down)]
    split = lambda v: v.reshape(pairs, 2, v.shape[0] // fs, v.shape[1])
    return pl.pallas_call(
        partial(attend_back_kernel, fs, n, slots, tok, 2),
        in_specs=[hbm, vmem, hbm, vmem] + [hbm] * 4,
        out_specs=[vmem] * 3,
        out_shape=[
            jax.ShapeDtypeStruct(x.shape, BF16),
            jax.ShapeDtypeStruct(shards[0], BF16),
            jax.ShapeDtypeStruct(shards[1], BF16),
        ],
        scratch_shapes=[pltpu.VMEM(x.shape, BF16), pltpu.VMEM(o.shape, BF16)]
        + [pltpu.VMEM(cosine.shape, F32)] * 2
        + [dma(4)]
        + [pltpu.VMEM((pairs, *shard), BF16) for shard in shards * 3]
        + [dma(2, pairs)] * 5
        + [
            pltpu.VMEM(g.shape, BF16),
            pltpu.VMEM(x.shape, BF16),
            pltpu.VMEM((length, HD), BF16),
            pltpu.VMEM((length, HD), BF16),
            pltpu.VMEM((HD, length), BF16),
            pltpu.VMEM((HD, length), BF16),
            pltpu.VMEM((1, length), F32),
            pltpu.VMEM((1, length), F32),
            pltpu.VMEM((HD, length), F32),
        ]
        + [dma(slots, n - 1), dma(slots, n)] * 3,
        compiler_params=pltpu.CompilerParams(vmem_limit_bytes=VMEM_LIMIT, collective_id=4, has_side_effects=True),
        cost_estimate=pl.CostEstimate(
            flops=40 * slots * length * length * HD, bytes_accessed=10**7, transcendentals=slots * length * length
        ),
        name="attend_back",
    )(x, g, o, lse, cosine, sine, split(g_pack), split(g_down))


GELU_C = math.sqrt(2.0 / math.pi)
GELU_A = 0.044715


def middle_kernel(
    blocks,
    tokens_hbm,
    cot_hbm,
    vec_ref,
    bias_ref,
    up_ref,
    down_ref,
    out_w_ref,
    mixed_ref,
    output_hbm,
    grad_hidden_hbm,
    sums_ref,
    bias_grad_ref,
    g_down_ref,
    g_pack_ref,
    grad_mixed_ref,
    attn_out_ref,
    mlp_in_ref,
    low_ref,
    back_ref,
    tokens_ref,
    cot_ref,
    output_ref,
    grad_hidden_ref,
    copy_s,
):
    j = pl.program_id(0)
    tok, width = tokens_ref.shape
    gate_attn, shift, scale, gate, gain, down_bias = (vec_ref[i : i + 1, :] for i in range(6))
    piece = min(256, tok)
    pieces = tok // piece

    @pl.when(j == 0)
    def _():
        fetch = ((tokens_hbm, tokens_ref), (cot_hbm, cot_ref))
        loads = [pltpu.make_async_copy(src, dst, copy_s.at[i]) for i, (src, dst) in enumerate(fetch)]
        for load in loads:
            load.start()
        attn_out_ref[...] = mm(mixed_ref[...], out_w_ref[...], 0, 0)
        for load in loads:
            load.wait()

        def prepare(i, _):
            rows = pl.ds(pl.multiple_of(i * piece, piece), piece)
            hidden = tokens_ref[rows, :] + gate_attn * attn_out_ref[rows, :]
            grad_hidden_ref[rows, :] = hidden
            hat, _ = normalize(hidden)
            mlp_in_ref[rows, :] = (hat * gain * (1.0 + scale) + shift).astype(BF16)
            low_ref[rows, :] = (gate * cot_ref[rows, :]).astype(BF16)
            return 0

        lax.fori_loop(0, pieces, prepare, 0)
        output_ref[...] = jnp.zeros_like(output_ref)
        back_ref[...] = jnp.zeros_like(back_ref)

    @pl.when(j < blocks)
    def _():
        mlp_in, low = mlp_in_ref[...], low_ref[...]
        x = mm(mlp_in, up_ref[...], 1, 0) + bias_ref[0]
        grad_act = mm(low, down_ref[...], 1, 1)
        square = x * x
        t = jnp.tanh(x * (GELU_C + GELU_C * GELU_A * square))
        half = 0.5 + 0.5 * t
        act = (x * half).astype(BF16)
        slope = half + x * (0.5 - 0.5 * t * t) * (GELU_C + 3.0 * GELU_C * GELU_A * square)
        grad_pre = grad_act * slope
        bias_grad_ref[0] = jnp.sum(grad_pre, axis=0, keepdims=True)
        pre_low = grad_pre.astype(BF16)
        output_ref[...] += mm(act, down_ref[...], 1, 0)
        back_ref[...] += mm(pre_low, up_ref[...], 1, 1)
        g_down_ref[...] = mm(act, low, 0, 0).astype(BF16)
        g_pack_ref[...] = mm(mlp_in, pre_low, 0, 0).astype(BF16)

    @pl.when(j == blocks)
    def _():
        def finish(i, sums):
            rows = pl.ds(pl.multiple_of(i * piece, piece), piece)
            cot = cot_ref[rows, :]
            branch = output_ref[rows, :] + down_bias
            hidden = grad_hidden_ref[rows, :]
            output_ref[rows, :] = hidden + gate * branch
            hat, inv = normalize(hidden)
            back = back_ref[rows, :]
            grad_hidden = cot + norm_back(back * ((1.0 + scale) * gain), hat, inv)
            grad_hidden_ref[rows, :] = grad_hidden
            low_ref[rows, :] = (gate_attn * grad_hidden).astype(BF16)
            adds = (grad_hidden * attn_out_ref[rows, :], back, back * hat, cot * branch, cot)
            return tuple(a + jnp.sum(v, axis=0, keepdims=True) for a, v in zip(sums, adds))

        zero = jnp.zeros((1, width), F32)
        sums = lax.fori_loop(0, pieces, finish, (zero,) * 5)
        for i in range(5):
            sums_ref[i : i + 1, :] = sums[i]
        results = ((output_ref, output_hbm), (grad_hidden_ref, grad_hidden_hbm))
        stores = [pltpu.make_async_copy(src, dst, copy_s.at[2 + i]) for i, (src, dst) in enumerate(results)]
        for store in stores:
            store.start()
        attn_low = low_ref[...]
        g_pack_ref[...] = mm(mixed_ref[...], attn_low, 1, 0).astype(BF16)
        grad_mixed_ref[...] = mm(out_w_ref[...], attn_low, 1, 1).astype(BF16)
        for store in stores:
            store.wait()


def middle(tokens, cot, vectors, up_bias, w_pack, w_down, mixed):
    tok, width = tokens.shape
    ff = w_down.shape[0]
    blocks = ff // width
    whole = lambda shape: pl.BlockSpec(shape, lambda j: (0,) * len(shape), pipeline_mode=pl.Buffered(1))
    fixed = lambda shape: pl.BlockSpec(shape, lambda j: (0,) * len(shape))
    last = blocks - 1
    flops = 2 * tok * width * (6 * ff + 3 * width)
    hbm = pl.BlockSpec(memory_space=pl.ANY)
    return pl.pallas_call(
        partial(middle_kernel, blocks),
        grid=(blocks + 1,),
        in_specs=[
            hbm,
            hbm,
            whole(vectors.shape),
            pl.BlockSpec((1, 1, width), lambda j: (jnp.minimum(j, last), 0, 0)),
            pl.BlockSpec((width, width), lambda j: (0, jnp.minimum(j, last))),
            pl.BlockSpec((width, width), lambda j: (jnp.minimum(j, last), 0)),
            pl.BlockSpec((width, width), lambda j: (0, blocks), pipeline_mode=pl.Buffered(1)),
        ]
        + [whole(mixed.shape)],
        out_specs=[
            hbm,
            hbm,
            fixed((8, width)),
            pl.BlockSpec((1, 1, width), lambda j: (jnp.minimum(j, last), 0, 0)),
            pl.BlockSpec((width, width), lambda j: (jnp.minimum(j, last), 0)),
            pl.BlockSpec((width, width), lambda j: (0, j)),
        ]
        + [fixed(mixed.shape)],
        out_shape=[
            jax.ShapeDtypeStruct((tok, width), F32),
            jax.ShapeDtypeStruct((tok, width), F32),
            jax.ShapeDtypeStruct((8, width), F32),
            jax.ShapeDtypeStruct((blocks, 1, width), F32),
            jax.ShapeDtypeStruct((ff, width), BF16),
            jax.ShapeDtypeStruct((width, ff + width), BF16),
        ]
        + [jax.ShapeDtypeStruct(mixed.shape, BF16)],
        scratch_shapes=[
            pltpu.VMEM((tok, width), F32),
            pltpu.VMEM((tok, width), BF16),
            pltpu.VMEM((tok, width), BF16),
            pltpu.VMEM((tok, width), F32),
        ]
        + [pltpu.VMEM((tok, width), F32)] * 4
        + [pltpu.SemaphoreType.DMA((4,))],
        compiler_params=pltpu.CompilerParams(vmem_limit_bytes=VMEM_LIMIT),
        cost_estimate=pl.CostEstimate(flops=flops, bytes_accessed=6 * ff * width * 2, transcendentals=tok * ff),
        name="middle",
    )(tokens, cot, vectors, up_bias, w_pack, w_down, w_pack, mixed)


def reduce_kernel(fs, nz, slots, counts, lengths, *refs):
    swapped_hbm, w_hbm, attn_in_hbm, tokens_hbm, hidden_hbm, vec_in_ref, sums_ref, up_bias_ref, *refs = refs
    bulk_refs, (mod_t_ref, cond_ref), refs = refs[:2], refs[2:4], refs[4:]
    inputs_hbm, qkv_out, up_hbm, out_hbm, down_hbm, total_out, mod_w_out, cond_out = refs[:8]
    (
        inputs_out,
        up_out,
        out_out,
        down_out,
        store_s,
        swapped_ref,
        attn_in_ref,
        swap_s,
        row_buf,
        w_buf,
        tokens_buf,
        hidden_buf,
        g_buf,
        pair_buf,
        sum_buf,
        recv_buf,
        own_buf,
        up_pack,
        up_down,
        up_qkv,
        part_pack,
        part_down,
        part_qkv,
        twin_pack,
        twin_down,
        twin_qkv,
        tot_pack,
        tot_down,
        tot_qkv,
        vec_buf,
        vec_z,
        vec_own,
        vec_all,
        cond_send,
        cond_recv,
        local_s,
        pair_s,
        pair_r,
        peer_s,
        peer_r,
        up_s,
        up_r,
        twin_s,
        twin_r,
        tot_s,
        tot_r,
        vecz_s,
        vecz_r,
        vec_s,
        vec_r,
        cond_s,
        cond_r,
    ) = refs[8:]
    me = lax.axis_index("fsdp")
    z = lax.axis_index("seq")
    pairs = fs // 2
    k, c = me // 2, lax.rem(me, 2)
    partner = me + 1 - 2 * c
    inner = jnp.logical_or(z == nz // 2 - 1, z == nz // 2)
    outer = jnp.logical_not(inner)
    twin = nz - 1 - z
    mate = z + 1 - 2 * lax.rem(z, 2)
    tok, width = tokens_buf.shape
    shard = g_buf.shape[3]
    groups = width // 128

    def swap_load(s):
        return pltpu.make_async_copy(swapped_hbm.at[s], swapped_ref.at[s], swap_s.at[s])

    first_load = pltpu.make_async_copy(attn_in_hbm, attn_in_ref, local_s.at[3])
    first_load.start()
    for s in range(slots):
        swap_load(s).start()
    fetch = ((w_hbm, w_buf), (tokens_hbm, tokens_buf), (hidden_hbm, hidden_buf))
    loads = [pltpu.make_async_copy(src, dst, local_s.at[i]) for i, (src, dst) in enumerate(fetch)]
    for load in loads:
        load.start()
    greet(me, z, fs, nz)

    bulk = [
        (src, up, part, other, tot, i)
        for src, up, part, other, tot, count in (
            (bulk_refs[0], up_pack, part_pack, twin_pack, tot_pack, counts[0]),
            (bulk_refs[1], up_down, part_down, twin_down, tot_down, counts[1]),
        )
        for i in range(count)
    ]
    halves = own_buf.shape[0] // slots
    last = [(own_buf, up_qkv, part_qkv, twin_qkv, tot_qkv, i) for i in range(slots * halves)]
    chain = list(enumerate(bulk + last))
    early, late = chain[: len(bulk)], chain[len(bulk) :]

    def up_copy(n, item):
        src, up, _, _, _, i = item
        return remote(src.at[i], up.at[i], up_s.at[n], up_r.at[n], seq=mate)

    def twin_copy(n, item):
        _, _, part, other, _, i = item
        return remote(part.at[i], other.at[i], twin_s.at[n], twin_r.at[n], seq=twin)

    def tot_copy(n, item):
        tot, i = item[4], item[5]
        return remote(tot.at[i], tot.at[i], tot_s.at[n], tot_r.at[n], seq=mate)

    def chain_in(n, item):
        src, up, part, _, _, i = item
        up_copy(n, item).wait_recv()
        part[i] = add_low(src[i], up[i])
        twin_copy(n, item).start()

    def chain_out(n, item):
        _, _, part, other, tot, i = item
        twin_copy(n, item).wait_recv()
        tot[i] = add_low(part[i], other[i])
        tot_copy(n, item).start()

    def plan(items):
        ahead = 2
        steps = [(chain_in, item) for item in items[:ahead]]
        for before, item in zip(items, items[ahead:]):
            steps += [(chain_in, item), (chain_out, before)]
        return steps + [(chain_out, item) for item in items[-ahead:]]

    steps = plan(early)

    def advance(count):
        todo = [steps.pop(0) for _ in range(min(count, len(steps)))]
        if todo:

            @pl.when(inner)
            def _():
                for step, (n, item) in todo:
                    step(n, item)

    half = len(early) - len(early) // 3

    @pl.when(outer)
    def _():
        for n, item in early[:half]:
            up_copy(n, item).start()

    def pair_copy(s, j):
        return remote(g_buf.at[s, j, 1 - c], pair_buf.at[s, j], pair_s.at[s, j], pair_r.at[s, j], fsdp=partner)

    def peer_copy(s, j):
        return remote(sum_buf.at[s, j], recv_buf.at[s, k], peer_s.at[s, j], peer_r.at[s, k], fsdp=2 * j + c)

    def peer_arrival(s, j):
        return remote(sum_buf.at[s, j], recv_buf.at[s, j], peer_s.at[s, j], peer_r.at[s, j], fsdp=2 * j + c)

    first_load.wait()

    def project_grad(s):
        swap_load(s).wait()
        for head in range(nz):
            for p in range(3):
                base = (p * nz + head) * HD
                row_buf[s, base : base + HD, :] = swapped_ref[s, head, p * HD : (p + 1) * HD, :]
        grad = mm(attn_in_ref[...], row_buf[s], 0, 1).astype(BF16)
        for i in range(fs):
            g_buf[s, i // 2, i % 2] = grad[i * shard : (i + 1) * shard]
        each(pairs, lambda i: pair_copy(s, lax.rem(k + 1 + i, pairs)).start())


    def forward(s, i):
        j = lax.rem(k + 1 + i, pairs)
        pair_copy(s, j).wait_recv()
        sum_buf[s, j] = add_low(g_buf[s, j, c], pair_buf[s, j])
        peer_copy(s, j).start()

    def stage(s):
        @pl.when(s < slots)
        def _():
            project_grad(s)

        @pl.when(s > 0)
        def _():
            each(pairs - 1, lambda i: forward(s - 1, i))

    each(slots + 1, stage)
    advance(3)
    for load in loads:
        load.wait()

    scale_mlp, gate_mlp, mlp_gain = (vec_in_ref[i : i + 1, :] for i in (2, 3, 4))
    attn_gain, scale_attn = (vec_in_ref[i : i + 1, :] for i in (6, 7))
    piece = min(256, tok)

    def norm_piece(i, kept):
        back_sum, hat_sum = kept
        rows = pl.ds(pl.multiple_of(i * piece, piece), piece)
        grad = None
        for s in range(slots):
            part = mm(row_buf[s, :, rows], w_buf[s], 0, 1)
            grad = part if grad is None else grad + part
        hat, inv = normalize(tokens_buf[rows, :])
        scaled = grad * ((1.0 + scale_attn) * attn_gain)
        inputs_out[rows, :] = hidden_buf[rows, :] + norm_back(scaled, hat, inv)
        back_sum = back_sum + jnp.sum(grad, axis=0, keepdims=True)
        hat_sum = hat_sum + jnp.sum(grad * hat, axis=0, keepdims=True)
        return back_sum, hat_sum

    zero = jnp.zeros((1, width), F32)
    kept = (zero, zero)
    for i in range(tok // piece):
        kept = norm_piece(i, kept)
        advance(4)
    back_sum, hat_sum = kept
    results = ((inputs_out, inputs_hbm), (up_out, up_hbm), (out_out, out_hbm), (down_out, down_hbm))
    stores = [pltpu.make_async_copy(src, dst, store_s.at[i]) for i, (src, dst) in enumerate(results)]
    stores[0].start()

    sums = [sums_ref[i : i + 1, :] for i in range(5)]
    vectors = [back_sum, hat_sum * attn_gain, sums[0], sums[1], sums[2] * mlp_gain, sums[3]]
    vectors += [hat_sum * (1.0 + scale_attn), sums[2] * (1.0 + scale_mlp)]
    vectors += [up_bias_ref[i] for i in range(up_bias_ref.shape[0])]
    vectors.append(sums[4] * gate_mlp)
    for p, v in enumerate(vectors):
        for i in range(groups):
            vec_buf[p * groups + i : p * groups + i + 1, :] = v[:, i * 128 : (i + 1) * 128]
    used = len(vectors) * groups
    vec_buf[used:, :] = jnp.zeros((vec_buf.shape[0] - used, 128), F32)
    vec_z[z] = vec_buf[...]

    def vecz_copy(i):
        return remote(vec_buf, vec_z.at[z], vecz_s.at[i], vecz_r.at[z], seq=lax.rem(z + 1 + i, nz))

    def vecz_arrival(i):
        peer = lax.rem(z + 1 + i, nz)
        return remote(vec_buf, vec_z.at[peer], vecz_s.at[i], vecz_r.at[peer], seq=peer)

    each(nz - 1, lambda i: vecz_copy(i).start())

    @pl.when(outer)
    def _():
        for n, item in early[half:]:
            up_copy(n, item).start()

    advance(max(0, len(steps) - 5))
    each(nz - 1, lambda i: vecz_arrival(i).wait_recv())
    summed = vec_z[0]
    for i in range(1, nz):
        summed = summed + vec_z[i]
    vec_own[...] = summed
    vec_all[me] = summed

    def vec_copy(i):
        return remote(vec_own, vec_all.at[me], vec_s.at[i], vec_r.at[me], fsdp=lax.rem(me + 1 + i, fs))

    def vec_arrival(i):
        peer = lax.rem(me + 1 + i, fs)
        return remote(vec_own, vec_all.at[peer], vec_s.at[i], vec_r.at[peer], fsdp=peer)

    each(fs - 1, lambda i: vec_copy(i).start())

    def gather_slot(s):
        pair_copy(s, k).wait_recv()
        own = g_buf[s, k, c].astype(F32) + pair_buf[s, k].astype(F32)

        def gather_in(i, acc):
            j = lax.rem(k + 1 + i, pairs)
            peer_arrival(s, j).wait_recv()
            return acc + recv_buf[s, j].astype(F32)

        own = lax.fori_loop(0, pairs - 1, gather_in, own).astype(BF16)
        for h in range(halves):
            i, n = halves * s + h, len(early) + halves * s + h
            own_buf[i] = own[h * own_buf.shape[1] : (h + 1) * own_buf.shape[1]]
            up = remote(own_buf.at[i], up_qkv.at[i], up_s.at[n], up_r.at[n], seq=mate)

            @pl.when(outer)
            def _(up=up):
                up.start()

    each(slots, gather_slot)
    advance(len(steps))
    steps.extend(plan(late))

    each(fs - 1, lambda i: vec_arrival(i).wait_recv())
    lane_from = lax.broadcasted_iota(jnp.int32, (256, 128), 0)
    lane_to = lax.broadcasted_iota(jnp.int32, (256, 128), 1)
    part, first, place = None, 0, 0
    for which, length in enumerate(lengths):
        block = length // fs
        for i in range(-(-block // 128)):
            offset = me * block + 128 * i
            row = first + offset // 128
            select = (lane_from == lane_to + lax.rem(offset, 128)).astype(F32)
            both = jnp.concatenate([vec_all[:, pl.ds(row, 1), :][:, 0], vec_all[:, pl.ds(row + 1, 1), :][:, 0]], axis=1)
            rows = lax.dot_general(
                both, select, (((1,), (0,)), ((), ())), precision=HIGHEST, preferred_element_type=F32
            )
            total_out[place : place + 1, :] = jnp.sum(rows, axis=0, keepdims=True)
            place += 1
            if which > 0:
                continue
            wide = min(128, block - i * 128)
            columns = slice(i * 128, i * 128 + wide)
            mod_rows = mod_t_ref[columns, :].astype(BF16).astype(F32)
            share = lax.dot_general(
                rows[:, :wide], mod_rows, (((1,), (0,)), ((), ())), precision=HIGHEST, preferred_element_type=F32
            )
            part = share if part is None else part + share
            outer_product = lax.dot_general(
                rows, cond_ref[...], (((0,), (0,)), ((), ())), precision=HIGHEST, preferred_element_type=F32
            )
            mod_w_out[columns, :] = outer_product[:wide]
        first += length // 128
    cond_send[...] = jnp.broadcast_to(part[:, None, :], cond_send.shape)

    def cond_copy(i):
        peer = lax.rem(me + 1 + i, fs)
        return remote(cond_send.at[peer], cond_recv.at[me], cond_s.at[i], cond_r.at[me], fsdp=peer)

    def cond_arrival(i):
        peer = lax.rem(me + 1 + i, fs)
        return remote(cond_send.at[peer], cond_recv.at[peer], cond_s.at[i], cond_r.at[peer], fsdp=peer)

    each(fs - 1, lambda i: cond_copy(i).start())
    advance(3)
    ff = up_out.shape[1]

    def write_pack(i):
        rows = pl.ds(i * tot_pack.shape[1], tot_pack.shape[1])
        up_out[rows, :] = tot_pack[i, :, :ff].astype(F32)
        out_out[rows, :] = tot_pack[i, :, ff:].astype(F32)

    def write_down(i):
        down_out[pl.ds(i * tot_down.shape[1], tot_down.shape[1]), :] = tot_down[i].astype(F32)

    @pl.when(outer)
    def _():
        for n, item in early:
            tot_copy(n, item).wait_recv()

    each(counts[0], write_pack)
    each(counts[1], write_down)
    for store in stores[1:]:
        store.start()
    advance(len(steps))
    cond_recv[me] = cond_send[me]
    each(fs - 1, lambda i: cond_arrival(i).wait_recv())
    cond_out[...] = jnp.sum(cond_recv[...], axis=0)

    @pl.when(outer)
    def _():
        for n, item in late:
            tot_copy(n, item).wait_recv()
        for n, item in chain:
            up_copy(n, item).wait_send()

    block = nz * HD
    for i in range(slots * halves):
        s, h = i // halves, i % halves
        rows = slice(h * tot_qkv.shape[1], (h + 1) * tot_qkv.shape[1])
        for p in range(3):
            columns = slice(p * width + s * block, p * width + (s + 1) * block)
            qkv_out[rows, columns] = tot_qkv[i, :, p * block : (p + 1) * block].astype(F32)

    @pl.when(inner)
    def _():
        for n, item in chain:
            twin_copy(n, item).wait_send()
            tot_copy(n, item).wait_send()

    def drain_peers(i):
        vec_copy(i).wait_send()
        cond_copy(i).wait_send()

    def drain_pairs(i):
        for s in range(slots):
            pair_copy(s, i).wait_send()

    def drain_sums(i):
        for s in range(slots):
            peer_copy(s, lax.rem(k + 1 + i, pairs)).wait_send()

    each(fs - 1, drain_peers)
    each(pairs, drain_pairs)
    each(pairs - 1, drain_sums)
    each(nz - 1, lambda i: vecz_copy(i).wait_send())
    for store in stores:
        store.wait()


def reduce_all(
    grad_rows, weights, attn_in, tokens, grad_hidden, vectors, sums, up_bias_sum, part_pack, part_down, mod_t, cond, fs, nz
):
    slots = grad_rows.shape[0]
    tok, width = tokens.shape
    shard = width // fs
    count = lambda a: 6 if a.shape[0] % 96 == 0 else 1
    counts = (count(part_pack), count(part_down))
    split = lambda a, n: a.reshape(n, a.shape[0] // n, a.shape[1])
    pack, down = split(part_pack, counts[0]), split(part_down, counts[1])
    pairs = fs // 2
    halves = 2 if shard % 32 == 0 else 1
    items = sum(counts) + slots * halves
    ff = up_bias_sum.size
    lengths = (6 * width, width, width, ff, width)
    rows = sum(lengths) // 128 + 2
    places = sum(-(-v // fs // 128) for v in lengths)
    vmem = pl.BlockSpec(memory_space=pltpu.VMEM)
    hbm = pl.BlockSpec(memory_space=pl.ANY)
    low = lambda *shape: pltpu.VMEM(shape, BF16)
    wide = lambda *shape: pltpu.VMEM(shape, F32)
    dma = lambda *shape: pltpu.SemaphoreType.DMA(shape)
    qkv_shape = (slots * halves, shard // halves, width)
    triple = [low(*pack.shape), low(*down.shape), low(*qkv_shape)]
    cols = grad_rows.shape[1] * grad_rows.shape[2]
    inputs_grad, qkv_sum, up_sum, out_sum, down_sum, total, mod_w, cond_grad = pl.pallas_call(
        partial(reduce_kernel, fs, nz, slots, counts, lengths),
        in_specs=[hbm] * 5 + [vmem] * 7,
        out_specs=[hbm, vmem, hbm, hbm, hbm, vmem, vmem, vmem],
        out_shape=[
            jax.ShapeDtypeStruct((tok, width), F32),
            jax.ShapeDtypeStruct((shard, 3 * width), F32),
            jax.ShapeDtypeStruct((shard, ff), F32),
            jax.ShapeDtypeStruct((shard, part_pack.shape[1] - ff), F32),
            jax.ShapeDtypeStruct(part_down.shape, F32),
            jax.ShapeDtypeStruct((places, 128), F32),
            jax.ShapeDtypeStruct(mod_t.shape, F32),
            jax.ShapeDtypeStruct((8, 128), F32),
        ],
        scratch_shapes=[
            wide(tok, width),
            wide(shard, ff),
            wide(shard, part_pack.shape[1] - ff),
            wide(*part_down.shape),
            dma(4),
            low(*grad_rows.shape),
            low(tok, width),
            dma(slots),
            low(slots, cols, tok),
            low(slots, width, cols),
            wide(tok, width),
            wide(tok, width),
            low(slots, pairs, 2, shard, width),
            low(slots, pairs, shard, width),
            low(slots, pairs, shard, width),
            low(slots, pairs, shard, width),
            low(*qkv_shape),
        ]
        + triple * 4
        + [
            wide(rows, 128),
            wide(nz, rows, 128),
            wide(rows, 128),
            wide(fs, rows, 128),
            wide(fs, 8, 128),
            wide(fs, 8, 128),
            dma(4),
            dma(slots, pairs),
            dma(slots, pairs),
            dma(slots, pairs),
            dma(slots, pairs),
        ]
        + [dma(items)] * 6
        + [dma(nz - 1), dma(nz), dma(fs - 1), dma(fs), dma(fs - 1), dma(fs)],
        compiler_params=pltpu.CompilerParams(vmem_limit_bytes=VMEM_LIMIT, collective_id=1, has_side_effects=True),
        cost_estimate=pl.CostEstimate(flops=12 * tok * width * cols, bytes_accessed=10**8, transcendentals=0),
        name="reduce_all",
    )(grad_rows, weights, attn_in, tokens, grad_hidden, vectors, sums, up_bias_sum, pack, down, mod_t, cond)
    blocks, place = [], 0
    for v in lengths:
        n = -(-v // fs // 128)
        blocks.append(total[place : place + n].reshape(-1)[: v // fs])
        place += n
    return inputs_grad, qkv_sum, up_sum, out_sum, down_sum, blocks, mod_w.T, cond_grad


def per_device(
    inputs,
    conditioning,
    cotangent,
    attn_gain,
    mlp_gain,
    qkv_weight,
    out_weight,
    up_weight,
    up_bias,
    down_weight,
    down_bias,
    mod_weight,
    mod_bias,
):
    n = lax.axis_size("seq")
    fs = lax.axis_size("fsdp")
    z = lax.axis_index("seq")
    tokens = inputs[0]
    tok, width = tokens.shape
    slots = H // n

    inv_freq = jnp.exp(-math.log(10000.0) * jnp.arange(HD // 2, dtype=F32) * (2.0 / HD))
    positions = jnp.arange(tok, dtype=F32)
    own_angles = inv_freq[:, None] * (positions + (z * tok).astype(F32))[None, :]
    starts = (jnp.arange(n) * tok).astype(F32)
    all_angles = inv_freq[None, :, None] * (positions[None, :] + starts[:, None])[:, None, :]
    cos_all, sin_all = jnp.cos(all_angles), jnp.sin(all_angles)

    x, heads_out, mixed, log_totals, qkv_slots, attn_in, vectors, up_bias_full, cond_low_all, pack, down = forward(
        qkv_weight,
        tokens,
        (attn_gain, mlp_gain, up_bias, down_bias),
        conditioning,
        mod_weight,
        mod_bias,
        jnp.cos(own_angles),
        jnp.sin(own_angles),
        (up_weight, out_weight, down_weight),
        fs,
        n,
    )
    w_pack, down_full = pack.reshape(width, -1), down.reshape(-1, width)
    output, grad_hidden, sums, up_bias_sum, g_down, g_pack, grad_mixed = middle(
        tokens, cotangent[0], vectors, up_bias_full, w_pack, down_full, mixed.reshape(width, tok)
    )
    grad_slots, part_pack, part_down = attend_back(
        x, grad_mixed.reshape(heads_out.shape), heads_out, log_totals, cos_all, sin_all, g_pack, g_down, fs
    )
    inputs_grad, qkv_weight_grad, up_sum, out_sum, down_sum, blocks, mod_weight_grad, cond_grad = reduce_all(
        grad_slots,
        qkv_slots.reshape(slots, width, -1),
        attn_in,
        tokens,
        grad_hidden,
        vectors,
        sums,
        up_bias_sum,
        part_pack,
        part_down,
        mod_weight.T,
        cond_low_all,
        fs,
        n,
    )
    mod_bias_grad, attn_gain_grad, mlp_gain_grad, up_bias_grad, down_bias_grad = blocks
    _, silu_pull = jax.vjp(jax.nn.silu, conditioning)
    conditioning_grad = silu_pull(cond_grad[:1])[0]
    return (
        output[None],
        inputs_grad[None],
        conditioning_grad,
        attn_gain_grad,
        mlp_gain_grad,
        qkv_weight_grad,
        out_sum,
        up_sum,
        up_bias_grad,
        down_sum,
        down_bias_grad,
        mod_weight_grad,
        mod_bias_grad,
    )


def solution(mesh):
    specs = (
        P("fsdp", "seq", None),
        P("fsdp", None),
        P("fsdp", "seq", None),
        P("fsdp"),
        P("fsdp"),
        P("fsdp", None),
        P("fsdp", None),
        P("fsdp", None),
        P("fsdp"),
        P("fsdp", None),
        P("fsdp"),
        P(None, "fsdp"),
        P("fsdp"),
    )
    out_specs = (specs[0], specs[0], specs[1]) + specs[3:]
    return jax.shard_map(per_device, mesh=mesh, in_specs=specs, out_specs=out_specs, check_vma=False)
```

```python
from functools import partial
import math

import jax
import jax.numpy as jnp
from jax import lax
from jax.experimental import pallas as pl
from jax.experimental.pallas import tpu as pltpu
from jax.sharding import PartitionSpec as P

H = 12
HD = 64
EPSILON = 1e-05
BF16 = jnp.bfloat16
F32 = jnp.float32
LOG2E = math.log2(math.e)
VMEM_LIMIT = 60 * 1024 * 1024


def mm(a, b, ca, cb):
    return lax.dot_general(a, b, (((ca,), (cb,)), ((), ())), preferred_element_type=F32)


def normalize(values):
    centre = jnp.mean(values, axis=-1, keepdims=True)
    shifted = values - centre
    variance = jnp.mean(shifted * shifted, axis=-1, keepdims=True)
    inv_std = lax.rsqrt(variance + EPSILON)
    return (shifted * inv_std, inv_std)


def norm_back(grad_hat, normed_hat, inv_std):
    mean_grad = jnp.mean(grad_hat, axis=-1, keepdims=True)
    mean_mixed = jnp.mean(grad_hat * normed_hat, axis=-1, keepdims=True)
    return inv_std * (grad_hat - mean_grad - normed_hat * mean_mixed)


MESH = pl.DeviceIdType.MESH
HIGHEST = lax.Precision.HIGHEST


def add_low(a, b):
    return (a.astype(F32) + b.astype(F32)).astype(BF16)


def remote(src, dst, s, r, **where):
    return pltpu.make_async_remote_copy(
        src_ref=src, dst_ref=dst, send_sem=s, recv_sem=r, device_id=where, device_id_type=MESH
    )


def each(count, body):
    lax.fori_loop(0, count, lambda i, _: (body(i), 0)[1], 0)


def greet(me, z, fs, nz):
    barrier = pltpu.get_barrier_semaphore()

    def hello_fsdp(i):
        peer = {"fsdp": lax.rem(me + 1 + i, fs)}
        pl.semaphore_signal(barrier, inc=1, device_id=peer, device_id_type=MESH)

    def hello_seq(i):
        peer = {"seq": lax.rem(z + 1 + i, nz)}
        pl.semaphore_signal(barrier, inc=1, device_id=peer, device_id_type=MESH)

    each(fs - 1, hello_fsdp)
    each(nz - 1, hello_seq)
    pl.semaphore_wait(barrier, fs + nz - 2)


def forward_kernel(fs, nz, slots, sub, *refs):
    (
        qkv_ref,
        tokens_hbm,
        attn_gain_ref,
        mlp_gain_ref,
        up_bias_ref,
        down_bias_ref,
        cond_ref,
        mod_w_ref,
        mod_b_ref,
        cos_ref,
        sin_ref,
        up_hbm,
        out_hbm,
        down_hbm,
        x_hbm,
        o_hbm,
        mixed_ref,
        lse_ref,
        w_hbm,
        attn_in_hbm,
        vec_ref,
        bias_ref,
        cond_out,
        pack_hbm,
        feed_hbm,
    ) = refs[:25]
    (
        x_ref,
        o_ref,
        w_ref,
        attn_in_ref,
        store_s,
        tokens_buf,
        up_buf,
        out_buf,
        down_buf,
        w_own,
        z_send,
        narrow,
        spread,
        mod_wide,
        small_send,
        small_all,
        mod_send,
        mod_recv,
        w_full,
        local_s,
        small_s,
        small_r,
        mod_s,
        mod_r,
        w_s,
        w_f,
        w_r,
        pack_own,
        feed_own,
        k_ref,
        x_s,
        x_r,
        o_s,
        o_r,
        p_s,
        p_f,
        p_r,
        own_s,
    ) = refs[25:]
    me = lax.axis_index("fsdp")
    z = lax.axis_index("seq")
    pairs = fs // 2
    k, c = me // 2, lax.rem(me, 2)
    partner = me + 1 - 2 * c
    tok, width = tokens_buf.shape
    shard = w_own.shape[1]
    ff = spread.shape[1]
    block = nz * HD

    fetch = ((tokens_hbm, tokens_buf), (up_hbm, up_buf), (out_hbm, out_buf), (down_hbm, down_buf))
    loads = [pltpu.make_async_copy(src, dst, local_s.at[i]) for i, (src, dst) in enumerate(fetch)]
    for load in loads:
        load.start()
    greet(me, z, fs, nz)

    narrow[...] = jnp.zeros_like(narrow)
    for i, piece in enumerate((attn_gain_ref, mlp_gain_ref, down_bias_ref)):
        narrow[i : i + 1, :shard] = piece[...].reshape(1, -1)
    spread[...] = jnp.zeros_like(spread)
    spread[0:1, : up_bias_ref.shape[0]] = up_bias_ref[...].reshape(1, -1)
    placed = pltpu.roll(narrow[...], me * shard, 1)
    for i in range(3):
        small_send[:, i * width : (i + 1) * width] = placed[i : i + 1]
    placed = pltpu.roll(spread[...], me * up_bias_ref.shape[0], 1)
    small_send[:, 3 * width : 3 * width + ff] = placed[0:1]
    small_send[:, 3 * width + ff :] = cond_ref[...]
    small_all[me] = small_send[...]

    def small_copy(i):
        return remote(small_send, small_all.at[me], small_s.at[i], small_r.at[me], fsdp=lax.rem(me + 1 + i, fs))

    def small_arrival(i):
        peer = lax.rem(me + 1 + i, fs)
        return remote(small_send, small_all.at[peer], small_s.at[i], small_r.at[peer], fsdp=peer)

    each(fs - 1, lambda i: small_copy(i).start())

    for s in range(slots):
        for part in range(3):
            columns = slice(part * width + s * block, part * width + (s + 1) * block)
            w_own[s, :, part * block : (part + 1) * block] = qkv_ref[:, columns].astype(BF16)
        w_ref[s, me] = w_own[s]

    def w_peer(s, i):
        j = lax.rem(k + 1 + i, pairs)
        return remote(w_own.at[s], w_ref.at[s, me], w_s.at[s, i], w_r.at[s, me], fsdp=2 * j + c)

    def w_partner(s):
        return remote(w_own.at[s], w_ref.at[s, me], w_s.at[s, pairs - 1], w_r.at[s, me], fsdp=partner)

    def w_arrival(s, j):
        return remote(w_own.at[s], w_ref.at[s, j], w_s.at[s, 0], w_r.at[s, j], fsdp=partner)

    def w_pass(s, i):
        j = 2 * lax.rem(k + 1 + i, pairs) + c
        return remote(w_ref.at[s, j], w_ref.at[s, j], w_f.at[s, i], w_r.at[s, j], fsdp=partner)

    def send_weight(s):
        each(pairs - 1, lambda i: w_peer(s, i).start())
        w_partner(s).start()

    def pass_weight(s):
        def step(i):
            w_arrival(s, 2 * lax.rem(k + 1 + i, pairs) + c).wait_recv()
            w_pass(s, i).start()

        each(pairs - 1, step)

    send_weight(0)

    each(fs - 1, lambda i: small_arrival(i).wait_recv())
    small_sum = jnp.sum(small_all[:, :, : 3 * width + ff], axis=0)
    cond_all = small_all[:, 0, 3 * width + ff :]
    cond_low = (cond_all / (1.0 + jnp.exp(-cond_all))).astype(BF16)
    cond_out[...] = cond_low.astype(F32)
    own_mod = mm(cond_low, mod_w_ref[...].astype(BF16), 1, 1) + mod_b_ref[...].reshape(1, -1)
    mod_wide[...] = jnp.zeros_like(mod_wide)
    mod_wide[:, : own_mod.shape[1]] = own_mod
    placed = pltpu.roll(mod_wide[...], me * own_mod.shape[1], 1)
    for i in range(fs):
        mod_send[i] = placed[i : i + 1]
    mod_recv[me] = mod_send[me]

    def mod_copy(i):
        peer = lax.rem(me + 1 + i, fs)
        return remote(mod_send.at[peer], mod_recv.at[me], mod_s.at[i], mod_r.at[me], fsdp=peer)

    def mod_arrival(i):
        peer = lax.rem(me + 1 + i, fs)
        return remote(mod_send.at[peer], mod_recv.at[peer], mod_s.at[i], mod_r.at[peer], fsdp=peer)

    each(fs - 1, lambda i: mod_copy(i).start())
    for s in range(1, slots):
        send_weight(s)

    attn_gain, mlp_gain, down_bias = (small_sum[:, i * width : (i + 1) * width] for i in range(3))
    for i in range(ff // width):
        bias_ref[i] = small_sum[:, (3 + i) * width : (4 + i) * width]
    for load in loads:
        load.wait()
    piece = min(256, tok)

    def normed_piece(i):
        rows = pl.ds(pl.multiple_of(i * piece, piece), piece)
        tokens_buf[rows, :] = normalize(tokens_buf[rows, :])[0] * attn_gain

    each(tok // piece, normed_piece)
    pass_weight(0)
    each(fs - 1, lambda i: mod_arrival(i).wait_recv())
    modulation = jnp.sum(mod_recv[...], axis=0)
    shift_attn, scale_attn, gate_attn, shift_mlp, scale_mlp, gate_mlp = (
        modulation[:, i * width : (i + 1) * width] for i in range(6)
    )
    kept = (gate_attn, shift_mlp, scale_mlp, gate_mlp, mlp_gain, down_bias, attn_gain, scale_attn)
    for i, v in enumerate(kept):
        vec_ref[i : i + 1, :] = v
    for i in range(tok // piece):
        rows = slice(i * piece, (i + 1) * piece)
        attn_in_ref[rows, :] = (tokens_buf[rows, :] * (1.0 + scale_attn) + shift_attn).astype(BF16)

    cosine, sine = cos_ref[...], sin_ref[...]
    half = HD // 2

    def project(s, out_ref):
        each(pairs, lambda j: w_arrival(s, 2 * j + 1 - c).wait_recv())
        if shard % 16 == 0:
            weight = w_ref[s].reshape(fs * shard, 3 * block)
        else:
            for i in range(fs):
                w_full[i * shard : (i + 1) * shard, :] = w_ref[s, i].astype(F32)
            weight = w_full[...].astype(BF16)
        rows = mm(weight, attn_in_ref[...], 0, 1).astype(BF16)
        for shard_of in range(nz):
            for part in range(3):
                base = (part * nz + shard_of) * HD
                if part == 2:
                    out_ref[shard_of, part * HD : (part + 1) * HD, :] = rows[base : base + HD]
                else:
                    a = rows[base : base + half].astype(F32)
                    b = rows[base + half : base + HD].astype(F32)
                    out_ref[shard_of, part * HD : part * HD + half, :] = (a * cosine - b * sine).astype(BF16)
                    out_ref[shard_of, part * HD + half : (part + 1) * HD, :] = (b * cosine + a * sine).astype(BF16)

    def x_copy(s, i):
        peer = lax.rem(z + 1 + i, nz)
        return remote(z_send.at[s, peer], x_ref.at[s, z], x_s.at[s, i], x_r.at[s, z], seq=peer)

    def x_arrival(s, i):
        peer = lax.rem(z + 1 + i, nz)
        return remote(z_send.at[s, peer], x_ref.at[s, peer], x_s.at[s, i], x_r.at[s, peer], seq=peer)

    def o_copy(s, i):
        peer = lax.rem(z + 1 + i, nz)
        return remote(o_ref.at[s, peer], mixed_ref.at[s, z], o_s.at[s, i], o_r.at[s, z], seq=peer)

    def o_arrival(s, i):
        peer = lax.rem(z + 1 + i, nz)
        return remote(o_ref.at[s, peer], mixed_ref.at[s, peer], o_s.at[s, i], o_r.at[s, peer], seq=peer)

    def send_slot(s):
        project(s, z_send.at[s])
        each(nz - 1, lambda i: x_copy(s, i).start())
        x_ref[s, z] = z_send[s, z]

    def next_slot(s):
        @pl.when(s > 0)
        def _():
            pass_weight(s)

        send_slot(s)

    each(slots, next_slot)
    results = ((w_ref, w_hbm), (attn_in_ref, attn_in_hbm), (x_ref, x_hbm), (o_ref, o_hbm))
    stores = [pltpu.make_async_copy(src, dst, store_s.at[i]) for i, (src, dst) in enumerate(results)]
    for store in stores[:2]:
        store.start()

    pack_own[:, :ff] = up_buf[...].astype(BF16)
    pack_own[:, ff:] = out_buf[...].astype(BF16)
    feed_own[...] = down_buf[...].astype(BF16)
    bulk = ((pack_own, pack_hbm), (feed_own, feed_hbm))

    def p_peer(a, i):
        j = lax.rem(k + 1 + i, pairs)
        own, whole = bulk[a]
        return remote(own, whole.at[me], p_s.at[a, i], p_r.at[a, me], fsdp=2 * j + c)

    def p_partner(a):
        own, whole = bulk[a]
        return remote(own, whole.at[me], p_s.at[a, pairs - 1], p_r.at[a, me], fsdp=partner)

    def p_arrival(a, j):
        own, whole = bulk[a]
        return remote(own, whole.at[j], p_s.at[a, 0], p_r.at[a, j], fsdp=partner)

    def p_pass(a, i):
        j = 2 * lax.rem(k + 1 + i, pairs) + c
        whole = bulk[a][1]
        return remote(whole.at[j], whole.at[j], p_f.at[a, i], p_r.at[a, j], fsdp=partner)

    def p_own(a):
        own, whole = bulk[a]
        return pltpu.make_async_copy(own, whole.at[me], own_s.at[a])

    for a in range(2):
        each(pairs - 1, lambda i: p_peer(a, i).start())
        p_partner(a).start()
        p_own(a).start()

    def pass_bulk(a):
        def step(i):
            p_arrival(a, 2 * lax.rem(k + 1 + i, pairs) + c).wait_recv()
            p_pass(a, i).start()

        each(pairs - 1, step)

    scale = LOG2E / math.sqrt(HD)
    part_width = tok // sub

    def soft(s):
        top = jnp.max(s, axis=0, keepdims=True) * scale
        p = jnp.exp2(s * scale - top)
        total = jnp.sum(p, axis=0, keepdims=True)
        return top, total, p.astype(BF16)

    def slot(s):
        each(nz - 1, lambda i: x_arrival(s, i).wait_recv())
        for shard_of in range(nz):
            k_ref[shard_of * tok : (shard_of + 1) * tok, :] = x_ref[s, shard_of, HD : 2 * HD, :].T

        def one_shard(i):
            step = lax.rem(z + 1 + i, nz)

            def score(j):
                q = x_ref[s, step, 0:HD, j * part_width : (j + 1) * part_width]
                return mm(k_ref[...], q, 1, 0)

            def mix(j, top, total, p):
                o = None
                for shard_of in range(nz):
                    part = mm(x_ref[s, shard_of, 2 * HD : 3 * HD, :], p[shard_of * tok : (shard_of + 1) * tok], 1, 0)
                    o = part if o is None else o + part
                o_ref[s, step, :, j * part_width : (j + 1) * part_width] = (o / total).astype(BF16)
                lse_ref[s, step, :, j * part_width : (j + 1) * part_width] = top + jnp.log2(total)

            scores = [score(0)]
            pending = None
            for j in range(sub):
                if j + 1 < sub:
                    scores.append(score(j + 1))
                done = soft(scores[j])
                if pending is not None:
                    mix(j - 1, *pending)
                pending = done
            mix(sub - 1, *pending)

            @pl.when(i < nz - 1)
            def _():
                o_copy(s, i).start()

        each(nz, one_shard)
        mixed_ref[s, z] = o_ref[s, z]

        @pl.when(s == slots - 2)
        def _():
            pass_bulk(0)

    each(slots, slot)
    for store in stores[2:]:
        store.start()
    pass_bulk(1)

    def drain_slots(s):
        each(nz - 1, lambda i: o_arrival(s, i).wait_recv())
        each(nz - 1, lambda i: o_copy(s, i).wait_send())
        each(nz - 1, lambda i: x_copy(s, i).wait_send())

    each(slots, drain_slots)
    for a in range(2):
        each(pairs, lambda j: p_arrival(a, 2 * j + 1 - c).wait_recv())
        each(pairs - 1, lambda i: p_peer(a, i).wait_send())
        each(pairs - 1, lambda i: p_pass(a, i).wait_send())
        p_partner(a).wait_send()
        p_own(a).wait()
    for store in stores:
        store.wait()

    def drain_peers(i):
        small_copy(i).wait_send()
        mod_copy(i).wait_send()

    def drain_weights(i):
        for s in range(slots):
            w_peer(s, i).wait_send()
            w_pass(s, i).wait_send()

    each(fs - 1, drain_peers)
    each(pairs - 1, drain_weights)
    for s in range(slots):
        w_partner(s).wait_send()


def forward(qkv_weight, tokens, gains, cond, mod_weight, mod_bias, cosine, sine, feed, fs, nz):
    slots = H // nz
    tok, width = tokens.shape
    shard = qkv_weight.shape[0]
    pairs = fs // 2
    up, out, down = feed
    ff = gains[2].shape[0] * fs
    vmem = pl.BlockSpec(memory_space=pltpu.VMEM)
    hbm = pl.BlockSpec(memory_space=pl.ANY)
    low = lambda *shape: pltpu.VMEM(shape, BF16)
    wide = lambda *shape: pltpu.VMEM(shape, F32)
    dma = lambda *shape: pltpu.SemaphoreType.DMA(shape)
    head_shape = (slots, nz, 3 * HD, tok)
    pack_shape = (shard, up.shape[1] + out.shape[1])
    length = nz * tok
    cols = 3 * nz * HD
    small = 3 * width + ff + cond.shape[-1]
    return pl.pallas_call(
        partial(forward_kernel, fs, nz, slots, 2),
        in_specs=[vmem, hbm] + [vmem] * 9 + [hbm] * 3,
        out_specs=[hbm, hbm, vmem, vmem, hbm, hbm, vmem, vmem, vmem, hbm, hbm],
        out_shape=[
            jax.ShapeDtypeStruct(head_shape, BF16),
            jax.ShapeDtypeStruct((slots, nz, HD, tok), BF16),
            jax.ShapeDtypeStruct((slots, nz, HD, tok), BF16),
            jax.ShapeDtypeStruct((slots, nz, 1, tok), F32),
            jax.ShapeDtypeStruct((slots, fs, shard, cols), BF16),
            jax.ShapeDtypeStruct((tok, width), BF16),
            jax.ShapeDtypeStruct((8, width), F32),
            jax.ShapeDtypeStruct((ff // width, 1, width), F32),
            jax.ShapeDtypeStruct((fs, cond.shape[-1]), F32),
            jax.ShapeDtypeStruct((fs, *pack_shape), BF16),
            jax.ShapeDtypeStruct((fs, *down.shape), BF16),
        ],
        scratch_shapes=[
            low(*head_shape),
            low(slots, nz, HD, tok),
            low(slots, fs, shard, cols),
            low(tok, width),
            dma(4),
            wide(tok, width),
            wide(*up.shape),
            wide(*out.shape),
            wide(*down.shape),
            low(slots, shard, cols),
            low(*head_shape),
            wide(8, width),
            wide(8, ff),
            wide(fs, 6 * width),
            wide(1, small),
            wide(fs, 1, small),
            wide(fs, 1, 6 * width),
            wide(fs, 1, 6 * width),
            wide(*((8, 128) if shard % 16 == 0 else (width, cols))),
            dma(4),
            dma(fs - 1),
            dma(fs),
            dma(fs - 1),
            dma(fs),
            dma(slots, pairs),
            dma(slots, pairs),
            dma(slots, fs),
            low(*pack_shape),
            low(*down.shape),
            low(length, HD),
            dma(slots, nz - 1),
            dma(slots, nz),
            dma(slots, nz - 1),
            dma(slots, nz),
            dma(2, pairs),
            dma(2, pairs),
            dma(2, fs),
            dma(2),
        ],
        compiler_params=pltpu.CompilerParams(vmem_limit_bytes=VMEM_LIMIT, collective_id=2, has_side_effects=True),
        cost_estimate=pl.CostEstimate(
            flops=16 * slots * length * length * HD, bytes_accessed=10**7, transcendentals=slots * length * length
        ),
        name="forward",
    )(
        qkv_weight,
        tokens,
        *gains,
        cond,
        mod_weight.T,
        mod_bias,
        cosine,
        sine,
        *feed,
    )


def attend_back_kernel(
    fs,
    n,
    slots,
    tok,
    sub,
    x_hbm,
    sent_ref,
    o_hbm,
    lse_ref,
    cos_hbm,
    sin_hbm,
    pack_hbm,
    down_hbm,
    out_ref,
    part_pack,
    part_down,
    x_ref,
    o_ref,
    cos_ref,
    sin_ref,
    load_s,
    own_pack,
    own_down,
    pair_pack,
    pair_down,
    recv_pack,
    recv_down,
    own_s,
    pair_s,
    pair_r,
    peer_s,
    peer_r,
    g_ref,
    d_ref,
    k_ref,
    v_ref,
    q_all,
    g_all,
    lse_all,
    centre_all,
    dq_ref,
    g_s,
    g_r,
    q_s,
    q_r,
    kv_s,
    kv_r,
):
    z = lax.axis_index("seq")
    half = HD // 2
    me = lax.axis_index("fsdp")
    pairs = fs // 2
    k, c = me // 2, lax.rem(me, 2)
    partner = me + 1 - 2 * c
    bulk = ((pack_hbm, own_pack, pair_pack, recv_pack, part_pack), (down_hbm, own_down, pair_down, recv_down, part_down))

    def own_load(a, j):
        return pltpu.make_async_copy(bulk[a][0].at[j, c], bulk[a][1].at[j], own_s.at[a, j])

    def pair_copy(a, j):
        return remote(bulk[a][0].at[j, 1 - c], bulk[a][2].at[j], pair_s.at[a, j], pair_r.at[a, j], fsdp=partner)

    def peer_copy(a, j):
        return remote(bulk[a][1].at[j], bulk[a][3].at[k], peer_s.at[a, j], peer_r.at[a, k], fsdp=2 * j + c)

    def peer_arrival(a, j):
        return remote(bulk[a][1].at[j], bulk[a][3].at[j], peer_s.at[a, j], peer_r.at[a, j], fsdp=2 * j + c)

    def forward_bulk(a):
        own, pair = bulk[a][1:3]

        def one(i):
            j = lax.rem(k + 1 + i, pairs)
            own_load(a, j).wait()
            pair_copy(a, j).wait_recv()
            own[j] = add_low(own[j], pair[j])
            peer_copy(a, j).start()

        each(pairs - 1, one)

    def finish_bulk(a):
        _, own, pair, recv, part = bulk[a]
        own_load(a, k).wait()
        pair_copy(a, k).wait_recv()
        each(pairs - 1, lambda i: peer_arrival(a, lax.rem(k + 1 + i, pairs)).wait_recv())
        height = part.shape[0]
        block = 32 if height % 32 == 0 else height

        def one(b):
            rows = pl.ds(b * block, block)
            total = own[k, rows].astype(F32) + pair[k, rows].astype(F32)
            for i in range(pairs - 1):
                total = total + recv[lax.rem(k + 1 + i, pairs), rows].astype(F32)
            part[rows, :] = total.astype(BF16)

        each(height // block, one)

    def drain_bulk(a):
        each(pairs, lambda j: pair_copy(a, j).wait_send())
        each(pairs - 1, lambda i: peer_copy(a, lax.rem(k + 1 + i, pairs)).wait_send())

    fetch = ((x_hbm, x_ref), (o_hbm, o_ref), (cos_hbm, cos_ref), (sin_hbm, sin_ref))
    loads = [pltpu.make_async_copy(src, dst, load_s.at[i]) for i, (src, dst) in enumerate(fetch)]
    for load in loads:
        load.start()
    for a in range(2):
        each(pairs, lambda j: own_load(a, j).start())
    greet(me, z, fs, n)

    def g_copy(s, i):
        peer = lax.rem(z + 1 + i, n)
        return remote(sent_ref.at[s, peer], g_ref.at[s, z], g_s.at[s, i], g_r.at[s, z], seq=peer)

    def g_arrival(s, i):
        peer = lax.rem(z + 1 + i, n)
        return remote(sent_ref.at[s, peer], g_ref.at[s, peer], g_s.at[s, i], g_r.at[s, peer], seq=peer)

    def part_copy(s, i, rows, send, recv, arrival):
        peer = lax.rem(z + 1 + i, n)
        slot = peer if arrival else z
        return remote(
            d_ref.at[s, peer, rows], out_ref.at[s, slot, rows], send.at[s, i], recv.at[s, slot], seq=peer
        )

    q_rows, kv_rows = pl.ds(0, HD), pl.ds(HD, 2 * HD)
    q_copy = lambda s, i, arrival=False: part_copy(s, i, q_rows, q_s, q_r, arrival)
    kv_copy = lambda s, i, arrival=False: part_copy(s, i, kv_rows, kv_s, kv_r, arrival)

    for s in range(slots):
        each(n - 1, lambda i: g_copy(s, i).start())
        g_ref[s, z] = sent_ref[s, z]
    for a in range(2):
        each(pairs, lambda i: pair_copy(a, lax.rem(k + 1 + i, pairs)).start())

    scale = LOG2E / math.sqrt(HD)
    width = tok // sub

    def turn_back(grad, cosine, sine):
        a, b = grad[:half], grad[half:]
        return (a * cosine + b * sine).astype(BF16), (b * cosine - a * sine).astype(BF16)

    def slot(s):
        for owner in range(n):
            cols = slice(owner * tok, (owner + 1) * tok)
            k_ref[cols, :] = x_ref[s, owner, HD : 2 * HD, :].T
            v_ref[cols, :] = x_ref[s, owner, 2 * HD : 3 * HD, :].T
            q_all[:, cols] = x_ref[s, owner, 0:HD, :]
            lse_all[:, cols] = lse_ref[s, owner]
        each(n - 1, lambda i: g_arrival(s, i).wait_recv())
        for owner in range(n):
            cols = slice(owner * tok, (owner + 1) * tok)
            g = g_ref[s, owner]
            g_all[:, cols] = g
            centre_all[:, cols] = jnp.sum(g.astype(F32) * o_ref[s, owner].astype(F32), axis=0, keepdims=True)
        dq_ref[...] = jnp.zeros_like(dq_ref)

        def shard(i):
            step = lax.rem(z + 1 + i, n)
            for j in range(sub):
                cols = slice(j * width, (j + 1) * width)
                rows = pl.ds(pl.multiple_of(step * tok + j * width, width), width)
                score = mm(k_ref[rows, :], q_all[...], 1, 0)
                dp = mm(v_ref[rows, :], g_all[...], 1, 0)
                p = jnp.exp2(score * scale - lse_all[...])
                p_low = p.astype(BF16)
                ds = (p * (dp - centre_all[...])).astype(BF16)
                dv = mm(g_all[...], p_low, 1, 1)
                dk = mm(q_all[...], ds, 1, 1) * (1.0 / math.sqrt(HD))
                dq_ref[...] += mm(x_ref[s, step, HD : 2 * HD, cols], ds, 1, 0)
                a, b = turn_back(dk, cos_ref[step, :, cols], sin_ref[step, :, cols])
                d_ref[s, step, HD : HD + half, cols] = a
                d_ref[s, step, HD + half : 2 * HD, cols] = b
                d_ref[s, step, 2 * HD : 3 * HD, cols] = dv.astype(BF16)

            @pl.when(i < n - 1)
            def _():
                kv_copy(s, i).start()

        each(n, shard)
        for owner in range(n):
            dq = dq_ref[:, owner * tok : (owner + 1) * tok] * (1.0 / math.sqrt(HD))
            a, b = turn_back(dq, cos_ref[owner], sin_ref[owner])
            d_ref[s, owner, 0:half, :] = a
            d_ref[s, owner, half:HD, :] = b
        each(n - 1, lambda i: q_copy(s, i).start())
        out_ref[s, z] = d_ref[s, z]

        @pl.when(s == 0)
        def _():
            for a in range(2):
                forward_bulk(a)

    for load in loads:
        load.wait()
    each(slots, slot)
    for a in range(2):
        finish_bulk(a)
        drain_bulk(a)

    def drain(s):
        def one(i):
            q_copy(s, i, True).wait_recv()
            kv_copy(s, i, True).wait_recv()
            g_copy(s, i).wait_send()
            q_copy(s, i).wait_send()
            kv_copy(s, i).wait_send()

        each(n - 1, one)

    each(slots, drain)


def attend_back(x, g, o, lse, cosine, sine, g_pack, g_down, fs):
    slots, n, _, tok = x.shape
    length = n * tok
    vmem, hbm = pl.BlockSpec(memory_space=pltpu.VMEM), pl.BlockSpec(memory_space=pl.ANY)
    dma = lambda *shape: pltpu.SemaphoreType.DMA(shape)
    pairs = fs // 2
    shards = [(v.shape[0] // fs, v.shape[1]) for v in (g_pack, g_down)]
    split = lambda v: v.reshape(pairs, 2, v.shape[0] // fs, v.shape[1])
    return pl.pallas_call(
        partial(attend_back_kernel, fs, n, slots, tok, 2),
        in_specs=[hbm, vmem, hbm, vmem] + [hbm] * 4,
        out_specs=[vmem] * 3,
        out_shape=[
            jax.ShapeDtypeStruct(x.shape, BF16),
            jax.ShapeDtypeStruct(shards[0], BF16),
            jax.ShapeDtypeStruct(shards[1], BF16),
        ],
        scratch_shapes=[pltpu.VMEM(x.shape, BF16), pltpu.VMEM(o.shape, BF16)]
        + [pltpu.VMEM(cosine.shape, F32)] * 2
        + [dma(4)]
        + [pltpu.VMEM((pairs, *shard), BF16) for shard in shards * 3]
        + [dma(2, pairs)] * 5
        + [
            pltpu.VMEM(g.shape, BF16),
            pltpu.VMEM(x.shape, BF16),
            pltpu.VMEM((length, HD), BF16),
            pltpu.VMEM((length, HD), BF16),
            pltpu.VMEM((HD, length), BF16),
            pltpu.VMEM((HD, length), BF16),
            pltpu.VMEM((1, length), F32),
            pltpu.VMEM((1, length), F32),
            pltpu.VMEM((HD, length), F32),
        ]
        + [dma(slots, n - 1), dma(slots, n)] * 3,
        compiler_params=pltpu.CompilerParams(vmem_limit_bytes=VMEM_LIMIT, collective_id=4, has_side_effects=True),
        cost_estimate=pl.CostEstimate(
            flops=40 * slots * length * length * HD, bytes_accessed=10**7, transcendentals=slots * length * length
        ),
        name="attend_back",
    )(x, g, o, lse, cosine, sine, split(g_pack), split(g_down))


GELU_C = math.sqrt(2.0 / math.pi)
GELU_A = 0.044715


def middle_kernel(
    blocks,
    tokens_hbm,
    cot_hbm,
    vec_ref,
    bias_ref,
    up_ref,
    down_ref,
    out_w_ref,
    mixed_ref,
    output_hbm,
    grad_hidden_hbm,
    sums_ref,
    bias_grad_ref,
    g_down_ref,
    g_pack_ref,
    grad_mixed_ref,
    attn_out_ref,
    mlp_in_ref,
    low_ref,
    back_ref,
    tokens_ref,
    cot_ref,
    output_ref,
    grad_hidden_ref,
    copy_s,
):
    j = pl.program_id(0)
    tok, width = tokens_ref.shape
    gate_attn, shift, scale, gate, gain, down_bias = (vec_ref[i : i + 1, :] for i in range(6))
    piece = min(256, tok)
    pieces = tok // piece

    @pl.when(j == 0)
    def _():
        fetch = ((tokens_hbm, tokens_ref), (cot_hbm, cot_ref))
        loads = [pltpu.make_async_copy(src, dst, copy_s.at[i]) for i, (src, dst) in enumerate(fetch)]
        for load in loads:
            load.start()
        attn_out_ref[...] = mm(mixed_ref[...], out_w_ref[...], 0, 0)
        for load in loads:
            load.wait()

        def prepare(i, _):
            rows = pl.ds(pl.multiple_of(i * piece, piece), piece)
            hidden = tokens_ref[rows, :] + gate_attn * attn_out_ref[rows, :]
            grad_hidden_ref[rows, :] = hidden
            hat, _ = normalize(hidden)
            mlp_in_ref[rows, :] = (hat * gain * (1.0 + scale) + shift).astype(BF16)
            low_ref[rows, :] = (gate * cot_ref[rows, :]).astype(BF16)
            return 0

        lax.fori_loop(0, pieces, prepare, 0)
        output_ref[...] = jnp.zeros_like(output_ref)
        back_ref[...] = jnp.zeros_like(back_ref)

    @pl.when(j < blocks)
    def _():
        mlp_in, low = mlp_in_ref[...], low_ref[...]
        x = mm(mlp_in, up_ref[...], 1, 0) + bias_ref[0]
        grad_act = mm(low, down_ref[...], 1, 1)
        square = x * x
        t = jnp.tanh(x * (GELU_C + GELU_C * GELU_A * square))
        half = 0.5 + 0.5 * t
        act = (x * half).astype(BF16)
        slope = half + x * (0.5 - 0.5 * t * t) * (GELU_C + 3.0 * GELU_C * GELU_A * square)
        grad_pre = grad_act * slope
        bias_grad_ref[0] = jnp.sum(grad_pre, axis=0, keepdims=True)
        pre_low = grad_pre.astype(BF16)
        output_ref[...] += mm(act, down_ref[...], 1, 0)
        back_ref[...] += mm(pre_low, up_ref[...], 1, 1)
        g_down_ref[...] = mm(act, low, 0, 0).astype(BF16)
        g_pack_ref[...] = mm(mlp_in, pre_low, 0, 0).astype(BF16)

    @pl.when(j == blocks)
    def _():
        def finish(i, sums):
            rows = pl.ds(pl.multiple_of(i * piece, piece), piece)
            cot = cot_ref[rows, :]
            branch = output_ref[rows, :] + down_bias
            hidden = grad_hidden_ref[rows, :]
            output_ref[rows, :] = hidden + gate * branch
            hat, inv = normalize(hidden)
            back = back_ref[rows, :]
            grad_hidden = cot + norm_back(back * ((1.0 + scale) * gain), hat, inv)
            grad_hidden_ref[rows, :] = grad_hidden
            low_ref[rows, :] = (gate_attn * grad_hidden).astype(BF16)
            adds = (grad_hidden * attn_out_ref[rows, :], back, back * hat, cot * branch, cot)
            return tuple(a + jnp.sum(v, axis=0, keepdims=True) for a, v in zip(sums, adds))

        zero = jnp.zeros((1, width), F32)
        sums = lax.fori_loop(0, pieces, finish, (zero,) * 5)
        for i in range(5):
            sums_ref[i : i + 1, :] = sums[i]
        results = ((output_ref, output_hbm), (grad_hidden_ref, grad_hidden_hbm))
        stores = [pltpu.make_async_copy(src, dst, copy_s.at[2 + i]) for i, (src, dst) in enumerate(results)]
        for store in stores:
            store.start()
        attn_low = low_ref[...]
        g_pack_ref[...] = mm(mixed_ref[...], attn_low, 1, 0).astype(BF16)
        grad_mixed_ref[...] = mm(out_w_ref[...], attn_low, 1, 1).astype(BF16)
        for store in stores:
            store.wait()


def middle(tokens, cot, vectors, up_bias, w_pack, w_down, mixed):
    tok, width = tokens.shape
    ff = w_down.shape[0]
    blocks = ff // width
    whole = lambda shape: pl.BlockSpec(shape, lambda j: (0,) * len(shape), pipeline_mode=pl.Buffered(1))
    fixed = lambda shape: pl.BlockSpec(shape, lambda j: (0,) * len(shape))
    last = blocks - 1
    flops = 2 * tok * width * (6 * ff + 3 * width)
    hbm = pl.BlockSpec(memory_space=pl.ANY)
    return pl.pallas_call(
        partial(middle_kernel, blocks),
        grid=(blocks + 1,),
        in_specs=[
            hbm,
            hbm,
            whole(vectors.shape),
            pl.BlockSpec((1, 1, width), lambda j: (jnp.minimum(j, last), 0, 0)),
            pl.BlockSpec((width, width), lambda j: (0, jnp.minimum(j, last))),
            pl.BlockSpec((width, width), lambda j: (jnp.minimum(j, last), 0)),
            pl.BlockSpec((width, width), lambda j: (0, blocks), pipeline_mode=pl.Buffered(1)),
        ]
        + [whole(mixed.shape)],
        out_specs=[
            hbm,
            hbm,
            fixed((8, width)),
            pl.BlockSpec((1, 1, width), lambda j: (jnp.minimum(j, last), 0, 0)),
            pl.BlockSpec((width, width), lambda j: (jnp.minimum(j, last), 0)),
            pl.BlockSpec((width, width), lambda j: (0, j)),
        ]
        + [fixed(mixed.shape)],
        out_shape=[
            jax.ShapeDtypeStruct((tok, width), F32),
            jax.ShapeDtypeStruct((tok, width), F32),
            jax.ShapeDtypeStruct((8, width), F32),
            jax.ShapeDtypeStruct((blocks, 1, width), F32),
            jax.ShapeDtypeStruct((ff, width), BF16),
            jax.ShapeDtypeStruct((width, ff + width), BF16),
        ]
        + [jax.ShapeDtypeStruct(mixed.shape, BF16)],
        scratch_shapes=[
            pltpu.VMEM((tok, width), F32),
            pltpu.VMEM((tok, width), BF16),
            pltpu.VMEM((tok, width), BF16),
            pltpu.VMEM((tok, width), F32),
        ]
        + [pltpu.VMEM((tok, width), F32)] * 4
        + [pltpu.SemaphoreType.DMA((4,))],
        compiler_params=pltpu.CompilerParams(vmem_limit_bytes=VMEM_LIMIT),
        cost_estimate=pl.CostEstimate(flops=flops, bytes_accessed=6 * ff * width * 2, transcendentals=tok * ff),
        name="middle",
    )(tokens, cot, vectors, up_bias, w_pack, w_down, w_pack, mixed)


def reduce_kernel(fs, nz, slots, counts, lengths, *refs):
    swapped_hbm, w_hbm, attn_in_hbm, tokens_hbm, hidden_hbm, vec_in_ref, sums_ref, up_bias_ref, *refs = refs
    bulk_refs, (mod_t_ref, cond_ref), refs = refs[:2], refs[2:4], refs[4:]
    inputs_hbm, qkv_out, up_hbm, out_hbm, down_hbm, total_out, mod_w_out, cond_out = refs[:8]
    (
        inputs_out,
        up_out,
        out_out,
        down_out,
        store_s,
        swapped_ref,
        attn_in_ref,
        swap_s,
        row_buf,
        w_buf,
        tokens_buf,
        hidden_buf,
        g_buf,
        pair_buf,
        sum_buf,
        recv_buf,
        own_buf,
        up_pack,
        up_down,
        up_qkv,
        part_pack,
        part_down,
        part_qkv,
        twin_pack,
        twin_down,
        twin_qkv,
        tot_pack,
        tot_down,
        tot_qkv,
        vec_buf,
        vec_z,
        vec_own,
        vec_all,
        cond_send,
        cond_recv,
        local_s,
        pair_s,
        pair_r,
        peer_s,
        peer_r,
        up_s,
        up_r,
        twin_s,
        twin_r,
        tot_s,
        tot_r,
        vecz_s,
        vecz_r,
        vec_s,
        vec_r,
        cond_s,
        cond_r,
    ) = refs[8:]
    me = lax.axis_index("fsdp")
    z = lax.axis_index("seq")
    pairs = fs // 2
    k, c = me // 2, lax.rem(me, 2)
    partner = me + 1 - 2 * c
    inner = jnp.logical_or(z == nz // 2 - 1, z == nz // 2)
    outer = jnp.logical_not(inner)
    twin = nz - 1 - z
    mate = z + 1 - 2 * lax.rem(z, 2)
    tok, width = tokens_buf.shape
    shard = g_buf.shape[3]
    groups = width // 128

    def swap_load(s):
        return pltpu.make_async_copy(swapped_hbm.at[s], swapped_ref.at[s], swap_s.at[s])

    first_load = pltpu.make_async_copy(attn_in_hbm, attn_in_ref, local_s.at[3])
    first_load.start()
    for s in range(slots):
        swap_load(s).start()
    fetch = ((w_hbm, w_buf), (tokens_hbm, tokens_buf), (hidden_hbm, hidden_buf))
    loads = [pltpu.make_async_copy(src, dst, local_s.at[i]) for i, (src, dst) in enumerate(fetch)]
    for load in loads:
        load.start()
    greet(me, z, fs, nz)

    bulk = [
        (src, up, part, other, tot, i)
        for src, up, part, other, tot, count in (
            (bulk_refs[0], up_pack, part_pack, twin_pack, tot_pack, counts[0]),
            (bulk_refs[1], up_down, part_down, twin_down, tot_down, counts[1]),
        )
        for i in range(count)
    ]
    halves = own_buf.shape[0] // slots
    last = [(own_buf, up_qkv, part_qkv, twin_qkv, tot_qkv, i) for i in range(slots * halves)]
    chain = list(enumerate(bulk + last))
    early, late = chain[: len(bulk)], chain[len(bulk) :]

    def up_copy(n, item):
        src, up, _, _, _, i = item
        return remote(src.at[i], up.at[i], up_s.at[n], up_r.at[n], seq=mate)

    def twin_copy(n, item):
        _, _, part, other, _, i = item
        return remote(part.at[i], other.at[i], twin_s.at[n], twin_r.at[n], seq=twin)

    def tot_copy(n, item):
        tot, i = item[4], item[5]
        return remote(tot.at[i], tot.at[i], tot_s.at[n], tot_r.at[n], seq=mate)

    def chain_in(n, item):
        src, up, part, _, _, i = item
        up_copy(n, item).wait_recv()
        part[i] = add_low(src[i], up[i])
        twin_copy(n, item).start()

    def chain_out(n, item):
        _, _, part, other, tot, i = item
        twin_copy(n, item).wait_recv()
        tot[i] = add_low(part[i], other[i])
        tot_copy(n, item).start()

    def plan(items):
        ahead = 2
        steps = [(chain_in, item) for item in items[:ahead]]
        for before, item in zip(items, items[ahead:]):
            steps += [(chain_in, item), (chain_out, before)]
        return steps + [(chain_out, item) for item in items[-ahead:]]

    steps = plan(early)

    def advance(count):
        todo = [steps.pop(0) for _ in range(min(count, len(steps)))]
        if todo:

            @pl.when(inner)
            def _():
                for step, (n, item) in todo:
                    step(n, item)

    half = len(early) - 1

    @pl.when(outer)
    def _():
        for n, item in early[:half]:
            up_copy(n, item).start()

    def pair_copy(s, j):
        return remote(g_buf.at[s, j, 1 - c], pair_buf.at[s, j], pair_s.at[s, j], pair_r.at[s, j], fsdp=partner)

    def peer_copy(s, j):
        return remote(sum_buf.at[s, j], recv_buf.at[s, k], peer_s.at[s, j], peer_r.at[s, k], fsdp=2 * j + c)

    def peer_arrival(s, j):
        return remote(sum_buf.at[s, j], recv_buf.at[s, j], peer_s.at[s, j], peer_r.at[s, j], fsdp=2 * j + c)

    first_load.wait()

    def project_grad(s):
        swap_load(s).wait()
        for head in range(nz):
            for p in range(3):
                base = (p * nz + head) * HD
                row_buf[s, base : base + HD, :] = swapped_ref[s, head, p * HD : (p + 1) * HD, :]
        grad = mm(attn_in_ref[...], row_buf[s], 0, 1).astype(BF16)
        for i in range(fs):
            g_buf[s, i // 2, i % 2] = grad[i * shard : (i + 1) * shard]
        each(pairs, lambda i: pair_copy(s, lax.rem(k + 1 + i, pairs)).start())


    def forward(s, i):
        j = lax.rem(k + 1 + i, pairs)
        pair_copy(s, j).wait_recv()
        sum_buf[s, j] = add_low(g_buf[s, j, c], pair_buf[s, j])
        peer_copy(s, j).start()

    def stage(s):
        @pl.when(s < slots)
        def _():
            project_grad(s)

        @pl.when(s > 0)
        def _():
            each(pairs - 1, lambda i: forward(s - 1, i))

    each(slots + 1, stage)
    advance(3)
    for load in loads:
        load.wait()

    scale_mlp, gate_mlp, mlp_gain = (vec_in_ref[i : i + 1, :] for i in (2, 3, 4))
    attn_gain, scale_attn = (vec_in_ref[i : i + 1, :] for i in (6, 7))
    piece = min(256, tok)

    def norm_piece(i, kept):
        back_sum, hat_sum = kept
        rows = pl.ds(pl.multiple_of(i * piece, piece), piece)
        grad = None
        for s in range(slots):
            part = mm(row_buf[s, :, rows], w_buf[s], 0, 1)
            grad = part if grad is None else grad + part
        hat, inv = normalize(tokens_buf[rows, :])
        scaled = grad * ((1.0 + scale_attn) * attn_gain)
        inputs_out[rows, :] = hidden_buf[rows, :] + norm_back(scaled, hat, inv)
        back_sum = back_sum + jnp.sum(grad, axis=0, keepdims=True)
        hat_sum = hat_sum + jnp.sum(grad * hat, axis=0, keepdims=True)
        return back_sum, hat_sum

    zero = jnp.zeros((1, width), F32)
    kept = (zero, zero)
    for i in range(tok // piece):
        kept = norm_piece(i, kept)
        advance(4)
    back_sum, hat_sum = kept
    results = ((inputs_out, inputs_hbm), (up_out, up_hbm), (out_out, out_hbm), (down_out, down_hbm))
    stores = [pltpu.make_async_copy(src, dst, store_s.at[i]) for i, (src, dst) in enumerate(results)]
    stores[0].start()

    sums = [sums_ref[i : i + 1, :] for i in range(5)]
    vectors = [back_sum, hat_sum * attn_gain, sums[0], sums[1], sums[2] * mlp_gain, sums[3]]
    vectors += [hat_sum * (1.0 + scale_attn), sums[2] * (1.0 + scale_mlp)]
    vectors += [up_bias_ref[i] for i in range(up_bias_ref.shape[0])]
    vectors.append(sums[4] * gate_mlp)
    for p, v in enumerate(vectors):
        for i in range(groups):
            vec_buf[p * groups + i : p * groups + i + 1, :] = v[:, i * 128 : (i + 1) * 128]
    used = len(vectors) * groups
    vec_buf[used:, :] = jnp.zeros((vec_buf.shape[0] - used, 128), F32)
    vec_z[z] = vec_buf[...]

    def vecz_copy(i):
        return remote(vec_buf, vec_z.at[z], vecz_s.at[i], vecz_r.at[z], seq=lax.rem(z + 1 + i, nz))

    def vecz_arrival(i):
        peer = lax.rem(z + 1 + i, nz)
        return remote(vec_buf, vec_z.at[peer], vecz_s.at[i], vecz_r.at[peer], seq=peer)

    each(nz - 1, lambda i: vecz_copy(i).start())

    @pl.when(outer)
    def _():
        for n, item in early[half:]:
            up_copy(n, item).start()

    advance(max(0, len(steps) - 5))
    each(nz - 1, lambda i: vecz_arrival(i).wait_recv())
    summed = vec_z[0]
    for i in range(1, nz):
        summed = summed + vec_z[i]
    vec_own[...] = summed
    vec_all[me] = summed

    def vec_copy(i):
        return remote(vec_own, vec_all.at[me], vec_s.at[i], vec_r.at[me], fsdp=lax.rem(me + 1 + i, fs))

    def vec_arrival(i):
        peer = lax.rem(me + 1 + i, fs)
        return remote(vec_own, vec_all.at[peer], vec_s.at[i], vec_r.at[peer], fsdp=peer)

    each(fs - 1, lambda i: vec_copy(i).start())

    def gather_slot(s):
        pair_copy(s, k).wait_recv()
        own = g_buf[s, k, c].astype(F32) + pair_buf[s, k].astype(F32)

        def gather_in(i, acc):
            j = lax.rem(k + 1 + i, pairs)
            peer_arrival(s, j).wait_recv()
            return acc + recv_buf[s, j].astype(F32)

        own = lax.fori_loop(0, pairs - 1, gather_in, own).astype(BF16)
        for h in range(halves):
            i, n = halves * s + h, len(early) + halves * s + h
            own_buf[i] = own[h * own_buf.shape[1] : (h + 1) * own_buf.shape[1]]
            up = remote(own_buf.at[i], up_qkv.at[i], up_s.at[n], up_r.at[n], seq=mate)

            @pl.when(outer)
            def _(up=up):
                up.start()

    each(slots, gather_slot)
    advance(len(steps))
    steps.extend(plan(late))

    each(fs - 1, lambda i: vec_arrival(i).wait_recv())
    lane_from = lax.broadcasted_iota(jnp.int32, (256, 128), 0)
    lane_to = lax.broadcasted_iota(jnp.int32, (256, 128), 1)
    part, first, place = None, 0, 0
    for which, length in enumerate(lengths):
        block = length // fs
        for i in range(-(-block // 128)):
            offset = me * block + 128 * i
            row = first + offset // 128
            select = (lane_from == lane_to + lax.rem(offset, 128)).astype(F32)
            both = jnp.concatenate([vec_all[:, pl.ds(row, 1), :][:, 0], vec_all[:, pl.ds(row + 1, 1), :][:, 0]], axis=1)
            rows = lax.dot_general(
                both, select, (((1,), (0,)), ((), ())), precision=HIGHEST, preferred_element_type=F32
            )
            total_out[place : place + 1, :] = jnp.sum(rows, axis=0, keepdims=True)
            place += 1
            if which > 0:
                continue
            wide = min(128, block - i * 128)
            columns = slice(i * 128, i * 128 + wide)
            mod_rows = mod_t_ref[columns, :].astype(BF16).astype(F32)
            share = lax.dot_general(
                rows[:, :wide], mod_rows, (((1,), (0,)), ((), ())), precision=HIGHEST, preferred_element_type=F32
            )
            part = share if part is None else part + share
            outer_product = lax.dot_general(
                rows, cond_ref[...], (((0,), (0,)), ((), ())), precision=HIGHEST, preferred_element_type=F32
            )
            mod_w_out[columns, :] = outer_product[:wide]
        first += length // 128
    cond_send[...] = jnp.broadcast_to(part[:, None, :], cond_send.shape)

    def cond_copy(i):
        peer = lax.rem(me + 1 + i, fs)
        return remote(cond_send.at[peer], cond_recv.at[me], cond_s.at[i], cond_r.at[me], fsdp=peer)

    def cond_arrival(i):
        peer = lax.rem(me + 1 + i, fs)
        return remote(cond_send.at[peer], cond_recv.at[peer], cond_s.at[i], cond_r.at[peer], fsdp=peer)

    each(fs - 1, lambda i: cond_copy(i).start())
    advance(3)
    ff = up_out.shape[1]

    def write_pack(i):
        rows = pl.ds(i * tot_pack.shape[1], tot_pack.shape[1])
        up_out[rows, :] = tot_pack[i, :, :ff].astype(F32)
        out_out[rows, :] = tot_pack[i, :, ff:].astype(F32)

    def write_down(i):
        down_out[pl.ds(i * tot_down.shape[1], tot_down.shape[1]), :] = tot_down[i].astype(F32)

    @pl.when(outer)
    def _():
        for n, item in early:
            tot_copy(n, item).wait_recv()

    each(counts[0], write_pack)
    each(counts[1], write_down)
    for store in stores[1:]:
        store.start()
    advance(len(steps))
    cond_recv[me] = cond_send[me]
    each(fs - 1, lambda i: cond_arrival(i).wait_recv())
    cond_out[...] = jnp.sum(cond_recv[...], axis=0)

    @pl.when(outer)
    def _():
        for n, item in late:
            tot_copy(n, item).wait_recv()
        for n, item in chain:
            up_copy(n, item).wait_send()

    block = nz * HD
    for i in range(slots * halves):
        s, h = i // halves, i % halves
        rows = slice(h * tot_qkv.shape[1], (h + 1) * tot_qkv.shape[1])
        for p in range(3):
            columns = slice(p * width + s * block, p * width + (s + 1) * block)
            qkv_out[rows, columns] = tot_qkv[i, :, p * block : (p + 1) * block].astype(F32)

    @pl.when(inner)
    def _():
        for n, item in chain:
            twin_copy(n, item).wait_send()
            tot_copy(n, item).wait_send()

    def drain_peers(i):
        vec_copy(i).wait_send()
        cond_copy(i).wait_send()

    def drain_pairs(i):
        for s in range(slots):
            pair_copy(s, i).wait_send()

    def drain_sums(i):
        for s in range(slots):
            peer_copy(s, lax.rem(k + 1 + i, pairs)).wait_send()

    each(fs - 1, drain_peers)
    each(pairs, drain_pairs)
    each(pairs - 1, drain_sums)
    each(nz - 1, lambda i: vecz_copy(i).wait_send())
    for store in stores:
        store.wait()


def reduce_all(
    grad_rows, weights, attn_in, tokens, grad_hidden, vectors, sums, up_bias_sum, part_pack, part_down, mod_t, cond, fs, nz
):
    slots = grad_rows.shape[0]
    tok, width = tokens.shape
    shard = width // fs
    count = lambda a: 6 if a.shape[0] % 96 == 0 else 1
    counts = (count(part_pack), count(part_down))
    split = lambda a, n: a.reshape(n, a.shape[0] // n, a.shape[1])
    pack, down = split(part_pack, counts[0]), split(part_down, counts[1])
    pairs = fs // 2
    halves = 2 if shard % 32 == 0 else 1
    items = sum(counts) + slots * halves
    ff = up_bias_sum.size
    lengths = (6 * width, width, width, ff, width)
    rows = sum(lengths) // 128 + 2
    places = sum(-(-v // fs // 128) for v in lengths)
    vmem = pl.BlockSpec(memory_space=pltpu.VMEM)
    hbm = pl.BlockSpec(memory_space=pl.ANY)
    low = lambda *shape: pltpu.VMEM(shape, BF16)
    wide = lambda *shape: pltpu.VMEM(shape, F32)
    dma = lambda *shape: pltpu.SemaphoreType.DMA(shape)
    qkv_shape = (slots * halves, shard // halves, width)
    triple = [low(*pack.shape), low(*down.shape), low(*qkv_shape)]
    cols = grad_rows.shape[1] * grad_rows.shape[2]
    inputs_grad, qkv_sum, up_sum, out_sum, down_sum, total, mod_w, cond_grad = pl.pallas_call(
        partial(reduce_kernel, fs, nz, slots, counts, lengths),
        in_specs=[hbm] * 5 + [vmem] * 7,
        out_specs=[hbm, vmem, hbm, hbm, hbm, vmem, vmem, vmem],
        out_shape=[
            jax.ShapeDtypeStruct((tok, width), F32),
            jax.ShapeDtypeStruct((shard, 3 * width), F32),
            jax.ShapeDtypeStruct((shard, ff), F32),
            jax.ShapeDtypeStruct((shard, part_pack.shape[1] - ff), F32),
            jax.ShapeDtypeStruct(part_down.shape, F32),
            jax.ShapeDtypeStruct((places, 128), F32),
            jax.ShapeDtypeStruct(mod_t.shape, F32),
            jax.ShapeDtypeStruct((8, 128), F32),
        ],
        scratch_shapes=[
            wide(tok, width),
            wide(shard, ff),
            wide(shard, part_pack.shape[1] - ff),
            wide(*part_down.shape),
            dma(4),
            low(*grad_rows.shape),
            low(tok, width),
            dma(slots),
            low(slots, cols, tok),
            low(slots, width, cols),
            wide(tok, width),
            wide(tok, width),
            low(slots, pairs, 2, shard, width),
            low(slots, pairs, shard, width),
            low(slots, pairs, shard, width),
            low(slots, pairs, shard, width),
            low(*qkv_shape),
        ]
        + triple * 4
        + [
            wide(rows, 128),
            wide(nz, rows, 128),
            wide(rows, 128),
            wide(fs, rows, 128),
            wide(fs, 8, 128),
            wide(fs, 8, 128),
            dma(4),
            dma(slots, pairs),
            dma(slots, pairs),
            dma(slots, pairs),
            dma(slots, pairs),
        ]
        + [dma(items)] * 6
        + [dma(nz - 1), dma(nz), dma(fs - 1), dma(fs), dma(fs - 1), dma(fs)],
        compiler_params=pltpu.CompilerParams(vmem_limit_bytes=VMEM_LIMIT, collective_id=1, has_side_effects=True),
        cost_estimate=pl.CostEstimate(flops=12 * tok * width * cols, bytes_accessed=10**8, transcendentals=0),
        name="reduce_all",
    )(grad_rows, weights, attn_in, tokens, grad_hidden, vectors, sums, up_bias_sum, pack, down, mod_t, cond)
    blocks, place = [], 0
    for v in lengths:
        n = -(-v // fs // 128)
        blocks.append(total[place : place + n].reshape(-1)[: v // fs])
        place += n
    return inputs_grad, qkv_sum, up_sum, out_sum, down_sum, blocks, mod_w.T, cond_grad


def per_device(
    inputs,
    conditioning,
    cotangent,
    attn_gain,
    mlp_gain,
    qkv_weight,
    out_weight,
    up_weight,
    up_bias,
    down_weight,
    down_bias,
    mod_weight,
    mod_bias,
):
    n = lax.axis_size("seq")
    fs = lax.axis_size("fsdp")
    z = lax.axis_index("seq")
    tokens = inputs[0]
    tok, width = tokens.shape
    slots = H // n

    inv_freq = jnp.exp(-math.log(10000.0) * jnp.arange(HD // 2, dtype=F32) * (2.0 / HD))
    positions = jnp.arange(tok, dtype=F32)
    own_angles = inv_freq[:, None] * (positions + (z * tok).astype(F32))[None, :]
    starts = (jnp.arange(n) * tok).astype(F32)
    all_angles = inv_freq[None, :, None] * (positions[None, :] + starts[:, None])[:, None, :]
    cos_all, sin_all = jnp.cos(all_angles), jnp.sin(all_angles)

    x, heads_out, mixed, log_totals, qkv_slots, attn_in, vectors, up_bias_full, cond_low_all, pack, down = forward(
        qkv_weight,
        tokens,
        (attn_gain, mlp_gain, up_bias, down_bias),
        conditioning,
        mod_weight,
        mod_bias,
        jnp.cos(own_angles),
        jnp.sin(own_angles),
        (up_weight, out_weight, down_weight),
        fs,
        n,
    )
    w_pack, down_full = pack.reshape(width, -1), down.reshape(-1, width)
    output, grad_hidden, sums, up_bias_sum, g_down, g_pack, grad_mixed = middle(
        tokens, cotangent[0], vectors, up_bias_full, w_pack, down_full, mixed.reshape(width, tok)
    )
    grad_slots, part_pack, part_down = attend_back(
        x, grad_mixed.reshape(heads_out.shape), heads_out, log_totals, cos_all, sin_all, g_pack, g_down, fs
    )
    inputs_grad, qkv_weight_grad, up_sum, out_sum, down_sum, blocks, mod_weight_grad, cond_grad = reduce_all(
        grad_slots,
        qkv_slots.reshape(slots, width, -1),
        attn_in,
        tokens,
        grad_hidden,
        vectors,
        sums,
        up_bias_sum,
        part_pack,
        part_down,
        mod_weight.T,
        cond_low_all,
        fs,
        n,
    )
    mod_bias_grad, attn_gain_grad, mlp_gain_grad, up_bias_grad, down_bias_grad = blocks
    _, silu_pull = jax.vjp(jax.nn.silu, conditioning)
    conditioning_grad = silu_pull(cond_grad[:1])[0]
    return (
        output[None],
        inputs_grad[None],
        conditioning_grad,
        attn_gain_grad,
        mlp_gain_grad,
        qkv_weight_grad,
        out_sum,
        up_sum,
        up_bias_grad,
        down_sum,
        down_bias_grad,
        mod_weight_grad,
        mod_bias_grad,
    )


def solution(mesh):
    specs = (
        P("fsdp", "seq", None),
        P("fsdp", None),
        P("fsdp", "seq", None),
        P("fsdp"),
        P("fsdp"),
        P("fsdp", None),
        P("fsdp", None),
        P("fsdp", None),
        P("fsdp"),
        P("fsdp", None),
        P("fsdp"),
        P(None, "fsdp"),
        P("fsdp"),
    )
    out_specs = (specs[0], specs[0], specs[1]) + specs[3:]
    return jax.shard_map(per_device, mesh=mesh, in_specs=specs, out_specs=out_specs, check_vma=False)
```
